32 devices in a mesh: twin: 2 (over x), dp: 16 (over z, y, core).
Axes of the slice: x: 2, y: 2, z: 4, core: 2. Of those that a mesh axis runs over, the one named last changes fastest.
Arguments:
- hidden: bfloat16 [64, 512, 768], P(('twin', 'dp')), may hold values from -6 to 6
- segment_ids: int32 [64, 512], P(('twin', 'dp')), may hold values from 0 to 7, never falling along the last dimension, each value on 1 to 128 neighbouring positions
- targets: int32 [256], replicated, may hold values from 0 to 255, each once
- w_qkv: bfloat16 [768, 2304], replicated, may hold values from -0.21875 to 0.21875
- b_query: bfloat16 [768], replicated, may hold values from -3 to 3
- b_value: bfloat16 [768], replicated, may hold values from -3 to 3
- w_out: bfloat16 [768, 768], replicated, may hold values from -1.25 to 1.25
- b_out: bfloat16 [768], replicated, may hold values from -3 to 3
- ln1_gain: bfloat16 [768], replicated, may hold values from 0.5 to 1.5
- ln1_bias: bfloat16 [768], replicated, may hold values from -2 to 2
- w_in: bfloat16 [768, 3072], replicated, may hold values from -0.21875 to 0.21875
- b_in: bfloat16 [3072], replicated, may hold values from -3 to 3
- w_down: bfloat16 [3072, 768], replicated, may hold values from -0.109375 to 0.109375
- b_down: bfloat16 [768], replicated, may hold values from -3 to 3
- ln2_gain: bfloat16 [768], replicated, may hold values from 0.5 to 1.5
- ln2_bias: bfloat16 [768], replicated, may hold values from -0.29882812 to 0.29882812
Outputs:
- losses: float32 [256], P(('twin', 'dp'))
- hidden_grad: bfloat16 [64, 512, 768], P(('twin', 'dp'))
- grad_w_qkv: float32 [768, 2304], P('dp')
- grad_b_query: float32 [768], P('dp')
- grad_b_value: float32 [768], P('dp')
- grad_w_out: float32 [768, 768], P('dp')
- grad_b_out: float32 [768], P('dp')
- grad_ln1_gain: float32 [768], P('dp')
- grad_ln1_bias: float32 [768], P('dp')
- grad_w_in: float32 [768, 3072], P('dp')
- grad_b_in: float32 [3072], P('dp')
- grad_w_down: float32 [3072, 768], P('dp')
- grad_b_down: float32 [768], P('dp')
- grad_ln2_gain: float32 [768], P('dp')
- grad_ln2_bias: float32 [768], P('dp')
The draws below stay inside these ranges and needn't reach their ends.
Inputs may be any that keep to these rules, and one draw needn't show every extreme that they name: `segment_ids`: in each row the ids never fall; every id of 0 to 7 occurs, on 1 to 128 tokens. `targets`: every positive is the target of exactly one anchor.
All inputs are finite; a program needn't handle non-finite values.
Results may differ from the reference program's by a relative error of at most 0.012.
Values may be sent and summed in bfloat16 or wider, within the bound.
No kernel may reach another device: no remote copies, remote signals or barrier semaphores. Data moves between devices by JAX's collectives and lax.ppermute only.
A program may use at most 192 MiB of HBM per device.

```python
import math
import jax
import jax.numpy as jnp
import numpy as np
from jax import lax

D = 768
HEADS = 12
HEAD_DIM = 64
FF = 3072
LEN = 512
SEG = 8
SENT_MOST = 128
ROWS = 64
ANCHORS = 256


def block_levels(own_key, dims, shards, smallest, largest):
    def one(position, parts):
        steps = jax.random.uniform(jax.random.fold_in(jax.random.fold_in(own_key, 6), position), (parts,), jnp.float32, smallest / len(shards), largest / len(shards))
        return jnp.repeat(jnp.exp(steps), dims[position] // parts).reshape((-1,) + (1,) * (len(dims) - position - 1))

    level = one(*shards[0])
    for cut in shards[1:]:
        level = level * one(*cut)
    return level


def split_up(amount, total, limit, lean):
    loads = [(1 << 20) // math.isqrt(rank ** lean) + 1 for rank in range(2, amount + 1)]
    surplus, holding = total - limit - (amount - 1), [1] * (amount - 1)
    while surplus > 0:
        candidates = [i for i in range(amount - 1) if holding[i] < limit]
        whole, budget = sum([loads[i] for i in candidates]), surplus
        for i in candidates:
            more = min(limit - holding[i], max(1, budget * loads[i] // whole), surplus)
            holding[i] = holding[i] + more
            surplus = surplus - more
    return np.array([limit] + holding)


def ragged_sizes(rng, count, total, bound, lean):
    if count == 2:
        one = jax.random.randint(rng, (), max(1, total - bound), min(bound, total - 1) + 1)
        return jnp.stack([one, total - one])
    tallies = jnp.asarray(split_up(count, total, bound, lean), jnp.int32)
    twos = (count - 1) // 2
    donor, receiver = tallies[1:1 + 2 * twos:2], tallies[2:2 + 2 * twos:2]
    margin = jnp.minimum(donor - 1, bound - receiver)
    passed = jax.random.randint(jax.random.fold_in(rng, 1), (twos,), 0, 1 << 20) % (margin + 1)
    tallies = tallies.at[1:1 + 2 * twos:2].set(donor - passed).at[2:2 + 2 * twos:2].set(receiver + passed)
    return tallies[jax.random.permutation(jax.random.fold_in(rng, 2), count)]


def noise(rng, dims, deviation, limit, cuts=(), kind=jnp.bfloat16):
    values = jax.random.normal(rng, dims, jnp.float32) * deviation
    if len(cuts) > 0:
        values = block_levels(rng, dims, cuts, -0.22, 0.18) * values
    return jnp.clip(values, min=-limit, max=limit).astype(kind)


def setup_inputs(seed: int = 0) -> dict:
    key_list = jax.random.split(jax.random.key(seed), 17)
    hidden = noise(key_list[0], (ROWS, LEN, D), 1.0, 6.0, ((0, 32),))
    segment_ids = jax.vmap(lambda own: jnp.searchsorted(jnp.cumsum(ragged_sizes(own, SEG, LEN, SENT_MOST, 1)), jnp.arange(LEN), side="right"))(jax.random.split(key_list[1], ROWS)).reshape((ROWS, LEN)).astype(jnp.int32)
    targets = jax.random.permutation(key_list[2], ANCHORS).astype(jnp.int32)
    w_qkv = noise(key_list[3], (D, 3 * D), D ** -0.5, 0.21875)
    b_query = noise(key_list[4], (D,), 0.5, 3.0)
    b_value = noise(key_list[5], (D,), 0.5, 3.0)
    w_out = noise(key_list[6], (D, D), (D // 32) ** -0.5, 1.25)
    b_out = noise(key_list[7], (D,), 0.5, 3.0)
    ln1_gain = jnp.clip(1.0 + 0.1 * jax.random.normal(key_list[8], (D,), jnp.float32), 0.5, 1.5).astype(jnp.bfloat16)
    ln1_bias = noise(key_list[9], (D,), 0.3, 2.0)
    w_in = noise(key_list[10], (D, FF), D ** -0.5, 0.21875)
    b_in = noise(key_list[11], (FF,), 0.5, 3.0)
    w_down = noise(key_list[12], (FF, D), FF ** -0.5, 0.109375)
    b_down = noise(key_list[13], (D,), 0.5, 3.0)
    ln2_gain = jnp.clip(1.0 + 0.1 * jax.random.normal(key_list[14], (D,), jnp.float32), 0.5, 1.5).astype(jnp.bfloat16)
    ln2_bias = noise(key_list[15], (D,), 0.05, 0.29882812)
    return {"hidden": hidden, "segment_ids": segment_ids, "targets": targets, "w_qkv": w_qkv, "b_query": b_query, "b_value": b_value, "w_out": w_out, "b_out": b_out, "ln1_gain": ln1_gain, "ln1_bias": ln1_bias, "w_in": w_in, "b_in": b_in, "w_down": w_down, "b_down": b_down, "ln2_gain": ln2_gain, "ln2_bias": ln2_bias}


cosine_scale = 64.0
loss_scale = 32.0
norm_epsilon = 1e-12
unit_epsilon = 1e-06
masked_score = -1e+30
highest = lax.Precision.HIGHEST

@jax.custom_vjp
def low(v):
    return lax.optimization_barrier(v.astype(jnp.bfloat16)).astype(jnp.float32)

@jax.custom_vjp
def low_back(v):
    return v

def low_keep(v):
    return (low(v), None)

def low_pass(kept, grad):
    return (grad,)

def back_keep(v):
    return (v, None)

def back_low(kept, grad):
    return (low(grad),)
low.defvjp(low_keep, low_pass)
low_back.defvjp(back_keep, back_low)

def both_ways(inputs):
    return low_back(low(inputs))

def matmul(left, right):
    return jnp.dot(left, right, precision=highest)

def layer_norm(inputs, norm_gain, norm_shift):
    middle = lax.optimization_barrier(jnp.mean(inputs, axis=-1, keepdims=True))
    centered = inputs - middle
    spread = lax.optimization_barrier(jnp.mean(centered * centered, axis=-1, keepdims=True))
    return centered * lax.rsqrt(spread + norm_epsilon) * norm_gain + norm_shift

def gelu_exact(inputs):
    return 0.5 * inputs * (1.0 + lax.erf(inputs * 0.5 ** 0.5))

def encode_row(row_x, row_seg, params):
    w_qkv, b_query, b_value, w_out, b_out, ln1_gain, ln1_bias, w_in, b_in, w_down, b_down, ln2_gain, ln2_bias = params
    length = row_x.shape[0]
    bias_qkv = jnp.concatenate([b_query, jnp.zeros_like(b_query), b_value])
    qkv_all = both_ways(matmul(row_x, w_qkv) + bias_qkv)
    query_heads = qkv_all[:, :D].reshape(length, HEADS, HEAD_DIM)
    key_heads = qkv_all[:, D:2 * D].reshape(length, HEADS, HEAD_DIM)
    value_heads = qkv_all[:, 2 * D:].reshape(length, HEADS, HEAD_DIM)
    scores = jnp.einsum('qhd,khd->hqk', query_heads, key_heads, precision=highest) * HEAD_DIM ** (-0.5)
    scores = low_back(scores)
    same_doc = (row_seg[:, None] == row_seg[None, :])[None]
    scores = jnp.where(same_doc, scores, masked_score)
    row_top = lax.optimization_barrier(jnp.max(scores, axis=-1, keepdims=True))
    weights = jnp.exp(scores - row_top)
    prob_rows = low(weights / lax.optimization_barrier(jnp.sum(weights, axis=-1, keepdims=True)))
    context = jnp.einsum('hqk,khd->qhd', prob_rows, value_heads, precision=highest).reshape(length, D)
    context = both_ways(context)
    attended = low_back(matmul(context, w_out) + b_out)
    normed_one = layer_norm(row_x + attended, ln1_gain, ln1_bias)
    hidden_pre = low_back(matmul(low(normed_one), w_in) + b_in)
    active = low(gelu_exact(hidden_pre))
    branch = low_back(matmul(active, w_down) + b_down)
    output = layer_norm(normed_one + branch, ln2_gain, ln2_bias)
    member = (row_seg[None, :] == jnp.arange(SEG, dtype=jnp.int32)[:, None]).astype(row_x.dtype)
    counts = lax.optimization_barrier(jnp.sum(member, axis=1, keepdims=True))
    pooled = matmul(member, output) / counts
    unit_rows = pooled * lax.rsqrt(lax.optimization_barrier(jnp.mean(pooled * pooled, axis=-1, keepdims=True)) + unit_epsilon)
    return low(unit_rows)

def forward(hidden_in, params, segment_ids, targets):
    row_count = hidden_in.shape[0]
    per_block = math.gcd(row_count, 8)
    blocks = row_count // per_block

    def encode_block(block):
        block_x, block_seg = block
        return jax.vmap(lambda row_x, row_seg: encode_row(row_x, row_seg, params))(block_x, block_seg)
    units = lax.map(jax.checkpoint(encode_block), (hidden_in.reshape(blocks, per_block, LEN, D), segment_ids.reshape(blocks, per_block, LEN)))
    units = units.reshape(row_count * SEG, D)
    anchors = units[:ANCHORS]
    positives = units[ANCHORS:]
    sims = low_back(matmul(anchors, positives.T) * (cosine_scale / D))
    row_top = lax.optimization_barrier(jnp.max(sims, axis=1, keepdims=True))
    log_total = row_top[:, 0] + jnp.log(lax.optimization_barrier(jnp.sum(jnp.exp(sims - row_top), axis=1)))
    picked = jnp.take_along_axis(sims, targets[:, None].astype(jnp.int32), axis=1)[:, 0]
    return log_total - picked

def reference(hidden, segment_ids, targets, w_qkv, b_query, b_value, w_out, b_out, ln1_gain, ln1_bias, w_in, b_in, w_down, b_down, ln2_gain, ln2_bias):
    params = jax.tree.map(lambda weight: weight.astype(jnp.float32), (w_qkv, b_query, b_value, w_out, b_out, ln1_gain, ln1_bias, w_in, b_in, w_down, b_down, ln2_gain, ln2_bias))
    hidden_in = hidden.astype(jnp.float32)

    def objective(states, weights):
        return forward(states, weights, segment_ids, targets)
    losses, pullback = jax.vjp(objective, hidden_in, params)
    hidden_back, grads = pullback(loss_scale * jnp.ones_like(losses))
    return (losses, hidden_back.astype(jnp.bfloat16), grads[0], grads[1], grads[2], grads[3], grads[4], grads[5], grads[6], grads[7], grads[8], grads[9], grads[10], grads[11], grads[12])
```

```python
import functools
import math

import jax
import jax.numpy as jnp
from jax import lax
from jax.experimental import pallas as pl
from jax.experimental.pallas import tpu as pltpu
from jax.sharding import PartitionSpec as P

D = 768
HEADS = 12
HEAD_DIM = 64
SEG = 8
QB = 128
MOST = 128

cosine_scale = 64.0
loss_scale = 32.0
norm_epsilon = 1e-12
unit_epsilon = 1e-06
masked_score = -1e30


def layer_norm(inputs, norm_gain, norm_shift):
    middle = jnp.mean(inputs, axis=-1, keepdims=True)
    centered = inputs - middle
    spread = jnp.mean(centered * centered, axis=-1, keepdims=True)
    return centered * lax.rsqrt(spread + norm_epsilon) * norm_gain + norm_shift


def gelu_exact(inputs):
    return 0.5 * inputs * (1.0 + lax.erf(inputs * 0.5**0.5))


def contract_rows(left, right):
    return lax.dot_general(
        left, right, (((0,), (0,)), ((), ())), preferred_element_type=jnp.float32
    )


def contract_cols(left, right):
    return lax.dot_general(
        left, right, (((1,), (1,)), ((), ())), preferred_element_type=jnp.float32
    )


def rank_loss(sims, wanted):
    row_top = jnp.max(sims, axis=1, keepdims=True)
    weights = jnp.exp(sims - row_top)
    row_total = jnp.sum(weights, axis=1, keepdims=True)
    column = lax.broadcasted_iota(jnp.int32, sims.shape, 1)
    target_hit = column == wanted[:, None]
    picked = jnp.sum(jnp.where(target_hit, sims, 0.0), axis=1)
    losses = row_top[:, 0] + jnp.log(row_total[:, 0]) - picked
    slope = (loss_scale * (weights / row_total - target_hit.astype(jnp.float32))).astype(
        jnp.bfloat16
    )
    return (losses, slope)


def windows(length):
    out = []
    for start in range(0, length, QB):
        out.append((start, max(0, start - MOST), min(length, start + QB + MOST)))
    return out


def pair_masks(shape):
    lane = lax.broadcasted_iota(jnp.int32, shape, 1)
    return lane < HEAD_DIM


def block_probs(q, k_pair, bias):
    scores = contract_cols(q, k_pair) + bias
    top = jnp.max(scores, axis=-1, keepdims=True)
    weights = jnp.exp(scores - top)
    return weights * (1.0 / jnp.sum(weights, axis=-1, keepdims=True))


def attend_fwd_kernel(q_ref, k_ref, v_ref, segc_ref, segr_ref, out_ref):
    length = q_ref.shape[0]
    zero = jnp.zeros((), jnp.bfloat16)
    for start, low, high in windows(length):
        rows = slice(start, start + QB)
        cols = slice(low, high)
        q_pair = q_ref[rows, :] * jnp.asarray(HEAD_DIM**-0.5, jnp.bfloat16)
        k_pair = k_ref[cols, :]
        v_pair = v_ref[cols, :]
        bias = jnp.where(segc_ref[rows, :] == segr_ref[:, cols], 0.0, masked_score)
        first_q = pair_masks(q_pair.shape)
        first_v = pair_masks(v_pair.shape)
        p0 = block_probs(jnp.where(first_q, q_pair, zero), k_pair, bias).astype(jnp.bfloat16)
        p1 = block_probs(jnp.where(first_q, zero, q_pair), k_pair, bias).astype(jnp.bfloat16)
        out = jnp.dot(
            p0, jnp.where(first_v, v_pair, zero), preferred_element_type=jnp.float32
        ) + jnp.dot(p1, jnp.where(first_v, zero, v_pair), preferred_element_type=jnp.float32)
        out_ref[rows, :] = out.astype(jnp.bfloat16)


def attend_forward(qkv, seg_col, seg_row):
    rows, length = seg_row.shape[0], seg_row.shape[2]
    pairs = HEADS // 2
    width = 2 * HEAD_DIM

    def block(part):
        return pl.BlockSpec((None, length, width), lambda r, h: (r, 0, part * pairs + h))

    return pl.pallas_call(
        attend_fwd_kernel,
        name="attend_fwd",
        grid=(rows, pairs),
        in_specs=[
            block(0),
            block(1),
            block(2),
            pl.BlockSpec((None, length, 1), lambda r, h: (r, 0, 0)),
            pl.BlockSpec((None, 1, length), lambda r, h: (r, 0, 0)),
        ],
        out_specs=pl.BlockSpec((None, length, width), lambda r, h: (r, 0, h)),
        out_shape=jax.ShapeDtypeStruct((rows, length, D), jnp.bfloat16),
        cost_estimate=pl.CostEstimate(
            flops=rows * HEADS * 4 * length * length * HEAD_DIM,
            bytes_accessed=rows * length * D * 8,
            transcendentals=rows * HEADS * length * length // 2,
        ),
        compiler_params=pltpu.CompilerParams(vmem_limit_bytes=24 << 20),
    )(qkv, qkv, qkv, seg_col, seg_row)


def attend_bwd_kernel(q_ref, k_ref, v_ref, g_ref, segc_ref, segr_ref, out_ref, dk_acc, dv_acc):
    length = q_ref.shape[0]
    zero = jnp.zeros((), jnp.bfloat16)
    scale = jnp.asarray(HEAD_DIM**-0.5, jnp.bfloat16)
    dk_acc[...] = jnp.zeros_like(dk_acc)
    dv_acc[...] = jnp.zeros_like(dv_acc)
    for start, low, high in windows(length):
        rows = slice(start, start + QB)
        cols = slice(low, high)
        q_pair = q_ref[rows, :] * scale
        k_pair = k_ref[cols, :]
        v_pair = v_ref[cols, :]
        g_pair = g_ref[rows, :]
        bias = jnp.where(segc_ref[rows, :] == segr_ref[:, cols], 0.0, masked_score)
        first_q = pair_masks(q_pair.shape)
        first_k = pair_masks(k_pair.shape)
        dq = None
        for head in range(2):
            pick = (lambda m, a: jnp.where(m, a, zero)) if head == 0 else (
                lambda m, a: jnp.where(m, zero, a)
            )
            q_one = pick(first_q, q_pair)
            g_one = pick(first_q, g_pair)
            k_one = pick(first_k, k_pair)
            p = block_probs(q_one, k_pair, bias)
            gp = contract_cols(g_one, v_pair)
            inner = jnp.sum(p * gp, axis=-1, keepdims=True)
            ds = (p * (gp - inner)).astype(jnp.bfloat16)
            p_low = p.astype(jnp.bfloat16)
            part = jnp.dot(ds, k_one, preferred_element_type=jnp.float32)
            dq = part if dq is None else dq + part
            dk_acc[cols, :] += contract_rows(ds, q_one)
            dv_acc[cols, :] += contract_rows(p_low, g_one)
        out_ref[0, rows, :] = (dq * HEAD_DIM**-0.5).astype(jnp.bfloat16)
    out_ref[1] = dk_acc[...].astype(jnp.bfloat16)
    out_ref[2] = dv_acc[...].astype(jnp.bfloat16)


def attend_backward(qkv, grad_context, seg_col, seg_row):
    rows, length = seg_row.shape[0], seg_row.shape[2]
    pairs = HEADS // 2
    width = 2 * HEAD_DIM

    def block(part):
        return pl.BlockSpec((None, length, width), lambda r, h: (r, 0, part * pairs + h))

    return pl.pallas_call(
        attend_bwd_kernel,
        name="attend_bwd",
        grid=(rows, pairs),
        in_specs=[
            block(0),
            block(1),
            block(2),
            pl.BlockSpec((None, length, width), lambda r, h: (r, 0, h)),
            pl.BlockSpec((None, length, 1), lambda r, h: (r, 0, 0)),
            pl.BlockSpec((None, 1, length), lambda r, h: (r, 0, 0)),
        ],
        out_specs=pl.BlockSpec((3, None, length, width), lambda r, h: (0, r, 0, h)),
        out_shape=jax.ShapeDtypeStruct((3, rows, length, D), jnp.bfloat16),
        scratch_shapes=[
            pltpu.VMEM((length, width), jnp.float32),
            pltpu.VMEM((length, width), jnp.float32),
        ],
        cost_estimate=pl.CostEstimate(
            flops=rows * HEADS * 10 * length * length * HEAD_DIM,
            bytes_accessed=rows * length * D * 14,
            transcendentals=rows * HEADS * length * length // 2,
        ),
        compiler_params=pltpu.CompilerParams(vmem_limit_bytes=24 << 20),
    )(qkv, qkv, qkv, grad_context, seg_col, seg_row)


def add_low(*parts):
    total = parts[0].astype(jnp.float32)
    for part in parts[1:]:
        total = total + part.astype(jnp.float32)
    return lax.optimization_barrier(total.astype(jnp.bfloat16))


def digits_of(devices):
    out, rest = [], devices // 2
    if rest > 1:
        out.append(2)
        rest //= 2
    while rest > 1:
        size = 4 if rest % 4 == 0 else 2
        out.append(size)
        rest //= size
    return out


def swap_dp(value, flip):
    devices = lax.axis_size("dp")
    return lax.ppermute(value, "dp", [(i, i ^ flip) for i in range(devices)])


def swap_twin(value):
    return lax.ppermute(value, "twin", [(0, 1), (1, 0)])


def digit_step(value, size, unit):
    mine = (lax.axis_index("dp") // unit) % size
    rest = value.shape[0] // size
    view = value.reshape((rest, size) + value.shape[1:])
    parts = [lax.dynamic_index_in_dim(view, mine, 1, keepdims=False)]
    for flip in range(1, size):
        send = lax.dynamic_index_in_dim(view, mine ^ flip, 1, keepdims=False)
        parts.append(swap_dp(send, flip * unit))
    return add_low(*parts)


def reduce_pair(left, right):
    twin = lax.axis_index("twin")
    devices = lax.axis_size("dp")
    digits = digits_of(devices)
    keep = lax.dynamic_index_in_dim(left, twin, 0, keepdims=False)
    send = lax.dynamic_index_in_dim(left, 1 - twin, 0, keepdims=False)
    a = add_low(keep, swap_twin(send))
    b = right
    unit = 2
    for size in digits:
        a = digit_step(a, size, unit)
        b = digit_step(b, size, unit)
        unit *= size
    a, b = a[0], b[0]
    other = swap_twin(a)
    low = jnp.where(twin == 0, a, other).astype(jnp.float32)
    high = jnp.where(twin == 0, other, a).astype(jnp.float32)
    return (low, high, b.astype(jnp.float32) + swap_twin(b).astype(jnp.float32))


def core_sum(value):
    core = lax.axis_index("dp") % 2
    view = value.reshape((value.shape[0] // 2, 2) + value.shape[1:])
    keep = lax.dynamic_index_in_dim(view, core, 1, keepdims=False)
    send = lax.dynamic_index_in_dim(view, 1 - core, 1, keepdims=False)
    return add_low(keep, swap_dp(send, 1))


def scatter_columns(grad, extra=None):
    devices = lax.axis_size("dp")
    total = core_sum(grad.reshape(devices, grad.shape[0] // devices, grad.shape[1]))
    quarter = grad.shape[1] // 4 // 128 * 128
    left = jnp.stack([total[:, :, :quarter], total[:, :, quarter : 2 * quarter]])
    low, high, rest = reduce_pair(left, total[:, :, 2 * quarter :])
    return jnp.concatenate([low, high, rest], axis=1)


def scatter_rows(grad):
    devices = lax.axis_size("dp")
    r = grad.shape[0] // devices
    total = core_sum(grad.reshape(devices, r, grad.shape[1]))
    quarter = r // 4
    left = jnp.stack([total[:, :quarter], total[:, quarter : 2 * quarter]])
    low, high, rest = reduce_pair(left, total[:, 2 * quarter :])
    return jnp.concatenate([low, high, rest], axis=0)


def body(
    hidden,
    segment_ids,
    targets,
    w_qkv,
    b_query,
    b_value,
    w_out,
    b_out,
    ln1_gain,
    ln1_bias,
    w_in,
    b_in,
    w_down,
    b_down,
    ln2_gain,
    ln2_bias,
):
    row_count, length, width = hidden.shape
    token_count = row_count * length
    devices = lax.axis_size("dp")
    tokens = hidden.reshape(token_count, width)
    bias_qkv = jnp.concatenate(
        [b_query.astype(jnp.float32), jnp.zeros((width,), jnp.float32), b_value.astype(jnp.float32)]
    )
    qkv_all = (jnp.dot(tokens, w_qkv, preferred_element_type=jnp.float32) + bias_qkv).astype(
        jnp.bfloat16
    )
    qkv_rows = qkv_all.reshape(row_count, length, 3 * width)
    seg_col = segment_ids.reshape(row_count, length, 1)
    seg_row = segment_ids.reshape(row_count, 1, length)
    context_flat = attend_forward(qkv_rows, seg_col, seg_row).reshape(token_count, width)
    attended = jnp.dot(context_flat, w_out, preferred_element_type=jnp.float32) + b_out.astype(
        jnp.float32
    )
    normed_one, norm_one_back = jax.vjp(
        layer_norm,
        tokens.astype(jnp.float32) + attended,
        ln1_gain.astype(jnp.float32),
        ln1_bias.astype(jnp.float32),
    )
    normed_low = normed_one.astype(jnp.bfloat16)
    hidden_pre = jnp.dot(normed_low, w_in, preferred_element_type=jnp.float32) + b_in.astype(
        jnp.float32
    )
    active, gelu_back = jax.vjp(gelu_exact, hidden_pre)
    active_low = active.astype(jnp.bfloat16)
    branch = jnp.dot(active_low, w_down, preferred_element_type=jnp.float32) + b_down.astype(
        jnp.float32
    )
    output, norm_two_back = jax.vjp(
        layer_norm, normed_one + branch, ln2_gain.astype(jnp.float32), ln2_bias.astype(jnp.float32)
    )
    member = (segment_ids[:, None, :] == jnp.arange(SEG, dtype=jnp.int32)[None, :, None]).astype(
        jnp.float32
    )
    counts = jnp.sum(member, axis=2, keepdims=True)

    def pool_units(out_rows):
        pooled = (
            jnp.einsum("rsl,rld->rsd", member, out_rows, precision=lax.Precision.HIGHEST) / counts
        )
        unit_rows = pooled * lax.rsqrt(
            jnp.mean(pooled * pooled, axis=-1, keepdims=True) + unit_epsilon
        )
        return unit_rows.reshape(row_count * SEG, width)

    unit_rows, pool_back = jax.vjp(pool_units, output.reshape(row_count, length, width))
    unit_low = unit_rows.astype(jnp.bfloat16)
    gathered = lax.all_gather(unit_low, ("twin", "dp"), axis=0, tiled=True)
    anchor_count = gathered.shape[0] // 2
    anchors = gathered[:anchor_count]
    positives = gathered[anchor_count:]
    factor = cosine_scale / width
    everyone = lax.axis_size(("twin", "dp"))
    loss_share = anchor_count // everyone
    loss_start = lax.axis_index(("twin", "dp")) * loss_share
    all_losses, slope = rank_loss(contract_cols(anchors, positives) * factor, targets)
    losses = lax.dynamic_slice_in_dim(all_losses, loss_start, loss_share, 0)
    sentences = unit_low.shape[0]
    offset = lax.axis_index("dp") * sentences
    anchor_rows = (
        jnp.dot(
            lax.dynamic_slice_in_dim(slope, offset, sentences, 0),
            positives,
            preferred_element_type=jnp.float32,
        )
        * factor
    )
    positive_rows = (
        contract_rows(lax.dynamic_slice_in_dim(slope, offset, sentences, 1), anchors) * factor
    )
    unit_grad = jnp.where(lax.axis_index("twin") == 0, anchor_rows, positive_rows)
    grad_output = pool_back(unit_grad)[0].reshape(token_count, width)
    grad_sum_two, grad_ln2_gain, grad_ln2_bias = norm_two_back(grad_output)
    grad_branch = grad_sum_two.astype(jnp.bfloat16)
    grad_w_down = contract_rows(active_low, grad_branch).astype(jnp.bfloat16)
    grad_w_down = scatter_rows(grad_w_down)
    grad_b_down = jnp.sum(grad_branch, axis=0, dtype=jnp.float32)
    grad_active = contract_cols(grad_branch, w_down)
    grad_pre = gelu_back(grad_active)[0].astype(jnp.bfloat16)
    grad_w_in = contract_rows(normed_low, grad_pre).astype(jnp.bfloat16)
    grad_w_in = scatter_columns(grad_w_in)
    grad_b_in = jnp.sum(grad_pre, axis=0, dtype=jnp.float32)
    grad_normed = contract_cols(grad_pre, w_in) + grad_sum_two
    grad_sum_one, grad_ln1_gain, grad_ln1_bias = norm_one_back(grad_normed)
    grad_attended = grad_sum_one.astype(jnp.bfloat16)
    grad_w_out = contract_rows(context_flat, grad_attended).astype(jnp.bfloat16)
    grad_b_out = jnp.sum(grad_attended, axis=0, dtype=jnp.float32)
    grad_context = (
        contract_cols(grad_attended, w_out).astype(jnp.bfloat16).reshape(row_count, length, width)
    )
    grad_parts = attend_backward(qkv_rows, grad_context, seg_col, seg_row).reshape(
        3, token_count, width
    )
    grad_qkv = jnp.concatenate([grad_parts[0], grad_parts[1], grad_parts[2]], axis=1)
    grad_w_qkv = contract_rows(tokens, grad_qkv).astype(jnp.bfloat16)
    sums = jnp.sum(grad_parts, axis=1, dtype=jnp.float32)
    hidden_grad = (
        (contract_cols(grad_qkv, w_qkv) + grad_sum_one)
        .astype(jnp.bfloat16)
        .reshape(row_count, length, width)
    )
    vectors = jnp.stack(
        [sums[0], sums[2], grad_b_out, grad_ln1_gain, grad_ln1_bias]
        + [grad_b_down, grad_ln2_gain, grad_ln2_bias]
    )
    share = width // devices
    wide = grad_b_in.reshape(devices, -1, share).transpose(1, 0, 2).reshape(-1, width)
    vectors = jnp.concatenate([vectors, wide])
    vectors = jnp.pad(vectors, ((0, 128 - vectors.shape[0]), (0, 0))).T.astype(jnp.bfloat16)
    last = scatter_columns(jnp.concatenate([grad_w_qkv, grad_w_out, vectors], axis=1))
    grad_w_qkv = last[:, : 3 * width]
    grad_w_out = last[:, 3 * width : 4 * width]
    small = last[:, 4 * width :].T
    return (
        losses,
        hidden_grad,
        grad_w_qkv,
        small[0],
        small[1],
        grad_w_out,
        small[2],
        small[3],
        small[4],
        grad_w_in,
        small[8 : 8 + wide.shape[0]].reshape(-1),
        grad_w_down,
        small[5],
        small[6],
        small[7],
    )


def solution(mesh):
    whole = (P(),) * 14
    placed = (P(("twin", "dp"), None, None), P(("twin", "dp"), None)) + whole
    return jax.shard_map(
        body,
        mesh=mesh,
        in_specs=placed,
        out_specs=(
            P(("twin", "dp")),
            P(("twin", "dp"), None, None),
            P("dp", None),
            P("dp"),
            P("dp"),
            P("dp", None),
            P("dp"),
            P("dp"),
            P("dp"),
            P("dp", None),
            P("dp"),
            P("dp", None),
            P("dp"),
            P("dp"),
            P("dp"),
        ),
        check_vma=False,
    )
```

```python
import functools

import jax
import jax.numpy as jnp
from jax import lax
from jax.experimental import pallas as pl
from jax.experimental.pallas import tpu as pltpu
from jax.sharding import PartitionSpec as P

D = 768
HEADS = 12
HEAD_DIM = 64
FF = 3072
SEG = 8
QB = 128
MOST = 128
PAIRS = HEADS // 2
PW = 2 * HEAD_DIM

cosine_scale = 64.0
loss_scale = 32.0
norm_epsilon = 1e-12
unit_epsilon = 1e-06
masked_score = -1e30

F32 = jnp.float32
BF16 = jnp.bfloat16
VMEM = pltpu.VMEM
ANY = pl.ANY
MIB = 1 << 20


def nn(left, right):
    return lax.dot_general(left, right, (((1,), (0,)), ((), ())), preferred_element_type=F32)


def nt(left, right):
    return lax.dot_general(left, right, (((1,), (1,)), ((), ())), preferred_element_type=F32)


def tn(left, right):
    return lax.dot_general(left, right, (((0,), (0,)), ((), ())), preferred_element_type=F32)


def vspec():
    return pl.BlockSpec(memory_space=VMEM)


def sspec():
    return pl.BlockSpec(memory_space=pltpu.SMEM)


def fixed(shape):
    return pl.BlockSpec(shape, lambda *_: (0,) * len(shape))


def shape_of(shape, dtype):
    return jax.ShapeDtypeStruct(shape, dtype)


def params(mib):
    return pltpu.CompilerParams(vmem_limit_bytes=mib * MIB)


def cost(flops, moved):
    return pl.CostEstimate(flops=int(flops), bytes_accessed=int(moved), transcendentals=0)


def windows(length):
    out, packed = [], 0
    for start in range(0, length, QB):
        low, high = max(0, start - MOST), min(length, start + QB + MOST)
        out.append((start, low, high, packed))
        packed += high - low
    return out, packed


def two_heads(pair):
    first = lax.broadcasted_iota(jnp.int32, pair.shape, 1) < HEAD_DIM
    zero = jnp.zeros((), pair.dtype)
    return jnp.concatenate([jnp.where(first, pair, zero), jnp.where(first, zero, pair)], axis=0)


def pick_heads(both):
    rows = both.shape[1] // 2
    return jnp.concatenate([both[:HEAD_DIM, :rows], both[HEAD_DIM:, rows:]], axis=0).T


def column_of(row):
    return jnp.broadcast_to(row, (8, row.shape[1])).T[:, :1]


def split_low(value):
    high = value.astype(BF16)
    return high, (value - high.astype(F32)).astype(BF16)


def normalise(value):
    middle = jnp.mean(value, axis=-1, keepdims=True)
    centered = value - middle
    spread = jnp.mean(centered * centered, axis=-1, keepdims=True)
    rstd = lax.rsqrt(spread + norm_epsilon)
    return centered * rstd, rstd


def forward_kernel(
    hid,
    seg,
    wqkv_h,
    bq,
    bv,
    wout_h,
    bout,
    g1,
    b1,
    win_h,
    bin_,
    wdown_h,
    bdown,
    g2,
    b2,
    qkv_o,
    p_o,
    ctx_o,
    n1_o,
    xh1_o,
    rs1_o,
    act_o,
    dg_o,
    xh2_o,
    rs2_o,
    unit_o,
    unitf_o,
    inv_o,
    wqkv,
    wout,
    win,
    wdown,
    bias_s,
    n1_s,
    sems,
):
    r = pl.program_id(0)
    length = hid.shape[0]
    blocks, _ = windows(length)
    pairs = ((wqkv_h, wqkv), (wout_h, wout), (win_h, win), (wdown_h, wdown))
    copies = [pltpu.make_async_copy(a, b, sems.at[i]) for i, (a, b) in enumerate(pairs)]

    @pl.when(r == 0)
    def _():
        for copy in copies:
            copy.start()

    seg_row = seg[pl.ds(r, 1), :].astype(F32)
    seg_col = column_of(seg_row)
    for start, low, high, packed in blocks:
        same = seg_col[low:high] == seg_row[:, start : start + QB]
        bias_s[packed : packed + high - low, :] = jnp.where(same, 0.0, masked_score)

    @pl.when(r == 0)
    def _():
        copies[0].wait()

    x = hid[...]
    for part in range(3):
        cols = slice(part * D, (part + 1) * D)
        value = nn(x, wqkv[:, cols])
        if part == 0:
            value = value + bq[...].astype(F32)
        if part == 2:
            value = value + bv[...].astype(F32)
        qkv_o[:, cols] = value.astype(BF16)

    def one_pair(h, carry):
        def lanes(part):
            return pl.ds(pl.multiple_of(part * D + h * PW, PW), PW)

        q_all = qkv_o[:, lanes(0)] * jnp.asarray(HEAD_DIM**-0.5, BF16)
        k_all = qkv_o[:, lanes(1)]
        v_turned = qkv_o[:, lanes(2)].T
        for start, low, high, packed in blocks:
            rows = slice(packed, packed + high - low)
            both = two_heads(q_all[start : start + QB])
            scores = nt(k_all[low:high], both)
            bias = bias_s[rows, :]
            parts = []
            for head in range(2):
                own = scores[:, head * QB : (head + 1) * QB] + bias
                top = jnp.max(own, axis=0, keepdims=True)
                weights = jnp.exp(own - top)
                total = jnp.sum(weights, axis=0, keepdims=True)
                parts.append((weights * (1.0 / total)).astype(BF16))
            p = jnp.concatenate(parts, axis=1)
            p_o[h, rows, :] = p
            out = nn(v_turned[:, low:high], p)
            ctx_o[start : start + QB, pl.ds(pl.multiple_of(h * PW, PW), PW)] = pick_heads(
                out.astype(BF16)
            )
        return carry

    lax.fori_loop(0, PAIRS, one_pair, 0)

    @pl.when(r == 0)
    def _():
        copies[1].wait()

    xhat, rstd = normalise(x.astype(F32) + (nn(ctx_o[...], wout[...]) + bout[...].astype(F32)))
    xh1_o[...] = xhat.astype(BF16)
    rs1_o[...] = jnp.broadcast_to(rstd, rs1_o.shape)
    n1 = xhat * g1[...].astype(F32) + b1[...].astype(F32)
    n1_s[...] = n1
    n1_o[...] = n1.astype(BF16)

    @pl.when(r == 0)
    def _():
        copies[2].wait()

    chunk = 512

    def one_chunk(c, carry):
        cols = pl.ds(pl.multiple_of(c * chunk, chunk), chunk)
        pre = nn(n1_o[...], win[:, cols]) + bin_[:, cols].astype(F32)
        half = 0.5 + 0.5 * lax.erf(pre * 0.5**0.5)
        act_o[:, cols] = (pre * half).astype(BF16)
        bell = jnp.exp(pre * pre * -0.5) * 0.3989422804014327
        dg_o[:, cols] = (half + pre * bell).astype(BF16)
        return carry

    lax.fori_loop(0, FF // chunk, one_chunk, 0)

    @pl.when(r == 0)
    def _():
        copies[3].wait()

    branch = nn(act_o[...], wdown[...]) + bdown[...].astype(F32)
    xhat, rstd = normalise(n1_s[...] + branch)
    xh2_o[...] = xhat.astype(BF16)
    rs2_o[...] = jnp.broadcast_to(rstd, rs2_o.shape)
    out = xhat * g2[...].astype(F32) + b2[...].astype(F32)
    member = (lax.broadcasted_iota(jnp.int32, (SEG, length), 0).astype(F32) == seg_row).astype(F32)
    counts = jnp.sum(member, axis=1, keepdims=True)
    high, low = split_low(out)
    member = member.astype(BF16)
    pooled = (nn(member, high) + nn(member, low)) / counts
    inv = lax.rsqrt(jnp.mean(pooled * pooled, axis=-1, keepdims=True) + unit_epsilon)
    unit = pooled * inv
    unitf_o[...] = unit
    unit_o[...] = unit.astype(BF16)
    inv_o[...] = jnp.broadcast_to(inv / counts, inv_o.shape)


def forward(hidden, seg, weights):
    rows, length, _ = hidden.shape
    tokens = rows * length
    _, packed = windows(length)
    wqkv, bq, bv, wout, bout, g1, b1, win, bin_, wdown, bdown, g2, b2 = weights

    def per_row(n):
        return pl.BlockSpec((length, n), lambda r: (r, 0))

    out_shape = [
        shape_of((tokens, 3 * D), BF16),
        shape_of((rows, PAIRS, packed, 2 * QB), BF16),
        shape_of((tokens, D), BF16),
        shape_of((tokens, D), BF16),
        shape_of((tokens, D), BF16),
        shape_of((tokens, 128), F32),
        shape_of((tokens, FF), BF16),
        shape_of((tokens, FF), BF16),
        shape_of((tokens, D), BF16),
        shape_of((tokens, 128), F32),
        shape_of((rows, SEG, D), BF16),
        shape_of((rows, SEG, D), F32),
        shape_of((rows, SEG, 128), F32),
    ]
    out_specs = [
        per_row(3 * D),
        pl.BlockSpec((None, PAIRS, packed, 2 * QB), lambda r: (r, 0, 0, 0)),
        per_row(D),
        per_row(D),
        per_row(D),
        per_row(128),
        per_row(FF),
        per_row(FF),
        per_row(D),
        per_row(128),
        pl.BlockSpec((None, SEG, D), lambda r: (r, 0, 0)),
        pl.BlockSpec((None, SEG, D), lambda r: (r, 0, 0)),
        pl.BlockSpec((None, SEG, 128), lambda r: (r, 0, 0)),
    ]
    hbm = pl.BlockSpec(memory_space=ANY)
    in_specs = [per_row(D), fixed(seg.shape)]
    in_specs += [hbm, fixed(bq.shape), fixed(bv.shape), hbm, fixed(bout.shape)]
    in_specs += [fixed(g1.shape), fixed(b1.shape), hbm, fixed(bin_.shape), hbm]
    in_specs += [fixed(bdown.shape), fixed(g2.shape), fixed(b2.shape)]
    return pl.pallas_call(
        forward_kernel,
        name="forward",
        grid=(rows,),
        in_specs=in_specs,
        out_specs=out_specs,
        out_shape=out_shape,
        scratch_shapes=[
            VMEM(wqkv.shape, BF16),
            VMEM(wout.shape, BF16),
            VMEM(win.shape, BF16),
            VMEM(wdown.shape, BF16),
            VMEM((packed, QB), F32),
            VMEM((length, D), F32),
            pltpu.SemaphoreType.DMA((4,)),
        ],
        cost_estimate=cost(1e9, 4e6),
        compiler_params=params(62),
    )(
        hidden.reshape(tokens, D),
        seg,
        wqkv,
        bq,
        bv,
        wout,
        bout,
        g1,
        b1,
        win,
        bin_,
        wdown,
        bdown,
        g2,
        b2,
    )


def loss_kernel(
    idx, units, targets, unitf, inv, seg, g2, xh2, rs2, loss_o, gb_o, vec_o, slope_s, rows_s
):
    twin, me = idx[0], idx[1]
    count = units.shape[0] // 2
    sentences = unitf.shape[0]
    rows, length = seg.shape
    step = min(count, 256)
    factor = cosine_scale / D
    positives = units.at[pl.ds(count, count)]
    own = pl.ds(pl.multiple_of(me * sentences, sentences), sentences)

    def one_block(i, carry):
        lanes = pl.ds(pl.multiple_of(i * step, step), step)
        sims = nt(positives[...], units[lanes, :]) * factor
        top = jnp.max(sims, axis=0, keepdims=True)
        weights = jnp.exp(sims - top)
        total = jnp.sum(weights, axis=0, keepdims=True)
        hit = lax.broadcasted_iota(jnp.int32, sims.shape, 0) == targets[:, lanes]
        picked = jnp.sum(jnp.where(hit, sims, 0.0), axis=0, keepdims=True)
        loss_o[:, lanes] = top + jnp.log(total) - picked
        slope = loss_scale * (weights * (1.0 / total) - hit.astype(F32))
        slope_s[:, lanes] = slope.astype(BF16)
        return carry

    if count == step:
        one_block(0, 0)
    else:
        lax.fori_loop(0, count // step, one_block, 0)

    @pl.when(twin == 0)
    def _():
        def part(i, carry):
            lanes = pl.ds(pl.multiple_of(i * step, step), step)
            rows_s[lanes, :] = tn(slope_s[:, lanes], positives[...])
            return carry

        lax.fori_loop(0, count // step, part, 0)
        rows_s[pl.ds(0, sentences), :] = rows_s[own, :]

    @pl.when(twin == 1)
    def _():
        rows_s[pl.ds(0, sentences), :] = nn(slope_s[own, :], units[pl.ds(0, count), :])

    gu = rows_s[pl.ds(0, sentences), :] * factor
    unit = unitf[...]
    gs = inv[:, :1] * (gu - unit * jnp.mean(gu * unit, axis=-1, keepdims=True))
    gy = gs * g2[...].astype(F32)
    u = gy - jnp.mean(gy, axis=-1, keepdims=True)
    gain = jnp.zeros((1, D), F32)
    shift = jnp.zeros((1, D), F32)
    summed = jnp.zeros((1, D), F32)
    for r in range(rows):
        part = slice(r * SEG, (r + 1) * SEG)
        tok = slice(r * length, (r + 1) * length)
        seg_row = seg[r : r + 1, :]
        hits = lax.broadcasted_iota(jnp.int32, (SEG, length), 0) == seg_row
        member = hits.astype(F32).astype(BF16)
        counts = jnp.sum(hits.astype(F32), axis=1, keepdims=True)
        xhat_low = xh2[tok, :]
        gain += jnp.sum(nn(member, xhat_low) * gs[part], axis=0, keepdims=True)
        shift += jnp.sum(counts * gs[part], axis=0, keepdims=True)
        xhat = xhat_low.astype(F32)
        high, low = split_low(u[part])
        spread = tn(member, high) + tn(member, low)
        inner = jnp.mean(spread * xhat, axis=-1, keepdims=True)
        grad = rs2[tok, :1] * (spread - xhat * inner)
        grad_low = grad.astype(BF16)
        gb_o[tok, :] = grad_low
        summed += jnp.sum(grad_low.astype(F32), axis=0, keepdims=True)
    vec_o[...] = jnp.concatenate([summed, gain, shift, jnp.zeros((5, D), F32)], axis=0)


def loss_stage(idx, units, targets, unitf, inv, seg, g2, xh2, rs2):
    tokens = xh2.shape[0]
    count = units.shape[0] // 2
    return pl.pallas_call(
        loss_kernel,
        name="loss",
        in_specs=[sspec()] + [vspec()] * 8,
        out_specs=[vspec()] * 3,
        out_shape=[
            shape_of((1, count), F32),
            shape_of((tokens, D), BF16),
            shape_of((8, D), F32),
        ],
        scratch_shapes=[VMEM((count, count), BF16), VMEM((count, D), F32)],
        cost_estimate=cost(1e8, 1e6),
        compiler_params=params(48),
    )(idx, units, targets, unitf, inv, seg, g2, xh2, rs2)


def pre_kernel(gb, wdown, dg, out):
    out[...] = (nt(gb[...], wdown[...]) * dg[...].astype(F32)).astype(BF16)


def pre_stage(gb, wdown, dg):
    tokens = gb.shape[0]
    n = 768
    return pl.pallas_call(
        pre_kernel,
        name="grad_pre",
        grid=(FF // n,),
        in_specs=[
            fixed(gb.shape),
            pl.BlockSpec((n, D), lambda j: (j, 0)),
            pl.BlockSpec((tokens, n), lambda j: (0, j)),
        ],
        out_specs=pl.BlockSpec((tokens, n), lambda j: (0, j)),
        out_shape=shape_of((tokens, FF), BF16),
        cost_estimate=cost(1e8, 1e6),
        compiler_params=params(40),
    )(gb, wdown, dg)


def normed_kernel(gp, win, gb, xh1, rs1, g1, wout, ga_o, gc_o, vec_o):
    grad = nt(gp[...], win[...]) + gb[...].astype(F32)
    xhat = xh1[...].astype(F32)
    gain = jnp.sum(grad * xhat, axis=0, keepdims=True)
    shift = jnp.sum(grad, axis=0, keepdims=True)
    gy = grad * g1[...].astype(F32)
    inner = jnp.mean(gy * xhat, axis=-1, keepdims=True)
    total = rs1[:, :1] * (gy - jnp.mean(gy, axis=-1, keepdims=True) - xhat * inner)
    low = total.astype(BF16)
    ga_o[...] = low
    summed = jnp.sum(low.astype(F32), axis=0, keepdims=True)
    gc_o[...] = nt(low, wout[...]).astype(BF16)
    rows = jnp.concatenate([summed, gain, shift, jnp.zeros((5, D), F32)], axis=0)

    @pl.when(pl.program_id(0) == 0)
    def _():
        vec_o[...] = rows

    @pl.when(pl.program_id(0) > 0)
    def _():
        vec_o[...] += rows


def normed_stage(gp, win, gb, xh1, rs1, g1, wout):
    tokens = gp.shape[0]
    m = 512

    def rows(n):
        return pl.BlockSpec((m, n), lambda i: (i, 0))

    return pl.pallas_call(
        normed_kernel,
        name="grad_normed",
        grid=(tokens // m,),
        in_specs=[
            rows(FF),
            fixed(win.shape),
            rows(D),
            rows(D),
            rows(128),
            fixed(g1.shape),
            fixed(wout.shape),
        ],
        out_specs=[rows(D), rows(D), fixed((8, D))],
        out_shape=[
            shape_of((tokens, D), BF16),
            shape_of((tokens, D), BF16),
            shape_of((8, D), F32),
        ],
        cost_estimate=cost(1e8, 1e6),
        compiler_params=params(48),
    )(gp, win, gb, xh1, rs1, g1, wout)


def attend_back_kernel(q_ref, k_ref, v_ref, g_ref, p_ref, out_ref, dk_acc, dv_acc):
    length = q_ref.shape[0]
    blocks, _ = windows(length)
    scale = HEAD_DIM**-0.5
    dk_acc[...] = jnp.zeros_like(dk_acc)
    dv_acc[...] = jnp.zeros_like(dv_acc)
    k_turned = k_ref[...].T
    for start, low, high, packed in blocks:
        q2 = two_heads(q_ref[start : start + QB, :])
        g2 = two_heads(g_ref[start : start + QB, :])
        p_low = p_ref[packed : packed + high - low, :]
        gp = nt(v_ref[low:high, :], g2)
        p = p_low.astype(F32)
        weighted = p * gp
        inner = jnp.sum(weighted, axis=0, keepdims=True)
        ds = (weighted - p * inner).astype(BF16)
        dv_acc[low:high, :] += nn(p_low, g2)
        dk_acc[low:high, :] += nn(ds, q2)
        dq = nn(k_turned[:, low:high], ds) * scale
        out_ref[0, start : start + QB, :] = pick_heads(dq.astype(BF16))
    out_ref[1] = (dk_acc[...] * scale).astype(BF16)
    out_ref[2] = dv_acc[...].astype(BF16)


def attend_back(qkv, grad_context, probs, rows, length):
    _, packed = windows(length)

    def block(part):
        return pl.BlockSpec((length, PW), lambda r, h: (r, part * PAIRS + h))

    return pl.pallas_call(
        attend_back_kernel,
        name="attend_back",
        grid=(rows, PAIRS),
        in_specs=[
            block(0),
            block(1),
            block(2),
            pl.BlockSpec((length, PW), lambda r, h: (r, h)),
            pl.BlockSpec((None, None, packed, 2 * QB), lambda r, h: (r, h, 0, 0)),
        ],
        out_specs=pl.BlockSpec((3, length, PW), lambda r, h: (0, r, h)),
        out_shape=shape_of((3, rows * length, D), BF16),
        scratch_shapes=[VMEM((length, PW), F32), VMEM((length, PW), F32)],
        cost_estimate=cost(1e8, 1e6),
        compiler_params=params(32),
    )(qkv, qkv, qkv, grad_context, probs)


def hidden_kernel(dqkv, wqkv, ga, out):
    total = ga[...].astype(F32)
    for part in range(3):
        total = total + nt(dqkv[part], wqkv[:, part * D : (part + 1) * D])
    out[...] = total.astype(BF16)


def hidden_stage(dqkv, wqkv, ga):
    tokens = ga.shape[0]
    m = 512
    return pl.pallas_call(
        hidden_kernel,
        name="hidden_grad",
        grid=(tokens // m,),
        in_specs=[
            pl.BlockSpec((3, m, D), lambda i: (0, i, 0)),
            fixed(wqkv.shape),
            pl.BlockSpec((m, D), lambda i: (i, 0)),
        ],
        out_specs=pl.BlockSpec((m, D), lambda i: (i, 0)),
        out_shape=shape_of((tokens, D), BF16),
        cost_estimate=cost(1e8, 1e6),
        compiler_params=params(40),
    )(dqkv, wqkv, ga)


HALF_A = (2, 8, 48, D)
HALF_B = (8, 48, 2 * D)


def place(core, value, keep, send):
    @pl.when(core == 0)
    def _():
        value(0, keep)
        value(1, send)

    @pl.when(core == 1)
    def _():
        value(1, keep)
        value(0, send)


def down_kernel(idx, act, gb, ka, kb, sa, sb):
    total = tn(act[...], gb[...]).astype(BF16)

    def store(parity, refs):
        a, b = refs
        for pair in range(2):
            base = (2 * pair + parity) * 192
            for q in range(4):
                piece = total[base + q * 48 : base + (q + 1) * 48]
                if q < 2:
                    a[q, pair] = piece
                else:
                    b[pair, :, (q - 2) * D : (q - 1) * D] = piece

    place(idx[2], store, (ka, kb), (sa, sb))


def down_stage(idx, act, gb):
    tokens = gb.shape[0]
    spec_a = pl.BlockSpec((2, 2, 48, D), lambda j: (0, j, 0, 0))
    spec_b = pl.BlockSpec((2, 48, 2 * D), lambda j: (j, 0, 0))
    return pl.pallas_call(
        down_kernel,
        name="grad_w_down",
        grid=(4,),
        in_specs=[sspec(), pl.BlockSpec((tokens, D), lambda j: (0, j)), fixed(gb.shape)],
        out_specs=[spec_a, spec_b] * 2,
        out_shape=[shape_of(HALF_A, BF16), shape_of(HALF_B, BF16)] * 2,
        cost_estimate=cost(1e8, 1e6),
        compiler_params=params(40),
    )(idx, act, gb)


def store_column(j, total, core, ka, kb, sa, sb):
    def store(parity, refs):
        a, b = refs

        @pl.when(j < 2)
        def _():
            for i in range(8):
                a[0, i] = total[(2 * i + parity) * 48 : (2 * i + parity + 1) * 48]

        @pl.when(j >= 2)
        def _():
            for i in range(8):
                b[i] = total[(2 * i + parity) * 48 : (2 * i + parity + 1) * 48]

    place(core, store, (ka, kb), (sa, sb))


SPEC_A = ((1, 8, 48, D), lambda j: (jnp.minimum(j, 1), 0, 0, 0))
SPEC_B = ((8, 48, D), lambda j: (0, 0, jnp.maximum(j - 2, 0)))


def in_kernel(idx, n1, gp, ka, kb, sa, sb, vec_o):
    j = pl.program_id(0)
    total = tn(n1[...], gp[...]).astype(BF16)
    store_column(j, total, idx[2], ka, kb, sa, sb)
    sums = tn(gp[...], jnp.ones((gp.shape[0], 128), BF16))
    lane = lax.broadcasted_iota(jnp.int32, (48, 128), 1)
    for block in range(4):
        acc = jnp.zeros((48, 128), F32)
        for q in range(4):
            base = block * 192 + q * 48
            acc = acc + jnp.where(lane == 8 + q, sums[base : base + 48], 0.0)
        vec_o[block] = acc


def in_stage(idx, n1, gp):
    tokens = gp.shape[0]
    return pl.pallas_call(
        in_kernel,
        name="grad_w_in",
        grid=(4,),
        in_specs=[sspec(), fixed(n1.shape), pl.BlockSpec((tokens, D), lambda j: (0, j))],
        out_specs=[pl.BlockSpec(*SPEC_A), pl.BlockSpec(*SPEC_B)] * 2
        + [pl.BlockSpec((4, 48, 128), lambda j: (j, 0, 0))],
        out_shape=[shape_of(HALF_A, BF16), shape_of(HALF_B, BF16)] * 2
        + [shape_of((16, 48, 128), F32)],
        cost_estimate=cost(1e8, 1e6),
        compiler_params=params(40),
    )(idx, n1, gp)


def last_kernel(idx, hid, dqkv, ctx, ga, vec2, vec1, vec_in, ka, kb, sa, sb, kv, sv, sums_s):
    j = pl.program_id(0)

    @pl.when(j < 3)
    def _():
        total = tn(hid[...], dqkv[...]).astype(BF16)
        store_column(j, total, idx[2], ka, kb, sa, sb)
        summed = jnp.sum(dqkv[...].astype(F32), axis=0, keepdims=True)

        @pl.when(j == 0)
        def _():
            sums_s[...] = jnp.zeros_like(sums_s)
            sums_s[0:1, :] = summed

        @pl.when(j == 2)
        def _():
            sums_s[1:2, :] = summed

    @pl.when(j == 3)
    def _():
        total = tn(ctx[...], ga[...]).astype(BF16)
        store_column(j, total, idx[2], ka, kb, sa, sb)
        sums_s[2:5, :] = vec1[0:3, :]
        sums_s[5:8, :] = vec2[0:3, :]
        turned = sums_s[...].T

        def store(parity, refs):
            (out,) = refs
            for i in range(8):
                block = 2 * i + parity
                out[i] = (turned[block * 48 : (block + 1) * 48] + vec_in[block]).astype(BF16)

        place(idx[2], store, (kv,), (sv,))


def last_stage(idx, hid, dqkv, ctx, ga, vec2, vec1, vec_in):
    tokens = ga.shape[0]
    return pl.pallas_call(
        last_kernel,
        name="grad_w_qkv",
        grid=(4,),
        in_specs=[
            sspec(),
            fixed(hid.shape),
            pl.BlockSpec((None, tokens, D), lambda j: (jnp.minimum(j, 2), 0, 0)),
            fixed(ctx.shape),
            fixed(ga.shape),
            fixed(vec2.shape),
            fixed(vec1.shape),
            fixed(vec_in.shape),
        ],
        out_specs=[pl.BlockSpec(*SPEC_A), pl.BlockSpec(*SPEC_B)] * 2 + [fixed((8, 48, 128))] * 2,
        out_shape=[shape_of(HALF_A, BF16), shape_of(HALF_B, BF16)] * 2
        + [shape_of((8, 48, 128), BF16)] * 2,
        scratch_shapes=[VMEM((128, D), F32)],
        cost_estimate=cost(1e8, 1e6),
        compiler_params=params(48),
    )(idx, hid, dqkv, ctx, ga, vec2, vec1, vec_in)


def swap_dp(value, flip):
    devices = lax.axis_size("dp")
    return lax.ppermute(value, "dp", [(i, i ^ flip) for i in range(devices)])


def swap_twin(value):
    return lax.ppermute(value, "twin", [(0, 1), (1, 0)])


def plus(*values):
    total = values[0].astype(F32)
    for value in values[1:]:
        total = total + value.astype(F32)
    return total.astype(BF16)


def call_small(kernel, name, idx, operands, outs):
    return pl.pallas_call(
        kernel,
        name=name,
        in_specs=[sspec()] + [vspec()] * len(operands),
        out_specs=[vspec()] * len(outs),
        out_shape=[shape_of(shape, dtype) for shape, dtype in outs],
        cost_estimate=cost(1e6, 1e5),
        compiler_params=params(32),
    )(idx, *operands)


def core_kernel(idx, ka, kb, ra, rb, as_o, ak_o, bs_o, bk_o):
    twin, y = idx[0], idx[3]
    as_o[...] = plus(ka[1 - twin], ra[1 - twin])
    ak_o[...] = plus(ka[twin], ra[twin])
    bs_o[0] = plus(kb[1 - y], rb[1 - y])
    bk_o[0] = plus(kb[y], rb[y])


def core_stage(idx, ka, kb, ra, rb):
    spec_a = pl.BlockSpec((2, 2, 48, D), lambda z: (0, z, 0, 0))
    spec_b = pl.BlockSpec((2, 48, 2 * D), lambda z: (z, 0, 0))
    out_a = pl.BlockSpec((2, 48, D), lambda z: (z, 0, 0))
    out_b = pl.BlockSpec((1, 48, 2 * D), lambda z: (z, 0, 0))
    return pl.pallas_call(
        core_kernel,
        name="core_sum",
        grid=(4,),
        in_specs=[sspec(), spec_a, spec_b, spec_a, spec_b],
        out_specs=[out_a, out_a, out_b, out_b],
        out_shape=[shape_of((8, 48, D), BF16)] * 2 + [shape_of((4, 48, 2 * D), BF16)] * 2,
        cost_estimate=cost(1e6, 1e5),
        compiler_params=params(32),
    )(idx, ka, kb, ra, rb)


def first_kernel(idx, ak, ar, bk, br, as_o, ak_o, b0, b1, b2, b3):
    y, z = idx[3], idx[4]
    for i in range(4):
        as_o[i] = plus(ak[2 * i + 1 - y], ar[2 * i + 1 - y])
        ak_o[i] = plus(ak[2 * i + y], ar[2 * i + y])
    for flip, out in enumerate((b0, b1, b2, b3)):
        out[...] = plus(bk[z ^ flip], br[z ^ flip])


def second_kernel(idx, ak, ar, b0, b1, b2, b3, a0, a1, a2, a3, b_o):
    z = idx[4]
    for flip, out in enumerate((a0, a1, a2, a3)):
        out[...] = plus(ak[z ^ flip], ar[z ^ flip])
    b_o[...] = plus(b0[...], b1[...], b2[...], b3[...])


def third_kernel(idx, a0, a1, a2, a3, a_o):
    a_o[...] = plus(a0[...], a1[...], a2[...], a3[...])


def fan_out(parts):
    return [swap_dp(part, flip * 4) for flip, part in enumerate(parts) if flip]


def exchange(idx, ka, kb, sa, sb):
    ra, rb = swap_dp(sa, 1), swap_dp(sb, 1)
    a_send, a_keep, b_send, b_keep = core_stage(idx, ka, kb, ra, rb)
    a_recv, b_recv = swap_twin(a_send), swap_dp(b_send, 2)
    quarter, wide = ((4, 48, D), BF16), ((48, 2 * D), BF16)
    a_send, a_keep, *b = call_small(
        first_kernel, "sum_x_y", idx, (a_keep, a_recv, b_keep, b_recv), [quarter] * 2 + [wide] * 4
    )
    a_recv, b_recv = swap_dp(a_send, 2), fan_out(b)
    *a, b_own = call_small(
        second_kernel,
        "sum_y_z",
        idx,
        (a_keep, a_recv, b[0], *b_recv),
        [((48, D), BF16)] * 4 + [wide],
    )
    a_recv, b_other = fan_out(a), swap_twin(b_own)
    (a_own,) = call_small(third_kernel, "sum_z", idx, (a[0], *a_recv), [((48, D), BF16)])
    return a_own, swap_twin(a_own), b_own, b_other


def vec_kernel(idx, keep, recv, s_o, k_o):
    y = idx[3]
    for i in range(4):
        s_o[i] = plus(keep[2 * i + 1 - y], recv[2 * i + 1 - y])
        k_o[i] = plus(keep[2 * i + y], recv[2 * i + y])


def vec_next_kernel(idx, keep, recv, o0, o1, o2, o3):
    z = idx[4]
    for flip, out in enumerate((o0, o1, o2, o3)):
        out[...] = plus(keep[z ^ flip], recv[z ^ flip])


def exchange_vec(idx, keep, send):
    recv = swap_dp(send, 1)
    send, keep = call_small(vec_kernel, "vec_core", idx, (keep, recv), [((4, 48, 128), BF16)] * 2)
    parts = call_small(
        vec_next_kernel, "vec_y", idx, (keep, swap_dp(send, 2)), [((48, 128), BF16)] * 4
    )
    recv = fan_out(parts)
    (own,) = call_small(third_kernel, "vec_z", idx, (parts[0], *recv), [((48, 128), BF16)])
    return own, swap_twin(own)


def final_kernel(idx, a, ao, b, bo, out):
    twin = idx[0]
    both = b[...].astype(F32) + bo[...].astype(F32)
    if out.shape[0] == 48:
        out[:, 2 * D :] = both

        @pl.when(twin == 0)
        def _():
            out[:, :D] = a[...].astype(F32)
            out[:, D : 2 * D] = ao[...].astype(F32)

        @pl.when(twin == 1)
        def _():
            out[:, :D] = ao[...].astype(F32)
            out[:, D : 2 * D] = a[...].astype(F32)
    else:
        out[96:144, :] = both[:, :D]
        out[144:, :] = both[:, D:]

        @pl.when(twin == 0)
        def _():
            out[:48, :] = a[...].astype(F32)
            out[48:96, :] = ao[...].astype(F32)

        @pl.when(twin == 1)
        def _():
            out[:48, :] = ao[...].astype(F32)
            out[48:96, :] = a[...].astype(F32)


def final_last_kernel(idx, a, ao, b, bo, v, vo, qkv_o, out_o, vec_o):
    twin = idx[0]
    both = b[...].astype(F32) + bo[...].astype(F32)
    qkv_o[:, 2 * D :] = both[:, :D]
    out_o[...] = both[:, D:]

    @pl.when(twin == 0)
    def _():
        qkv_o[:, :D] = a[...].astype(F32)
        qkv_o[:, D : 2 * D] = ao[...].astype(F32)

    @pl.when(twin == 1)
    def _():
        qkv_o[:, :D] = ao[...].astype(F32)
        qkv_o[:, D : 2 * D] = a[...].astype(F32)

    both = v[...].astype(F32) + vo[...].astype(F32)
    vec_o[...] = jnp.concatenate([both, jnp.zeros((80, 128), F32)], axis=0).T[:16]


def add_low(*parts):
    return lax.optimization_barrier(plus(*parts))


def digits_of(devices):
    out, rest = [], devices // 2
    while rest > 1:
        size = 4 if rest % 4 == 0 else 2
        out.append(size)
        rest //= size
    return out


def pick(value, index, axis):
    return lax.dynamic_index_in_dim(value, index, axis, keepdims=False)


def scatter(grad):
    devices = lax.axis_size("dp")
    me = lax.axis_index("dp")
    value = grad.reshape(devices, grad.shape[0] // devices, grad.shape[1])
    unit = 1
    for size in [2] + digits_of(devices):
        mine = (me // unit) % size
        view = value.reshape((value.shape[0] // size, size) + value.shape[1:])
        parts = [pick(view, mine, 1)]
        for flip in range(1, size):
            parts.append(swap_dp(pick(view, mine ^ flip, 1), flip * unit))
        value = add_low(*parts)
        unit *= size
    value = value[0]
    return value.astype(F32) + swap_twin(value).astype(F32)


def body(
    hidden,
    segment_ids,
    targets,
    w_qkv,
    b_query,
    b_value,
    w_out,
    b_out,
    ln1_gain,
    ln1_bias,
    w_in,
    b_in,
    w_down,
    b_down,
    ln2_gain,
    ln2_bias,
):
    row_count, length, width = hidden.shape
    tokens = row_count * length
    devices = lax.axis_size("dp")
    everyone = lax.axis_size(("twin", "dp"))
    me = lax.axis_index("dp")
    twin = lax.axis_index("twin")
    idx = jnp.stack([twin, me, me % 2, (me // 2) % 2, me // 4]).astype(jnp.int32)
    row = lambda v: v.reshape(1, -1)
    weights = (w_qkv, row(b_query), row(b_value), w_out, row(b_out), row(ln1_gain), row(ln1_bias))
    weights += (w_in, row(b_in), w_down, row(b_down), row(ln2_gain), row(ln2_bias))
    qkv, probs, ctx, n1, xh1, rs1, act, dg, xh2, rs2, unit, unitf, inv = forward(
        hidden, segment_ids, weights
    )
    sentences = row_count * SEG
    gathered = lax.all_gather(unit.reshape(sentences, width), ("twin", "dp"), axis=0, tiled=True)
    losses, gb, vec2 = loss_stage(
        idx,
        gathered,
        row(targets),
        unitf.reshape(sentences, width),
        inv.reshape(sentences, 128),
        segment_ids,
        row(ln2_gain),
        xh2,
        rs2,
    )
    share = losses.shape[1] // everyone
    losses = lax.dynamic_slice_in_dim(
        losses[0], lax.axis_index(("twin", "dp")) * share, share, 0
    )
    flat = hidden.reshape(tokens, width)
    if devices == 16 and width == D:
        down = exchange(idx, *down_stage(idx, act, gb))
        gp = pre_stage(gb, w_down, dg)
        *into, vec_in = in_stage(idx, n1, gp)
        into = exchange(idx, *into)
        ga, gc, vec1 = normed_stage(gp, w_in, gb, xh1, rs1, row(ln1_gain), w_out)
        dqkv = attend_back(qkv, gc, probs, row_count, length)
        *last, kv, sv = last_stage(idx, flat, dqkv, ctx, ga, vec2, vec1, vec_in)
        last = exchange(idx, *last)
        small = exchange_vec(idx, kv, sv)
        hidden_grad = hidden_stage(dqkv, w_qkv, ga)
        (grad_w_down,) = call_small(final_kernel, "final_down", idx, down, [((192, D), F32)])
        (grad_w_in,) = call_small(final_kernel, "final_in", idx, into, [((48, FF), F32)])
        grad_w_qkv, grad_w_out, vec = call_small(
            final_last_kernel,
            "final_qkv",
            idx,
            (*last, *small),
            [((48, 3 * D), F32), ((48, D), F32), ((16, 128), F32)],
        )
        vec = vec[:, :48]
        vecs = [vec[i] for i in range(8)]
        grad_b_in = vec[8:12].reshape(-1)
    else:
        gp = pre_stage(gb, w_down, dg)
        ga, gc, vec1 = normed_stage(gp, w_in, gb, xh1, rs1, row(ln1_gain), w_out)
        dqkv = attend_back(qkv, gc, probs, row_count, length)
        hidden_grad = hidden_stage(dqkv, w_qkv, ga)
        grad_w_down = scatter(tn(act, gb).astype(BF16))
        grad_w_in = scatter(tn(n1, gp).astype(BF16))
        wide = jnp.concatenate([dqkv[0], dqkv[1], dqkv[2]], axis=1)
        grad_w_qkv = scatter(tn(flat, wide).astype(BF16))
        grad_w_out = scatter(tn(ctx, ga).astype(BF16))
        sums = jnp.sum(dqkv, axis=1, dtype=F32)
        vec = jnp.concatenate([sums[0:1], sums[2:3], vec1[:3], vec2[:3]])
        vec = scatter(jnp.pad(vec, ((0, 120), (0, 0))).T.astype(BF16)).T
        vecs = [vec[i] for i in range(8)]
        bias = jnp.sum(gp, axis=0, dtype=F32)
        grad_b_in = scatter(jnp.broadcast_to(bias[:, None], (FF, 128)).astype(BF16))[:, 0]
    return (
        losses,
        hidden_grad.reshape(row_count, length, width),
        grad_w_qkv,
        vecs[0],
        vecs[1],
        grad_w_out,
        vecs[2],
        vecs[3],
        vecs[4],
        grad_w_in,
        grad_b_in,
        grad_w_down,
        vecs[5],
        vecs[6],
        vecs[7],
    )


def solution(mesh):
    whole = (P(),) * 14
    placed = (P(("twin", "dp"), None, None), P(("twin", "dp"), None)) + whole
    return jax.shard_map(
        body,
        mesh=mesh,
        in_specs=placed,
        out_specs=(
            P(("twin", "dp")),
            P(("twin", "dp"), None, None),
            P("dp", None),
            P("dp"),
            P("dp"),
            P("dp", None),
            P("dp"),
            P("dp"),
            P("dp"),
            P("dp", None),
            P("dp"),
            P("dp", None),
            P("dp"),
            P("dp"),
            P("dp"),
        ),
        check_vma=False,
    )
```

```python
import functools

import jax
import jax.numpy as jnp
from jax import lax
from jax.experimental import pallas as pl
from jax.experimental.pallas import tpu as pltpu
from jax.sharding import PartitionSpec as P

D = 768
HEADS = 12
HEAD_DIM = 64
FF = 3072
SEG = 8
QB = 128
MOST = 128
PAIRS = HEADS // 2
PW = 2 * HEAD_DIM

cosine_scale = 64.0
loss_scale = 32.0
norm_epsilon = 1e-12
unit_epsilon = 1e-06
masked_score = -1e30

F32 = jnp.float32
BF16 = jnp.bfloat16
VMEM = pltpu.VMEM
ANY = pl.ANY
MIB = 1 << 20


def nn(left, right):
    return lax.dot_general(left, right, (((1,), (0,)), ((), ())), preferred_element_type=F32)


def nt(left, right):
    return lax.dot_general(left, right, (((1,), (1,)), ((), ())), preferred_element_type=F32)


def tn(left, right):
    return lax.dot_general(left, right, (((0,), (0,)), ((), ())), preferred_element_type=F32)


def vspec():
    return pl.BlockSpec(memory_space=VMEM)


def sspec():
    return pl.BlockSpec(memory_space=pltpu.SMEM)


def fixed(shape):
    return pl.BlockSpec(shape, lambda *_: (0,) * len(shape))


def shape_of(shape, dtype):
    return jax.ShapeDtypeStruct(shape, dtype)


def params(mib):
    return pltpu.CompilerParams(vmem_limit_bytes=mib * MIB)


def cost(flops, moved):
    return pl.CostEstimate(flops=int(flops), bytes_accessed=int(moved), transcendentals=0)


def windows(length):
    out, packed = [], 0
    for start in range(0, length, QB):
        low, high = max(0, start - MOST), min(length, start + QB + MOST)
        out.append((start, low, high, packed))
        packed += high - low
    return out, packed


def two_heads(pair):
    first = lax.broadcasted_iota(jnp.int32, pair.shape, 1) < HEAD_DIM
    zero = jnp.zeros((), pair.dtype)
    return jnp.concatenate([jnp.where(first, pair, zero), jnp.where(first, zero, pair)], axis=0)


def pick_heads(both):
    rows = both.shape[1] // 2
    return jnp.concatenate([both[:HEAD_DIM, :rows], both[HEAD_DIM:, rows:]], axis=0).T


def column_of(row):
    return jnp.broadcast_to(row, (8, row.shape[1])).T[:, :1]


def split_low(value):
    high = value.astype(BF16)
    return high, (value - high.astype(F32)).astype(BF16)


def normalise(value):
    middle = jnp.mean(value, axis=-1, keepdims=True)
    centered = value - middle
    spread = jnp.mean(centered * centered, axis=-1, keepdims=True)
    rstd = lax.rsqrt(spread + norm_epsilon)
    return centered * rstd, rstd


def vector(ref):
    return ref[...].astype(F32).reshape(1, ref.shape[0])


def softmax_down(own):
    top = jnp.max(own, axis=0, keepdims=True)
    weights = jnp.exp(own - top)
    total = jnp.sum(weights, axis=0, keepdims=True)
    return (weights * (1.0 / total)).astype(BF16)


def attend(length, qkv, bias, p_s, ctx_s):
    blocks, _ = windows(length)

    def lanes(part, h):
        return slice(part * D + h * PW, part * D + (h + 1) * PW)

    def score(h):
        q_all = qkv[:, lanes(0, h)] * jnp.asarray(HEAD_DIM**-0.5, BF16)
        k_all = qkv[:, lanes(1, h)]
        out = []
        for start, low, high, _ in blocks:
            out.append(nt(k_all[low:high], two_heads(q_all[start : start + QB])))
        return out, qkv[:, lanes(2, h)].T

    ahead = score(0)
    for h in range(PAIRS):
        scores, v_turned = ahead
        if h + 1 < PAIRS:
            ahead = score(h + 1)
        probs = []
        for own, (_, low, high, packed) in zip(scores, blocks):
            mask = bias[packed : packed + high - low, :]
            halves = [softmax_down(own[:, :QB] + mask), softmax_down(own[:, QB:] + mask)]
            probs.append(jnp.concatenate(halves, axis=1))
        for p, (_, low, high, packed) in zip(probs, blocks):
            p_s[h, packed : packed + high - low, :] = p
        outs = [nn(v_turned[:, low:high], p) for p, (_, low, high, _) in zip(probs, blocks)]
        ctx_s[:, lanes(0, h)] = jnp.concatenate([pick_heads(o.astype(BF16)) for o in outs], axis=0)


def forward_kernel(*refs):
    (hid, seg, wqkv_h, bq, bv, wout_h, bout, g1, b1, win_h, bin_, wdown_h, bdown, g2, b2) = refs[:15]
    outs, (unit_o, unitf_o, inv_o) = refs[15:25], refs[25:28]
    wqkv, wout, win, wdown, bias_s, n1_s = refs[28:34]
    kept = refs[34:44]
    sems, osems = refs[44:46]
    qkv_s, p_s, ctx_s, nl_s, xh1_s, rs1_s, act_s, dg_s, xh2_s, rs2_s = kept
    r = pl.program_id(0)
    length = hid.shape[0]
    blocks, _ = windows(length)
    pairs = ((wqkv_h, wqkv), (wout_h, wout), (win_h, win), (wdown_h, wdown))
    copies = [pltpu.make_async_copy(a, b, sems.at[i]) for i, (a, b) in enumerate(pairs)]

    def leaving(i):
        if i == 1:
            return pltpu.make_async_copy(kept[i], outs[i].at[r], osems.at[i])
        rows = pl.ds(pl.multiple_of(r * length, length), length)
        return pltpu.make_async_copy(kept[i], outs[i].at[rows], osems.at[i])

    def settle(*which):
        @pl.when(r > 0)
        def _():
            for i in which:
                leaving(i).wait()

    def send(*which):
        for i in which:
            leaving(i).start()

    @pl.when(r == 0)
    def _():
        for copy in copies:
            copy.start()

    seg_row = seg[pl.ds(r, 1), :].astype(F32)
    seg_col = column_of(seg_row)
    for start, low, high, packed in blocks:
        same = seg_col[low:high] == seg_row[:, start : start + QB]
        bias_s[packed : packed + high - low, :] = jnp.where(same, 0.0, masked_score)

    settle(0, 1, 2, 3, 4, 5)

    @pl.when(r == 0)
    def _():
        copies[0].wait()

    for part in range(3):
        cols = slice(part * D, (part + 1) * D)
        value = nn(hid[...], wqkv[:, cols])
        if part == 0:
            value = value + vector(bq)
        if part == 2:
            value = value + vector(bv)
        qkv_s[:, cols] = value.astype(BF16)
    send(0)
    attend(length, qkv_s, bias_s, p_s, ctx_s)
    send(1, 2)

    @pl.when(r == 0)
    def _():
        copies[1].wait()

    xhat, rstd = normalise(hid[...].astype(F32) + (nn(ctx_s[...], wout[...]) + vector(bout)))
    xh1_s[...] = xhat.astype(BF16)
    rs1_s[...] = jnp.broadcast_to(rstd, rs1_s.shape)
    n1 = xhat * vector(g1) + vector(b1)
    n1_s[...] = n1
    nl_s[...] = n1.astype(BF16)
    send(3, 4, 5)
    settle(6, 7, 8, 9)

    @pl.when(r == 0)
    def _():
        copies[2].wait()

    chunk = 512
    bias_in = vector(bin_)

    def rise(c):
        cols = slice(c * chunk, (c + 1) * chunk)
        return nn(nl_s[...], win[:, cols]) + bias_in[:, cols]

    ahead = rise(0)
    for c in range(FF // chunk):
        pre = ahead
        if c + 1 < FF // chunk:
            ahead = rise(c + 1)
        cols = slice(c * chunk, (c + 1) * chunk)
        half = 0.5 + 0.5 * lax.erf(pre * 0.5**0.5)
        act_s[:, cols] = (pre * half).astype(BF16)
        bell = jnp.exp(pre * pre * -0.5) * 0.3989422804014327
        dg_s[:, cols] = (half + pre * bell).astype(BF16)
    send(6, 7)

    @pl.when(r == 0)
    def _():
        copies[3].wait()

    branch = nn(act_s[...], wdown[...]) + vector(bdown)
    xhat, rstd = normalise(n1_s[...] + branch)
    xh2_s[...] = xhat.astype(BF16)
    rs2_s[...] = jnp.broadcast_to(rstd, rs2_s.shape)
    send(8, 9)
    out = xhat * vector(g2) + vector(b2)
    member = (lax.broadcasted_iota(jnp.int32, (SEG, length), 0).astype(F32) == seg_row).astype(F32)
    counts = jnp.sum(member, axis=1, keepdims=True)
    high, low = split_low(out)
    member = member.astype(BF16)
    pooled = (nn(member, high) + nn(member, low)) / counts
    inv = lax.rsqrt(jnp.mean(pooled * pooled, axis=-1, keepdims=True) + unit_epsilon)
    unit = pooled * inv
    unitf_o[...] = unit
    unit_o[...] = unit.astype(BF16)
    inv_o[...] = jnp.broadcast_to(inv / counts, inv_o.shape)

    @pl.when(r == pl.num_programs(0) - 1)
    def _():
        for i in range(10):
            leaving(i).wait()


def forward(hidden, seg, weights):
    rows, length, _ = hidden.shape
    tokens = rows * length
    _, packed = windows(length)
    wide = [(3 * D, BF16), None, (D, BF16), (D, BF16), (D, BF16), (128, F32)]
    wide += [(FF, BF16), (FF, BF16), (D, BF16), (128, F32)]
    out_shape, kept = [], []
    for item in wide:
        if item is None:
            out_shape.append(shape_of((rows, PAIRS, packed, 2 * QB), BF16))
            kept.append(VMEM((PAIRS, packed, 2 * QB), BF16))
        else:
            out_shape.append(shape_of((tokens, item[0]), item[1]))
            kept.append(VMEM((length, item[0]), item[1]))
    hbm = pl.BlockSpec(memory_space=ANY)
    out_specs = [hbm] * 10 + [
        pl.BlockSpec((None, SEG, D), lambda r: (r, 0, 0)),
        pl.BlockSpec((None, SEG, D), lambda r: (r, 0, 0)),
        pl.BlockSpec((None, SEG, 128), lambda r: (r, 0, 0)),
    ]
    out_shape += [
        shape_of((rows, SEG, D), BF16),
        shape_of((rows, SEG, D), F32),
        shape_of((rows, SEG, 128), F32),
    ]
    large = (0, 3, 7, 9)
    in_specs = [pl.BlockSpec((length, D), lambda r: (r, 0)), vspec()]
    in_specs += [hbm if i in large else vspec() for i in range(13)]
    return pl.pallas_call(
        forward_kernel,
        name="forward",
        grid=(rows,),
        in_specs=in_specs,
        out_specs=out_specs,
        out_shape=out_shape,
        scratch_shapes=[VMEM(weights[i].shape, BF16) for i in large]
        + [VMEM((packed, QB), F32), VMEM((length, D), F32)]
        + kept
        + [pltpu.SemaphoreType.DMA((4,)), pltpu.SemaphoreType.DMA((10,))],
        cost_estimate=cost(1e9, 4e6),
        compiler_params=params(60),
    )(hidden.reshape(tokens, D), seg, *weights)


def loss_kernel(flips, idx, *refs):
    pieces, refs = refs[: len(flips)], refs[len(flips) :]
    targets, unitf, inv, seg, g2, xh2, rs2, loss_o, gb_o, vec_o, slope_s, rows_s, units = refs
    twin, me = idx[0], idx[1]
    count = units.shape[0] // 2
    sentences = unitf.shape[0]
    for piece, own_flips in zip(pieces, flips):
        if own_flips is None:
            units[...] = piece[...]
            continue
        for i, (twin_flip, flip) in enumerate(own_flips):
            at = (twin ^ twin_flip) * count + (me ^ flip) * sentences
            at = pl.multiple_of(at, sentences)
            units[pl.ds(at, sentences), :] = piece[i * sentences : (i + 1) * sentences, :]
    rows, length = seg.shape
    step = min(count, 256)
    factor = cosine_scale / D
    positives = units.at[pl.ds(count, count)]
    own = pl.ds(pl.multiple_of(me * sentences, sentences), sentences)

    def one_block(i, carry):
        lanes = pl.ds(pl.multiple_of(i * step, step), step)
        sims = nt(positives[...], units[lanes, :]) * factor
        top = jnp.max(sims, axis=0, keepdims=True)
        weights = jnp.exp(sims - top)
        total = jnp.sum(weights, axis=0, keepdims=True)
        hit = lax.broadcasted_iota(jnp.int32, sims.shape, 0) == targets[:, lanes]
        picked = jnp.sum(jnp.where(hit, sims, 0.0), axis=0, keepdims=True)
        loss_o[:, lanes] = top + jnp.log(total) - picked
        slope = loss_scale * (weights * (1.0 / total) - hit.astype(F32))
        slope_s[:, lanes] = slope.astype(BF16)
        return carry

    if count == step:
        one_block(0, 0)
    else:
        lax.fori_loop(0, count // step, one_block, 0)

    @pl.when(twin == 0)
    def _():
        def part(i, carry):
            lanes = pl.ds(pl.multiple_of(i * step, step), step)
            rows_s[lanes, :] = tn(slope_s[:, lanes], positives[...])
            return carry

        lax.fori_loop(0, count // step, part, 0)
        rows_s[pl.ds(0, sentences), :] = rows_s[own, :]

    @pl.when(twin == 1)
    def _():
        rows_s[pl.ds(0, sentences), :] = nn(slope_s[own, :], units[pl.ds(0, count), :])

    gu = rows_s[pl.ds(0, sentences), :] * factor
    unit = unitf[...]
    gs = inv[:, :1] * (gu - unit * jnp.mean(gu * unit, axis=-1, keepdims=True))
    gy = gs * vector(g2)
    u = gy - jnp.mean(gy, axis=-1, keepdims=True)
    gain = jnp.zeros((1, D), F32)
    shift = jnp.zeros((1, D), F32)
    summed = jnp.zeros((1, D), F32)
    for r in range(rows):
        part = slice(r * SEG, (r + 1) * SEG)
        tok = slice(r * length, (r + 1) * length)
        seg_row = seg[r : r + 1, :]
        hits = lax.broadcasted_iota(jnp.int32, (SEG, length), 0) == seg_row
        member = hits.astype(F32).astype(BF16)
        counts = jnp.sum(hits.astype(F32), axis=1, keepdims=True)
        xhat_low = xh2[tok, :]
        gain += jnp.sum(nn(member, xhat_low) * gs[part], axis=0, keepdims=True)
        shift += jnp.sum(counts * gs[part], axis=0, keepdims=True)
        xhat = xhat_low.astype(F32)
        high, low = split_low(u[part])
        spread = tn(member, high) + tn(member, low)
        inner = jnp.mean(spread * xhat, axis=-1, keepdims=True)
        grad = rs2[tok, :1] * (spread - xhat * inner)
        grad_low = grad.astype(BF16)
        gb_o[tok, :] = grad_low
        summed += jnp.sum(grad_low.astype(F32), axis=0, keepdims=True)
    vec_o[...] = jnp.concatenate([summed, gain, shift, jnp.zeros((5, D), F32)], axis=0)


def loss_stage(idx, gathered, targets, unitf, inv, seg, g2, xh2, rs2):
    pieces, flips = gathered
    tokens = xh2.shape[0]
    count = targets.shape[1]
    return pl.pallas_call(
        functools.partial(loss_kernel, flips),
        name="loss",
        in_specs=[sspec()] + [vspec()] * (7 + len(pieces)),
        out_specs=[vspec()] * 3,
        out_shape=[
            shape_of((1, count), F32),
            shape_of((tokens, D), BF16),
            shape_of((8, D), F32),
        ],
        scratch_shapes=[VMEM((count, count), BF16), VMEM((count, D), F32), VMEM((2 * count, D), BF16)],
        cost_estimate=cost(1e8, 1e6),
        compiler_params=params(48),
    )(idx, *pieces, targets, unitf, inv, seg, g2, xh2, rs2)


def pre_kernel(gb, wdown, dg, out):
    out[...] = (nt(gb[...], wdown[...]) * dg[...].astype(F32)).astype(BF16)


def pre_stage(gb, wdown, dg):
    tokens = gb.shape[0]
    n = 768
    return pl.pallas_call(
        pre_kernel,
        name="grad_pre",
        grid=(FF // n,),
        in_specs=[
            fixed(gb.shape),
            pl.BlockSpec((n, D), lambda j: (j, 0)),
            pl.BlockSpec((tokens, n), lambda j: (0, j)),
        ],
        out_specs=pl.BlockSpec((tokens, n), lambda j: (0, j)),
        out_shape=shape_of((tokens, FF), BF16),
        cost_estimate=cost(1e8, 1e6),
        compiler_params=params(40),
    )(gb, wdown, dg)


def normed_kernel(gp, win, gb, xh1, rs1, g1, wout, ga_o, gc_o, vec_o):
    m = 512
    count = gp.shape[0] // m
    gain, shift, summed = [jnp.zeros((1, D), F32) for _ in range(3)]
    grads = [nt(gp[i * m : (i + 1) * m, :], win[...]) for i in range(count)]
    for i in range(count):
        rows = slice(i * m, (i + 1) * m)
        grad = grads[i] + gb[rows, :].astype(F32)
        xhat = xh1[rows, :].astype(F32)
        gain += jnp.sum(grad * xhat, axis=0, keepdims=True)
        shift += jnp.sum(grad, axis=0, keepdims=True)
        gy = grad * vector(g1)
        inner = jnp.mean(gy * xhat, axis=-1, keepdims=True)
        total = rs1[rows, :1] * (gy - jnp.mean(gy, axis=-1, keepdims=True) - xhat * inner)
        low = total.astype(BF16)
        ga_o[rows, :] = low
        summed += jnp.sum(low.astype(F32), axis=0, keepdims=True)
    for i in range(count):
        rows = slice(i * m, (i + 1) * m)
        gc_o[rows, :] = nt(ga_o[rows, :], wout[...]).astype(BF16)
    vec_o[...] = jnp.concatenate([summed, gain, shift, jnp.zeros((5, D), F32)], axis=0)


def normed_stage(gp, win, gb, xh1, rs1, g1, wout):
    tokens = gp.shape[0]
    return pl.pallas_call(
        normed_kernel,
        name="grad_normed",
        in_specs=[vspec()] * 7,
        out_specs=[vspec()] * 3,
        out_shape=[
            shape_of((tokens, D), BF16),
            shape_of((tokens, D), BF16),
            shape_of((8, D), F32),
        ],
        cost_estimate=cost(1e8, 1e6),
        compiler_params=params(40),
    )(gp, win, gb, xh1, rs1, g1, wout)


def attend_back_kernel(q_ref, k_ref, v_ref, g_ref, p_ref, out_ref):
    length = q_ref.shape[0]
    blocks, _ = windows(length)
    group = q_ref.shape[1] // PW
    scale = HEAD_DIM**-0.5
    loaded, grads = [], []
    for h in range(group):
        lanes = slice(h * PW, (h + 1) * PW)
        q2 = [two_heads(q_ref[b[0] : b[0] + QB, lanes]) for b in blocks]
        g2 = [two_heads(g_ref[b[0] : b[0] + QB, lanes]) for b in blocks]
        loaded.append((q2, g2, k_ref[:, lanes].T))
        v_all = v_ref[:, lanes]
        grads.append([nt(v_all[b[1] : b[2]], g) for b, g in zip(blocks, g2)])
    slopes = []
    for h in range(group):
        own = []
        for gp, (_, low, high, packed) in zip(grads[h], blocks):
            p = p_ref[h, packed : packed + high - low, :].astype(F32)
            weighted = p * gp
            inner = jnp.sum(weighted, axis=0, keepdims=True)
            own.append((weighted - p * inner).astype(BF16))
        slopes.append(own)

    def gather(parts):
        out = []
        for block in range(len(blocks)):
            total = None
            for part, (_, low, high, _) in zip(parts, blocks):
                base = block * QB - low
                if 0 <= base < high - low:
                    piece = part[base : base + QB]
                    total = piece if total is None else total + piece
            out.append(total)
        return jnp.concatenate(out, axis=0)

    for h in range(group):
        lanes = slice(h * PW, (h + 1) * PW)
        q2, g2, k_turned = loaded[h]
        dq = [nn(k_turned[:, b[1] : b[2]], s) for b, s in zip(blocks, slopes[h])]
        dv = [nn(p_ref[h, b[3] : b[3] + b[2] - b[1], :], g) for b, g in zip(blocks, g2)]
        dk = [nn(s, q) for s, q in zip(slopes[h], q2)]
        turned = [pick_heads((part * scale).astype(BF16)) for part in dq]
        out_ref[0, :, lanes] = jnp.concatenate(turned, axis=0)
        out_ref[1, :, lanes] = (gather(dk) * scale).astype(BF16)
        out_ref[2, :, lanes] = gather(dv).astype(BF16)


def attend_back(qkv, grad_context, probs, rows, length):
    _, packed = windows(length)
    group = 3
    steps = PAIRS // group
    width = group * PW

    def block(part):
        return pl.BlockSpec((length, width), lambda r, h: (r, part * steps + h))

    return pl.pallas_call(
        attend_back_kernel,
        name="attend_back",
        grid=(rows, steps),
        in_specs=[
            block(0),
            block(1),
            block(2),
            pl.BlockSpec((length, width), lambda r, h: (r, h)),
            pl.BlockSpec((None, group, packed, 2 * QB), lambda r, h: (r, h, 0, 0)),
        ],
        out_specs=pl.BlockSpec((3, length, width), lambda r, h: (0, r, h)),
        out_shape=shape_of((3, rows * length, D), BF16),
        cost_estimate=cost(1e8, 1e6),
        compiler_params=params(40),
    )(qkv, qkv, qkv, grad_context, probs)


def hidden_kernel(dqkv, wqkv, ga, out):
    m = 512
    for i in range(ga.shape[0] // m):
        rows = slice(i * m, (i + 1) * m)
        total = ga[rows, :].astype(F32)
        for part in range(3):
            total = total + nt(dqkv[part, rows, :], wqkv[:, part * D : (part + 1) * D])
        out[rows, :] = total.astype(BF16)


def hidden_stage(dqkv, wqkv, ga):
    return pl.pallas_call(
        hidden_kernel,
        name="hidden_grad",
        in_specs=[vspec()] * 3,
        out_specs=vspec(),
        out_shape=shape_of(ga.shape, BF16),
        cost_estimate=cost(1e8, 1e6),
        compiler_params=params(32),
    )(dqkv, wqkv, ga)


def place_of(half, quarter, owner):
    c, y, z0, z1 = owner & 1, (owner >> 1) & 1, (owner >> 2) & 1, owner >> 3
    order = (quarter, y, z0, z1, c) if half == 0 else (y, z0, z1, quarter, c)
    out = 0
    for bit in order:
        out = 2 * out + bit
    return out


def halves(core, store):
    @pl.when(core == 0)
    def _():
        store(0, 0)
        store(1, 1)

    @pl.when(core == 1)
    def _():
        store(0, 1)
        store(1, 0)


def down_kernel(idx, act, gb, keep, send):
    refs = (keep, send)
    n = 768
    for j in range(FF // n):
        total = tn(act[:, j * n : (j + 1) * n], gb[...]).astype(BF16)

        def store(half, which):
            for local in range(4):
                for quarter in range(2):
                    base = local * 192 + (2 * half + quarter) * 48
                    at = place_of(half, quarter, 4 * j + local)
                    refs[which][at] = total[base : base + 48]

        halves(idx[2], store)


def down_stage(idx, act, gb):
    return pl.pallas_call(
        down_kernel,
        name="grad_w_down",
        in_specs=[sspec(), vspec(), vspec()],
        out_specs=[vspec()] * 2,
        out_shape=[shape_of((32, 48, D), BF16)] * 2,
        cost_estimate=cost(1e8, 1e6),
        compiler_params=params(40),
    )(idx, act, gb)


def store_quarter(refs, half, which, quarter, total, lanes):
    for owner in range(16):
        refs[which][place_of(half, quarter, owner), :, lanes] = total[owner * 48 : (owner + 1) * 48]


def in_kernel(idx, n1, gp, keep, send, vec_o, turned):
    refs = (keep, send)
    turned[...] = n1[...].T
    for j in range(4):
        total = nn(turned[...], gp[:, j * D : (j + 1) * D]).astype(BF16)

        @pl.when(idx[2] == j // 2)
        def _():
            store_quarter(refs, j // 2, 0, j % 2, total, slice(0, D))

        @pl.when(idx[2] != j // 2)
        def _():
            store_quarter(refs, j // 2, 1, j % 2, total, slice(0, D))

    vec_o[...] = jnp.sum(gp[...].astype(F32), axis=0, keepdims=True)


def in_stage(idx, n1, gp):
    return pl.pallas_call(
        in_kernel,
        name="grad_w_in",
        in_specs=[sspec(), vspec(), vspec()],
        out_specs=[vspec()] * 3,
        out_shape=[shape_of((32, 48, D), BF16)] * 2 + [shape_of((1, FF), F32)],
        scratch_shapes=[VMEM((D, n1.shape[0]), BF16)],
        cost_estimate=cost(1e8, 1e6),
        compiler_params=params(40),
    )(idx, n1, gp)


def last_kernel(idx, hid, dqkv, ctx, ga, vecs, keep, send, turned, sums_s):
    refs = (keep, send)
    turned[...] = hid[...].T
    lanes = slice(0, D)
    sums_s[...] = jnp.zeros_like(sums_s)
    for j in range(4):
        if j < 3:
            total = nn(turned[...], dqkv[j]).astype(BF16)
        else:
            total = tn(ctx[...], ga[...]).astype(BF16)

        @pl.when(idx[2] == j // 2)
        def _():
            store_quarter(refs, j // 2, 0, j % 2, total, lanes)

        @pl.when(idx[2] != j // 2)
        def _():
            store_quarter(refs, j // 2, 1, j % 2, total, lanes)

    sums_s[:16, :] = vecs[...]
    sums_s[0:1, :] = jnp.sum(dqkv[0].astype(F32), axis=0, keepdims=True)
    sums_s[1:2, :] = jnp.sum(dqkv[2].astype(F32), axis=0, keepdims=True)
    small = sums_s[...].T.astype(BF16)
    lanes = slice(D, D + 128)

    def store(half, which):
        for quarter in range(2):
            store_quarter(refs, half, which, quarter, small, lanes)

    halves(idx[2], store)


def last_stage(idx, hid, dqkv, ctx, ga, vecs):
    return pl.pallas_call(
        last_kernel,
        name="grad_w_qkv",
        in_specs=[sspec()] + [vspec()] * 5,
        out_specs=[vspec()] * 2,
        out_shape=[shape_of((32, 48, D + 128), BF16)] * 2,
        scratch_shapes=[VMEM((D, hid.shape[0]), BF16), VMEM((128, D), F32)],
        cost_estimate=cost(1e8, 1e6),
        compiler_params=params(48),
    )(idx, hid, dqkv, ctx, ga, vecs)


def swap_dp(value, flip):
    devices = lax.axis_size("dp")
    return lax.ppermute(value, "dp", [(i, i ^ flip) for i in range(devices)])


def swap_twin(value):
    return lax.ppermute(value, "twin", [(0, 1), (1, 0)])


TWIN = 16
ROUTES = ((TWIN, 2, 4, 8, TWIN), (2, 4, 8, TWIN, TWIN))


def step_swap(value, step):
    pairs = [(i, i ^ ROUTES[i & 1][step]) for i in range(2 * TWIN)]
    return lax.ppermute(value, ("twin", "dp"), pairs)


def plus(*values):
    total = values[0].astype(F32)
    for value in values[1:]:
        total = total + value.astype(F32)
    return total.astype(BF16)


def call_small(kernel, name, idx, operands, outs):
    return pl.pallas_call(
        kernel,
        name=name,
        in_specs=[sspec()] + [vspec()] * len(operands),
        out_specs=[vspec()] * len(outs),
        out_shape=[shape_of(shape, dtype) for shape, dtype in outs],
        cost_estimate=cost(1e6, 1e5),
        compiler_params=params(32),
    )(idx, *operands)


def half_kernel(step, idx, keep, recv, keep_o, send_o):
    count = keep_o.shape[0]
    bit = idx[3 + step]
    mine = pl.ds(bit * count, count)
    other = pl.ds((1 - bit) * count, count)
    keep_o[...] = plus(keep[mine], recv[mine])
    send_o[...] = plus(keep[other], recv[other])


def half_step(idx, step, keep, recv):
    count, rows, width = keep.shape
    shape = (count // 2, rows, width)
    kernel = functools.partial(half_kernel, step)
    if count < 32:
        return call_small(kernel, "sum_" + str(step), idx, (keep, recv), [(shape, BF16)] * 2)
    pieces = 4
    block = (2, shape[0] // pieces, rows, width)

    def blocked(idx, keep, recv, keep_o, send_o):
        bit = idx[3 + step]
        keep_o[...] = plus(keep[bit], recv[bit])
        send_o[...] = plus(keep[1 - bit], recv[1 - bit])

    whole = (2, count // 2, rows, width)
    spec = pl.BlockSpec(block, lambda i: (0, i, 0, 0))
    return pl.pallas_call(
        blocked,
        name="sum_core",
        grid=(pieces,),
        in_specs=[sspec(), spec, spec],
        out_specs=[pl.BlockSpec(block[1:], lambda i: (i, 0, 0))] * 2,
        out_shape=[shape_of(shape, BF16)] * 2,
        cost_estimate=cost(1e6, 1e5),
        compiler_params=params(32),
    )(idx, keep.reshape(whole), recv.reshape(whole))


def own_kernel(idx, keep, recv, out):
    out[...] = plus(keep[...], recv[...])


def turn_kernel(idx, own, other, keep_o, send_o):
    twin, core = idx[0], idx[2]
    keep_o[twin] = own[core]
    keep_o[1 - twin] = other[core]
    send_o[twin] = own[1 - core]
    send_o[1 - twin] = other[1 - core]


class Order:
    def __init__(self):
        self.last = None

    def after(self, value):
        if self.last is None:
            return value
        return lax.optimization_barrier((value, self.last))[0]

    def done(self, value):
        self.last = value
        return value


class Exchange:
    def __init__(self, order, idx, keep, send):
        self.order, self.idx, self.step = order, idx, 0
        self.keep, self.recv = keep, swap_dp(send, 1)

    def advance(self):
        idx, order = self.idx, self.order
        keep, recv = order.after(self.keep), self.recv
        if self.step < 4:
            keep, send = half_step(idx, self.step, keep, recv)
            recv = step_swap(send, self.step)
        elif self.step == 4:
            shape = keep.shape
            (keep,) = call_small(own_kernel, "sum_4", idx, (keep, recv), [(shape, BF16)])
            recv = step_swap(keep, 4)
        else:
            shape = keep.shape
            keep, send = call_small(turn_kernel, "turn", idx, (keep, recv), [(shape, BF16)] * 2)
            recv = swap_dp(send, 1)
        order.done(keep)
        self.keep, self.recv = keep, recv
        self.step += 1

    def finish(self, kernel, name, outs):
        keep = self.order.after(self.keep)
        out = call_small(kernel, name, self.idx, (keep, self.recv), outs)
        self.order.done(out[0])
        return out


def gather_units(unit):
    flips = [(0, 0)]
    for flip in (8, 4):
        unit = jnp.concatenate([unit, swap_dp(unit, flip)], axis=0)
        flips = flips + [(t, f ^ flip) for t, f in flips]
    pairs = [(i, i ^ (TWIN + 2)) for i in range(2 * TWIN)]
    far = lax.ppermute(unit, ("twin", "dp"), pairs)
    unit = jnp.concatenate([unit, swap_dp(unit, 2), swap_twin(unit), far], axis=0)
    flips = [(t ^ a, f ^ b) for a, b in ((0, 0), (0, 2), (1, 0), (1, 2)) for t, f in flips]
    return (unit, swap_dp(unit, 1)), (flips, [(t, f ^ 1) for t, f in flips])


def final_column_kernel(idx, keep, recv, *outs):
    width = keep.shape[2]

    def write(first, second):
        for quarter in range(4):
            part = (first if quarter < 2 else second)[quarter % 2].astype(F32)
            if len(outs) == 1:
                outs[0][:, quarter * D : (quarter + 1) * D] = part
            elif quarter < 3:
                outs[0][:, quarter * D : (quarter + 1) * D] = part[:, :D]
            else:
                outs[1][...] = part[:, :D]
                small = jnp.concatenate([part[:, D:], jnp.zeros((80, 128), F32)], axis=0)
                outs[2][...] = small.T[:16]

    del width

    @pl.when(idx[2] == 0)
    def _():
        write(keep, recv)

    @pl.when(idx[2] == 1)
    def _():
        write(recv, keep)


def final_row_kernel(idx, keep, recv, out):
    def write(first, second):
        for quarter in range(4):
            part = (first if quarter < 2 else second)[quarter % 2].astype(F32)
            out[quarter * 48 : (quarter + 1) * 48, :] = part

    @pl.when(idx[2] == 0)
    def _():
        write(keep, recv)

    @pl.when(idx[2] == 1)
    def _():
        write(recv, keep)


def add_low(*parts):
    return lax.optimization_barrier(plus(*parts))


def digits_of(devices):
    out, rest = [], devices // 2
    while rest > 1:
        size = 4 if rest % 4 == 0 else 2
        out.append(size)
        rest //= size
    return out


def pick(value, index, axis):
    return lax.dynamic_index_in_dim(value, index, axis, keepdims=False)


def scatter(grad):
    devices = lax.axis_size("dp")
    me = lax.axis_index("dp")
    value = grad.reshape(devices, grad.shape[0] // devices, grad.shape[1])
    unit = 1
    for size in [2] + digits_of(devices):
        mine = (me // unit) % size
        view = value.reshape((value.shape[0] // size, size) + value.shape[1:])
        parts = [pick(view, mine, 1)]
        for flip in range(1, size):
            parts.append(swap_dp(pick(view, mine ^ flip, 1), flip * unit))
        value = add_low(*parts)
        unit *= size
    value = value[0]
    return value.astype(F32) + swap_twin(value).astype(F32)


def body(
    hidden,
    segment_ids,
    targets,
    w_qkv,
    b_query,
    b_value,
    w_out,
    b_out,
    ln1_gain,
    ln1_bias,
    w_in,
    b_in,
    w_down,
    b_down,
    ln2_gain,
    ln2_bias,
):
    row_count, length, width = hidden.shape
    tokens = row_count * length
    devices = lax.axis_size("dp")
    everyone = lax.axis_size(("twin", "dp"))
    me = lax.axis_index("dp")
    twin = lax.axis_index("twin")
    core, y, z0, z1 = me & 1, (me >> 1) & 1, (me >> 2) & 1, me >> 3
    first = core == 0
    bits = [jnp.where(first, a, b) for a, b in ((twin, y), (y, z0), (z0, z1), (z1, twin))]
    idx = jnp.stack([twin, me, core] + bits).astype(jnp.int32)
    weights = (w_qkv, b_query, b_value, w_out, b_out, ln1_gain, ln1_bias)
    weights += (w_in, b_in, w_down, b_down, ln2_gain, ln2_bias)
    qkv, probs, ctx, n1, xh1, rs1, act, dg, xh2, rs2, unit, unitf, inv = forward(
        hidden, segment_ids, weights
    )
    sentences = row_count * SEG
    unit = unit.reshape(sentences, width)
    direct = devices == TWIN and sentences == 16
    if direct:
        gathered = gather_units(unit)
    else:
        gathered = ((lax.all_gather(unit, ("twin", "dp"), axis=0, tiled=True),), (None,))
    losses, gb, vec2 = loss_stage(
        idx,
        gathered,
        targets.reshape(1, -1),
        unitf.reshape(sentences, width),
        inv.reshape(sentences, 128),
        segment_ids,
        ln2_gain,
        xh2,
        rs2,
    )
    share = losses.shape[1] // everyone
    losses = lax.dynamic_slice_in_dim(
        losses[0], lax.axis_index(("twin", "dp")) * share, share, 0
    )
    flat = hidden.reshape(tokens, width)
    if direct:
        order = Order()
        keep, send = down_stage(idx, act, gb)
        order.done(keep)
        down = Exchange(order, idx, keep, send)
        gp = order.done(pre_stage(order.after(gb), w_down, dg))
        down.advance()
        keep, send, sums = in_stage(idx, order.after(n1), gp)
        order.done(keep)
        into = Exchange(order, idx, keep, send)
        ga, gc, vec1 = normed_stage(order.after(gp), w_in, gb, xh1, rs1, ln1_gain, w_out)
        order.done(ga)
        into.advance()
        down.advance()
        dqkv = order.done(attend_back(qkv, order.after(gc), probs, row_count, length))
        down.advance()
        into.advance()
        wide = sums.reshape(devices, 4, 48).transpose(1, 0, 2).reshape(4, width)
        nothing = jnp.zeros((2, width), F32)
        vecs = jnp.concatenate([nothing, vec1[:3], vec2[:3], wide, nothing, nothing])
        keep, send = last_stage(idx, order.after(flat), dqkv, ctx, ga, vecs)
        order.done(keep)
        last = Exchange(order, idx, keep, send)
        down.advance()
        into.advance()
        last.advance()
        down.advance()
        into.advance()
        hidden_grad = order.done(hidden_stage(order.after(dqkv), w_qkv, ga))
        down.advance()
        into.advance()
        last.advance()
        (grad_w_down,) = down.finish(final_row_kernel, "final_down", [((192, D), F32)])
        into.advance()
        last.advance()
        (grad_w_in,) = into.finish(final_column_kernel, "final_in", [((48, FF), F32)])
        last.advance()
        last.advance()
        last.advance()
        shapes = [((48, 3 * D), F32), ((48, D), F32), ((16, 128), F32)]
        grad_w_qkv, grad_w_out, vec = last.finish(final_column_kernel, "final_qkv", shapes)
        vec = vec[:, :48]
        vecs = [vec[i] for i in range(8)]
        grad_b_in = vec[8:12].reshape(-1)
    else:
        gp = pre_stage(gb, w_down, dg)
        ga, gc, vec1 = normed_stage(gp, w_in, gb, xh1, rs1, ln1_gain, w_out)
        dqkv = attend_back(qkv, gc, probs, row_count, length)
        hidden_grad = hidden_stage(dqkv, w_qkv, ga)
        grad_w_down = scatter(tn(act, gb).astype(BF16))
        grad_w_in = scatter(tn(n1, gp).astype(BF16))
        wide = jnp.concatenate([dqkv[0], dqkv[1], dqkv[2]], axis=1)
        grad_w_qkv = scatter(tn(flat, wide).astype(BF16))
        grad_w_out = scatter(tn(ctx, ga).astype(BF16))
        sums = jnp.sum(dqkv, axis=1, dtype=F32)
        vec = jnp.concatenate([sums[0:1], sums[2:3], vec1[:3], vec2[:3]])
        vec = scatter(jnp.pad(vec, ((0, 120), (0, 0))).T.astype(BF16)).T
        vecs = [vec[i] for i in range(8)]
        bias = jnp.sum(gp, axis=0, dtype=F32)
        grad_b_in = scatter(jnp.broadcast_to(bias[:, None], (FF, 128)).astype(BF16))[:, 0]
    return (
        losses,
        hidden_grad.reshape(row_count, length, width),
        grad_w_qkv,
        vecs[0],
        vecs[1],
        grad_w_out,
        vecs[2],
        vecs[3],
        vecs[4],
        grad_w_in,
        grad_b_in,
        grad_w_down,
        vecs[5],
        vecs[6],
        vecs[7],
    )


def solution(mesh):
    whole = (P(),) * 14
    placed = (P(("twin", "dp"), None, None), P(("twin", "dp"), None)) + whole
    return jax.shard_map(
        body,
        mesh=mesh,
        in_specs=placed,
        out_specs=(
            P(("twin", "dp")),
            P(("twin", "dp"), None, None),
            P("dp", None),
            P("dp"),
            P("dp"),
            P("dp", None),
            P("dp"),
            P("dp"),
            P("dp"),
            P("dp", None),
            P("dp"),
            P("dp", None),
            P("dp"),
            P("dp"),
            P("dp"),
        ),
        check_vma=False,
    )
```

```python
import functools

import jax
import jax.numpy as jnp
from jax import lax
from jax.experimental import pallas as pl
from jax.experimental.pallas import tpu as pltpu
from jax.sharding import PartitionSpec as P

D = 768
HEADS = 12
HEAD_DIM = 64
FF = 3072
SEG = 8
QB = 128
MOST = 128
PAIRS = HEADS // 2
PW = 2 * HEAD_DIM

cosine_scale = 64.0
loss_scale = 32.0
norm_epsilon = 1e-12
unit_epsilon = 1e-06
masked_score = -1e30

F32 = jnp.float32
BF16 = jnp.bfloat16
VMEM = pltpu.VMEM
ANY = pl.ANY
MIB = 1 << 20


def nn(left, right):
    return lax.dot_general(left, right, (((1,), (0,)), ((), ())), preferred_element_type=F32)


def nt(left, right):
    return lax.dot_general(left, right, (((1,), (1,)), ((), ())), preferred_element_type=F32)


def tn(left, right):
    return lax.dot_general(left, right, (((0,), (0,)), ((), ())), preferred_element_type=F32)


def vspec():
    return pl.BlockSpec(memory_space=VMEM)


def sspec():
    return pl.BlockSpec(memory_space=pltpu.SMEM)


def hspec():
    return pl.BlockSpec(memory_space=pltpu.HBM)


class Fetch:
    def __init__(self, sems, pairs):
        self.copies = [pltpu.make_async_copy(a, b, sems.at[i]) for i, (a, b) in enumerate(pairs)]
        for copy in self.copies:
            copy.start()

    def wait(self, *which):
        for i in which:
            self.copies[i].wait()


def fixed(shape):
    return pl.BlockSpec(shape, lambda *_: (0,) * len(shape))


def shape_of(shape, dtype):
    return jax.ShapeDtypeStruct(shape, dtype)


def params(mib):
    return pltpu.CompilerParams(vmem_limit_bytes=mib * MIB)


def cost(flops, moved):
    return pl.CostEstimate(flops=int(flops), bytes_accessed=int(moved), transcendentals=0)


def windows(length):
    out, packed = [], 0
    for start in range(0, length, QB):
        low, high = max(0, start - MOST), min(length, start + QB + MOST)
        out.append((start, low, high, packed))
        packed += high - low
    return out, packed


def two_heads(pair):
    first = lax.broadcasted_iota(jnp.int32, pair.shape, 1) < HEAD_DIM
    zero = jnp.zeros((), pair.dtype)
    return jnp.concatenate([jnp.where(first, pair, zero), jnp.where(first, zero, pair)], axis=0)


def pick_heads(both):
    rows = both.shape[1] // 2
    return jnp.concatenate([both[:HEAD_DIM, :rows], both[HEAD_DIM:, rows:]], axis=0).T


def column_of(row):
    return jnp.broadcast_to(row, (8, row.shape[1])).T[:, :1]


def split_low(value):
    high = value.astype(BF16)
    return high, (value - high.astype(F32)).astype(BF16)


def normalise(value):
    middle = jnp.mean(value, axis=-1, keepdims=True)
    centered = value - middle
    spread = jnp.mean(centered * centered, axis=-1, keepdims=True)
    rstd = lax.rsqrt(spread + norm_epsilon)
    return centered * rstd, rstd


def vector(ref):
    return ref[...].astype(F32).reshape(1, ref.shape[0])


def softmax_down(own):
    top = jnp.max(own, axis=0, keepdims=True)
    weights = jnp.exp(own - top)
    total = jnp.sum(weights, axis=0, keepdims=True)
    return (weights * (1.0 / total)).astype(BF16)


def attend(length, qkv, bias, p_s, ctx_s):
    blocks, _ = windows(length)

    def lanes(part, h):
        return slice(part * D + h * PW, part * D + (h + 1) * PW)

    def score(h):
        q_all = qkv[:, lanes(0, h)] * jnp.asarray(HEAD_DIM**-0.5, BF16)
        k_all = qkv[:, lanes(1, h)]
        out = []
        for start, low, high, _ in blocks:
            out.append(nt(k_all[low:high], two_heads(q_all[start : start + QB])))
        return out, qkv[:, lanes(2, h)].T

    ahead = score(0)
    for h in range(PAIRS):
        scores, v_turned = ahead
        if h + 1 < PAIRS:
            ahead = score(h + 1)
        probs = []
        for own, (_, low, high, packed) in zip(scores, blocks):
            mask = bias[packed : packed + high - low, :]
            halves = [softmax_down(own[:, :QB] + mask), softmax_down(own[:, QB:] + mask)]
            probs.append(jnp.concatenate(halves, axis=1))
        for p, (_, low, high, packed) in zip(probs, blocks):
            p_s[h, packed : packed + high - low, :] = p
        outs = [nn(v_turned[:, low:high], p) for p, (_, low, high, _) in zip(probs, blocks)]
        ctx_s[:, lanes(0, h)] = jnp.concatenate([pick_heads(o.astype(BF16)) for o in outs], axis=0)


def forward_kernel(*refs):
    (hid, seg, wqkv_h, bq, bv, wout_h, bout, g1, b1, win_h, bin_, wdown_h, bdown, g2, b2) = refs[:15]
    outs, (unit_o, unitf_o, inv_o) = refs[15:25], refs[25:28]
    wqkv, wout, win, wdown, bias_s, n1_s = refs[28:34]
    kept = refs[34:44]
    sems, osems = refs[44:46]
    qkv_s, p_s, ctx_s, nl_s, xh1_s, rs1_s, act_s, dg_s, xh2_s, rs2_s = kept
    r = pl.program_id(0)
    length = hid.shape[0]
    blocks, _ = windows(length)
    pairs = ((wqkv_h, wqkv), (wout_h, wout), (win_h, win), (wdown_h, wdown))
    copies = [pltpu.make_async_copy(a, b, sems.at[i]) for i, (a, b) in enumerate(pairs)]

    def leaving(i):
        if i == 1:
            return pltpu.make_async_copy(kept[i], outs[i].at[r], osems.at[i])
        rows = pl.ds(pl.multiple_of(r * length, length), length)
        return pltpu.make_async_copy(kept[i], outs[i].at[rows], osems.at[i])

    def settle(*which):
        @pl.when(r > 0)
        def _():
            for i in which:
                leaving(i).wait()

    def send(*which):
        for i in which:
            leaving(i).start()

    @pl.when(r == 0)
    def _():
        for copy in copies:
            copy.start()

    seg_row = seg[pl.ds(r, 1), :].astype(F32)
    seg_col = column_of(seg_row)
    for start, low, high, packed in blocks:
        same = seg_col[low:high] == seg_row[:, start : start + QB]
        bias_s[packed : packed + high - low, :] = jnp.where(same, 0.0, masked_score)

    settle(0, 1, 2, 3, 4, 5)

    @pl.when(r == 0)
    def _():
        copies[0].wait()

    for part in range(3):
        cols = slice(part * D, (part + 1) * D)
        value = nn(hid[...], wqkv[:, cols])
        if part == 0:
            value = value + vector(bq)
        if part == 2:
            value = value + vector(bv)
        qkv_s[:, cols] = value.astype(BF16)
    send(0)
    attend(length, qkv_s, bias_s, p_s, ctx_s)
    send(1, 2)

    @pl.when(r == 0)
    def _():
        copies[1].wait()

    xhat, rstd = normalise(hid[...].astype(F32) + (nn(ctx_s[...], wout[...]) + vector(bout)))
    xh1_s[...] = xhat.astype(BF16)
    rs1_s[...] = jnp.broadcast_to(rstd, rs1_s.shape)
    n1 = xhat * vector(g1) + vector(b1)
    n1_s[...] = n1
    nl_s[...] = n1.astype(BF16)
    send(3, 4, 5)
    settle(6, 7, 8, 9)

    @pl.when(r == 0)
    def _():
        copies[2].wait()

    chunk = 512
    bias_in = vector(bin_)

    def rise(c):
        cols = slice(c * chunk, (c + 1) * chunk)
        return nn(nl_s[...], win[:, cols]) + bias_in[:, cols]

    ahead = rise(0)
    for c in range(FF // chunk):
        pre = ahead
        if c + 1 < FF // chunk:
            ahead = rise(c + 1)
        cols = slice(c * chunk, (c + 1) * chunk)
        half = 0.5 + 0.5 * lax.erf(pre * 0.5**0.5)
        act_s[:, cols] = (pre * half).astype(BF16)
        bell = jnp.exp(pre * pre * -0.5) * 0.3989422804014327
        dg_s[:, cols] = (half + pre * bell).astype(BF16)
    send(6, 7)

    @pl.when(r == 0)
    def _():
        copies[3].wait()

    branch = nn(act_s[...], wdown[...]) + vector(bdown)
    xhat, rstd = normalise(n1_s[...] + branch)
    xh2_s[...] = xhat.astype(BF16)
    rs2_s[...] = jnp.broadcast_to(rstd, rs2_s.shape)
    send(8, 9)
    out = xhat * vector(g2) + vector(b2)
    member = (lax.broadcasted_iota(jnp.int32, (SEG, length), 0).astype(F32) == seg_row).astype(F32)
    counts = jnp.sum(member, axis=1, keepdims=True)
    high, low = split_low(out)
    member = member.astype(BF16)
    pooled = (nn(member, high) + nn(member, low)) / counts
    inv = lax.rsqrt(jnp.mean(pooled * pooled, axis=-1, keepdims=True) + unit_epsilon)
    unit = pooled * inv
    unitf_o[...] = unit
    unit_o[...] = unit.astype(BF16)
    inv_o[...] = jnp.broadcast_to(inv / counts, inv_o.shape)

    @pl.when(r == pl.num_programs(0) - 1)
    def _():
        for i in range(10):
            leaving(i).wait()


def forward(hidden, seg, weights):
    rows, length, _ = hidden.shape
    tokens = rows * length
    _, packed = windows(length)
    wide = [(3 * D, BF16), None, (D, BF16), (D, BF16), (D, BF16), (128, F32)]
    wide += [(FF, BF16), (FF, BF16), (D, BF16), (128, F32)]
    out_shape, kept = [], []
    for item in wide:
        if item is None:
            out_shape.append(shape_of((rows, PAIRS, packed, 2 * QB), BF16))
            kept.append(VMEM((PAIRS, packed, 2 * QB), BF16))
        else:
            out_shape.append(shape_of((tokens, item[0]), item[1]))
            kept.append(VMEM((length, item[0]), item[1]))
    hbm = hspec()
    out_specs = [hbm] * 10 + [
        pl.BlockSpec((None, SEG, D), lambda r: (r, 0, 0)),
        pl.BlockSpec((None, SEG, D), lambda r: (r, 0, 0)),
        pl.BlockSpec((None, SEG, 128), lambda r: (r, 0, 0)),
    ]
    out_shape += [
        shape_of((rows, SEG, D), BF16),
        shape_of((rows, SEG, D), F32),
        shape_of((rows, SEG, 128), F32),
    ]
    large = (0, 3, 7, 9)
    in_specs = [pl.BlockSpec((length, D), lambda r: (r, 0)), vspec()]
    in_specs += [hbm if i in large else vspec() for i in range(13)]
    return pl.pallas_call(
        forward_kernel,
        name="forward",
        grid=(rows,),
        in_specs=in_specs,
        out_specs=out_specs,
        out_shape=out_shape,
        scratch_shapes=[VMEM(weights[i].shape, BF16) for i in large]
        + [VMEM((packed, QB), F32), VMEM((length, D), F32)]
        + kept
        + [pltpu.SemaphoreType.DMA((4,)), pltpu.SemaphoreType.DMA((10,))],
        cost_estimate=cost(1e9, 4e6),
        compiler_params=params(50),
    )(hidden.reshape(tokens, D), seg, *weights)


def loss_kernel(flips, idx, *refs):
    pieces, refs = refs[: len(flips)], refs[len(flips) :]
    targets, seg, g2, unitf_h, inv_h, xh2_h, rs2_h, loss_o, gb_o, vec_o = refs[:10]
    slope_s, rows_s, units, unitf, inv, xh2, rs2, sems = refs[10:]
    fetch = Fetch(sems, ((unitf_h, unitf), (inv_h, inv), (xh2_h, xh2), (rs2_h, rs2)))
    twin, me = idx[0], idx[1]
    count = units.shape[0] // 2
    sentences = unitf.shape[0]
    for piece, own_flips in zip(pieces, flips):
        if own_flips is None:
            units[...] = piece[...]
            continue
        for i, (twin_flip, flip) in enumerate(own_flips):
            at = (twin ^ twin_flip) * count + (me ^ flip) * sentences
            at = pl.multiple_of(at, sentences)
            units[pl.ds(at, sentences), :] = piece[i * sentences : (i + 1) * sentences, :]
    rows, length = seg.shape
    step = min(count, 256)
    factor = cosine_scale / D
    positives = units.at[pl.ds(count, count)]
    own = pl.ds(pl.multiple_of(me * sentences, sentences), sentences)

    def one_block(i, carry):
        lanes = pl.ds(pl.multiple_of(i * step, step), step)
        sims = nt(positives[...], units[lanes, :]) * factor
        top = jnp.max(sims, axis=0, keepdims=True)
        weights = jnp.exp(sims - top)
        total = jnp.sum(weights, axis=0, keepdims=True)
        hit = lax.broadcasted_iota(jnp.int32, sims.shape, 0) == targets[:, lanes]
        picked = jnp.sum(jnp.where(hit, sims, 0.0), axis=0, keepdims=True)
        loss_o[:, lanes] = top + jnp.log(total) - picked
        slope = loss_scale * (weights * (1.0 / total) - hit.astype(F32))
        slope_s[:, lanes] = slope.astype(BF16)
        return carry

    if count == step:
        one_block(0, 0)
    else:
        lax.fori_loop(0, count // step, one_block, 0)

    @pl.when(twin == 0)
    def _():
        def part(i, carry):
            lanes = pl.ds(pl.multiple_of(i * step, step), step)
            rows_s[lanes, :] = tn(slope_s[:, lanes], positives[...])
            return carry

        lax.fori_loop(0, count // step, part, 0)
        rows_s[pl.ds(0, sentences), :] = rows_s[own, :]

    @pl.when(twin == 1)
    def _():
        rows_s[pl.ds(0, sentences), :] = nn(slope_s[own, :], units[pl.ds(0, count), :])

    fetch.wait(0, 1, 2, 3)
    gu = rows_s[pl.ds(0, sentences), :] * factor
    unit = unitf[...]
    gs = inv[:, :1] * (gu - unit * jnp.mean(gu * unit, axis=-1, keepdims=True))
    gy = gs * vector(g2)
    u = gy - jnp.mean(gy, axis=-1, keepdims=True)
    gain = jnp.zeros((1, D), F32)
    shift = jnp.zeros((1, D), F32)
    summed = jnp.zeros((1, D), F32)
    for r in range(rows):
        part = slice(r * SEG, (r + 1) * SEG)
        tok = slice(r * length, (r + 1) * length)
        seg_row = seg[r : r + 1, :]
        hits = lax.broadcasted_iota(jnp.int32, (SEG, length), 0) == seg_row
        member = hits.astype(F32).astype(BF16)
        counts = jnp.sum(hits.astype(F32), axis=1, keepdims=True)
        xhat_low = xh2[tok, :]
        gain += jnp.sum(nn(member, xhat_low) * gs[part], axis=0, keepdims=True)
        shift += jnp.sum(counts * gs[part], axis=0, keepdims=True)
        xhat = xhat_low.astype(F32)
        high, low = split_low(u[part])
        spread = tn(member, high) + tn(member, low)
        inner = jnp.mean(spread * xhat, axis=-1, keepdims=True)
        grad = rs2[tok, :1] * (spread - xhat * inner)
        grad_low = grad.astype(BF16)
        gb_o[tok, :] = grad_low
        summed += jnp.sum(grad_low.astype(F32), axis=0, keepdims=True)
    vec_o[...] = jnp.concatenate([summed, gain, shift, jnp.zeros((5, D), F32)], axis=0)


def loss_stage(idx, gathered, targets, unitf, inv, seg, g2, xh2, rs2):
    pieces, flips = gathered
    tokens = xh2.shape[0]
    count = targets.shape[1]
    return pl.pallas_call(
        functools.partial(loss_kernel, flips),
        name="loss",
        in_specs=[sspec()] + [vspec()] * (3 + len(pieces)) + [hspec()] * 4,
        out_specs=[vspec()] * 3,
        out_shape=[
            shape_of((1, count), F32),
            shape_of((tokens, D), BF16),
            shape_of((8, D), F32),
        ],
        scratch_shapes=[VMEM((count, count), BF16), VMEM((count, D), F32), VMEM((2 * count, D), BF16)]
        + [VMEM(a.shape, a.dtype) for a in (unitf, inv, xh2, rs2)]
        + [pltpu.SemaphoreType.DMA((4,))],
        cost_estimate=cost(1e8, 1e6),
        compiler_params=params(22 if count <= 256 else 56),
    )(idx, *pieces, targets, seg, g2, unitf, inv, xh2, rs2)


def pre_kernel(gb, wdown_h, dg_h, out, wdown, dg, sems):
    n = 768
    pairs = []
    for j in range(FF // n):
        part = slice(j * n, (j + 1) * n)
        pairs += [(wdown_h.at[part, :], wdown.at[part, :]), (dg_h.at[:, part], dg.at[:, part])]
    fetch = Fetch(sems, pairs)

    def product(j):
        fetch.wait(2 * j)
        return nt(gb[...], wdown[j * n : (j + 1) * n, :])

    ahead = product(0)
    for j in range(FF // n):
        value = ahead
        if j + 1 < FF // n:
            ahead = product(j + 1)
        fetch.wait(2 * j + 1)
        part = slice(j * n, (j + 1) * n)
        out[:, part] = (value * dg[:, part].astype(F32)).astype(BF16)


def pre_stage(gb, wdown, dg):
    return pl.pallas_call(
        pre_kernel,
        name="grad_pre",
        in_specs=[vspec(), hspec(), hspec()],
        out_specs=vspec(),
        out_shape=shape_of(dg.shape, BF16),
        scratch_shapes=[
            VMEM(wdown.shape, BF16),
            VMEM(dg.shape, BF16),
            pltpu.SemaphoreType.DMA((2 * FF // 768,)),
        ],
        cost_estimate=cost(1e8, 1e6),
        compiler_params=params(32),
    )(gb, wdown, dg)


def normed_kernel(
    gp, win_h, gb, xh1_h, rs1_h, g1, wout_h, ga_o, gc_o, vec_o, win, xh1, rs1, wout, sems
):
    m = 512
    count = gp.shape[0] // m
    fetch = Fetch(sems, ((win_h, win), (xh1_h, xh1), (rs1_h, rs1), (wout_h, wout)))
    gain, shift, summed = [jnp.zeros((1, D), F32) for _ in range(3)]
    fetch.wait(0)
    grads = [nt(gp[i * m : (i + 1) * m, :], win[...]) for i in range(count)]
    fetch.wait(1, 2)
    for i in range(count):
        rows = slice(i * m, (i + 1) * m)
        grad = grads[i] + gb[rows, :].astype(F32)
        xhat = xh1[rows, :].astype(F32)
        gain += jnp.sum(grad * xhat, axis=0, keepdims=True)
        shift += jnp.sum(grad, axis=0, keepdims=True)
        gy = grad * vector(g1)
        inner = jnp.mean(gy * xhat, axis=-1, keepdims=True)
        total = rs1[rows, :1] * (gy - jnp.mean(gy, axis=-1, keepdims=True) - xhat * inner)
        low = total.astype(BF16)
        ga_o[rows, :] = low
        summed += jnp.sum(low.astype(F32), axis=0, keepdims=True)
    fetch.wait(3)
    for i in range(count):
        rows = slice(i * m, (i + 1) * m)
        gc_o[rows, :] = nt(ga_o[rows, :], wout[...]).astype(BF16)
    vec_o[...] = jnp.concatenate([summed, gain, shift, jnp.zeros((5, D), F32)], axis=0)


def normed_stage(gp, win, gb, xh1, rs1, g1, wout):
    tokens = gp.shape[0]
    hbm = hspec()
    return pl.pallas_call(
        normed_kernel,
        name="grad_normed",
        in_specs=[vspec(), hbm, vspec(), hbm, hbm, vspec(), hbm],
        out_specs=[vspec()] * 3,
        out_shape=[
            shape_of((tokens, D), BF16),
            shape_of((tokens, D), BF16),
            shape_of((8, D), F32),
        ],
        scratch_shapes=[VMEM(a.shape, a.dtype) for a in (win, xh1, rs1, wout)]
        + [pltpu.SemaphoreType.DMA((4,))],
        cost_estimate=cost(1e8, 1e6),
        compiler_params=params(30),
    )(gp, win, gb, xh1, rs1, g1, wout)


def attend_back_kernel(q_ref, k_ref, v_ref, g_ref, p_ref, out_ref):
    length = q_ref.shape[0]
    blocks, _ = windows(length)
    group = q_ref.shape[1] // PW
    scale = HEAD_DIM**-0.5
    loaded, grads = [], []
    for h in range(group):
        lanes = slice(h * PW, (h + 1) * PW)
        q2 = [two_heads(q_ref[b[0] : b[0] + QB, lanes]) for b in blocks]
        g2 = [two_heads(g_ref[b[0] : b[0] + QB, lanes]) for b in blocks]
        loaded.append((q2, g2, k_ref[:, lanes].T))
        v_all = v_ref[:, lanes]
        grads.append([nt(v_all[b[1] : b[2]], g) for b, g in zip(blocks, g2)])
    slopes = []
    for h in range(group):
        own = []
        for gp, (_, low, high, packed) in zip(grads[h], blocks):
            p = p_ref[h, packed : packed + high - low, :].astype(F32)
            weighted = p * gp
            inner = jnp.sum(weighted, axis=0, keepdims=True)
            own.append((weighted - p * inner).astype(BF16))
        slopes.append(own)

    def gather(parts):
        out = []
        for block in range(len(blocks)):
            total = None
            for part, (_, low, high, _) in zip(parts, blocks):
                base = block * QB - low
                if 0 <= base < high - low:
                    piece = part[base : base + QB]
                    total = piece if total is None else total + piece
            out.append(total)
        return jnp.concatenate(out, axis=0)

    for h in range(group):
        lanes = slice(h * PW, (h + 1) * PW)
        q2, g2, k_turned = loaded[h]
        dq = [nn(k_turned[:, b[1] : b[2]], s) for b, s in zip(blocks, slopes[h])]
        dv = [nn(p_ref[h, b[3] : b[3] + b[2] - b[1], :], g) for b, g in zip(blocks, g2)]
        dk = [nn(s, q) for s, q in zip(slopes[h], q2)]
        turned = [pick_heads((part * scale).astype(BF16)) for part in dq]
        out_ref[0, :, lanes] = jnp.concatenate(turned, axis=0)
        out_ref[1, :, lanes] = (gather(dk) * scale).astype(BF16)
        out_ref[2, :, lanes] = gather(dv).astype(BF16)


def attend_back(qkv, grad_context, probs, rows, length, first, pairs):
    _, packed = windows(length)
    group = 2
    steps = pairs // group
    base = first // group
    width = group * PW

    def block(part):
        return pl.BlockSpec((length, width), lambda r, h: (r, part * (D // width) + base + h))

    return pl.pallas_call(
        attend_back_kernel,
        name="attend_back",
        grid=(rows, steps),
        in_specs=[
            block(0),
            block(1),
            block(2),
            block(0),
            pl.BlockSpec((None, group, packed, 2 * QB), lambda r, h: (r, base + h, 0, 0)),
        ],
        out_specs=pl.BlockSpec((3, length, width), lambda r, h: (0, r, h)),
        out_shape=shape_of((3, rows * length, pairs * PW), BF16),
        cost_estimate=cost(1e8, 1e6),
        compiler_params=params(20),
    )(qkv, qkv, qkv, grad_context, probs)


def hidden_kernel(da, db, wqkv_h, ga, out, wqkv, sems):
    m = 512
    pairs = []
    for part in range(3):
        cols = slice(part * D, (part + 1) * D)
        pairs.append((wqkv_h.at[:, cols], wqkv.at[:, cols]))
    fetch = Fetch(sems, pairs)
    fetch.wait(0, 1, 2)
    for i in range(ga.shape[0] // m):
        rows = slice(i * m, (i + 1) * m)
        total = ga[rows, :].astype(F32)
        for part in range(3):
            both = jnp.concatenate([da[part, rows, :], db[part, rows, :]], axis=1)
            total = total + nt(both, wqkv[:, part * D : (part + 1) * D])
        out[rows, :] = total.astype(BF16)


def hidden_stage(da, db, wqkv, ga):
    return pl.pallas_call(
        hidden_kernel,
        name="hidden_grad",
        in_specs=[vspec(), vspec(), hspec(), vspec()],
        out_specs=vspec(),
        out_shape=shape_of(ga.shape, BF16),
        scratch_shapes=[VMEM(wqkv.shape, BF16), pltpu.SemaphoreType.DMA((3,))],
        cost_estimate=cost(1e8, 1e6),
        compiler_params=params(22),
    )(da, db, wqkv, ga)


def place_of(half, quarter, owner):
    c, y, z0, z1 = owner & 1, (owner >> 1) & 1, (owner >> 2) & 1, owner >> 3
    order = (quarter, y, z0, z1, c) if half == 0 else (y, z0, z1, quarter, c)
    out = 0
    for bit in order:
        out = 2 * out + bit
    return out


def store_piece(first, keep, send, quarter, owner, piece_a, piece_b, lanes):
    at_a, at_b = place_of(0, quarter, owner), place_of(1, quarter, owner)
    keep[jnp.where(first, at_a, at_b), :, lanes] = jnp.where(first, piece_a, piece_b)
    send[jnp.where(first, at_b, at_a), :, lanes] = jnp.where(first, piece_b, piece_a)


def down_kernel(idx, act_h, gb, keep, send, act, sems):
    first = idx[2] == 0
    n = 768
    pairs = []
    for j in range(FF // n):
        part = slice(j * n, (j + 1) * n)
        pairs.append((act_h.at[:, part], act.at[:, part]))
    fetch = Fetch(sems, pairs)

    def product(j):
        fetch.wait(j)
        return tn(act[:, j * n : (j + 1) * n], gb[...])

    ahead = product(0)
    for j in range(FF // n):
        total = ahead.astype(BF16)
        if j + 1 < FF // n:
            ahead = product(j + 1)
        for local in range(4):
            for quarter in range(2):
                base = local * 192 + quarter * 48
                a, b = total[base : base + 48], total[base + 96 : base + 144]
                store_piece(first, keep, send, quarter, 4 * j + local, a, b, slice(0, D))


def down_stage(idx, act, gb):
    return pl.pallas_call(
        down_kernel,
        name="grad_w_down",
        in_specs=[sspec(), hspec(), vspec()],
        out_specs=[vspec()] * 2,
        out_shape=[shape_of((32, 48, D), BF16)] * 2,
        scratch_shapes=[VMEM(act.shape, BF16), pltpu.SemaphoreType.DMA((4,))],
        cost_estimate=cost(1e8, 1e6),
        compiler_params=params(26),
    )(idx, act, gb)


def in_kernel(idx, n1_h, gp, keep, send, vec_o, n1, turned, sems):
    first = idx[2] == 0
    fetch = Fetch(sems, ((n1_h, n1),))
    fetch.wait(0)
    turned[...] = n1[...].T

    def products(quarter):
        out = []
        for half in range(2):
            j = 2 * half + quarter
            out.append(nn(turned[...], gp[:, j * D : (j + 1) * D]))
        return out

    ahead = products(0)
    for quarter in range(2):
        a, b = [part.astype(BF16) for part in ahead]
        if quarter == 0:
            ahead = products(1)
        for owner in range(16):
            rows = slice(owner * 48, (owner + 1) * 48)
            store_piece(first, keep, send, quarter, owner, a[rows], b[rows], slice(0, D))
    vec_o[...] = jnp.sum(gp[...].astype(F32), axis=0, keepdims=True)


def in_stage(idx, n1, gp):
    return pl.pallas_call(
        in_kernel,
        name="grad_w_in",
        in_specs=[sspec(), hspec(), vspec()],
        out_specs=[vspec()] * 3,
        out_shape=[shape_of((32, 48, D), BF16)] * 2 + [shape_of((1, FF), F32)],
        scratch_shapes=[
            VMEM(n1.shape, BF16),
            VMEM((D, n1.shape[0]), BF16),
            pltpu.SemaphoreType.DMA((1,)),
        ],
        cost_estimate=cost(1e8, 1e6),
        compiler_params=params(30),
    )(idx, n1, gp)


WIDE, NARROW = 640, 256


def store_all(first, keep, send, whole, width):
    for quarter in range(2):
        a = whole[:, quarter * width : (quarter + 1) * width]
        b = whole[:, (2 + quarter) * width : (3 + quarter) * width]
        for owner in range(16):
            rows = slice(owner * 48, (owner + 1) * 48)
            store_piece(first, keep, send, quarter, owner, a[rows], b[rows], slice(0, width))


def wide_kernel(idx, hid_h, da, ctx_h, ga, keep, send, turned_o, hid, ctx, whole, sems):
    fetch = Fetch(sems, ((hid_h, hid), (ctx_h, ctx)))
    n = da.shape[2]
    fetch.wait(0)
    turned_o[...] = hid[...].T
    for part in range(3):
        whole[:, part * n : (part + 1) * n] = nn(turned_o[...], da[part]).astype(BF16)
    fetch.wait(1)
    whole[:, 3 * n : 3 * n + D] = tn(ctx[...], ga[...]).astype(BF16)
    whole[:, 3 * n + D :] = jnp.zeros((D, 4 * WIDE - 3 * n - D), BF16)
    store_all(idx[2] == 0, keep, send, whole, WIDE)


def wide_stage(idx, hid, da, ctx, ga):
    tokens = hid.shape[0]
    return pl.pallas_call(
        wide_kernel,
        name="grad_w_wide",
        in_specs=[sspec(), hspec(), vspec(), hspec(), vspec()],
        out_specs=[vspec()] * 3,
        out_shape=[shape_of((32, 48, WIDE), BF16)] * 2 + [shape_of((D, tokens), BF16)],
        scratch_shapes=[
            VMEM(hid.shape, BF16),
            VMEM(ctx.shape, BF16),
            VMEM((D, 4 * WIDE), BF16),
            pltpu.SemaphoreType.DMA((2,)),
        ],
        cost_estimate=cost(1e8, 1e6),
        compiler_params=params(28),
    )(idx, hid, da, ctx, ga)


def narrow_kernel(idx, turned, da, db, vecs, keep, send, whole, sums_s):
    n = db.shape[2]
    for part in range(3):
        whole[:, part * n : (part + 1) * n] = nn(turned[...], db[part]).astype(BF16)
    sums_s[...] = jnp.zeros_like(sums_s)
    sums_s[:16, :] = vecs[...]
    for row, part in ((0, 0), (1, 2)):
        for base, grads in ((0, da), (D - n, db)):
            lanes = slice(base, base + grads.shape[2])
            total = jnp.sum(grads[part].astype(F32), axis=0, keepdims=True)
            sums_s[row : row + 1, lanes] = total
    whole[:, 3 * n : 3 * n + 128] = sums_s[...].T.astype(BF16)
    whole[:, 3 * n + 128 :] = jnp.zeros((D, 4 * NARROW - 3 * n - 128), BF16)
    store_all(idx[2] == 0, keep, send, whole, NARROW)


def narrow_stage(idx, turned, da, db, vecs):
    return pl.pallas_call(
        narrow_kernel,
        name="grad_w_narrow",
        in_specs=[sspec()] + [vspec()] * 4,
        out_specs=[vspec()] * 2,
        out_shape=[shape_of((32, 48, NARROW), BF16)] * 2,
        scratch_shapes=[VMEM((D, 4 * NARROW), BF16), VMEM((128, D), F32)],
        cost_estimate=cost(1e8, 1e6),
        compiler_params=params(22),
    )(idx, turned, da, db, vecs)


def swap_dp(value, flip):
    devices = lax.axis_size("dp")
    return lax.ppermute(value, "dp", [(i, i ^ flip) for i in range(devices)])


def swap_twin(value):
    return lax.ppermute(value, "twin", [(0, 1), (1, 0)])


TWIN = 16
ROUTES = ((TWIN, 2, 4, 8, TWIN), (2, 4, 8, TWIN, TWIN))


def step_swap(value, step):
    pairs = [(i, i ^ ROUTES[i & 1][step]) for i in range(2 * TWIN)]
    return lax.ppermute(value, ("twin", "dp"), pairs)


def plus(*values):
    total = values[0].astype(F32)
    for value in values[1:]:
        total = total + value.astype(F32)
    return total.astype(BF16)


def call_small(kernel, name, idx, operands, outs):
    return pl.pallas_call(
        kernel,
        name=name,
        in_specs=[sspec()] + [vspec()] * len(operands),
        out_specs=[vspec()] * len(outs),
        out_shape=[shape_of(shape, dtype) for shape, dtype in outs],
        cost_estimate=cost(1e6, 1e5),
        compiler_params=params(12),
    )(idx, *operands)


def half_kernel(step, split, idx, keep, *refs):
    keep_o, send_o = refs[-2:]
    count = keep_o.shape[0]
    bit = idx[3 + step]
    mine = pl.ds(bit * count, count)
    other = pl.ds((1 - bit) * count, count)
    if not split:
        keep_o[...] = plus(keep[mine], refs[0][mine])
        send_o[...] = plus(keep[other], refs[0][other])
        return
    same = bit == 0
    low, high = refs[0][...], refs[1][...]
    keep_o[...] = plus(keep[mine], jnp.where(same, low, high))
    send_o[...] = plus(keep[other], jnp.where(same, high, low))


def half_step(idx, step, keep, recv):
    count, rows, width = keep.shape
    shape = (count // 2, rows, width)
    kernel = functools.partial(half_kernel, step, len(recv) > 1)
    return call_small(kernel, "sum_" + str(step), idx, (keep, *recv), [(shape, BF16)] * 2)


def core_step(idx, keep, recv, split):
    count, rows, width = keep.shape
    half = count // 2
    pieces = 4
    part = half // pieces

    def kernel(idx, keep, recv, keep_o, *sends):
        bit = idx[3]
        keep_o[...] = plus(keep[bit], recv[bit])
        total = plus(keep[1 - bit], recv[1 - bit])
        if not split:
            sends[0][...] = total
            return

        @pl.when(pl.program_id(0) < pieces // 2)
        def _():
            sends[0][...] = total

        @pl.when(pl.program_id(0) >= pieces // 2)
        def _():
            sends[1][...] = total

    spec = pl.BlockSpec((2, part, rows, width), lambda i: (0, i, 0, 0))
    block = (part, rows, width)
    out_specs = [pl.BlockSpec(block, lambda i: (i, 0, 0))]
    out_shape = [shape_of((half, rows, width), BF16)]
    if split:
        out_specs.append(pl.BlockSpec(block, lambda i: (jnp.minimum(i, pieces // 2 - 1), 0, 0)))
        out_specs.append(pl.BlockSpec(block, lambda i: (jnp.maximum(i - pieces // 2, 0), 0, 0)))
        out_shape += [shape_of((half // 2, rows, width), BF16)] * 2
    else:
        out_specs += out_specs
        out_shape += out_shape
    whole = (2, half, rows, width)
    keep, *sends = pl.pallas_call(
        kernel,
        name="sum_core",
        grid=(pieces,),
        in_specs=[sspec(), spec, spec],
        out_specs=out_specs,
        out_shape=out_shape,
        cost_estimate=cost(1e6, 1e5),
        compiler_params=params(10),
    )(idx, keep.reshape(whole), recv.reshape(whole))
    return keep, sends


def own_kernel(idx, keep, recv, out):
    out[...] = plus(keep[...], recv[...])


def turn_kernel(idx, own, other, keep_o, send_o):
    twin, core = idx[0], idx[2]
    keep_o[twin] = own[core]
    keep_o[1 - twin] = other[core]
    send_o[twin] = own[1 - core]
    send_o[1 - twin] = other[1 - core]


class Order:
    def __init__(self):
        self.last = None

    def after(self, value, *others):
        if self.last is None:
            return value
        return lax.optimization_barrier((value, self.last) + others)[0]

    def done(self, value):
        self.last = value
        return value


class Exchange:
    def __init__(self, order, idx, keep, send, split=False):
        self.order, self.idx, self.step, self.split = order, idx, 0, split
        self.keep, self.recv = keep, [swap_dp(send, 1)]

    def advance(self):
        idx, order = self.idx, self.order
        keep, recv = order.after(self.keep), self.recv
        if self.step == 0:
            keep, sends = core_step(idx, keep, recv[0], self.split)
            recv = [step_swap(send, 0) for send in sends]
        elif self.step < 4:
            keep, send = half_step(idx, self.step, keep, recv)
            recv = [step_swap(send, self.step)]
        elif self.step == 4:
            shape = keep.shape
            (keep,) = call_small(own_kernel, "sum_4", idx, (keep, *recv), [(shape, BF16)])
            recv = [step_swap(keep, 4)]
        else:
            shape = keep.shape
            keep, send = call_small(turn_kernel, "turn", idx, (keep, *recv), [(shape, BF16)] * 2)
            recv = [swap_dp(send, 1)]
        order.done(keep)
        self.keep, self.recv = keep, recv
        self.step += 1

    def result(self):
        return self.keep, self.recv[0]


def gather_units(unit):
    flips = [(0, 0)]
    for flip in (8, 4):
        unit = jnp.concatenate([unit, swap_dp(unit, flip)], axis=0)
        flips = flips + [(t, f ^ flip) for t, f in flips]
    pairs = [(i, i ^ (TWIN + 2)) for i in range(2 * TWIN)]
    far = lax.ppermute(unit, ("twin", "dp"), pairs)
    unit = jnp.concatenate([unit, swap_dp(unit, 2), swap_twin(unit), far], axis=0)
    flips = [(t ^ a, f ^ b) for a, b in ((0, 0), (0, 2), (1, 0), (1, 2)) for t, f in flips]
    return (unit, swap_dp(unit, 1)), (flips, [(t, f ^ 1) for t, f in flips])


def four_quarters(idx, keep, recv):
    first = idx[2] == 0
    low = [jnp.where(first, keep[i], recv[i]) for i in range(2)]
    high = [jnp.where(first, recv[i], keep[i]) for i in range(2)]
    return low + high


def final_in_kernel(idx, keep, recv, out):
    for i, part in enumerate(four_quarters(idx, keep, recv)):
        out[:, i * D : (i + 1) * D] = part.astype(F32)


def final_down_kernel(idx, keep, recv, out):
    for i, part in enumerate(four_quarters(idx, keep, recv)):
        out[i * 48 : (i + 1) * 48, :] = part.astype(F32)


def final_last_kernel(idx, wide_k, wide_r, narrow_k, narrow_r, qkv_o, out_o, vec_o):
    wide = jnp.concatenate(four_quarters(idx, wide_k, wide_r), axis=1).astype(F32)
    narrow = jnp.concatenate(four_quarters(idx, narrow_k, narrow_r), axis=1).astype(F32)
    low, high = 2 * D // 3, D // 3
    for part in range(3):
        qkv_o[:, part * D : part * D + low] = wide[:, part * low : (part + 1) * low]
        qkv_o[:, part * D + low : (part + 1) * D] = narrow[:, part * high : (part + 1) * high]
    out_o[...] = wide[:, 3 * low : 3 * low + D]
    small = narrow[:, 3 * high : 3 * high + 128]
    vec_o[...] = jnp.concatenate([small, jnp.zeros((80, 128), F32)], axis=0).T[:16]


def finish(order, idx, kernel, name, chunks, outs):
    operands = [value for chunk in chunks for value in chunk.result()]
    operands[0] = order.after(operands[0])
    out = call_small(kernel, name, idx, operands, outs)
    order.done(out[0])
    return out


def add_low(*parts):
    return lax.optimization_barrier(plus(*parts))


def digits_of(devices):
    out, rest = [], devices // 2
    while rest > 1:
        size = 4 if rest % 4 == 0 else 2
        out.append(size)
        rest //= size
    return out


def pick(value, index, axis):
    return lax.dynamic_index_in_dim(value, index, axis, keepdims=False)


def scatter(grad):
    devices = lax.axis_size("dp")
    me = lax.axis_index("dp")
    value = grad.reshape(devices, grad.shape[0] // devices, grad.shape[1])
    unit = 1
    for size in [2] + digits_of(devices):
        mine = (me // unit) % size
        view = value.reshape((value.shape[0] // size, size) + value.shape[1:])
        parts = [pick(view, mine, 1)]
        for flip in range(1, size):
            parts.append(swap_dp(pick(view, mine ^ flip, 1), flip * unit))
        value = add_low(*parts)
        unit *= size
    value = value[0]
    return value.astype(F32) + swap_twin(value).astype(F32)


def body(
    hidden,
    segment_ids,
    targets,
    w_qkv,
    b_query,
    b_value,
    w_out,
    b_out,
    ln1_gain,
    ln1_bias,
    w_in,
    b_in,
    w_down,
    b_down,
    ln2_gain,
    ln2_bias,
):
    row_count, length, width = hidden.shape
    tokens = row_count * length
    devices = lax.axis_size("dp")
    everyone = lax.axis_size(("twin", "dp"))
    me = lax.axis_index("dp")
    twin = lax.axis_index("twin")
    core, y, z0, z1 = me & 1, (me >> 1) & 1, (me >> 2) & 1, me >> 3
    first = core == 0
    bits = [jnp.where(first, a, b) for a, b in ((twin, y), (y, z0), (z0, z1), (z1, twin))]
    idx = jnp.stack([twin, me, core] + bits).astype(jnp.int32)
    weights = (w_qkv, b_query, b_value, w_out, b_out, ln1_gain, ln1_bias)
    weights += (w_in, b_in, w_down, b_down, ln2_gain, ln2_bias)
    qkv, probs, ctx, n1, xh1, rs1, act, dg, xh2, rs2, unit, unitf, inv = forward(
        hidden, segment_ids, weights
    )
    sentences = row_count * SEG
    unit = unit.reshape(sentences, width)
    direct = devices == TWIN and sentences == 16
    if direct:
        gathered = gather_units(unit)
    else:
        gathered = ((lax.all_gather(unit, ("twin", "dp"), axis=0, tiled=True),), (None,))
    losses, gb, vec2 = loss_stage(
        idx,
        gathered,
        targets.reshape(1, -1),
        unitf.reshape(sentences, width),
        inv.reshape(sentences, 128),
        segment_ids,
        ln2_gain,
        xh2,
        rs2,
    )
    share = losses.shape[1] // everyone
    losses = lax.dynamic_slice_in_dim(
        losses[0], lax.axis_index(("twin", "dp")) * share, share, 0
    )
    flat = hidden.reshape(tokens, width)
    if direct:
        order = Order()
        keep, send = down_stage(idx, act, gb)
        order.done(keep)
        down = Exchange(order, idx, keep, send, split=True)
        gp = order.done(pre_stage(order.after(gb), w_down, dg))
        down.advance()
        keep, send, sums = in_stage(idx, order.after(n1), gp)
        order.done(keep)
        into = Exchange(order, idx, keep, send, split=True)
        gp_next = order.after(gp, down.recv[0])
        ga, gc, vec1 = normed_stage(gp_next, w_in, gb, xh1, rs1, ln1_gain, w_out)
        order.done(ga)
        into.advance()
        down.advance()
        gc = order.after(gc)
        da = order.done(attend_back(qkv, gc, probs, row_count, length, 0, 4))
        down.advance()
        flat_next = order.after(flat, into.recv[0])
        keep, send, turned = wide_stage(idx, flat_next, da, ctx, ga)
        order.done(keep)
        wide = Exchange(order, idx, keep, send)
        into.advance()
        down.advance()
        db = order.done(attend_back(qkv, order.after(gc), probs, row_count, length, 4, 2))
        wide.advance()
        rest = sums.reshape(devices, 4, 48).transpose(1, 0, 2).reshape(4, width)
        nothing = jnp.zeros((2, width), F32)
        vecs = jnp.concatenate([nothing, vec1[:3], vec2[:3], rest, nothing, nothing])
        keep, send = narrow_stage(idx, turned, da, order.after(db), vecs)
        order.done(keep)
        narrow = Exchange(order, idx, keep, send)
        into.advance()
        down.advance()
        hidden_grad = order.done(hidden_stage(da, order.after(db), w_qkv, ga))
        narrow.advance()
        wide.advance()
        into.advance()
        down.advance()
        narrow.advance()
        wide.advance()
        into.advance()
        (grad_w_down,) = finish(
            order, idx, final_down_kernel, "final_down", [down], [((192, D), F32)]
        )
        narrow.advance()
        wide.advance()
        into.advance()
        narrow.advance()
        wide.advance()
        (grad_w_in,) = finish(order, idx, final_in_kernel, "final_in", [into], [((48, FF), F32)])
        narrow.advance()
        wide.advance()
        narrow.advance()
        shapes = [((48, 3 * D), F32), ((48, D), F32), ((16, 128), F32)]
        grad_w_qkv, grad_w_out, vec = finish(
            order, idx, final_last_kernel, "final_last", [wide, narrow], shapes
        )
        vec = vec[:, :48]
        vecs = [vec[i] for i in range(8)]
        grad_b_in = vec[8:12].reshape(-1)
    else:
        gp = pre_stage(gb, w_down, dg)
        ga, gc, vec1 = normed_stage(gp, w_in, gb, xh1, rs1, ln1_gain, w_out)
        da = attend_back(qkv, gc, probs, row_count, length, 0, 4)
        db = attend_back(qkv, gc, probs, row_count, length, 4, 2)
        hidden_grad = hidden_stage(da, db, w_qkv, ga)
        dqkv = jnp.concatenate([da, db], axis=2)
        grad_w_down = scatter(tn(act, gb).astype(BF16))
        grad_w_in = scatter(tn(n1, gp).astype(BF16))
        wide = jnp.concatenate([dqkv[0], dqkv[1], dqkv[2]], axis=1)
        grad_w_qkv = scatter(tn(flat, wide).astype(BF16))
        grad_w_out = scatter(tn(ctx, ga).astype(BF16))
        sums = jnp.sum(dqkv, axis=1, dtype=F32)
        vec = jnp.concatenate([sums[0:1], sums[2:3], vec1[:3], vec2[:3]])
        vec = scatter(jnp.pad(vec, ((0, 120), (0, 0))).T.astype(BF16)).T
        vecs = [vec[i] for i in range(8)]
        bias = jnp.sum(gp, axis=0, dtype=F32)
        grad_b_in = scatter(jnp.broadcast_to(bias[:, None], (FF, 128)).astype(BF16))[:, 0]
    return (
        losses,
        hidden_grad.reshape(row_count, length, width),
        grad_w_qkv,
        vecs[0],
        vecs[1],
        grad_w_out,
        vecs[2],
        vecs[3],
        vecs[4],
        grad_w_in,
        grad_b_in,
        grad_w_down,
        vecs[5],
        vecs[6],
        vecs[7],
    )


def solution(mesh):
    whole = (P(),) * 14
    placed = (P(("twin", "dp"), None, None), P(("twin", "dp"), None)) + whole
    return jax.shard_map(
        body,
        mesh=mesh,
        in_specs=placed,
        out_specs=(
            P(("twin", "dp")),
            P(("twin", "dp"), None, None),
            P("dp", None),
            P("dp"),
            P("dp"),
            P("dp", None),
            P("dp"),
            P("dp"),
            P("dp"),
            P("dp", None),
            P("dp"),
            P("dp", None),
            P("dp"),
            P("dp"),
            P("dp"),
        ),
        check_vma=False,
    )
```

```python
import functools

import jax
import jax.numpy as jnp
from jax import lax
from jax.experimental import pallas as pl
from jax.experimental.pallas import tpu as pltpu
from jax.sharding import PartitionSpec as P

D = 768
HEADS = 12
HEAD_DIM = 64
FF = 3072
SEG = 8
QB = 128
MOST = 128
PAIRS = HEADS // 2
PW = 2 * HEAD_DIM

cosine_scale = 64.0
loss_scale = 32.0
norm_epsilon = 1e-12
unit_epsilon = 1e-06
masked_score = -1e30

F32 = jnp.float32
BF16 = jnp.bfloat16
VMEM = pltpu.VMEM
ANY = pl.ANY
MIB = 1 << 20


def nn(left, right):
    return lax.dot_general(left, right, (((1,), (0,)), ((), ())), preferred_element_type=F32)


def nt(left, right):
    return lax.dot_general(left, right, (((1,), (1,)), ((), ())), preferred_element_type=F32)


def tn(left, right):
    return lax.dot_general(left, right, (((0,), (0,)), ((), ())), preferred_element_type=F32)


def vspec():
    return pl.BlockSpec(memory_space=VMEM)


def sspec():
    return pl.BlockSpec(memory_space=pltpu.SMEM)


def hspec():
    return pl.BlockSpec(memory_space=pltpu.HBM)


def far(*values):
    return [pltpu.with_memory_space_constraint(value, pltpu.HBM) for value in values]


class Fetch:
    def __init__(self, sems, pairs):
        self.copies = [pltpu.make_async_copy(a, b, sems.at[i]) for i, (a, b) in enumerate(pairs)]
        for copy in self.copies:
            copy.start()

    def wait(self, *which):
        for i in which:
            self.copies[i].wait()


def fixed(shape):
    return pl.BlockSpec(shape, lambda *_: (0,) * len(shape))


def shape_of(shape, dtype):
    return jax.ShapeDtypeStruct(shape, dtype)


def params(mib):
    return pltpu.CompilerParams(vmem_limit_bytes=mib * MIB)


def cost(flops, moved):
    return pl.CostEstimate(flops=int(flops), bytes_accessed=int(moved), transcendentals=0)


def windows(length):
    out, packed = [], 0
    for start in range(0, length, QB):
        low, high = max(0, start - MOST), min(length, start + QB + MOST)
        out.append((start, low, high, packed))
        packed += high - low
    return out, packed


def two_heads(pair):
    first = lax.broadcasted_iota(jnp.int32, pair.shape, 1) < HEAD_DIM
    zero = jnp.zeros((), pair.dtype)
    return jnp.concatenate([jnp.where(first, pair, zero), jnp.where(first, zero, pair)], axis=0)


def pick_heads(both):
    rows = both.shape[1] // 2
    return jnp.concatenate([both[:HEAD_DIM, :rows], both[HEAD_DIM:, rows:]], axis=0).T


def column_of(row):
    return jnp.broadcast_to(row, (8, row.shape[1])).T[:, :1]


def split_low(value):
    high = value.astype(BF16)
    return high, (value - high.astype(F32)).astype(BF16)


def normalise(value):
    middle = jnp.mean(value, axis=-1, keepdims=True)
    centered = value - middle
    spread = jnp.mean(centered * centered, axis=-1, keepdims=True)
    rstd = lax.rsqrt(spread + norm_epsilon)
    return centered * rstd, rstd


def vector(ref):
    return ref[...].astype(F32).reshape(1, ref.shape[0])


def softmax_down(own):
    top = jnp.max(own, axis=0, keepdims=True)
    weights = jnp.exp(own - top)
    total = jnp.sum(weights, axis=0, keepdims=True)
    return (weights * (1.0 / total)).astype(BF16)


def attend(length, qkv, bias, p_s, ctx_s):
    blocks, _ = windows(length)

    def lanes(part, h):
        return slice(part * D + h * PW, part * D + (h + 1) * PW)

    def score(h):
        q_all = qkv[:, lanes(0, h)] * jnp.asarray(HEAD_DIM**-0.5, BF16)
        k_all = qkv[:, lanes(1, h)]
        out = []
        for start, low, high, _ in blocks:
            out.append(nt(k_all[low:high], two_heads(q_all[start : start + QB])))
        return out, qkv[:, lanes(2, h)].T

    ahead = score(0)
    for h in range(PAIRS):
        scores, v_turned = ahead
        if h + 1 < PAIRS:
            ahead = score(h + 1)
        probs = []
        for own, (_, low, high, packed) in zip(scores, blocks):
            mask = bias[packed : packed + high - low, :]
            halves = [softmax_down(own[:, :QB] + mask), softmax_down(own[:, QB:] + mask)]
            probs.append(jnp.concatenate(halves, axis=1))
        for p, (_, low, high, packed) in zip(probs, blocks):
            p_s[h, packed : packed + high - low, :] = p
        outs = [nn(v_turned[:, low:high], p) for p, (_, low, high, _) in zip(probs, blocks)]
        ctx_s[:, lanes(0, h)] = jnp.concatenate([pick_heads(o.astype(BF16)) for o in outs], axis=0)


def forward_kernel(*refs):
    (hid, seg, wqkv_h, bq, bv, wout_h, bout, g1, b1, win_h, bin_, wdown_h, bdown, g2, b2) = refs[:15]
    outs, (unit_o, unitf_o, inv_o) = refs[15:25], refs[25:28]
    wqkv, wout, win, wdown, bias_s, n1_s = refs[28:34]
    kept = refs[34:44]
    sems, osems = refs[44:46]
    qkv_s, p_s, ctx_s, nl_s, xh1_s, rs1_s, act_s, dg_s, xh2_s, rs2_s = kept
    r = pl.program_id(0)
    length = hid.shape[0]
    blocks, _ = windows(length)
    pairs = ((wqkv_h, wqkv), (wout_h, wout), (win_h, win), (wdown_h, wdown))
    copies = [pltpu.make_async_copy(a, b, sems.at[i]) for i, (a, b) in enumerate(pairs)]

    def leaving(i):
        if i == 1:
            return pltpu.make_async_copy(kept[i], outs[i].at[r], osems.at[i])
        rows = pl.ds(pl.multiple_of(r * length, length), length)
        return pltpu.make_async_copy(kept[i], outs[i].at[rows], osems.at[i])

    def settle(*which):
        @pl.when(r > 0)
        def _():
            for i in which:
                leaving(i).wait()

    def send(*which):
        for i in which:
            leaving(i).start()

    @pl.when(r == 0)
    def _():
        for copy in copies:
            copy.start()

    seg_row = seg[pl.ds(r, 1), :].astype(F32)
    seg_col = column_of(seg_row)
    for start, low, high, packed in blocks:
        same = seg_col[low:high] == seg_row[:, start : start + QB]
        bias_s[packed : packed + high - low, :] = jnp.where(same, 0.0, masked_score)

    settle(0, 1, 2, 3, 4, 5)

    @pl.when(r == 0)
    def _():
        copies[0].wait()

    for part in range(3):
        cols = slice(part * D, (part + 1) * D)
        value = nn(hid[...], wqkv[:, cols])
        if part == 0:
            value = value + vector(bq)
        if part == 2:
            value = value + vector(bv)
        qkv_s[:, cols] = value.astype(BF16)
    send(0)
    attend(length, qkv_s, bias_s, p_s, ctx_s)
    send(1, 2)

    @pl.when(r == 0)
    def _():
        copies[1].wait()

    xhat, rstd = normalise(hid[...].astype(F32) + (nn(ctx_s[...], wout[...]) + vector(bout)))
    xh1_s[...] = xhat.astype(BF16)
    rs1_s[...] = jnp.broadcast_to(rstd, rs1_s.shape)
    n1 = xhat * vector(g1) + vector(b1)
    n1_s[...] = n1
    nl_s[...] = n1.astype(BF16)
    send(3, 4, 5)
    settle(6, 7, 8, 9)

    @pl.when(r == 0)
    def _():
        copies[2].wait()

    chunk = 512
    bias_in = vector(bin_)

    def rise(c):
        cols = slice(c * chunk, (c + 1) * chunk)
        return nn(nl_s[...], win[:, cols]) + bias_in[:, cols]

    ahead = rise(0)
    for c in range(FF // chunk):
        pre = ahead
        if c + 1 < FF // chunk:
            ahead = rise(c + 1)
        cols = slice(c * chunk, (c + 1) * chunk)
        half = 0.5 + 0.5 * lax.erf(pre * 0.5**0.5)
        act_s[:, cols] = (pre * half).astype(BF16)
        bell = jnp.exp(pre * pre * -0.5) * 0.3989422804014327
        dg_s[:, cols] = (half + pre * bell).astype(BF16)
    send(6, 7)

    @pl.when(r == 0)
    def _():
        copies[3].wait()

    branch = nn(act_s[...], wdown[...]) + vector(bdown)
    xhat, rstd = normalise(n1_s[...] + branch)
    xh2_s[...] = xhat.astype(BF16)
    rs2_s[...] = jnp.broadcast_to(rstd, rs2_s.shape)
    send(8, 9)
    out = xhat * vector(g2) + vector(b2)
    member = (lax.broadcasted_iota(jnp.int32, (SEG, length), 0).astype(F32) == seg_row).astype(F32)
    counts = jnp.sum(member, axis=1, keepdims=True)
    high, low = split_low(out)
    member = member.astype(BF16)
    pooled = (nn(member, high) + nn(member, low)) / counts
    inv = lax.rsqrt(jnp.mean(pooled * pooled, axis=-1, keepdims=True) + unit_epsilon)
    unit = pooled * inv
    unitf_o[...] = unit
    unit_o[...] = unit.astype(BF16)
    inv_o[...] = jnp.broadcast_to(inv / counts, inv_o.shape)

    @pl.when(r == pl.num_programs(0) - 1)
    def _():
        for i in range(10):
            leaving(i).wait()


def forward(hidden, seg, weights):
    rows, length, _ = hidden.shape
    tokens = rows * length
    _, packed = windows(length)
    wide = [(3 * D, BF16), None, (D, BF16), (D, BF16), (D, BF16), (128, F32)]
    wide += [(FF, BF16), (FF, BF16), (D, BF16), (128, F32)]
    out_shape, kept = [], []
    for item in wide:
        if item is None:
            out_shape.append(pltpu.HBM((rows, PAIRS, packed, 2 * QB), BF16))
            kept.append(VMEM((PAIRS, packed, 2 * QB), BF16))
        else:
            out_shape.append(pltpu.HBM((tokens, item[0]), item[1]))
            kept.append(VMEM((length, item[0]), item[1]))
    hbm = hspec()
    out_specs = [hbm] * 10 + [
        pl.BlockSpec((None, SEG, D), lambda r: (r, 0, 0)),
        pl.BlockSpec((None, SEG, D), lambda r: (r, 0, 0)),
        pl.BlockSpec((None, SEG, 128), lambda r: (r, 0, 0)),
    ]
    out_shape += [
        shape_of((rows, SEG, D), BF16),
        shape_of((rows, SEG, D), F32),
        shape_of((rows, SEG, 128), F32),
    ]
    large = (0, 3, 7, 9)
    in_specs = [pl.BlockSpec((length, D), lambda r: (r, 0)), vspec()]
    in_specs += [hbm if i in large else vspec() for i in range(13)]
    return pl.pallas_call(
        forward_kernel,
        name="forward",
        grid=(rows,),
        in_specs=in_specs,
        out_specs=out_specs,
        out_shape=out_shape,
        scratch_shapes=[VMEM(weights[i].shape, BF16) for i in large]
        + [VMEM((packed, QB), F32), VMEM((length, D), F32)]
        + kept
        + [pltpu.SemaphoreType.DMA((4,)), pltpu.SemaphoreType.DMA((10,))],
        cost_estimate=cost(1e9, 4e6),
        compiler_params=params(50),
    )(*far(hidden.reshape(tokens, D), seg, *weights))


def loss_kernel(flips, idx, *refs):
    pieces, refs = refs[: len(flips)], refs[len(flips) :]
    targets, seg, g2, unitf_h, inv_h, xh2_h, rs2_h, loss_o, gb_o, vec_o = refs[:10]
    slope_s, rows_s, units, unitf, inv, xh2, rs2, sems = refs[10:]
    fetch = Fetch(sems, ((unitf_h, unitf), (inv_h, inv), (xh2_h, xh2), (rs2_h, rs2)))
    twin, me = idx[0], idx[1]
    count = units.shape[0] // 2
    sentences = unitf.shape[0]
    for piece, own_flips in zip(pieces, flips):
        if own_flips is None:
            units[...] = piece[...]
            continue
        for i, (twin_flip, flip) in enumerate(own_flips):
            at = (twin ^ twin_flip) * count + (me ^ flip) * sentences
            at = pl.multiple_of(at, sentences)
            units[pl.ds(at, sentences), :] = piece[i * sentences : (i + 1) * sentences, :]
    rows, length = seg.shape
    step = min(count, 256)
    factor = cosine_scale / D
    positives = units.at[pl.ds(count, count)]
    own = pl.ds(pl.multiple_of(me * sentences, sentences), sentences)

    def one_block(i, carry):
        lanes = pl.ds(pl.multiple_of(i * step, step), step)
        sims = nt(positives[...], units[lanes, :]) * factor
        top = jnp.max(sims, axis=0, keepdims=True)
        weights = jnp.exp(sims - top)
        total = jnp.sum(weights, axis=0, keepdims=True)
        hit = lax.broadcasted_iota(jnp.int32, sims.shape, 0) == targets[:, lanes]
        picked = jnp.sum(jnp.where(hit, sims, 0.0), axis=0, keepdims=True)
        loss_o[:, lanes] = top + jnp.log(total) - picked
        slope = loss_scale * (weights * (1.0 / total) - hit.astype(F32))
        slope_s[:, lanes] = slope.astype(BF16)
        return carry

    if count == step:
        one_block(0, 0)
    else:
        lax.fori_loop(0, count // step, one_block, 0)

    @pl.when(twin == 0)
    def _():
        def part(i, carry):
            lanes = pl.ds(pl.multiple_of(i * step, step), step)
            rows_s[lanes, :] = tn(slope_s[:, lanes], positives[...])
            return carry

        lax.fori_loop(0, count // step, part, 0)
        rows_s[pl.ds(0, sentences), :] = rows_s[own, :]

    @pl.when(twin == 1)
    def _():
        rows_s[pl.ds(0, sentences), :] = nn(slope_s[own, :], units[pl.ds(0, count), :])

    fetch.wait(0, 1, 2, 3)
    gu = rows_s[pl.ds(0, sentences), :] * factor
    unit = unitf[...]
    gs = inv[:, :1] * (gu - unit * jnp.mean(gu * unit, axis=-1, keepdims=True))
    gy = gs * vector(g2)
    u = gy - jnp.mean(gy, axis=-1, keepdims=True)
    gain = jnp.zeros((1, D), F32)
    shift = jnp.zeros((1, D), F32)
    summed = jnp.zeros((1, D), F32)
    for r in range(rows):
        part = slice(r * SEG, (r + 1) * SEG)
        tok = slice(r * length, (r + 1) * length)
        seg_row = seg[r : r + 1, :]
        hits = lax.broadcasted_iota(jnp.int32, (SEG, length), 0) == seg_row
        member = hits.astype(F32).astype(BF16)
        counts = jnp.sum(hits.astype(F32), axis=1, keepdims=True)
        xhat_low = xh2[tok, :]
        gain += jnp.sum(nn(member, xhat_low) * gs[part], axis=0, keepdims=True)
        shift += jnp.sum(counts * gs[part], axis=0, keepdims=True)
        xhat = xhat_low.astype(F32)
        high, low = split_low(u[part])
        spread = tn(member, high) + tn(member, low)
        inner = jnp.mean(spread * xhat, axis=-1, keepdims=True)
        grad = rs2[tok, :1] * (spread - xhat * inner)
        grad_low = grad.astype(BF16)
        gb_o[tok, :] = grad_low
        summed += jnp.sum(grad_low.astype(F32), axis=0, keepdims=True)
    vec_o[...] = jnp.concatenate([summed, gain, shift, jnp.zeros((5, D), F32)], axis=0)


def loss_stage(idx, gathered, targets, unitf, inv, seg, g2, xh2, rs2):
    pieces, flips = gathered
    tokens = xh2.shape[0]
    count = targets.shape[1]
    return pl.pallas_call(
        functools.partial(loss_kernel, flips),
        name="loss",
        in_specs=[sspec()] + [vspec()] * (3 + len(pieces)) + [hspec()] * 4,
        out_specs=[vspec()] * 3,
        out_shape=[
            shape_of((1, count), F32),
            shape_of((tokens, D), BF16),
            shape_of((8, D), F32),
        ],
        scratch_shapes=[VMEM((count, count), BF16), VMEM((count, D), F32), VMEM((2 * count, D), BF16)]
        + [VMEM(a.shape, a.dtype) for a in (unitf, inv, xh2, rs2)]
        + [pltpu.SemaphoreType.DMA((4,))],
        cost_estimate=cost(1e8, 1e6),
        compiler_params=params(22 if count <= 256 else 56),
    )(idx, *pieces, *far(targets, seg, g2, unitf, inv, xh2, rs2))


def pre_kernel(gb, wdown_h, dg_h, out, wdown, dg, sems):
    n = 768
    pairs = []
    for j in range(FF // n):
        part = slice(j * n, (j + 1) * n)
        pairs += [(wdown_h.at[part, :], wdown.at[part, :]), (dg_h.at[:, part], dg.at[:, part])]
    fetch = Fetch(sems, pairs)

    def product(j):
        fetch.wait(2 * j)
        return nt(gb[...], wdown[j * n : (j + 1) * n, :])

    ahead = product(0)
    for j in range(FF // n):
        value = ahead
        if j + 1 < FF // n:
            ahead = product(j + 1)
        fetch.wait(2 * j + 1)
        part = slice(j * n, (j + 1) * n)
        out[:, part] = (value * dg[:, part].astype(F32)).astype(BF16)


def pre_stage(gb, wdown, dg):
    return pl.pallas_call(
        pre_kernel,
        name="grad_pre",
        in_specs=[vspec(), hspec(), hspec()],
        out_specs=vspec(),
        out_shape=shape_of(dg.shape, BF16),
        scratch_shapes=[
            VMEM(wdown.shape, BF16),
            VMEM(dg.shape, BF16),
            pltpu.SemaphoreType.DMA((2 * FF // 768,)),
        ],
        cost_estimate=cost(1e8, 1e6),
        compiler_params=params(32),
    )(gb, *far(wdown, dg))


def normed_kernel(
    gp, win_h, gb, xh1_h, rs1_h, g1, wout_h, ga_o, gc_o, vec_o, win, xh1, rs1, wout, sems
):
    m = 512
    count = gp.shape[0] // m
    fetch = Fetch(sems, ((win_h, win), (xh1_h, xh1), (rs1_h, rs1), (wout_h, wout)))
    gain, shift, summed = [jnp.zeros((1, D), F32) for _ in range(3)]
    fetch.wait(0)
    grads = [nt(gp[i * m : (i + 1) * m, :], win[...]) for i in range(count)]
    fetch.wait(1, 2)
    for i in range(count):
        rows = slice(i * m, (i + 1) * m)
        grad = grads[i] + gb[rows, :].astype(F32)
        xhat = xh1[rows, :].astype(F32)
        gain += jnp.sum(grad * xhat, axis=0, keepdims=True)
        shift += jnp.sum(grad, axis=0, keepdims=True)
        gy = grad * vector(g1)
        inner = jnp.mean(gy * xhat, axis=-1, keepdims=True)
        total = rs1[rows, :1] * (gy - jnp.mean(gy, axis=-1, keepdims=True) - xhat * inner)
        low = total.astype(BF16)
        ga_o[rows, :] = low
        summed += jnp.sum(low.astype(F32), axis=0, keepdims=True)
    fetch.wait(3)
    for i in range(count):
        rows = slice(i * m, (i + 1) * m)
        gc_o[rows, :] = nt(ga_o[rows, :], wout[...]).astype(BF16)
    vec_o[...] = jnp.concatenate([summed, gain, shift, jnp.zeros((5, D), F32)], axis=0)


def normed_stage(gp, win, gb, xh1, rs1, g1, wout):
    tokens = gp.shape[0]
    hbm = hspec()
    return pl.pallas_call(
        normed_kernel,
        name="grad_normed",
        in_specs=[vspec(), hbm, vspec(), hbm, hbm, vspec(), hbm],
        out_specs=[vspec()] * 3,
        out_shape=[
            shape_of((tokens, D), BF16),
            shape_of((tokens, D), BF16),
            shape_of((8, D), F32),
        ],
        scratch_shapes=[VMEM(a.shape, a.dtype) for a in (win, xh1, rs1, wout)]
        + [pltpu.SemaphoreType.DMA((4,))],
        cost_estimate=cost(1e8, 1e6),
        compiler_params=params(30),
    )(gp, *far(win), gb, *far(xh1, rs1, g1, wout))


def attend_back_kernel(q_ref, k_ref, v_ref, g_ref, p_ref, out_ref):
    length = q_ref.shape[0]
    blocks, _ = windows(length)
    group = q_ref.shape[1] // PW
    scale = HEAD_DIM**-0.5
    loaded, grads = [], []
    for h in range(group):
        lanes = slice(h * PW, (h + 1) * PW)
        q2 = [two_heads(q_ref[b[0] : b[0] + QB, lanes]) for b in blocks]
        g2 = [two_heads(g_ref[b[0] : b[0] + QB, lanes]) for b in blocks]
        loaded.append((q2, g2, k_ref[:, lanes].T))
        v_all = v_ref[:, lanes]
        grads.append([nt(v_all[b[1] : b[2]], g) for b, g in zip(blocks, g2)])
    slopes = []
    for h in range(group):
        own = []
        for gp, (_, low, high, packed) in zip(grads[h], blocks):
            p = p_ref[h, packed : packed + high - low, :].astype(F32)
            weighted = p * gp
            inner = jnp.sum(weighted, axis=0, keepdims=True)
            own.append((weighted - p * inner).astype(BF16))
        slopes.append(own)

    def gather(parts):
        out = []
        for block in range(len(blocks)):
            total = None
            for part, (_, low, high, _) in zip(parts, blocks):
                base = block * QB - low
                if 0 <= base < high - low:
                    piece = part[base : base + QB]
                    total = piece if total is None else total + piece
            out.append(total)
        return jnp.concatenate(out, axis=0)

    for h in range(group):
        lanes = slice(h * PW, (h + 1) * PW)
        q2, g2, k_turned = loaded[h]
        dq = [nn(k_turned[:, b[1] : b[2]], s) for b, s in zip(blocks, slopes[h])]
        dv = [nn(p_ref[h, b[3] : b[3] + b[2] - b[1], :], g) for b, g in zip(blocks, g2)]
        dk = [nn(s, q) for s, q in zip(slopes[h], q2)]
        turned = [pick_heads((part * scale).astype(BF16)) for part in dq]
        out_ref[0, :, lanes] = jnp.concatenate(turned, axis=0)
        out_ref[1, :, lanes] = (gather(dk) * scale).astype(BF16)
        out_ref[2, :, lanes] = gather(dv).astype(BF16)


def attend_back(qkv, grad_context, probs, rows, length, first, pairs):
    _, packed = windows(length)
    group = 2
    steps = pairs // group
    base = first // group
    width = group * PW

    def block(part):
        return pl.BlockSpec((length, width), lambda r, h: (r, part * (D // width) + base + h))

    return pl.pallas_call(
        attend_back_kernel,
        name="attend_back",
        grid=(rows, steps),
        in_specs=[
            block(0),
            block(1),
            block(2),
            block(0),
            pl.BlockSpec((None, group, packed, 2 * QB), lambda r, h: (r, base + h, 0, 0)),
        ],
        out_specs=pl.BlockSpec((3, length, width), lambda r, h: (0, r, h)),
        out_shape=shape_of((3, rows * length, pairs * PW), BF16),
        cost_estimate=cost(1e8, 1e6),
        compiler_params=params(20),
    )(*far(qkv, qkv, qkv), grad_context, *far(probs))


def hidden_kernel(da, db, wqkv_h, ga, out, wqkv, sems):
    m = 512
    pairs = []
    for part in range(3):
        cols = slice(part * D, (part + 1) * D)
        pairs.append((wqkv_h.at[:, cols], wqkv.at[:, cols]))
    fetch = Fetch(sems, pairs)
    fetch.wait(0, 1, 2)
    for i in range(ga.shape[0] // m):
        rows = slice(i * m, (i + 1) * m)
        total = ga[rows, :].astype(F32)
        for part in range(3):
            both = jnp.concatenate([da[part, rows, :], db[part, rows, :]], axis=1)
            total = total + nt(both, wqkv[:, part * D : (part + 1) * D])
        out[rows, :] = total.astype(BF16)


def hidden_stage(da, db, wqkv, ga):
    return pl.pallas_call(
        hidden_kernel,
        name="hidden_grad",
        in_specs=[vspec(), vspec(), hspec(), vspec()],
        out_specs=vspec(),
        out_shape=shape_of(ga.shape, BF16),
        scratch_shapes=[VMEM(wqkv.shape, BF16), pltpu.SemaphoreType.DMA((3,))],
        cost_estimate=cost(1e8, 1e6),
        compiler_params=params(22),
    )(da, db, *far(wqkv), ga)


def place_of(half, quarter, owner):
    c, y, z0, z1 = owner & 1, (owner >> 1) & 1, (owner >> 2) & 1, owner >> 3
    order = (quarter, y, z0, z1, c) if half == 0 else (y, z0, z1, quarter, c)
    out = 0
    for bit in order:
        out = 2 * out + bit
    return out


def lanes_of(width):
    most = 128 if width <= 256 else 256
    return [(low, min(most, width - low)) for low in range(0, width, most)]


def half_shapes(width):
    shapes = [shape_of((32, 48, width), BF16)]
    return shapes + [shape_of((32, 48, n), BF16) for _, n in lanes_of(width)]


def store_piece(first, keep, sends, quarter, owner, piece_a, piece_b):
    at_a, at_b = place_of(0, quarter, owner), place_of(1, quarter, owner)
    keep[jnp.where(first, at_a, at_b)] = jnp.where(first, piece_a, piece_b)
    other = jnp.where(first, piece_b, piece_a)
    at = jnp.where(first, at_b, at_a)
    for send, (low, n) in zip(sends, lanes_of(keep.shape[2])):
        send[at] = other[:, low : low + n]


def down_kernel(idx, act_h, gb, keep, *refs):
    send, (act, sems) = refs[:-2], refs[-2:]
    first = idx[2] == 0
    n = 768
    pairs = []
    for j in range(FF // n):
        part = slice(j * n, (j + 1) * n)
        pairs.append((act_h.at[:, part], act.at[:, part]))
    fetch = Fetch(sems, pairs)

    def product(j):
        fetch.wait(j)
        return tn(act[:, j * n : (j + 1) * n], gb[...])

    ahead = product(0)
    for j in range(FF // n):
        total = ahead.astype(BF16)
        if j + 1 < FF // n:
            ahead = product(j + 1)
        for local in range(4):
            for quarter in range(2):
                base = local * 192 + quarter * 48
                a, b = total[base : base + 48], total[base + 96 : base + 144]
                store_piece(first, keep, send, quarter, 4 * j + local, a, b)


def down_stage(idx, act, gb):
    return pl.pallas_call(
        down_kernel,
        name="grad_w_down",
        in_specs=[sspec(), hspec(), vspec()],
        out_specs=[vspec()] * len(half_shapes(D)),
        out_shape=half_shapes(D),
        scratch_shapes=[VMEM(act.shape, BF16), pltpu.SemaphoreType.DMA((4,))],
        cost_estimate=cost(1e8, 1e6),
        compiler_params=params(26),
    )(idx, *far(act), gb)


def in_kernel(idx, n1_h, gp, vec_o, keep, *refs):
    send, (n1, turned, sems) = refs[:-3], refs[-3:]
    first = idx[2] == 0
    fetch = Fetch(sems, ((n1_h, n1),))
    fetch.wait(0)
    turned[...] = n1[...].T

    def products(quarter):
        out = []
        for half in range(2):
            j = 2 * half + quarter
            out.append(nn(turned[...], gp[:, j * D : (j + 1) * D]))
        return out

    ahead = products(0)
    for quarter in range(2):
        a, b = [part.astype(BF16) for part in ahead]
        if quarter == 0:
            ahead = products(1)
        for owner in range(16):
            rows = slice(owner * 48, (owner + 1) * 48)
            store_piece(first, keep, send, quarter, owner, a[rows], b[rows])
    vec_o[...] = jnp.sum(gp[...].astype(F32), axis=0, keepdims=True)


def in_stage(idx, n1, gp):
    return pl.pallas_call(
        in_kernel,
        name="grad_w_in",
        in_specs=[sspec(), hspec(), vspec()],
        out_specs=[vspec()] * (1 + len(half_shapes(D))),
        out_shape=[shape_of((1, FF), F32)] + half_shapes(D),
        scratch_shapes=[
            VMEM(n1.shape, BF16),
            VMEM((D, n1.shape[0]), BF16),
            pltpu.SemaphoreType.DMA((1,)),
        ],
        cost_estimate=cost(1e8, 1e6),
        compiler_params=params(30),
    )(idx, *far(n1), gp)


WIDE, NARROW = 640, 256


def store_all(first, keep, send, whole, width):
    for quarter in range(2):
        a = whole[:, quarter * width : (quarter + 1) * width]
        b = whole[:, (2 + quarter) * width : (3 + quarter) * width]
        for owner in range(16):
            rows = slice(owner * 48, (owner + 1) * 48)
            store_piece(first, keep, send, quarter, owner, a[rows], b[rows])


def wide_kernel(idx, hid_h, da, ctx_h, ga, turned_o, keep, *refs):
    send, (hid, ctx, whole, sems) = refs[:-4], refs[-4:]
    fetch = Fetch(sems, ((hid_h, hid), (ctx_h, ctx)))
    n = da.shape[2]
    fetch.wait(0)
    turned_o[...] = hid[...].T
    for part in range(3):
        whole[:, part * n : (part + 1) * n] = nn(turned_o[...], da[part]).astype(BF16)
    fetch.wait(1)
    whole[:, 3 * n : 3 * n + D] = tn(ctx[...], ga[...]).astype(BF16)
    whole[:, 3 * n + D :] = jnp.zeros((D, 4 * WIDE - 3 * n - D), BF16)
    store_all(idx[2] == 0, keep, send, whole, WIDE)


def wide_stage(idx, hid, da, ctx, ga):
    tokens = hid.shape[0]
    return pl.pallas_call(
        wide_kernel,
        name="grad_w_wide",
        in_specs=[sspec(), hspec(), vspec(), hspec(), vspec()],
        out_specs=[vspec()] * (1 + len(half_shapes(WIDE))),
        out_shape=[shape_of((D, tokens), BF16)] + half_shapes(WIDE),
        scratch_shapes=[
            VMEM(hid.shape, BF16),
            VMEM(ctx.shape, BF16),
            VMEM((D, 4 * WIDE), BF16),
            pltpu.SemaphoreType.DMA((2,)),
        ],
        cost_estimate=cost(1e8, 1e6),
        compiler_params=params(28),
    )(idx, *far(hid), da, *far(ctx), ga)


def narrow_kernel(idx, turned, da, db, vecs, keep, *refs):
    send, (whole, sums_s) = refs[:-2], refs[-2:]
    n = db.shape[2]
    for part in range(3):
        whole[:, part * n : (part + 1) * n] = nn(turned[...], db[part]).astype(BF16)
    sums_s[...] = jnp.zeros_like(sums_s)
    sums_s[:16, :] = vecs[...]
    for row, part in ((0, 0), (1, 2)):
        for base, grads in ((0, da), (D - n, db)):
            lanes = slice(base, base + grads.shape[2])
            total = jnp.sum(grads[part].astype(F32), axis=0, keepdims=True)
            sums_s[row : row + 1, lanes] = total
    whole[:, 3 * n : 3 * n + 128] = sums_s[...].T.astype(BF16)
    whole[:, 3 * n + 128 :] = jnp.zeros((D, 4 * NARROW - 3 * n - 128), BF16)
    store_all(idx[2] == 0, keep, send, whole, NARROW)


def narrow_stage(idx, turned, da, db, vecs):
    return pl.pallas_call(
        narrow_kernel,
        name="grad_w_narrow",
        in_specs=[sspec()] + [vspec()] * 4,
        out_specs=[vspec()] * len(half_shapes(NARROW)),
        out_shape=half_shapes(NARROW),
        scratch_shapes=[VMEM((D, 4 * NARROW), BF16), VMEM((128, D), F32)],
        cost_estimate=cost(1e8, 1e6),
        compiler_params=params(22),
    )(idx, turned, da, db, vecs)


def swap_dp(value, flip):
    devices = lax.axis_size("dp")
    return lax.ppermute(value, "dp", [(i, i ^ flip) for i in range(devices)])


def swap_twin(value):
    return lax.ppermute(value, "twin", [(0, 1), (1, 0)])


TWIN = 16
ROUTES = ((TWIN, 2, 4, 8, TWIN), (2, 4, 8, TWIN, TWIN))


def step_swap(value, step):
    pairs = [(i, i ^ ROUTES[i & 1][step]) for i in range(2 * TWIN)]
    return lax.ppermute(value, ("twin", "dp"), pairs)


def plus(*values):
    total = values[0].astype(F32)
    for value in values[1:]:
        total = total + value.astype(F32)
    return total.astype(BF16)


def call_small(kernel, name, idx, operands, outs):
    return pl.pallas_call(
        kernel,
        name=name,
        in_specs=[sspec()] + [vspec()] * len(operands),
        out_specs=[vspec()] * len(outs),
        out_shape=[shape_of(shape, dtype) for shape, dtype in outs],
        cost_estimate=cost(1e6, 1e5),
        compiler_params=params(12),
    )(idx, *operands)


def half_kernel(step, idx, keep, recv, keep_o, send_o):
    count = keep_o.shape[0]
    bit = idx[3 + step]
    mine = pl.ds(bit * count, count)
    other = pl.ds((1 - bit) * count, count)
    keep_o[...] = plus(keep[mine], recv[mine])
    send_o[...] = plus(keep[other], recv[other])


def half_step(idx, step, keep, recv):
    count, rows, width = keep.shape
    shape = (count // 2, rows, width)
    kernel = functools.partial(half_kernel, step)
    return call_small(kernel, "sum_" + str(step), idx, (keep, recv), [(shape, BF16)] * 2)


def core_kernel(idx, keep, *refs):
    recvs, (keep_o, send_o) = refs[:-2], refs[-2:]
    bit = idx[3]
    for recv, (low, n) in zip(recvs, lanes_of(keep.shape[3])):
        lanes = slice(low, low + n)
        keep_o[:, :, lanes] = plus(keep[bit, :, :, lanes], recv[bit])
        send_o[:, :, lanes] = plus(keep[1 - bit, :, :, lanes], recv[1 - bit])


def core_step(idx, keep, recvs):
    count, rows, width = keep.shape
    half = count // 2
    pieces = 4
    part = half // pieces

    def spec(n):
        return pl.BlockSpec((2, part, rows, n), lambda i: (0, i, 0, 0))

    return pl.pallas_call(
        core_kernel,
        name="sum_core",
        grid=(pieces,),
        in_specs=[sspec(), spec(width)] + [spec(n) for _, n in lanes_of(width)],
        out_specs=[pl.BlockSpec((part, rows, width), lambda i: (i, 0, 0))] * 2,
        out_shape=[shape_of((half, rows, width), BF16)] * 2,
        cost_estimate=cost(1e6, 1e5),
        compiler_params=params(10),
    )(
        idx,
        keep.reshape(2, half, rows, width),
        *[recv.reshape(2, half, rows, recv.shape[2]) for recv in recvs],
    )


def own_kernel(idx, keep, recv, out):
    out[...] = plus(keep[...], recv[...])


def turn_kernel(idx, own, other, keep_o, send_o):
    twin, core = idx[0], idx[2]
    keep_o[twin] = own[core]
    keep_o[1 - twin] = other[core]
    send_o[twin] = own[1 - core]
    send_o[1 - twin] = other[1 - core]


class Order:
    def __init__(self):
        self.last = None

    def after(self, value, *others):
        if self.last is None:
            return value
        return lax.optimization_barrier((value, self.last) + others)[0]

    def done(self, value):
        self.last = value
        return value


class Exchange:
    def __init__(self, order, idx, keep, sends):
        self.order, self.idx, self.step = order, idx, 0
        self.keep, self.recv = keep, [swap_dp(send, 1) for send in sends]

    def advance(self):
        idx, order = self.idx, self.order
        keep, recv = order.after(self.keep), self.recv
        if self.step == 0:
            keep, send = core_step(idx, keep, recv)
            recv = step_swap(send, 0)
        elif self.step < 4:
            keep, send = half_step(idx, self.step, keep, recv)
            recv = step_swap(send, self.step)
        elif self.step == 4:
            shape = keep.shape
            (keep,) = call_small(own_kernel, "sum_4", idx, (keep, recv), [(shape, BF16)])
            recv = step_swap(keep, 4)
        else:
            shape = keep.shape
            keep, send = call_small(turn_kernel, "turn", idx, (keep, recv), [(shape, BF16)] * 2)
            recv = swap_dp(send, 1)
        order.done(keep)
        self.keep, self.recv = keep, recv
        self.step += 1

    def result(self):
        return self.keep, self.recv


def gather_units(unit):
    flips = [(0, 0)]
    for flip in (8, 4):
        unit = jnp.concatenate([unit, swap_dp(unit, flip)], axis=0)
        flips = flips + [(t, f ^ flip) for t, f in flips]
    pairs = [(i, i ^ (TWIN + 2)) for i in range(2 * TWIN)]
    far = lax.ppermute(unit, ("twin", "dp"), pairs)
    unit = jnp.concatenate([unit, swap_dp(unit, 2), swap_twin(unit), far], axis=0)
    flips = [(t ^ a, f ^ b) for a, b in ((0, 0), (0, 2), (1, 0), (1, 2)) for t, f in flips]
    return (unit, swap_dp(unit, 1)), (flips, [(t, f ^ 1) for t, f in flips])


def four_quarters(idx, keep, recv):
    first = idx[2] == 0
    low = [jnp.where(first, keep[i], recv[i]) for i in range(2)]
    high = [jnp.where(first, recv[i], keep[i]) for i in range(2)]
    return low + high


def final_in_kernel(idx, keep, recv, out):
    for i, part in enumerate(four_quarters(idx, keep, recv)):
        out[:, i * D : (i + 1) * D] = part.astype(F32)


def final_down_kernel(idx, keep, recv, out):
    for i, part in enumerate(four_quarters(idx, keep, recv)):
        out[i * 48 : (i + 1) * 48, :] = part.astype(F32)


def final_last_kernel(idx, wide_k, wide_r, narrow_k, narrow_r, qkv_o, out_o, vec_o):
    wide = jnp.concatenate(four_quarters(idx, wide_k, wide_r), axis=1).astype(F32)
    narrow = jnp.concatenate(four_quarters(idx, narrow_k, narrow_r), axis=1).astype(F32)
    low, high = 2 * D // 3, D // 3
    for part in range(3):
        qkv_o[:, part * D : part * D + low] = wide[:, part * low : (part + 1) * low]
        qkv_o[:, part * D + low : (part + 1) * D] = narrow[:, part * high : (part + 1) * high]
    out_o[...] = wide[:, 3 * low : 3 * low + D]
    small = narrow[:, 3 * high : 3 * high + 128]
    vec_o[...] = jnp.concatenate([small, jnp.zeros((80, 128), F32)], axis=0).T[:16]


def finish(order, idx, kernel, name, chunks, outs):
    operands = [value for chunk in chunks for value in chunk.result()]
    operands[0] = order.after(operands[0])
    out = call_small(kernel, name, idx, operands, outs)
    order.done(out[0])
    return out


def add_low(*parts):
    return lax.optimization_barrier(plus(*parts))


def digits_of(devices):
    out, rest = [], devices // 2
    while rest > 1:
        size = 4 if rest % 4 == 0 else 2
        out.append(size)
        rest //= size
    return out


def pick(value, index, axis):
    return lax.dynamic_index_in_dim(value, index, axis, keepdims=False)


def scatter(grad):
    devices = lax.axis_size("dp")
    me = lax.axis_index("dp")
    value = grad.reshape(devices, grad.shape[0] // devices, grad.shape[1])
    unit = 1
    for size in [2] + digits_of(devices):
        mine = (me // unit) % size
        view = value.reshape((value.shape[0] // size, size) + value.shape[1:])
        parts = [pick(view, mine, 1)]
        for flip in range(1, size):
            parts.append(swap_dp(pick(view, mine ^ flip, 1), flip * unit))
        value = add_low(*parts)
        unit *= size
    value = value[0]
    return value.astype(F32) + swap_twin(value).astype(F32)


def body(
    hidden,
    segment_ids,
    targets,
    w_qkv,
    b_query,
    b_value,
    w_out,
    b_out,
    ln1_gain,
    ln1_bias,
    w_in,
    b_in,
    w_down,
    b_down,
    ln2_gain,
    ln2_bias,
):
    row_count, length, width = hidden.shape
    tokens = row_count * length
    devices = lax.axis_size("dp")
    everyone = lax.axis_size(("twin", "dp"))
    me = lax.axis_index("dp")
    twin = lax.axis_index("twin")
    core, y, z0, z1 = me & 1, (me >> 1) & 1, (me >> 2) & 1, me >> 3
    first = core == 0
    bits = [jnp.where(first, a, b) for a, b in ((twin, y), (y, z0), (z0, z1), (z1, twin))]
    idx = jnp.stack([twin, me, core] + bits).astype(jnp.int32)
    weights = (w_qkv, b_query, b_value, w_out, b_out, ln1_gain, ln1_bias)
    weights += (w_in, b_in, w_down, b_down, ln2_gain, ln2_bias)
    qkv, probs, ctx, n1, xh1, rs1, act, dg, xh2, rs2, unit, unitf, inv = forward(
        hidden, segment_ids, weights
    )
    sentences = row_count * SEG
    unit = unit.reshape(sentences, width)
    direct = devices == TWIN and sentences == 16
    if direct:
        gathered = gather_units(unit)
    else:
        gathered = ((lax.all_gather(unit, ("twin", "dp"), axis=0, tiled=True),), (None,))
    losses, gb, vec2 = loss_stage(
        idx,
        gathered,
        targets.reshape(1, -1),
        unitf.reshape(sentences, width),
        inv.reshape(sentences, 128),
        segment_ids,
        ln2_gain,
        xh2,
        rs2,
    )
    share = losses.shape[1] // everyone
    losses = lax.dynamic_slice_in_dim(
        losses[0], lax.axis_index(("twin", "dp")) * share, share, 0
    )
    flat = hidden.reshape(tokens, width)
    if direct:
        order = Order()
        keep, *sends = down_stage(idx, act, gb)
        order.done(keep)
        down = Exchange(order, idx, keep, sends)
        gp = order.done(pre_stage(order.after(gb), w_down, dg))
        down.advance()
        sums, keep, *sends = in_stage(idx, n1, order.after(gp))
        order.done(keep)
        into = Exchange(order, idx, keep, sends)
        ga, gc, vec1 = normed_stage(order.after(gp), w_in, gb, xh1, rs1, ln1_gain, w_out)
        order.done(ga)
        into.advance()
        down.advance()
        gc = order.after(gc)
        da = order.done(attend_back(qkv, gc, probs, row_count, length, 0, 4))
        turned, keep, *sends = wide_stage(idx, flat, order.after(da), ctx, ga)
        order.done(keep)
        wide = Exchange(order, idx, keep, sends)
        down.advance()
        db = order.done(attend_back(qkv, order.after(gc), probs, row_count, length, 4, 2))
        wide.advance()
        into.advance()
        rest = sums.reshape(devices, 4, 48).transpose(1, 0, 2).reshape(4, width)
        nothing = jnp.zeros((2, width), F32)
        vecs = jnp.concatenate([nothing, vec1[:3], vec2[:3], rest, nothing, nothing])
        keep, *sends = narrow_stage(idx, turned, da, order.after(db), vecs)
        order.done(keep)
        narrow = Exchange(order, idx, keep, sends)
        down.advance()
        hidden_grad = order.done(hidden_stage(da, order.after(db), w_qkv, ga))
        narrow.advance()
        down.advance()
        into.advance()
        wide.advance()
        down.advance()
        narrow.advance()
        (grad_w_down,) = finish(
            order, idx, final_down_kernel, "final_down", [down], [((192, D), F32)]
        )
        into.advance()
        wide.advance()
        narrow.advance()
        into.advance()
        wide.advance()
        narrow.advance()
        into.advance()
        wide.advance()
        narrow.advance()
        (grad_w_in,) = finish(order, idx, final_in_kernel, "final_in", [into], [((48, FF), F32)])
        wide.advance()
        narrow.advance()
        shapes = [((48, 3 * D), F32), ((48, D), F32), ((16, 128), F32)]
        grad_w_qkv, grad_w_out, vec = finish(
            order, idx, final_last_kernel, "final_last", [wide, narrow], shapes
        )
        vec = vec[:, :48]
        vecs = [vec[i] for i in range(8)]
        grad_b_in = vec[8:12].reshape(-1)
    else:
        gp = pre_stage(gb, w_down, dg)
        ga, gc, vec1 = normed_stage(gp, w_in, gb, xh1, rs1, ln1_gain, w_out)
        da = attend_back(qkv, gc, probs, row_count, length, 0, 4)
        db = attend_back(qkv, gc, probs, row_count, length, 4, 2)
        hidden_grad = hidden_stage(da, db, w_qkv, ga)
        dqkv = jnp.concatenate([da, db], axis=2)
        grad_w_down = scatter(tn(act, gb).astype(BF16))
        grad_w_in = scatter(tn(n1, gp).astype(BF16))
        wide = jnp.concatenate([dqkv[0], dqkv[1], dqkv[2]], axis=1)
        grad_w_qkv = scatter(tn(flat, wide).astype(BF16))
        grad_w_out = scatter(tn(ctx, ga).astype(BF16))
        sums = jnp.sum(dqkv, axis=1, dtype=F32)
        vec = jnp.concatenate([sums[0:1], sums[2:3], vec1[:3], vec2[:3]])
        vec = scatter(jnp.pad(vec, ((0, 120), (0, 0))).T.astype(BF16)).T
        vecs = [vec[i] for i in range(8)]
        bias = jnp.sum(gp, axis=0, dtype=F32)
        grad_b_in = scatter(jnp.broadcast_to(bias[:, None], (FF, 128)).astype(BF16))[:, 0]
    return (
        losses,
        hidden_grad.reshape(row_count, length, width),
        grad_w_qkv,
        vecs[0],
        vecs[1],
        grad_w_out,
        vecs[2],
        vecs[3],
        vecs[4],
        grad_w_in,
        grad_b_in,
        grad_w_down,
        vecs[5],
        vecs[6],
        vecs[7],
    )


def solution(mesh):
    whole = (P(),) * 14
    placed = (P(("twin", "dp"), None, None), P(("twin", "dp"), None)) + whole
    return jax.shard_map(
        body,
        mesh=mesh,
        in_specs=placed,
        out_specs=(
            P(("twin", "dp")),
            P(("twin", "dp"), None, None),
            P("dp", None),
            P("dp"),
            P("dp"),
            P("dp", None),
            P("dp"),
            P("dp"),
            P("dp"),
            P("dp", None),
            P("dp"),
            P("dp", None),
            P("dp"),
            P("dp"),
            P("dp"),
        ),
        check_vma=False,
    )
```

```python
import functools

import jax
import jax.numpy as jnp
from jax import lax
from jax.experimental import pallas as pl
from jax.experimental.pallas import tpu as pltpu
from jax.sharding import PartitionSpec as P

D = 768
HEADS = 12
HEAD_DIM = 64
FF = 3072
SEG = 8
QB = 128
MOST = 128
PAIRS = HEADS // 2
PW = 2 * HEAD_DIM

cosine_scale = 64.0
loss_scale = 32.0
norm_epsilon = 1e-12
unit_epsilon = 1e-06
masked_score = -1e30

F32 = jnp.float32
BF16 = jnp.bfloat16
VMEM = pltpu.VMEM
ANY = pl.ANY
MIB = 1 << 20


def nn(left, right):
    return lax.dot_general(left, right, (((1,), (0,)), ((), ())), preferred_element_type=F32)


def nt(left, right):
    return lax.dot_general(left, right, (((1,), (1,)), ((), ())), preferred_element_type=F32)


def tn(left, right):
    return lax.dot_general(left, right, (((0,), (0,)), ((), ())), preferred_element_type=F32)


def vspec():
    return pl.BlockSpec(memory_space=VMEM)


def sspec():
    return pl.BlockSpec(memory_space=pltpu.SMEM)


def hspec():
    return pl.BlockSpec(memory_space=pltpu.HBM)


def far(*values):
    return [pltpu.with_memory_space_constraint(value, pltpu.HBM) for value in values]


class Fetch:
    def __init__(self, sems, pairs):
        self.copies = [pltpu.make_async_copy(a, b, sems.at[i]) for i, (a, b) in enumerate(pairs)]
        for copy in self.copies:
            copy.start()

    def wait(self, *which):
        for i in which:
            self.copies[i].wait()


def carrying(kernel, n_in, n_out, n_carry):
    def wrapped(*refs):
        refs, sems = refs[:-1], refs[-1]
        ins, refs = refs[:n_in], refs[n_in:]
        sources, refs = refs[:n_carry], refs[n_carry:]
        outs, refs = refs[:n_out], refs[n_out:]
        targets, rest = refs[:n_carry], refs[n_carry:]
        fetch = Fetch(sems, tuple(zip(sources, targets)))
        kernel(*ins, *outs, *rest)
        fetch.wait(*range(n_carry))

    return wrapped


def carry_call(kernel, name, us, mib, operands, specs, outs, scratch, carry):
    n_carry = len(carry)
    return pl.pallas_call(
        carrying(kernel, len(operands), len(outs), n_carry),
        name=name,
        in_specs=list(specs) + [hspec()] * n_carry,
        out_specs=[vspec()] * (len(outs) + n_carry),
        out_shape=list(outs) + [VMEM(a.shape, a.dtype) for a in carry],
        scratch_shapes=list(scratch) + [pltpu.SemaphoreType.DMA((max(n_carry, 1),))],
        cost_estimate=took(us),
        compiler_params=params(mib),
    )(*operands, *far(*carry))


def fixed(shape):
    return pl.BlockSpec(shape, lambda *_: (0,) * len(shape))


def shape_of(shape, dtype):
    return jax.ShapeDtypeStruct(shape, dtype)


def params(mib):
    return pltpu.CompilerParams(vmem_limit_bytes=mib * MIB)


SCALE = 0.4


def took(us):
    return pl.CostEstimate(flops=int(us * SCALE * 1.15e9), bytes_accessed=0, transcendentals=0)


def windows(length):
    out, packed = [], 0
    for start in range(0, length, QB):
        low, high = max(0, start - MOST), min(length, start + QB + MOST)
        out.append((start, low, high, packed))
        packed += high - low
    return out, packed


def two_heads(pair):
    first = lax.broadcasted_iota(jnp.int32, pair.shape, 1) < HEAD_DIM
    zero = jnp.zeros((), pair.dtype)
    return jnp.concatenate([jnp.where(first, pair, zero), jnp.where(first, zero, pair)], axis=0)


def pick_heads(both):
    rows = both.shape[1] // 2
    return jnp.concatenate([both[:HEAD_DIM, :rows], both[HEAD_DIM:, rows:]], axis=0).T


def column_of(row):
    return jnp.broadcast_to(row, (8, row.shape[1])).T[:, :1]


def split_low(value):
    high = value.astype(BF16)
    return high, (value - high.astype(F32)).astype(BF16)


def normalise(value):
    middle = jnp.mean(value, axis=-1, keepdims=True)
    centered = value - middle
    spread = jnp.mean(centered * centered, axis=-1, keepdims=True)
    rstd = lax.rsqrt(spread + norm_epsilon)
    return centered * rstd, rstd


def vector(ref):
    return ref[...].astype(F32).reshape(1, ref.shape[0])


def softmax_down(own):
    top = jnp.max(own, axis=0, keepdims=True)
    weights = jnp.exp(own - top)
    total = jnp.sum(weights, axis=0, keepdims=True)
    return (weights * (1.0 / total)).astype(BF16)


def attend(length, qkv, bias, p_s, ctx_s):
    blocks, _ = windows(length)

    def lanes(part, h):
        return slice(part * D + h * PW, part * D + (h + 1) * PW)

    def score(h):
        q_all = qkv[:, lanes(0, h)] * jnp.asarray(HEAD_DIM**-0.5, BF16)
        k_all = qkv[:, lanes(1, h)]
        out = []
        for start, low, high, _ in blocks:
            out.append(nt(k_all[low:high], two_heads(q_all[start : start + QB])))
        return out, qkv[:, lanes(2, h)].T

    ahead = score(0)
    for h in range(PAIRS):
        scores, v_turned = ahead
        if h + 1 < PAIRS:
            ahead = score(h + 1)
        probs = []
        for own, (_, low, high, packed) in zip(scores, blocks):
            mask = bias[packed : packed + high - low, :]
            halves = [softmax_down(own[:, :QB] + mask), softmax_down(own[:, QB:] + mask)]
            probs.append(jnp.concatenate(halves, axis=1))
        for p, (_, low, high, packed) in zip(probs, blocks):
            p_s[h, packed : packed + high - low, :] = p
        outs = [nn(v_turned[:, low:high], p) for p, (_, low, high, _) in zip(probs, blocks)]
        ctx_s[:, lanes(0, h)] = jnp.concatenate([pick_heads(o.astype(BF16)) for o in outs], axis=0)


def forward_kernel(*refs):
    (hid, seg, wqkv_h, bq, bv, wout_h, bout, g1, b1, win_h, bin_, wdown_h, bdown, g2, b2) = refs[:15]
    outs, (unit_o, unitf_o, inv_o) = refs[15:25], refs[25:28]
    wqkv, wout, win, wdown, bias_s, n1_s = refs[28:34]
    kept = refs[34:44]
    sems, osems = refs[44:46]
    qkv_s, p_s, ctx_s, nl_s, xh1_s, rs1_s, act_s, dg_s, xh2_s, rs2_s = kept
    r = pl.program_id(0)
    length = hid.shape[0]
    blocks, _ = windows(length)
    pairs = ((wqkv_h, wqkv), (wout_h, wout), (win_h, win), (wdown_h, wdown))
    copies = [pltpu.make_async_copy(a, b, sems.at[i]) for i, (a, b) in enumerate(pairs)]

    def leaving(i):
        if i == 1:
            return pltpu.make_async_copy(kept[i], outs[i].at[r], osems.at[i])
        rows = pl.ds(pl.multiple_of(r * length, length), length)
        return pltpu.make_async_copy(kept[i], outs[i].at[rows], osems.at[i])

    def settle(*which):
        @pl.when(r > 0)
        def _():
            for i in which:
                leaving(i).wait()

    def send(*which):
        for i in which:
            leaving(i).start()

    @pl.when(r == 0)
    def _():
        for copy in copies:
            copy.start()

    seg_row = seg[pl.ds(r, 1), :].astype(F32)
    seg_col = column_of(seg_row)
    for start, low, high, packed in blocks:
        same = seg_col[low:high] == seg_row[:, start : start + QB]
        bias_s[packed : packed + high - low, :] = jnp.where(same, 0.0, masked_score)

    settle(0, 1, 2, 3, 4, 5)

    @pl.when(r == 0)
    def _():
        copies[0].wait()

    for part in range(3):
        cols = slice(part * D, (part + 1) * D)
        value = nn(hid[...], wqkv[:, cols])
        if part == 0:
            value = value + vector(bq)
        if part == 2:
            value = value + vector(bv)
        qkv_s[:, cols] = value.astype(BF16)
    send(0)
    attend(length, qkv_s, bias_s, p_s, ctx_s)
    send(1, 2)

    @pl.when(r == 0)
    def _():
        copies[1].wait()

    xhat, rstd = normalise(hid[...].astype(F32) + (nn(ctx_s[...], wout[...]) + vector(bout)))
    xh1_s[...] = xhat.astype(BF16)
    rs1_s[...] = jnp.broadcast_to(rstd, rs1_s.shape)
    n1 = xhat * vector(g1) + vector(b1)
    n1_s[...] = n1
    nl_s[...] = n1.astype(BF16)
    send(3, 4, 5)
    settle(6, 7, 8, 9)

    @pl.when(r == 0)
    def _():
        copies[2].wait()

    chunk = 512
    bias_in = vector(bin_)

    def rise(c):
        cols = slice(c * chunk, (c + 1) * chunk)
        return nn(nl_s[...], win[:, cols]) + bias_in[:, cols]

    ahead = rise(0)
    for c in range(FF // chunk):
        pre = ahead
        if c + 1 < FF // chunk:
            ahead = rise(c + 1)
        cols = slice(c * chunk, (c + 1) * chunk)
        half = 0.5 + 0.5 * lax.erf(pre * 0.5**0.5)
        act_s[:, cols] = (pre * half).astype(BF16)
        bell = jnp.exp(pre * pre * -0.5) * 0.3989422804014327
        dg_s[:, cols] = (half + pre * bell).astype(BF16)
    send(6, 7)

    @pl.when(r == 0)
    def _():
        copies[3].wait()

    branch = nn(act_s[...], wdown[...]) + vector(bdown)
    xhat, rstd = normalise(n1_s[...] + branch)
    xh2_s[...] = xhat.astype(BF16)
    rs2_s[...] = jnp.broadcast_to(rstd, rs2_s.shape)
    send(8, 9)
    out = xhat * vector(g2) + vector(b2)
    member = (lax.broadcasted_iota(jnp.int32, (SEG, length), 0).astype(F32) == seg_row).astype(F32)
    counts = jnp.sum(member, axis=1, keepdims=True)
    high, low = split_low(out)
    member = member.astype(BF16)
    pooled = (nn(member, high) + nn(member, low)) / counts
    inv = lax.rsqrt(jnp.mean(pooled * pooled, axis=-1, keepdims=True) + unit_epsilon)
    unit = pooled * inv
    unitf_o[...] = unit
    unit_o[...] = unit.astype(BF16)
    inv_o[...] = jnp.broadcast_to(inv / counts, inv_o.shape)

    @pl.when(r == pl.num_programs(0) - 1)
    def _():
        for i in range(10):
            leaving(i).wait()


def forward(hidden, seg, weights):
    rows, length, _ = hidden.shape
    tokens = rows * length
    _, packed = windows(length)
    wide = [(3 * D, BF16), None, (D, BF16), (D, BF16), (D, BF16), (128, F32)]
    wide += [(FF, BF16), (FF, BF16), (D, BF16), (128, F32)]
    out_shape, kept = [], []
    for item in wide:
        if item is None:
            out_shape.append(pltpu.HBM((rows, PAIRS, packed, 2 * QB), BF16))
            kept.append(VMEM((PAIRS, packed, 2 * QB), BF16))
        else:
            out_shape.append(pltpu.HBM((tokens, item[0]), item[1]))
            kept.append(VMEM((length, item[0]), item[1]))
    hbm = hspec()
    out_specs = [hbm] * 10 + [
        pl.BlockSpec((None, SEG, D), lambda r: (r, 0, 0)),
        pl.BlockSpec((None, SEG, D), lambda r: (r, 0, 0)),
        pl.BlockSpec((None, SEG, 128), lambda r: (r, 0, 0)),
    ]
    out_shape += [
        shape_of((rows, SEG, D), BF16),
        shape_of((rows, SEG, D), F32),
        shape_of((rows, SEG, 128), F32),
    ]
    large = (0, 3, 7, 9)
    in_specs = [pl.BlockSpec((length, D), lambda r: (r, 0)), vspec()]
    in_specs += [hbm if i in large else vspec() for i in range(13)]
    return pl.pallas_call(
        forward_kernel,
        name="forward",
        grid=(rows,),
        in_specs=in_specs,
        out_specs=out_specs,
        out_shape=out_shape,
        scratch_shapes=[VMEM(weights[i].shape, BF16) for i in large]
        + [VMEM((packed, QB), F32), VMEM((length, D), F32)]
        + kept
        + [pltpu.SemaphoreType.DMA((4,)), pltpu.SemaphoreType.DMA((10,))],
        cost_estimate=took(36),
        compiler_params=params(50),
    )(*far(hidden.reshape(tokens, D), seg, *weights))


def loss_kernel(flips, idx, *refs):
    pieces, refs = refs[: len(flips)], refs[len(flips) :]
    targets, seg, g2, unitf_h, inv_h, xh2_h, rs2_h, loss_o, gb_o, vec_o = refs[:10]
    slope_s, rows_s, units, unitf, inv, xh2, rs2, sems = refs[10:]
    fetch = Fetch(sems, ((unitf_h, unitf), (inv_h, inv), (xh2_h, xh2), (rs2_h, rs2)))
    twin, me = idx[0], idx[1]
    count = units.shape[0] // 2
    sentences = unitf.shape[0]
    for piece, own_flips in zip(pieces, flips):
        if own_flips is None:
            units[...] = piece[...]
            continue
        for i, (twin_flip, flip) in enumerate(own_flips):
            at = (twin ^ twin_flip) * count + (me ^ flip) * sentences
            at = pl.multiple_of(at, sentences)
            units[pl.ds(at, sentences), :] = piece[i * sentences : (i + 1) * sentences, :]
    rows, length = seg.shape
    step = min(count, 256)
    factor = cosine_scale / D
    positives = units.at[pl.ds(count, count)]
    own = pl.ds(pl.multiple_of(me * sentences, sentences), sentences)

    def one_block(i, carry):
        lanes = pl.ds(pl.multiple_of(i * step, step), step)
        sims = nt(positives[...], units[lanes, :]) * factor
        top = jnp.max(sims, axis=0, keepdims=True)
        weights = jnp.exp(sims - top)
        total = jnp.sum(weights, axis=0, keepdims=True)
        hit = lax.broadcasted_iota(jnp.int32, sims.shape, 0) == targets[:, lanes]
        picked = jnp.sum(jnp.where(hit, sims, 0.0), axis=0, keepdims=True)
        loss_o[:, lanes] = top + jnp.log(total) - picked
        slope = loss_scale * (weights * (1.0 / total) - hit.astype(F32))
        slope_s[:, lanes] = slope.astype(BF16)
        return carry

    if count == step:
        one_block(0, 0)
    else:
        lax.fori_loop(0, count // step, one_block, 0)

    @pl.when(twin == 0)
    def _():
        def part(i, carry):
            lanes = pl.ds(pl.multiple_of(i * step, step), step)
            rows_s[lanes, :] = tn(slope_s[:, lanes], positives[...])
            return carry

        lax.fori_loop(0, count // step, part, 0)
        rows_s[pl.ds(0, sentences), :] = rows_s[own, :]

    @pl.when(twin == 1)
    def _():
        rows_s[pl.ds(0, sentences), :] = nn(slope_s[own, :], units[pl.ds(0, count), :])

    fetch.wait(0, 1, 2, 3)
    gu = rows_s[pl.ds(0, sentences), :] * factor
    unit = unitf[...]
    gs = inv[:, :1] * (gu - unit * jnp.mean(gu * unit, axis=-1, keepdims=True))
    gy = gs * vector(g2)
    u = gy - jnp.mean(gy, axis=-1, keepdims=True)
    gain = jnp.zeros((1, D), F32)
    shift = jnp.zeros((1, D), F32)
    summed = jnp.zeros((1, D), F32)
    for r in range(rows):
        part = slice(r * SEG, (r + 1) * SEG)
        tok = slice(r * length, (r + 1) * length)
        seg_row = seg[r : r + 1, :]
        hits = lax.broadcasted_iota(jnp.int32, (SEG, length), 0) == seg_row
        member = hits.astype(F32).astype(BF16)
        counts = jnp.sum(hits.astype(F32), axis=1, keepdims=True)
        xhat_low = xh2[tok, :]
        gain += jnp.sum(nn(member, xhat_low) * gs[part], axis=0, keepdims=True)
        shift += jnp.sum(counts * gs[part], axis=0, keepdims=True)
        xhat = xhat_low.astype(F32)
        high, low = split_low(u[part])
        spread = tn(member, high) + tn(member, low)
        inner = jnp.mean(spread * xhat, axis=-1, keepdims=True)
        grad = rs2[tok, :1] * (spread - xhat * inner)
        grad_low = grad.astype(BF16)
        gb_o[tok, :] = grad_low
        summed += jnp.sum(grad_low.astype(F32), axis=0, keepdims=True)
    vec_o[...] = jnp.concatenate([summed, gain, shift, jnp.zeros((5, D), F32)], axis=0)


def loss_stage(idx, gathered, targets, unitf, inv, seg, g2, xh2, rs2, carry):
    pieces, flips = gathered
    tokens = xh2.shape[0]
    count = targets.shape[1]
    return carry_call(
        functools.partial(loss_kernel, flips),
        "loss",
        4,
        22 if count <= 256 else 52,
        (idx, *pieces, *far(targets, seg, g2, unitf, inv, xh2, rs2)),
        [sspec()] + [vspec()] * (3 + len(pieces)) + [hspec()] * 4,
        [shape_of((1, count), F32), shape_of((tokens, D), BF16), shape_of((8, D), F32)],
        [VMEM((count, count), BF16), VMEM((count, D), F32), VMEM((2 * count, D), BF16)]
        + [VMEM(a.shape, a.dtype) for a in (unitf, inv, xh2, rs2)]
        + [pltpu.SemaphoreType.DMA((4,))],
        carry,
    )


def pre_kernel(gb, wdown, dg, out):
    n = 768

    def product(j):
        return nt(gb[...], wdown[j * n : (j + 1) * n, :])

    ahead = product(0)
    for j in range(FF // n):
        value = ahead
        if j + 1 < FF // n:
            ahead = product(j + 1)
        part = slice(j * n, (j + 1) * n)
        out[:, part] = (value * dg[:, part].astype(F32)).astype(BF16)


def pre_stage(gb, wdown, dg, carry):
    outs = [VMEM(dg.shape, BF16)]
    return carry_call(
        pre_kernel, "grad_pre", 7.6, 24, (gb, wdown, dg), [vspec()] * 3, outs, [], carry
    )


def normed_kernel(gp, win, gb, xh1, rs1, g1, wout, ga_o, gc_o, vec_o):
    m = 512
    count = gp.shape[0] // m
    gain, shift, summed = [jnp.zeros((1, D), F32) for _ in range(3)]
    grads = [nt(gp[i * m : (i + 1) * m, :], win[...]) for i in range(count)]
    for i in range(count):
        rows = slice(i * m, (i + 1) * m)
        grad = grads[i] + gb[rows, :].astype(F32)
        xhat = xh1[rows, :].astype(F32)
        gain += jnp.sum(grad * xhat, axis=0, keepdims=True)
        shift += jnp.sum(grad, axis=0, keepdims=True)
        gy = grad * vector(g1)
        inner = jnp.mean(gy * xhat, axis=-1, keepdims=True)
        total = rs1[rows, :1] * (gy - jnp.mean(gy, axis=-1, keepdims=True) - xhat * inner)
        low = total.astype(BF16)
        ga_o[rows, :] = low
        summed += jnp.sum(low.astype(F32), axis=0, keepdims=True)
    for i in range(count):
        rows = slice(i * m, (i + 1) * m)
        gc_o[rows, :] = nt(ga_o[rows, :], wout[...]).astype(BF16)
    vec_o[...] = jnp.concatenate([summed, gain, shift, jnp.zeros((5, D), F32)], axis=0)


def normed_stage(gp, win, gb, xh1, rs1, g1, wout, carry):
    tokens = gp.shape[0]
    outs = [shape_of((tokens, D), BF16), shape_of((tokens, D), BF16), shape_of((8, D), F32)]
    operands = (gp, win, gb, xh1, rs1, *far(g1), wout)
    return carry_call(
        normed_kernel, "grad_normed", 9, 28, operands, [vspec()] * 7, outs, [], carry
    )


def attend_back_kernel(q_ref, k_ref, v_ref, g_ref, p_ref, out_ref):
    length = q_ref.shape[0]
    blocks, _ = windows(length)
    group = q_ref.shape[1] // PW
    scale = HEAD_DIM**-0.5
    loaded, grads = [], []
    for h in range(group):
        lanes = slice(h * PW, (h + 1) * PW)
        q2 = [two_heads(q_ref[b[0] : b[0] + QB, lanes]) for b in blocks]
        g2 = [two_heads(g_ref[b[0] : b[0] + QB, lanes]) for b in blocks]
        loaded.append((q2, g2, k_ref[:, lanes].T))
        v_all = v_ref[:, lanes]
        grads.append([nt(v_all[b[1] : b[2]], g) for b, g in zip(blocks, g2)])
    slopes = []
    for h in range(group):
        own = []
        for gp, (_, low, high, packed) in zip(grads[h], blocks):
            p = p_ref[h, packed : packed + high - low, :].astype(F32)
            weighted = p * gp
            inner = jnp.sum(weighted, axis=0, keepdims=True)
            own.append((weighted - p * inner).astype(BF16))
        slopes.append(own)

    def gather(parts):
        out = []
        for block in range(len(blocks)):
            total = None
            for part, (_, low, high, _) in zip(parts, blocks):
                base = block * QB - low
                if 0 <= base < high - low:
                    piece = part[base : base + QB]
                    total = piece if total is None else total + piece
            out.append(total)
        return jnp.concatenate(out, axis=0)

    for h in range(group):
        lanes = slice(h * PW, (h + 1) * PW)
        q2, g2, k_turned = loaded[h]
        dq = [nn(k_turned[:, b[1] : b[2]], s) for b, s in zip(blocks, slopes[h])]
        dv = [nn(p_ref[h, b[3] : b[3] + b[2] - b[1], :], g) for b, g in zip(blocks, g2)]
        dk = [nn(s, q) for s, q in zip(slopes[h], q2)]
        turned = [pick_heads((part * scale).astype(BF16)) for part in dq]
        out_ref[0, :, lanes] = jnp.concatenate(turned, axis=0)
        out_ref[1, :, lanes] = (gather(dk) * scale).astype(BF16)
        out_ref[2, :, lanes] = gather(dv).astype(BF16)


def attend_back(qkv, grad_context, probs, rows, length, first, pairs):
    _, packed = windows(length)
    group = 2
    steps = pairs // group
    base = first // group
    width = group * PW

    def block(part):
        return pl.BlockSpec((length, width), lambda r, h: (r, part * (D // width) + base + h))

    return pl.pallas_call(
        attend_back_kernel,
        name="attend_back",
        grid=(rows, steps),
        in_specs=[
            block(0),
            block(1),
            block(2),
            block(0),
            pl.BlockSpec((None, group, packed, 2 * QB), lambda r, h: (r, base + h, 0, 0)),
        ],
        out_specs=pl.BlockSpec((3, length, width), lambda r, h: (0, r, h)),
        out_shape=shape_of((3, rows * length, pairs * PW), BF16),
        cost_estimate=took(2.0 * pairs),
        compiler_params=params(20),
    )(*far(qkv, qkv, qkv), grad_context, *far(probs))


def hidden_kernel(da, db, wqkv, ga, out):
    m = 512
    for i in range(ga.shape[0] // m):
        rows = slice(i * m, (i + 1) * m)
        total = ga[rows, :].astype(F32)
        for part in range(3):
            both = jnp.concatenate([da[part, rows, :], db[part, rows, :]], axis=1)
            total = total + nt(both, wqkv[:, part * D : (part + 1) * D])
        out[rows, :] = total.astype(BF16)


def hidden_stage(da, db, wqkv, ga):
    return pl.pallas_call(
        hidden_kernel,
        name="hidden_grad",
        in_specs=[vspec()] * 4,
        out_specs=vspec(),
        out_shape=shape_of(ga.shape, BF16),
        cost_estimate=took(5.7),
        compiler_params=params(22),
    )(da, db, wqkv, ga)


def place_of(half, quarter, owner):
    c, y, z0, z1 = owner & 1, (owner >> 1) & 1, (owner >> 2) & 1, owner >> 3
    order = (quarter, y, z0, z1, c) if half == 0 else (y, z0, z1, quarter, c)
    out = 0
    for bit in order:
        out = 2 * out + bit
    return out


def lanes_of(width):
    most = 128 if width <= 256 else 256
    return [(low, min(most, width - low)) for low in range(0, width, most)]


def half_shapes(width):
    shapes = [shape_of((32, 48, width), BF16)]
    return shapes + [shape_of((32, 48, n), BF16) for _, n in lanes_of(width)]


def store_piece(first, keep, sends, quarter, owner, piece_a, piece_b):
    at_a, at_b = place_of(0, quarter, owner), place_of(1, quarter, owner)
    keep[jnp.where(first, at_a, at_b)] = jnp.where(first, piece_a, piece_b)
    other = jnp.where(first, piece_b, piece_a)
    at = jnp.where(first, at_b, at_a)
    for send, (low, n) in zip(sends, lanes_of(keep.shape[2])):
        send[at] = other[:, low : low + n]


def down_kernel(idx, act, gb, keep, *sends):
    first = idx[2] == 0
    n = 768

    def product(j):
        return tn(act[:, j * n : (j + 1) * n], gb[...])

    ahead = product(0)
    for j in range(FF // n):
        total = ahead.astype(BF16)
        if j + 1 < FF // n:
            ahead = product(j + 1)
        for local in range(4):
            for quarter in range(2):
                base = local * 192 + quarter * 48
                a, b = total[base : base + 48], total[base + 96 : base + 144]
                store_piece(first, keep, sends, quarter, 4 * j + local, a, b)


def down_stage(idx, act, gb, carry):
    operands, specs = (idx, act, gb), [sspec(), vspec(), vspec()]
    return carry_call(
        down_kernel, "grad_w_down", 7.5, 22, operands, specs, half_shapes(D), [], carry
    )


def in_kernel(idx, n1, gp, vec_o, keep, *refs):
    sends, turned = refs[:-1], refs[-1]
    first = idx[2] == 0
    turned[...] = n1[...].T

    def products(quarter):
        out = []
        for half in range(2):
            j = 2 * half + quarter
            out.append(nn(turned[...], gp[:, j * D : (j + 1) * D]))
        return out

    ahead = products(0)
    for quarter in range(2):
        a, b = [part.astype(BF16) for part in ahead]
        if quarter == 0:
            ahead = products(1)
        for owner in range(16):
            rows = slice(owner * 48, (owner + 1) * 48)
            store_piece(first, keep, sends, quarter, owner, a[rows], b[rows])
    vec_o[...] = jnp.sum(gp[...].astype(F32), axis=0, keepdims=True)


def in_stage(idx, n1, gp):
    shapes = half_shapes(D)
    return pl.pallas_call(
        in_kernel,
        name="grad_w_in",
        in_specs=[sspec(), vspec(), vspec()],
        out_specs=[vspec()] * (1 + len(shapes)),
        out_shape=[shape_of((1, FF), F32)] + shapes,
        scratch_shapes=[VMEM((D, n1.shape[0]), BF16)],
        cost_estimate=took(7.4),
        compiler_params=params(24),
    )(idx, n1, gp)


WIDE, NARROW = 640, 256


def store_all(first, keep, send, whole, width):
    for quarter in range(2):
        a = whole[:, quarter * width : (quarter + 1) * width]
        b = whole[:, (2 + quarter) * width : (3 + quarter) * width]
        for owner in range(16):
            rows = slice(owner * 48, (owner + 1) * 48)
            store_piece(first, keep, send, quarter, owner, a[rows], b[rows])


def wide_kernel(idx, hid, da, ctx, ga, turned_o, keep, *refs):
    sends, whole = refs[:-1], refs[-1]
    n = da.shape[2]
    turned_o[...] = hid[...].T
    for part in range(3):
        whole[:, part * n : (part + 1) * n] = nn(turned_o[...], da[part]).astype(BF16)
    whole[:, 3 * n : 3 * n + D] = tn(ctx[...], ga[...]).astype(BF16)
    whole[:, 3 * n + D :] = jnp.zeros((D, 4 * WIDE - 3 * n - D), BF16)
    store_all(idx[2] == 0, keep, sends, whole, WIDE)


def wide_stage(idx, hid, da, ctx, ga):
    shapes = half_shapes(WIDE)
    return pl.pallas_call(
        wide_kernel,
        name="grad_w_wide",
        in_specs=[sspec()] + [vspec()] * 4,
        out_specs=[vspec()] * (1 + len(shapes)),
        out_shape=[shape_of((D, hid.shape[0]), BF16)] + shapes,
        scratch_shapes=[VMEM((D, 4 * WIDE), BF16)],
        cost_estimate=took(6),
        compiler_params=params(24),
    )(idx, hid, da, ctx, ga)


def narrow_kernel(idx, turned, da, db, vecs, keep, *refs):
    send, (whole, sums_s) = refs[:-2], refs[-2:]
    n = db.shape[2]
    for part in range(3):
        whole[:, part * n : (part + 1) * n] = nn(turned[...], db[part]).astype(BF16)
    sums_s[...] = jnp.zeros_like(sums_s)
    sums_s[:16, :] = vecs[...]
    for row, part in ((0, 0), (1, 2)):
        for base, grads in ((0, da), (D - n, db)):
            lanes = slice(base, base + grads.shape[2])
            total = jnp.sum(grads[part].astype(F32), axis=0, keepdims=True)
            sums_s[row : row + 1, lanes] = total
    whole[:, 3 * n : 3 * n + 128] = sums_s[...].T.astype(BF16)
    whole[:, 3 * n + 128 :] = jnp.zeros((D, 4 * NARROW - 3 * n - 128), BF16)
    store_all(idx[2] == 0, keep, send, whole, NARROW)


def narrow_stage(idx, turned, da, db, vecs):
    return pl.pallas_call(
        narrow_kernel,
        name="grad_w_narrow",
        in_specs=[sspec()] + [vspec()] * 4,
        out_specs=[vspec()] * len(half_shapes(NARROW)),
        out_shape=half_shapes(NARROW),
        scratch_shapes=[VMEM((D, 4 * NARROW), BF16), VMEM((128, D), F32)],
        cost_estimate=took(2.4),
        compiler_params=params(22),
    )(idx, turned, da, db, vecs)


def swap_dp(value, flip):
    devices = lax.axis_size("dp")
    return lax.ppermute(value, "dp", [(i, i ^ flip) for i in range(devices)])


def swap_twin(value):
    return lax.ppermute(value, "twin", [(0, 1), (1, 0)])


TWIN = 16
ROUTES = ((TWIN, 2, 4, 8, TWIN), (2, 4, 8, TWIN, TWIN))


def step_swap(value, step):
    pairs = [(i, i ^ ROUTES[i & 1][step]) for i in range(2 * TWIN)]
    return lax.ppermute(value, ("twin", "dp"), pairs)


def plus(*values):
    total = values[0].astype(F32)
    for value in values[1:]:
        total = total + value.astype(F32)
    return total.astype(BF16)


def call_small(kernel, name, idx, operands, outs):
    return pl.pallas_call(
        kernel,
        name=name,
        in_specs=[sspec()] + [vspec()] * len(operands),
        out_specs=[vspec()] * len(outs),
        out_shape=[shape_of(shape, dtype) for shape, dtype in outs],
        cost_estimate=took(2.4),
        compiler_params=params(12),
    )(idx, *operands)


def half_kernel(step, idx, keep, recv, keep_o, send_o):
    count = keep_o.shape[0]
    bit = idx[3 + step]
    mine = pl.ds(bit * count, count)
    other = pl.ds((1 - bit) * count, count)
    keep_o[...] = plus(keep[mine], recv[mine])
    send_o[...] = plus(keep[other], recv[other])


def half_step(idx, step, keep, recv):
    count, rows, width = keep.shape
    shape = (count // 2, rows, width)
    kernel = functools.partial(half_kernel, step)
    return call_small(kernel, "sum_" + str(step), idx, (keep, recv), [(shape, BF16)] * 2)


def core_kernel(idx, keep, *refs):
    recvs, (keep_o, send_o) = refs[:-2], refs[-2:]
    bit = idx[3]
    for recv, (low, n) in zip(recvs, lanes_of(keep.shape[3])):
        lanes = slice(low, low + n)
        keep_o[:, :, lanes] = plus(keep[bit, :, :, lanes], recv[bit])
        send_o[:, :, lanes] = plus(keep[1 - bit, :, :, lanes], recv[1 - bit])


def core_step(idx, keep, recvs):
    count, rows, width = keep.shape
    half = count // 2
    pieces = 4
    part = half // pieces

    def spec(n):
        return pl.BlockSpec((2, part, rows, n), lambda i: (0, i, 0, 0))

    return pl.pallas_call(
        core_kernel,
        name="sum_core",
        grid=(pieces,),
        in_specs=[sspec(), spec(width)] + [spec(n) for _, n in lanes_of(width)],
        out_specs=[pl.BlockSpec((part, rows, width), lambda i: (i, 0, 0))] * 2,
        out_shape=[shape_of((half, rows, width), BF16)] * 2,
        cost_estimate=took(1.7),
        compiler_params=params(10),
    )(
        idx,
        keep.reshape(2, half, rows, width),
        *[recv.reshape(2, half, rows, recv.shape[2]) for recv in recvs],
    )


def own_kernel(idx, keep, recv, out):
    out[...] = plus(keep[...], recv[...])


def turn_kernel(idx, own, other, keep_o, send_o):
    twin, core = idx[0], idx[2]
    keep_o[twin] = own[core]
    keep_o[1 - twin] = other[core]
    send_o[twin] = own[1 - core]
    send_o[1 - twin] = other[1 - core]


class Order:
    def __init__(self):
        self.last = None

    def after(self, value, *others):
        if self.last is None:
            return value
        return lax.optimization_barrier((value, self.last) + others)[0]

    def done(self, value):
        self.last = value
        return value


class Exchange:
    def __init__(self, order, idx, keep, sends):
        self.order, self.idx, self.step = order, idx, 0
        self.keep, self.recv = keep, [swap_dp(send, 1) for send in sends]

    def advance(self):
        idx, order = self.idx, self.order
        keep, recv = order.after(self.keep), self.recv
        if self.step == 0:
            keep, send = core_step(idx, keep, recv)
            recv = step_swap(send, 0)
        elif self.step < 4:
            keep, send = half_step(idx, self.step, keep, recv)
            recv = step_swap(send, self.step)
        elif self.step == 4:
            shape = keep.shape
            (keep,) = call_small(own_kernel, "sum_4", idx, (keep, recv), [(shape, BF16)])
            recv = step_swap(keep, 4)
        else:
            shape = keep.shape
            keep, send = call_small(turn_kernel, "turn", idx, (keep, recv), [(shape, BF16)] * 2)
            recv = swap_dp(send, 1)
        order.done(keep)
        self.keep, self.recv = keep, recv
        self.step += 1

    def result(self):
        return self.keep, self.recv


def gather_units(unit):
    flips = [(0, 0)]
    for flip in (8, 4):
        unit = jnp.concatenate([unit, swap_dp(unit, flip)], axis=0)
        flips = flips + [(t, f ^ flip) for t, f in flips]
    pairs = [(i, i ^ (TWIN + 2)) for i in range(2 * TWIN)]
    far = lax.ppermute(unit, ("twin", "dp"), pairs)
    unit = jnp.concatenate([unit, swap_dp(unit, 2), swap_twin(unit), far], axis=0)
    flips = [(t ^ a, f ^ b) for a, b in ((0, 0), (0, 2), (1, 0), (1, 2)) for t, f in flips]
    return (unit, swap_dp(unit, 1)), (flips, [(t, f ^ 1) for t, f in flips])


def four_quarters(idx, keep, recv):
    first = idx[2] == 0
    low = [jnp.where(first, keep[i], recv[i]) for i in range(2)]
    high = [jnp.where(first, recv[i], keep[i]) for i in range(2)]
    return low + high


def final_in_kernel(idx, keep, recv, out):
    for i, part in enumerate(four_quarters(idx, keep, recv)):
        out[:, i * D : (i + 1) * D] = part.astype(F32)


def final_down_kernel(idx, keep, recv, out):
    for i, part in enumerate(four_quarters(idx, keep, recv)):
        out[i * 48 : (i + 1) * 48, :] = part.astype(F32)


def final_last_kernel(idx, wide_k, wide_r, narrow_k, narrow_r, qkv_o, out_o, vec_o):
    wide = jnp.concatenate(four_quarters(idx, wide_k, wide_r), axis=1).astype(F32)
    narrow = jnp.concatenate(four_quarters(idx, narrow_k, narrow_r), axis=1).astype(F32)
    low, high = 2 * D // 3, D // 3
    for part in range(3):
        qkv_o[:, part * D : part * D + low] = wide[:, part * low : (part + 1) * low]
        qkv_o[:, part * D + low : (part + 1) * D] = narrow[:, part * high : (part + 1) * high]
    out_o[...] = wide[:, 3 * low : 3 * low + D]
    small = narrow[:, 3 * high : 3 * high + 128]
    vec_o[...] = jnp.concatenate([small, jnp.zeros((80, 128), F32)], axis=0).T[:16]


def finish(order, idx, kernel, name, chunks, outs):
    operands = [value for chunk in chunks for value in chunk.result()]
    operands[0] = order.after(operands[0])
    out = call_small(kernel, name, idx, operands, outs)
    order.done(out[0])
    return out


def add_low(*parts):
    return lax.optimization_barrier(plus(*parts))


def digits_of(devices):
    out, rest = [], devices // 2
    while rest > 1:
        size = 4 if rest % 4 == 0 else 2
        out.append(size)
        rest //= size
    return out


def pick(value, index, axis):
    return lax.dynamic_index_in_dim(value, index, axis, keepdims=False)


def scatter(grad):
    devices = lax.axis_size("dp")
    me = lax.axis_index("dp")
    value = grad.reshape(devices, grad.shape[0] // devices, grad.shape[1])
    unit = 1
    for size in [2] + digits_of(devices):
        mine = (me // unit) % size
        view = value.reshape((value.shape[0] // size, size) + value.shape[1:])
        parts = [pick(view, mine, 1)]
        for flip in range(1, size):
            parts.append(swap_dp(pick(view, mine ^ flip, 1), flip * unit))
        value = add_low(*parts)
        unit *= size
    value = value[0]
    return value.astype(F32) + swap_twin(value).astype(F32)


SEQUENCE = (
    "down", "pre", "d", "in", "normed", "i", "d", "attend_a", "d", "wide", "i", "attend_b", "w",
    "d", "narrow", "i", "hidden", "n", "d", "w", "i", "n", "d", "w", "i", "n", "final_d", "i",
    "w", "n", "final_i", "w", "n", "w", "n",
)


def body(
    hidden,
    segment_ids,
    targets,
    w_qkv,
    b_query,
    b_value,
    w_out,
    b_out,
    ln1_gain,
    ln1_bias,
    w_in,
    b_in,
    w_down,
    b_down,
    ln2_gain,
    ln2_bias,
):
    row_count, length, width = hidden.shape
    tokens = row_count * length
    devices = lax.axis_size("dp")
    everyone = lax.axis_size(("twin", "dp"))
    me = lax.axis_index("dp")
    twin = lax.axis_index("twin")
    core, y, z0, z1 = me & 1, (me >> 1) & 1, (me >> 2) & 1, me >> 3
    first = core == 0
    bits = [jnp.where(first, a, b) for a, b in ((twin, y), (y, z0), (z0, z1), (z1, twin))]
    idx = jnp.stack([twin, me, core] + bits).astype(jnp.int32)
    weights = (w_qkv, b_query, b_value, w_out, b_out, ln1_gain, ln1_bias)
    weights += (w_in, b_in, w_down, b_down, ln2_gain, ln2_bias)
    qkv, probs, ctx, n1, xh1, rs1, act, dg, xh2, rs2, unit, unitf, inv = forward(
        hidden, segment_ids, weights
    )
    sentences = row_count * SEG
    unit = unit.reshape(sentences, width)
    direct = devices == TWIN and sentences == 16
    if direct:
        gathered = gather_units(unit)
    else:
        gathered = ((lax.all_gather(unit, ("twin", "dp"), axis=0, tiled=True),), (None,))
    losses, gb, vec2, act_near = loss_stage(
        idx,
        gathered,
        targets.reshape(1, -1),
        unitf.reshape(sentences, width),
        inv.reshape(sentences, 128),
        segment_ids,
        ln2_gain,
        xh2,
        rs2,
        (act,),
    )
    share = losses.shape[1] // everyone
    losses = lax.dynamic_slice_in_dim(
        losses[0], lax.axis_index(("twin", "dp")) * share, share, 0
    )
    flat = hidden.reshape(tokens, width)
    if direct:
        order = Order()
        chunks = {}

        def begin(name, keep, sends):
            order.done(keep)
            chunks[name] = Exchange(order, idx, keep, sends)

        for stage in SEQUENCE:
            if stage == "down":
                *halves_d, dg_near = down_stage(idx, act_near, order.after(gb), (dg,))
                begin("d", halves_d[0], halves_d[1:])
            elif stage == "pre":
                near = (n1, xh1, rs1)
                gp, *near = pre_stage(order.after(gb), w_down, dg_near, near)
                order.done(gp)
            elif stage == "in":
                sums, *halves_in = in_stage(idx, near[0], order.after(gp))
                begin("i", halves_in[0], halves_in[1:])
            elif stage == "normed":
                ga, gc, vec1, *later = normed_stage(
                    order.after(gp), w_in, gb, near[1], near[2], ln1_gain, w_out, (flat, ctx)
                )
                order.done(ga)
            elif stage == "attend_a":
                da = order.done(attend_back(qkv, order.after(gc), probs, row_count, length, 0, 4))
            elif stage == "attend_b":
                db = order.done(attend_back(qkv, order.after(gc), probs, row_count, length, 4, 2))
            elif stage == "wide":
                turned, *halves_w = wide_stage(idx, later[0], order.after(da), later[1], ga)
                begin("w", halves_w[0], halves_w[1:])
            elif stage == "narrow":
                rest = sums.reshape(devices, 4, 48).transpose(1, 0, 2).reshape(4, width)
                nothing = jnp.zeros((2, width), F32)
                vecs = jnp.concatenate([nothing, vec1[:3], vec2[:3], rest, nothing, nothing])
                halves_n = narrow_stage(idx, turned, da, order.after(db), vecs)
                begin("n", halves_n[0], halves_n[1:])
            elif stage == "hidden":
                hidden_grad = order.done(hidden_stage(da, order.after(db), w_qkv, ga))
            elif stage == "final_d":
                outs = [((192, D), F32)]
                (grad_w_down,) = finish(order, idx, final_down_kernel, stage, [chunks["d"]], outs)
            elif stage == "final_i":
                outs = [((48, FF), F32)]
                (grad_w_in,) = finish(order, idx, final_in_kernel, stage, [chunks["i"]], outs)
            else:
                chunks[stage].advance()
        wide, narrow = chunks["w"], chunks["n"]
        shapes = [((48, 3 * D), F32), ((48, D), F32), ((16, 128), F32)]
        grad_w_qkv, grad_w_out, vec = finish(
            order, idx, final_last_kernel, "final_last", [wide, narrow], shapes
        )
        vec = vec[:, :48]
        vecs = [vec[i] for i in range(8)]
        grad_b_in = vec[8:12].reshape(-1)
    else:
        gp, dg_near = pre_stage(gb, w_down, dg, (dg,))
        ga, gc, vec1, _ = normed_stage(gp, w_in, gb, xh1, rs1, ln1_gain, w_out, (ctx,))
        da = attend_back(qkv, gc, probs, row_count, length, 0, 4)
        db = attend_back(qkv, gc, probs, row_count, length, 4, 2)
        hidden_grad = hidden_stage(da, db, w_qkv, ga)
        dqkv = jnp.concatenate([da, db], axis=2)
        grad_w_down = scatter(tn(act, gb).astype(BF16))
        grad_w_in = scatter(tn(n1, gp).astype(BF16))
        wide = jnp.concatenate([dqkv[0], dqkv[1], dqkv[2]], axis=1)
        grad_w_qkv = scatter(tn(flat, wide).astype(BF16))
        grad_w_out = scatter(tn(ctx, ga).astype(BF16))
        sums = jnp.sum(dqkv, axis=1, dtype=F32)
        vec = jnp.concatenate([sums[0:1], sums[2:3], vec1[:3], vec2[:3]])
        vec = scatter(jnp.pad(vec, ((0, 120), (0, 0))).T.astype(BF16)).T
        vecs = [vec[i] for i in range(8)]
        bias = jnp.sum(gp, axis=0, dtype=F32)
        grad_b_in = scatter(jnp.broadcast_to(bias[:, None], (FF, 128)).astype(BF16))[:, 0]
    return (
        losses,
        hidden_grad.reshape(row_count, length, width),
        grad_w_qkv,
        vecs[0],
        vecs[1],
        grad_w_out,
        vecs[2],
        vecs[3],
        vecs[4],
        grad_w_in,
        grad_b_in,
        grad_w_down,
        vecs[5],
        vecs[6],
        vecs[7],
    )


def solution(mesh):
    whole = (P(),) * 14
    placed = (P(("twin", "dp"), None, None), P(("twin", "dp"), None)) + whole
    return jax.shard_map(
        body,
        mesh=mesh,
        in_specs=placed,
        out_specs=(
            P(("twin", "dp")),
            P(("twin", "dp"), None, None),
            P("dp", None),
            P("dp"),
            P("dp"),
            P("dp", None),
            P("dp"),
            P("dp"),
            P("dp"),
            P("dp", None),
            P("dp"),
            P("dp", None),
            P("dp"),
            P("dp"),
            P("dp"),
        ),
        check_vma=False,
    )
```

```python
import functools

import jax
import jax.numpy as jnp
from jax import lax
from jax.experimental import pallas as pl
from jax.experimental.pallas import tpu as pltpu
from jax.sharding import PartitionSpec as P

D = 768
HEADS = 12
HEAD_DIM = 64
FF = 3072
SEG = 8
QB = 128
MOST = 128
PAIRS = HEADS // 2
PW = 2 * HEAD_DIM

cosine_scale = 64.0
loss_scale = 32.0
norm_epsilon = 1e-12
unit_epsilon = 1e-06
masked_score = -1e30

F32 = jnp.float32
BF16 = jnp.bfloat16
VMEM = pltpu.VMEM
ANY = pl.ANY
MIB = 1 << 20


def nn(left, right):
    return lax.dot_general(left, right, (((1,), (0,)), ((), ())), preferred_element_type=F32)


def nt(left, right):
    return lax.dot_general(left, right, (((1,), (1,)), ((), ())), preferred_element_type=F32)


def tn(left, right):
    return lax.dot_general(left, right, (((0,), (0,)), ((), ())), preferred_element_type=F32)


def vspec():
    return pl.BlockSpec(memory_space=VMEM)


def sspec():
    return pl.BlockSpec(memory_space=pltpu.SMEM)


def hspec():
    return pl.BlockSpec(memory_space=pltpu.HBM)


def far(*values):
    return [pltpu.with_memory_space_constraint(value, pltpu.HBM) for value in values]


class Fetch:
    def __init__(self, sems, pairs):
        self.copies = [pltpu.make_async_copy(a, b, sems.at[i]) for i, (a, b) in enumerate(pairs)]
        for copy in self.copies:
            copy.start()

    def wait(self, *which):
        for i in which:
            self.copies[i].wait()


def carrying(kernel, n_in, n_out, n_carry):
    def wrapped(*refs):
        refs, sems = refs[:-1], refs[-1]
        ins, refs = refs[:n_in], refs[n_in:]
        sources, refs = refs[:n_carry], refs[n_carry:]
        outs, refs = refs[:n_out], refs[n_out:]
        targets, rest = refs[:n_carry], refs[n_carry:]
        fetch = Fetch(sems, tuple(zip(sources, targets)))
        kernel(*ins, *outs, *rest)
        fetch.wait(*range(n_carry))

    return wrapped


def carry_call(kernel, name, us, mib, operands, specs, outs, scratch, carry):
    n_carry = len(carry)
    return pl.pallas_call(
        carrying(kernel, len(operands), len(outs), n_carry),
        name=name,
        in_specs=list(specs) + [hspec()] * n_carry,
        out_specs=[vspec()] * (len(outs) + n_carry),
        out_shape=list(outs) + [VMEM(a.shape, a.dtype) for a in carry],
        scratch_shapes=list(scratch) + [pltpu.SemaphoreType.DMA((max(n_carry, 1),))],
        cost_estimate=took(us),
        compiler_params=params(mib),
    )(*operands, *far(*carry))


def fixed(shape):
    return pl.BlockSpec(shape, lambda *_: (0,) * len(shape))


def shape_of(shape, dtype):
    return jax.ShapeDtypeStruct(shape, dtype)


def params(mib):
    return pltpu.CompilerParams(vmem_limit_bytes=mib * MIB)


SCALE = 0.4


def took(us):
    return pl.CostEstimate(flops=int(us * SCALE * 1.15e9), bytes_accessed=0, transcendentals=0)


def windows(length):
    out, packed = [], 0
    for start in range(0, length, QB):
        low, high = max(0, start - MOST), min(length, start + QB + MOST)
        out.append((start, low, high, packed))
        packed += high - low
    return out, packed


def two_heads(pair):
    first = lax.broadcasted_iota(jnp.int32, pair.shape, 1) < HEAD_DIM
    zero = jnp.zeros((), pair.dtype)
    return jnp.concatenate([jnp.where(first, pair, zero), jnp.where(first, zero, pair)], axis=0)


def pick_heads(both):
    rows = both.shape[1] // 2
    return jnp.concatenate([both[:HEAD_DIM, :rows], both[HEAD_DIM:, rows:]], axis=0).T


def column_of(row):
    return jnp.broadcast_to(row, (8, row.shape[1])).T[:, :1]


def split_low(value):
    high = value.astype(BF16)
    return high, (value - high.astype(F32)).astype(BF16)


def normalise(value):
    middle = jnp.mean(value, axis=-1, keepdims=True)
    centered = value - middle
    spread = jnp.mean(centered * centered, axis=-1, keepdims=True)
    rstd = lax.rsqrt(spread + norm_epsilon)
    return centered * rstd, rstd


def vector(ref):
    return ref[...].astype(F32).reshape(1, ref.shape[0])


def softmax_down(own):
    top = jnp.max(own, axis=0, keepdims=True)
    weights = jnp.exp(own - top)
    total = jnp.sum(weights, axis=0, keepdims=True)
    return (weights * (1.0 / total)).astype(BF16)


def attend(length, qkv, bias, p_s, ctx_s):
    blocks, _ = windows(length)

    def lanes(part, h):
        return slice(part * D + h * PW, part * D + (h + 1) * PW)

    def score(h):
        q_all = qkv[:, lanes(0, h)] * jnp.asarray(HEAD_DIM**-0.5, BF16)
        k_all = qkv[:, lanes(1, h)]
        out = []
        for start, low, high, _ in blocks:
            out.append(nt(k_all[low:high], two_heads(q_all[start : start + QB])))
        return out, qkv[:, lanes(2, h)].T

    ahead = score(0)
    for h in range(PAIRS):
        scores, v_turned = ahead
        if h + 1 < PAIRS:
            ahead = score(h + 1)
        probs = []
        for own, (_, low, high, packed) in zip(scores, blocks):
            mask = bias[packed : packed + high - low, :]
            halves = [softmax_down(own[:, :QB] + mask), softmax_down(own[:, QB:] + mask)]
            probs.append(jnp.concatenate(halves, axis=1))
        for p, (_, low, high, packed) in zip(probs, blocks):
            p_s[h, packed : packed + high - low, :] = p
        outs = [nn(v_turned[:, low:high], p) for p, (_, low, high, _) in zip(probs, blocks)]
        ctx_s[:, lanes(0, h)] = jnp.concatenate([pick_heads(o.astype(BF16)) for o in outs], axis=0)


def forward_kernel(*refs):
    (hid_h, seg, wqkv_h, bq, bv, wout_h, bout, g1, b1, win_h, bin_, wdown_h, bdown, g2, b2) = refs[:15]
    outs, (act_o, dg_o, xh2_o, rs2_o, unit_o, unitf_o, inv_o) = refs[15:21], refs[21:28]
    hid, wqkv, wout, win, wdown, bias_s, n1_s = refs[28:35]
    kept = refs[35:41]
    sems, osems = refs[41:43]
    qkv_s, p_s, ctx_s, nl_s, xh1_s, rs1_s = kept
    rows = seg.shape[0]
    length = hid.shape[0] // rows
    blocks, _ = windows(length)
    toks = [slice(r * length, (r + 1) * length) for r in range(rows)]
    parts = [slice(part * D, (part + 1) * D) for part in range(3)]

    pairs = [(hid_h.at[toks[0]], hid.at[toks[0]])]
    pairs += [(wqkv_h.at[:, cols], wqkv.at[:, cols]) for cols in parts]
    first = Fetch(sems, pairs)
    later = []

    def fetch_rest():
        rest = [(wout_h, wout), (win_h, win), (wdown_h, wdown)]
        rest += [(hid_h.at[tok], hid.at[tok]) for tok in toks[1:]]
        for i, (source, target) in enumerate(rest):
            copy = pltpu.make_async_copy(source, target, sems.at[4 + i])
            copy.start()
            later.append(copy)

    def leaving(i, r):
        if i == 1:
            return pltpu.make_async_copy(p_s, outs[1].at[r], osems.at[r, 1])
        source = kept[i] if i in (0, 2) else kept[i].at[toks[r]]
        return pltpu.make_async_copy(source, outs[i].at[toks[r]], osems.at[r, i])

    seg_rows = [seg[r : r + 1, :].astype(F32) for r in range(rows)]

    def mask(r):
        seg_col = column_of(seg_rows[r])
        for start, low, high, packed in blocks:
            same = seg_col[low:high] == seg_rows[r][:, start : start + QB]
            bias_s[packed : packed + high - low, :] = jnp.where(same, 0.0, masked_score)

    def project(r):
        if r > 0:
            leaving(0, r - 1).wait()
            later[2 + r].wait()
        for part, cols in enumerate(parts):
            if r == 0:
                first.wait(*((0, 1) if part == 0 else (part + 1,)))
                if part == 0:
                    fetch_rest()
            value = nn(hid[toks[r], :], wqkv[:, cols])
            if part == 0:
                value = value + vector(bq)
            if part == 2:
                value = value + vector(bv)
            qkv_s[:, cols] = value.astype(BF16)
        leaving(0, r).start()

    def attention(r):
        if r > 0:
            leaving(1, r - 1).wait()
            leaving(2, r - 1).wait()
        attend(length, qkv_s, bias_s, p_s, ctx_s)
        leaving(1, r).start()
        leaving(2, r).start()

    def mix(r):
        if r == 0:
            later[0].wait()
        return nn(ctx_s[...], wout[...])

    def norm_one(r, attended):
        tok = toks[r]
        xhat, rstd = normalise(hid[tok, :].astype(F32) + (attended + vector(bout)))
        xh1_s[tok, :] = xhat.astype(BF16)
        rs1_s[tok, :] = jnp.broadcast_to(rstd, (length, rs1_s.shape[1]))
        n1 = xhat * vector(g1) + vector(b1)
        n1_s[tok, :] = n1
        nl_s[tok, :] = n1.astype(BF16)
        for i in (3, 4, 5):
            leaving(i, r).start()

    chunk = 768
    count = FF // chunk
    bias_in = vector(bin_)

    def rise(r, c):
        cols = slice(c * chunk, (c + 1) * chunk)
        return nn(nl_s[toks[r], :], win[:, cols]) + bias_in[:, cols]

    def bend(r, c, pre):
        cols = slice(c * chunk, (c + 1) * chunk)
        half = 0.5 + 0.5 * lax.erf(pre * 0.5**0.5)
        act_o[toks[r], cols] = (pre * half).astype(BF16)
        bell = jnp.exp(pre * pre * -0.5) * 0.3989422804014327
        dg_o[toks[r], cols] = (half + pre * bell).astype(BF16)

    def norm_two(r, fallen):
        tok = toks[r]
        xhat, rstd = normalise(n1_s[tok, :] + (fallen + vector(bdown)))
        xh2_o[tok, :] = xhat.astype(BF16)
        rs2_o[tok, :] = jnp.broadcast_to(rstd, (length, rs2_o.shape[1]))
        out = xhat * vector(g2) + vector(b2)
        index = lax.broadcasted_iota(jnp.int32, (SEG, length), 0).astype(F32)
        member = (index == seg_rows[r]).astype(F32)
        counts = jnp.sum(member, axis=1, keepdims=True)
        high, low = split_low(out)
        member = member.astype(BF16)
        pooled = (nn(member, high) + nn(member, low)) / counts
        inv = lax.rsqrt(jnp.mean(pooled * pooled, axis=-1, keepdims=True) + unit_epsilon)
        unit = pooled * inv
        unitf_o[r] = unit
        unit_o[r] = unit.astype(BF16)
        inv_o[r] = jnp.broadcast_to(inv / counts, inv_o.shape[1:])

    mixed = None
    for r in range(rows):
        mask(r)
        project(r)
        if r > 0:
            norm_one(r - 1, mixed)
        attention(r)
        mixed = mix(r)
    steps = [(r, c) for r in range(rows) for c in range(count)]
    later[1].wait()
    if rows > 1:
        ahead = rise(0, 0)
        norm_one(rows - 1, mixed)
    else:
        norm_one(0, mixed)
        ahead = rise(0, 0)
    fallen = None
    for i, (r, c) in enumerate(steps):
        pre = ahead
        if i + 1 < len(steps):
            ahead = rise(*steps[i + 1])
        bend(r, c, pre)
        if c == 1 and fallen is not None:
            norm_two(r - 1, fallen)
        if c == count - 1:
            if r == 0:
                later[2].wait()
            fallen = nn(act_o[toks[r], :], wdown[...])
    norm_two(rows - 1, fallen)
    for r in range(rows):
        for i in range(6):
            if r == rows - 1 or i > 2:
                leaving(i, r).wait()


def forward(hidden, seg, weights):
    rows, length, _ = hidden.shape
    tokens = rows * length
    _, packed = windows(length)
    packed_shape = (PAIRS, packed, 2 * QB)
    far_shapes = [((tokens, 3 * D), BF16), ((rows,) + packed_shape, BF16)]
    far_shapes += [((tokens, D), BF16)] * 3 + [((tokens, 128), F32)]
    near_shapes = [((tokens, FF), BF16)] * 2 + [((tokens, D), BF16), ((tokens, 128), F32)]
    near_shapes += [((rows, SEG, D), BF16), ((rows, SEG, D), F32), ((rows, SEG, 128), F32)]
    kept = [VMEM((length, 3 * D), BF16), VMEM(packed_shape, BF16), VMEM((length, D), BF16)]
    kept += [VMEM((tokens, D), BF16), VMEM((tokens, D), BF16), VMEM((tokens, 128), F32)]
    large = (0, 3, 7, 9)
    hbm = hspec()
    return pl.pallas_call(
        forward_kernel,
        name="forward",
        in_specs=[hbm, vspec()] + [hbm if i in large else vspec() for i in range(13)],
        out_specs=[hbm] * 6 + [vspec()] * 7,
        out_shape=[pltpu.HBM(*a) for a in far_shapes] + [VMEM(*a) for a in near_shapes],
        scratch_shapes=[VMEM((tokens, D), BF16)]
        + [VMEM(weights[i].shape, BF16) for i in large]
        + [VMEM((packed, QB), F32), VMEM((tokens, D), F32)]
        + kept
        + [pltpu.SemaphoreType.DMA((7 + rows,)), pltpu.SemaphoreType.DMA((rows, 6))],
        cost_estimate=took(36),
        compiler_params=params(44),
    )(*far(hidden.reshape(tokens, D), seg, *weights))


def loss_kernel(flips, idx, *refs):
    pieces, refs = refs[: len(flips)], refs[len(flips) :]
    targets, seg, g2, unitf, inv, xh2, rs2, loss_o, gb_o, vec_o, slope_s, rows_s, units = refs
    twin, me = idx[0], idx[1]
    count = units.shape[0] // 2
    sentences = unitf.shape[0]
    for piece, own_flips in zip(pieces, flips):
        if own_flips is None:
            units[...] = piece[...]
            continue
        for i, (twin_flip, flip) in enumerate(own_flips):
            at = (twin ^ twin_flip) * count + (me ^ flip) * sentences
            at = pl.multiple_of(at, sentences)
            units[pl.ds(at, sentences), :] = piece[i * sentences : (i + 1) * sentences, :]
    rows, length = seg.shape
    step = min(count, 256)
    factor = cosine_scale / D
    positives = units.at[pl.ds(count, count)]
    own = pl.ds(pl.multiple_of(me * sentences, sentences), sentences)

    def one_block(i, carry):
        lanes = pl.ds(pl.multiple_of(i * step, step), step)
        sims = nt(positives[...], units[lanes, :]) * factor
        top = jnp.max(sims, axis=0, keepdims=True)
        weights = jnp.exp(sims - top)
        total = jnp.sum(weights, axis=0, keepdims=True)
        hit = lax.broadcasted_iota(jnp.int32, sims.shape, 0) == targets[:, lanes]
        picked = jnp.sum(jnp.where(hit, sims, 0.0), axis=0, keepdims=True)
        loss_o[:, lanes] = top + jnp.log(total) - picked
        slope = loss_scale * (weights * (1.0 / total) - hit.astype(F32))
        slope_s[:, lanes] = slope.astype(BF16)
        return carry

    if count == step:
        one_block(0, 0)
    else:
        lax.fori_loop(0, count // step, one_block, 0)

    @pl.when(twin == 0)
    def _():
        def part(i, carry):
            lanes = pl.ds(pl.multiple_of(i * step, step), step)
            rows_s[lanes, :] = tn(slope_s[:, lanes], positives[...])
            return carry

        lax.fori_loop(0, count // step, part, 0)
        rows_s[pl.ds(0, sentences), :] = rows_s[own, :]

    @pl.when(twin == 1)
    def _():
        rows_s[pl.ds(0, sentences), :] = nn(slope_s[own, :], units[pl.ds(0, count), :])

    gu = rows_s[pl.ds(0, sentences), :] * factor
    unit = unitf[...]
    gs = inv[:, :1] * (gu - unit * jnp.mean(gu * unit, axis=-1, keepdims=True))
    gy = gs * vector(g2)
    u = gy - jnp.mean(gy, axis=-1, keepdims=True)
    gain = jnp.zeros((1, D), F32)
    shift = jnp.zeros((1, D), F32)
    summed = jnp.zeros((1, D), F32)
    for r in range(rows):
        part = slice(r * SEG, (r + 1) * SEG)
        tok = slice(r * length, (r + 1) * length)
        seg_row = seg[r : r + 1, :]
        hits = lax.broadcasted_iota(jnp.int32, (SEG, length), 0) == seg_row
        member = hits.astype(F32).astype(BF16)
        counts = jnp.sum(hits.astype(F32), axis=1, keepdims=True)
        xhat_low = xh2[tok, :]
        gain += jnp.sum(nn(member, xhat_low) * gs[part], axis=0, keepdims=True)
        shift += jnp.sum(counts * gs[part], axis=0, keepdims=True)
        xhat = xhat_low.astype(F32)
        high, low = split_low(u[part])
        spread = tn(member, high) + tn(member, low)
        inner = jnp.mean(spread * xhat, axis=-1, keepdims=True)
        grad = rs2[tok, :1] * (spread - xhat * inner)
        grad_low = grad.astype(BF16)
        gb_o[tok, :] = grad_low
        summed += jnp.sum(grad_low.astype(F32), axis=0, keepdims=True)
    vec_o[...] = jnp.concatenate([summed, gain, shift, jnp.zeros((5, D), F32)], axis=0)


def loss_stage(idx, gathered, targets, unitf, inv, seg, g2, xh2, rs2):
    pieces, flips = gathered
    tokens = xh2.shape[0]
    count = targets.shape[1]
    return pl.pallas_call(
        functools.partial(loss_kernel, flips),
        name="loss",
        in_specs=[sspec()] + [vspec()] * (7 + len(pieces)),
        out_specs=[vspec()] * 3,
        out_shape=[shape_of((1, count), F32), shape_of((tokens, D), BF16), shape_of((8, D), F32)],
        scratch_shapes=[
            VMEM((count, count), BF16),
            VMEM((count, D), F32),
            VMEM((2 * count, D), BF16),
        ],
        cost_estimate=took(4),
        compiler_params=params(20 if count <= 256 else 44),
    )(idx, *pieces, *far(targets, seg, g2), unitf, inv, xh2, rs2)


def pre_kernel(gb, wdown, dg, out):
    n = 768

    def product(j):
        return nt(gb[...], wdown[j * n : (j + 1) * n, :])

    ahead = product(0)
    for j in range(FF // n):
        value = ahead
        if j + 1 < FF // n:
            ahead = product(j + 1)
        part = slice(j * n, (j + 1) * n)
        out[:, part] = (value * dg[:, part].astype(F32)).astype(BF16)


def pre_stage(gb, wdown, dg, carry):
    outs = [VMEM(dg.shape, BF16)]
    return carry_call(
        pre_kernel, "grad_pre", 7.6, 24, (gb, wdown, dg), [vspec()] * 3, outs, [], carry
    )


def normed_kernel(gp, win, gb, xh1, rs1, g1, wout, ga_o, gc_o, vec_o):
    m = 512
    count = gp.shape[0] // m
    gain, shift, summed = [jnp.zeros((1, D), F32) for _ in range(3)]
    grads = [nt(gp[i * m : (i + 1) * m, :], win[...]) for i in range(count)]
    for i in range(count):
        rows = slice(i * m, (i + 1) * m)
        grad = grads[i] + gb[rows, :].astype(F32)
        xhat = xh1[rows, :].astype(F32)
        gain += jnp.sum(grad * xhat, axis=0, keepdims=True)
        shift += jnp.sum(grad, axis=0, keepdims=True)
        gy = grad * vector(g1)
        inner = jnp.mean(gy * xhat, axis=-1, keepdims=True)
        total = rs1[rows, :1] * (gy - jnp.mean(gy, axis=-1, keepdims=True) - xhat * inner)
        low = total.astype(BF16)
        ga_o[rows, :] = low
        summed += jnp.sum(low.astype(F32), axis=0, keepdims=True)
    for i in range(count):
        rows = slice(i * m, (i + 1) * m)
        gc_o[rows, :] = nt(ga_o[rows, :], wout[...]).astype(BF16)
    vec_o[...] = jnp.concatenate([summed, gain, shift, jnp.zeros((5, D), F32)], axis=0)


def normed_stage(gp, win, gb, xh1, rs1, g1, wout, carry):
    tokens = gp.shape[0]
    outs = [shape_of((tokens, D), BF16), shape_of((tokens, D), BF16), shape_of((8, D), F32)]
    operands = (gp, win, gb, xh1, rs1, *far(g1), wout)
    return carry_call(
        normed_kernel, "grad_normed", 9, 28, operands, [vspec()] * 7, outs, [], carry
    )


def attend_back_kernel(q_ref, k_ref, v_ref, g_ref, p_ref, out_ref):
    length = q_ref.shape[0]
    blocks, _ = windows(length)
    group = q_ref.shape[1] // PW
    scale = HEAD_DIM**-0.5
    loaded, grads = [], []
    for h in range(group):
        lanes = slice(h * PW, (h + 1) * PW)
        q2 = [two_heads(q_ref[b[0] : b[0] + QB, lanes]) for b in blocks]
        g2 = [two_heads(g_ref[b[0] : b[0] + QB, lanes]) for b in blocks]
        loaded.append((q2, g2, k_ref[:, lanes].T))
        v_all = v_ref[:, lanes]
        grads.append([nt(v_all[b[1] : b[2]], g) for b, g in zip(blocks, g2)])
    slopes = []
    for h in range(group):
        own = []
        for gp, (_, low, high, packed) in zip(grads[h], blocks):
            p = p_ref[h, packed : packed + high - low, :].astype(F32)
            weighted = p * gp
            inner = jnp.sum(weighted, axis=0, keepdims=True)
            own.append((weighted - p * inner).astype(BF16))
        slopes.append(own)

    def gather(parts):
        out = []
        for block in range(len(blocks)):
            total = None
            for part, (_, low, high, _) in zip(parts, blocks):
                base = block * QB - low
                if 0 <= base < high - low:
                    piece = part[base : base + QB]
                    total = piece if total is None else total + piece
            out.append(total)
        return jnp.concatenate(out, axis=0)

    for h in range(group):
        lanes = slice(h * PW, (h + 1) * PW)
        q2, g2, k_turned = loaded[h]
        dq = [nn(k_turned[:, b[1] : b[2]], s) for b, s in zip(blocks, slopes[h])]
        dv = [nn(p_ref[h, b[3] : b[3] + b[2] - b[1], :], g) for b, g in zip(blocks, g2)]
        dk = [nn(s, q) for s, q in zip(slopes[h], q2)]
        turned = [pick_heads((part * scale).astype(BF16)) for part in dq]
        out_ref[0, :, lanes] = jnp.concatenate(turned, axis=0)
        out_ref[1, :, lanes] = (gather(dk) * scale).astype(BF16)
        out_ref[2, :, lanes] = gather(dv).astype(BF16)


def attend_back(qkv, grad_context, probs, rows, length, first, pairs):
    _, packed = windows(length)
    group = 2
    steps = pairs // group
    base = first // group
    width = group * PW

    def block(part):
        return pl.BlockSpec((length, width), lambda r, h: (r, part * (D // width) + base + h))

    return pl.pallas_call(
        attend_back_kernel,
        name="attend_back",
        grid=(rows, steps),
        in_specs=[
            block(0),
            block(1),
            block(2),
            block(0),
            pl.BlockSpec((None, group, packed, 2 * QB), lambda r, h: (r, base + h, 0, 0)),
        ],
        out_specs=pl.BlockSpec((3, length, width), lambda r, h: (0, r, h)),
        out_shape=shape_of((3, rows * length, pairs * PW), BF16),
        cost_estimate=took(2.0 * pairs),
        compiler_params=params(20),
    )(*far(qkv, qkv, qkv), grad_context, *far(probs))


def hidden_kernel(da, db, wqkv, ga, out):
    m = 512
    for i in range(ga.shape[0] // m):
        rows = slice(i * m, (i + 1) * m)
        total = ga[rows, :].astype(F32)
        for part in range(3):
            both = jnp.concatenate([da[part, rows, :], db[part, rows, :]], axis=1)
            total = total + nt(both, wqkv[:, part * D : (part + 1) * D])
        out[rows, :] = total.astype(BF16)


def hidden_stage(da, db, wqkv, ga):
    return pl.pallas_call(
        hidden_kernel,
        name="hidden_grad",
        in_specs=[vspec()] * 4,
        out_specs=vspec(),
        out_shape=shape_of(ga.shape, BF16),
        cost_estimate=took(5.7),
        compiler_params=params(22),
    )(da, db, wqkv, ga)


def place_of(half, quarter, owner):
    c, y, z0, z1 = owner & 1, (owner >> 1) & 1, (owner >> 2) & 1, owner >> 3
    order = (quarter, y, z0, z1, c) if half == 0 else (y, z0, z1, quarter, c)
    out = 0
    for bit in order:
        out = 2 * out + bit
    return out


def lanes_of(width):
    most = 128 if width <= 256 else 256
    return [(low, min(most, width - low)) for low in range(0, width, most)]


def half_shapes(width):
    shapes = [shape_of((32, 48, width), BF16)]
    return shapes + [shape_of((32, 48, n), BF16) for _, n in lanes_of(width)]


def store_piece(first, keep, sends, quarter, owner, piece_a, piece_b):
    at_a, at_b = place_of(0, quarter, owner), place_of(1, quarter, owner)
    keep[jnp.where(first, at_a, at_b)] = jnp.where(first, piece_a, piece_b)
    other = jnp.where(first, piece_b, piece_a)
    at = jnp.where(first, at_b, at_a)
    for send, (low, n) in zip(sends, lanes_of(keep.shape[2])):
        send[at] = other[:, low : low + n]


def down_kernel(idx, act, gb, keep, *sends):
    first = idx[2] == 0
    n = 768

    def product(j):
        return tn(act[:, j * n : (j + 1) * n], gb[...])

    ahead = product(0)
    for j in range(FF // n):
        total = ahead.astype(BF16)
        if j + 1 < FF // n:
            ahead = product(j + 1)
        for local in range(4):
            for quarter in range(2):
                base = local * 192 + quarter * 48
                a, b = total[base : base + 48], total[base + 96 : base + 144]
                store_piece(first, keep, sends, quarter, 4 * j + local, a, b)


def down_stage(idx, act, gb):
    shapes = half_shapes(D)
    return pl.pallas_call(
        down_kernel,
        name="grad_w_down",
        in_specs=[sspec(), vspec(), vspec()],
        out_specs=[vspec()] * len(shapes),
        out_shape=shapes,
        cost_estimate=took(7.5),
        compiler_params=params(22),
    )(idx, act, gb)


def in_kernel(idx, n1, gp, vec_o, keep, *refs):
    sends, turned = refs[:-1], refs[-1]
    first = idx[2] == 0
    turned[...] = n1[...].T

    def products(quarter):
        out = []
        for half in range(2):
            j = 2 * half + quarter
            out.append(nn(turned[...], gp[:, j * D : (j + 1) * D]))
        return out

    ahead = products(0)
    for quarter in range(2):
        a, b = [part.astype(BF16) for part in ahead]
        if quarter == 0:
            ahead = products(1)
        for owner in range(16):
            rows = slice(owner * 48, (owner + 1) * 48)
            store_piece(first, keep, sends, quarter, owner, a[rows], b[rows])
    vec_o[...] = jnp.sum(gp[...].astype(F32), axis=0, keepdims=True)


def in_stage(idx, n1, gp):
    shapes = half_shapes(D)
    return pl.pallas_call(
        in_kernel,
        name="grad_w_in",
        in_specs=[sspec(), vspec(), vspec()],
        out_specs=[vspec()] * (1 + len(shapes)),
        out_shape=[shape_of((1, FF), F32)] + shapes,
        scratch_shapes=[VMEM((D, n1.shape[0]), BF16)],
        cost_estimate=took(7.4),
        compiler_params=params(24),
    )(idx, n1, gp)


WIDE, NARROW = 640, 256


def store_all(first, keep, send, whole, width):
    for quarter in range(2):
        a = whole[:, quarter * width : (quarter + 1) * width]
        b = whole[:, (2 + quarter) * width : (3 + quarter) * width]
        for owner in range(16):
            rows = slice(owner * 48, (owner + 1) * 48)
            store_piece(first, keep, send, quarter, owner, a[rows], b[rows])


def wide_kernel(idx, hid, da, ctx, ga, turned_o, keep, *refs):
    sends, whole = refs[:-1], refs[-1]
    n = da.shape[2]
    turned_o[...] = hid[...].T
    for part in range(3):
        whole[:, part * n : (part + 1) * n] = nn(turned_o[...], da[part]).astype(BF16)
    whole[:, 3 * n : 3 * n + D] = tn(ctx[...], ga[...]).astype(BF16)
    whole[:, 3 * n + D :] = jnp.zeros((D, 4 * WIDE - 3 * n - D), BF16)
    store_all(idx[2] == 0, keep, sends, whole, WIDE)


def wide_stage(idx, hid, da, ctx, ga):
    shapes = half_shapes(WIDE)
    return pl.pallas_call(
        wide_kernel,
        name="grad_w_wide",
        in_specs=[sspec()] + [vspec()] * 4,
        out_specs=[vspec()] * (1 + len(shapes)),
        out_shape=[shape_of((D, hid.shape[0]), BF16)] + shapes,
        scratch_shapes=[VMEM((D, 4 * WIDE), BF16)],
        cost_estimate=took(6),
        compiler_params=params(24),
    )(idx, hid, da, ctx, ga)


def narrow_kernel(idx, turned, da, db, vec1, vec2, bias, keep, *refs):
    send, (whole, sums_s) = refs[:-2], refs[-2:]
    n = db.shape[2]
    for part in range(3):
        whole[:, part * n : (part + 1) * n] = nn(turned[...], db[part]).astype(BF16)
    sums_s[...] = jnp.zeros_like(sums_s)
    sums_s[2:5, :] = vec1[0:3, :]
    sums_s[5:8, :] = vec2[0:3, :]
    for row, part in ((0, 0), (1, 2)):
        for base, grads in ((0, da), (D - n, db)):
            lanes = slice(base, base + grads.shape[2])
            total = jnp.sum(grads[part].astype(F32), axis=0, keepdims=True)
            sums_s[row : row + 1, lanes] = total
    small = sums_s[...].T
    groups = [bias[:, i * 384 : (i + 1) * 384] for i in range(FF // 384)]
    folded = jnp.concatenate(groups, axis=0)
    turned_bias = [folded[:, i * 48 : (i + 1) * 48].T for i in range(8)]
    lane = lax.broadcasted_iota(jnp.int32, (48, 128), 1)
    for owner in range(16):
        own = small[owner * 48 : (owner + 1) * 48]
        for k in range(4):
            column = turned_bias[4 * (owner % 2) + k][:, owner // 2 : owner // 2 + 1]
            own = jnp.where(lane == 8 + k, column, own)
        whole[owner * 48 : (owner + 1) * 48, 3 * n : 3 * n + 128] = own.astype(BF16)
    whole[:, 3 * n + 128 :] = jnp.zeros((D, 4 * NARROW - 3 * n - 128), BF16)
    store_all(idx[2] == 0, keep, send, whole, NARROW)


def narrow_stage(idx, turned, da, db, vec1, vec2, bias):
    return pl.pallas_call(
        narrow_kernel,
        name="grad_w_narrow",
        in_specs=[sspec()] + [vspec()] * 6,
        out_specs=[vspec()] * len(half_shapes(NARROW)),
        out_shape=half_shapes(NARROW),
        scratch_shapes=[VMEM((D, 4 * NARROW), BF16), VMEM((128, D), F32)],
        cost_estimate=took(2.4),
        compiler_params=params(22),
    )(idx, turned, da, db, vec1, vec2, bias)


def swap_dp(value, flip):
    devices = lax.axis_size("dp")
    return lax.ppermute(value, "dp", [(i, i ^ flip) for i in range(devices)])


def swap_twin(value):
    return lax.ppermute(value, "twin", [(0, 1), (1, 0)])


TWIN = 16
ROUTES = ((TWIN, 2, 4, 8, TWIN), (2, 4, 8, TWIN, TWIN))


def step_swap(value, step):
    pairs = [(i, i ^ ROUTES[i & 1][step]) for i in range(2 * TWIN)]
    return lax.ppermute(value, ("twin", "dp"), pairs)


def plus(*values):
    total = values[0].astype(F32)
    for value in values[1:]:
        total = total + value.astype(F32)
    return total.astype(BF16)


def call_small(kernel, name, idx, operands, outs):
    return pl.pallas_call(
        kernel,
        name=name,
        in_specs=[sspec()] + [vspec()] * len(operands),
        out_specs=[vspec()] * len(outs),
        out_shape=[shape_of(shape, dtype) for shape, dtype in outs],
        cost_estimate=took(2.4),
        compiler_params=params(12),
    )(idx, *operands)


def half_kernel(step, idx, keep, recv, keep_o, send_o):
    count = keep_o.shape[0]
    bit = idx[3 + step]
    mine = pl.ds(bit * count, count)
    other = pl.ds((1 - bit) * count, count)
    keep_o[...] = plus(keep[mine], recv[mine])
    send_o[...] = plus(keep[other], recv[other])


def half_step(idx, step, keep, recv):
    count, rows, width = keep.shape
    shape = (count // 2, rows, width)
    kernel = functools.partial(half_kernel, step)
    return call_small(kernel, "sum_" + str(step), idx, (keep, recv), [(shape, BF16)] * 2)


def core_kernel(idx, keep, *refs):
    recvs, (keep_o, send_o) = refs[:-2], refs[-2:]
    bit = idx[3]
    for recv, (low, n) in zip(recvs, lanes_of(keep.shape[3])):
        lanes = slice(low, low + n)
        keep_o[:, :, lanes] = plus(keep[bit, :, :, lanes], recv[bit])
        send_o[:, :, lanes] = plus(keep[1 - bit, :, :, lanes], recv[1 - bit])


def core_step(idx, keep, recvs):
    count, rows, width = keep.shape
    half = count // 2
    pieces = 4
    part = half // pieces

    def spec(n):
        return pl.BlockSpec((2, part, rows, n), lambda i: (0, i, 0, 0))

    return pl.pallas_call(
        core_kernel,
        name="sum_core",
        grid=(pieces,),
        in_specs=[sspec(), spec(width)] + [spec(n) for _, n in lanes_of(width)],
        out_specs=[pl.BlockSpec((part, rows, width), lambda i: (i, 0, 0))] * 2,
        out_shape=[shape_of((half, rows, width), BF16)] * 2,
        cost_estimate=took(1.7),
        compiler_params=params(10),
    )(
        idx,
        keep.reshape(2, half, rows, width),
        *[recv.reshape(2, half, rows, recv.shape[2]) for recv in recvs],
    )


def own_kernel(idx, keep, recv, out):
    out[...] = plus(keep[...], recv[...])


def turn_kernel(idx, own, other, keep_o, send_o):
    twin, core = idx[0], idx[2]
    keep_o[twin] = own[core]
    keep_o[1 - twin] = other[core]
    send_o[twin] = own[1 - core]
    send_o[1 - twin] = other[1 - core]


class Order:
    def __init__(self):
        self.last = None

    def after(self, value, *others):
        if self.last is None:
            return value
        return lax.optimization_barrier((value, self.last) + others)[0]

    def done(self, value):
        self.last = value
        return value


class Exchange:
    def __init__(self, order, idx, keep, sends):
        self.order, self.idx, self.step = order, idx, 0
        self.keep, self.recv = keep, [swap_dp(send, 1) for send in sends]

    def advance(self):
        idx, order = self.idx, self.order
        keep, recv = order.after(self.keep), self.recv
        if self.step == 0:
            keep, send = core_step(idx, keep, recv)
            recv = step_swap(send, 0)
        elif self.step < 4:
            keep, send = half_step(idx, self.step, keep, recv)
            recv = step_swap(send, self.step)
        elif self.step == 4:
            shape = keep.shape
            (keep,) = call_small(own_kernel, "sum_4", idx, (keep, recv), [(shape, BF16)])
            recv = step_swap(keep, 4)
        else:
            shape = keep.shape
            keep, send = call_small(turn_kernel, "turn", idx, (keep, recv), [(shape, BF16)] * 2)
            recv = swap_dp(send, 1)
        order.done(keep)
        self.keep, self.recv = keep, recv
        self.step += 1

    def result(self):
        return self.keep, self.recv


def gather_units(unit):
    flips = [(0, 0)]
    for flip in (8, 4):
        unit = jnp.concatenate([unit, swap_dp(unit, flip)], axis=0)
        flips = flips + [(t, f ^ flip) for t, f in flips]
    pairs = [(i, i ^ (TWIN + 2)) for i in range(2 * TWIN)]
    far = lax.ppermute(unit, ("twin", "dp"), pairs)
    unit = jnp.concatenate([unit, swap_dp(unit, 2), swap_twin(unit), far], axis=0)
    flips = [(t ^ a, f ^ b) for a, b in ((0, 0), (0, 2), (1, 0), (1, 2)) for t, f in flips]
    return (unit, swap_dp(unit, 1)), (flips, [(t, f ^ 1) for t, f in flips])


def four_quarters(idx, keep, recv):
    first = idx[2] == 0
    low = [jnp.where(first, keep[i], recv[i]) for i in range(2)]
    high = [jnp.where(first, recv[i], keep[i]) for i in range(2)]
    return low + high


def final_in_kernel(idx, keep, recv, out):
    for i, part in enumerate(four_quarters(idx, keep, recv)):
        out[:, i * D : (i + 1) * D] = part.astype(F32)


def final_down_kernel(idx, keep, recv, out):
    for i, part in enumerate(four_quarters(idx, keep, recv)):
        out[i * 48 : (i + 1) * 48, :] = part.astype(F32)


def final_last_kernel(idx, wide_k, wide_r, narrow_k, narrow_r, qkv_o, out_o, vec_o):
    wide = jnp.concatenate(four_quarters(idx, wide_k, wide_r), axis=1).astype(F32)
    narrow = jnp.concatenate(four_quarters(idx, narrow_k, narrow_r), axis=1).astype(F32)
    low, high = 2 * D // 3, D // 3
    for part in range(3):
        qkv_o[:, part * D : part * D + low] = wide[:, part * low : (part + 1) * low]
        qkv_o[:, part * D + low : (part + 1) * D] = narrow[:, part * high : (part + 1) * high]
    out_o[...] = wide[:, 3 * low : 3 * low + D]
    small = narrow[:, 3 * high : 3 * high + 128]
    vec_o[...] = jnp.concatenate([small, jnp.zeros((80, 128), F32)], axis=0).T[:16]


def finish(order, idx, kernel, name, chunks, outs):
    operands = [value for chunk in chunks for value in chunk.result()]
    operands[0] = order.after(operands[0])
    out = call_small(kernel, name, idx, operands, outs)
    order.done(out[0])
    return out


def add_low(*parts):
    return lax.optimization_barrier(plus(*parts))


def digits_of(devices):
    out, rest = [], devices // 2
    while rest > 1:
        size = 4 if rest % 4 == 0 else 2
        out.append(size)
        rest //= size
    return out


def pick(value, index, axis):
    return lax.dynamic_index_in_dim(value, index, axis, keepdims=False)


def scatter(grad):
    devices = lax.axis_size("dp")
    me = lax.axis_index("dp")
    value = grad.reshape(devices, grad.shape[0] // devices, grad.shape[1])
    unit = 1
    for size in [2] + digits_of(devices):
        mine = (me // unit) % size
        view = value.reshape((value.shape[0] // size, size) + value.shape[1:])
        parts = [pick(view, mine, 1)]
        for flip in range(1, size):
            parts.append(swap_dp(pick(view, mine ^ flip, 1), flip * unit))
        value = add_low(*parts)
        unit *= size
    value = value[0]
    return value.astype(F32) + swap_twin(value).astype(F32)


SEQUENCE = (
    "down", "pre", "d", "in", "normed", "i", "d", "attend_a", "d", "wide", "i", "attend_b", "w",
    "d", "narrow", "i", "hidden", "n", "d", "w", "i", "n", "d", "w", "i", "n", "final_d", "i",
    "w", "n", "final_i", "w", "n", "w", "n",
)


def body(
    hidden,
    segment_ids,
    targets,
    w_qkv,
    b_query,
    b_value,
    w_out,
    b_out,
    ln1_gain,
    ln1_bias,
    w_in,
    b_in,
    w_down,
    b_down,
    ln2_gain,
    ln2_bias,
):
    row_count, length, width = hidden.shape
    tokens = row_count * length
    devices = lax.axis_size("dp")
    everyone = lax.axis_size(("twin", "dp"))
    me = lax.axis_index("dp")
    twin = lax.axis_index("twin")
    core, y, z0, z1 = me & 1, (me >> 1) & 1, (me >> 2) & 1, me >> 3
    first = core == 0
    bits = [jnp.where(first, a, b) for a, b in ((twin, y), (y, z0), (z0, z1), (z1, twin))]
    idx = jnp.stack([twin, me, core] + bits).astype(jnp.int32)
    weights = (w_qkv, b_query, b_value, w_out, b_out, ln1_gain, ln1_bias)
    weights += (w_in, b_in, w_down, b_down, ln2_gain, ln2_bias)
    qkv, probs, ctx, n1, xh1, rs1, act, dg, xh2, rs2, unit, unitf, inv = forward(
        hidden, segment_ids, weights
    )
    sentences = row_count * SEG
    unit = unit.reshape(sentences, width)
    direct = devices == TWIN and sentences == 16
    if direct:
        gathered = gather_units(unit)
    else:
        gathered = ((lax.all_gather(unit, ("twin", "dp"), axis=0, tiled=True),), (None,))
    losses, gb, vec2 = loss_stage(
        idx,
        gathered,
        targets.reshape(1, -1),
        unitf.reshape(sentences, width),
        inv.reshape(sentences, 128),
        segment_ids,
        ln2_gain,
        xh2,
        rs2,
    )
    share = losses.shape[1] // everyone
    losses = lax.dynamic_slice_in_dim(
        losses[0], lax.axis_index(("twin", "dp")) * share, share, 0
    )
    flat = hidden.reshape(tokens, width)
    if direct:
        order = Order()
        chunks = {}

        def begin(name, keep, sends):
            order.done(keep)
            chunks[name] = Exchange(order, idx, keep, sends)

        for stage in SEQUENCE:
            if stage == "down":
                halves_d = down_stage(idx, act, order.after(gb))
                begin("d", halves_d[0], halves_d[1:])
            elif stage == "pre":
                near = (n1, xh1, rs1)
                gp, *near = pre_stage(order.after(gb), w_down, dg, near)
                order.done(gp)
            elif stage == "in":
                sums, *halves_in = in_stage(idx, near[0], order.after(gp))
                begin("i", halves_in[0], halves_in[1:])
            elif stage == "normed":
                ga, gc, vec1, *later = normed_stage(
                    order.after(gp), w_in, gb, near[1], near[2], ln1_gain, w_out, (flat, ctx)
                )
                order.done(ga)
            elif stage == "attend_a":
                da = order.done(attend_back(qkv, order.after(gc), probs, row_count, length, 0, 4))
            elif stage == "attend_b":
                db = order.done(attend_back(qkv, order.after(gc), probs, row_count, length, 4, 2))
            elif stage == "wide":
                turned, *halves_w = wide_stage(idx, later[0], order.after(da), later[1], ga)
                begin("w", halves_w[0], halves_w[1:])
            elif stage == "narrow":
                halves_n = narrow_stage(idx, turned, da, order.after(db), vec1, vec2, sums)
                begin("n", halves_n[0], halves_n[1:])
            elif stage == "hidden":
                hidden_grad = order.done(hidden_stage(da, order.after(db), w_qkv, ga))
            elif stage == "final_d":
                outs = [((192, D), F32)]
                (grad_w_down,) = finish(order, idx, final_down_kernel, stage, [chunks["d"]], outs)
            elif stage == "final_i":
                outs = [((48, FF), F32)]
                (grad_w_in,) = finish(order, idx, final_in_kernel, stage, [chunks["i"]], outs)
            else:
                chunks[stage].advance()
        wide, narrow = chunks["w"], chunks["n"]
        shapes = [((48, 3 * D), F32), ((48, D), F32), ((16, 128), F32)]
        grad_w_qkv, grad_w_out, vec = finish(
            order, idx, final_last_kernel, "final_last", [wide, narrow], shapes
        )
        vec = vec[:, :48]
        vecs = [vec[i] for i in range(8)]
        grad_b_in = vec[8:12].reshape(-1)
    else:
        gp, _ = pre_stage(gb, w_down, dg, (n1,))
        ga, gc, vec1, _ = normed_stage(gp, w_in, gb, xh1, rs1, ln1_gain, w_out, (ctx,))
        da = attend_back(qkv, gc, probs, row_count, length, 0, 4)
        db = attend_back(qkv, gc, probs, row_count, length, 4, 2)
        hidden_grad = hidden_stage(da, db, w_qkv, ga)
        dqkv = jnp.concatenate([da, db], axis=2)
        grad_w_down = scatter(tn(act, gb).astype(BF16))
        grad_w_in = scatter(tn(n1, gp).astype(BF16))
        wide = jnp.concatenate([dqkv[0], dqkv[1], dqkv[2]], axis=1)
        grad_w_qkv = scatter(tn(flat, wide).astype(BF16))
        grad_w_out = scatter(tn(ctx, ga).astype(BF16))
        sums = jnp.sum(dqkv, axis=1, dtype=F32)
        vec = jnp.concatenate([sums[0:1], sums[2:3], vec1[:3], vec2[:3]])
        vec = scatter(jnp.pad(vec, ((0, 120), (0, 0))).T.astype(BF16)).T
        vecs = [vec[i] for i in range(8)]
        bias = jnp.sum(gp, axis=0, dtype=F32)
        grad_b_in = scatter(jnp.broadcast_to(bias[:, None], (FF, 128)).astype(BF16))[:, 0]
    return (
        losses,
        hidden_grad.reshape(row_count, length, width),
        grad_w_qkv,
        vecs[0],
        vecs[1],
        grad_w_out,
        vecs[2],
        vecs[3],
        vecs[4],
        grad_w_in,
        grad_b_in,
        grad_w_down,
        vecs[5],
        vecs[6],
        vecs[7],
    )


def solution(mesh):
    whole = (P(),) * 14
    placed = (P(("twin", "dp"), None, None), P(("twin", "dp"), None)) + whole
    return jax.shard_map(
        body,
        mesh=mesh,
        in_specs=placed,
        out_specs=(
            P(("twin", "dp")),
            P(("twin", "dp"), None, None),
            P("dp", None),
            P("dp"),
            P("dp"),
            P("dp", None),
            P("dp"),
            P("dp"),
            P("dp"),
            P("dp", None),
            P("dp"),
            P("dp", None),
            P("dp"),
            P("dp"),
            P("dp"),
        ),
        check_vma=False,
    )
```

```python
import functools

import jax
import jax.numpy as jnp
from jax import lax
from jax.experimental import pallas as pl
from jax.experimental.pallas import tpu as pltpu
from jax.sharding import PartitionSpec as P

D = 768
HEADS = 12
HEAD_DIM = 64
FF = 3072
SEG = 8
QB = 128
MOST = 128
PAIRS = HEADS // 2
PW = 2 * HEAD_DIM

cosine_scale = 64.0
loss_scale = 32.0
norm_epsilon = 1e-12
unit_epsilon = 1e-06
masked_score = -1e30

F32 = jnp.float32
BF16 = jnp.bfloat16
VMEM = pltpu.VMEM
ANY = pl.ANY
MIB = 1 << 20


def nn(left, right):
    return lax.dot_general(left, right, (((1,), (0,)), ((), ())), preferred_element_type=F32)


def nt(left, right):
    return lax.dot_general(left, right, (((1,), (1,)), ((), ())), preferred_element_type=F32)


def tn(left, right):
    return lax.dot_general(left, right, (((0,), (0,)), ((), ())), preferred_element_type=F32)


def vspec():
    return pl.BlockSpec(memory_space=VMEM)


def sspec():
    return pl.BlockSpec(memory_space=pltpu.SMEM)


def hspec():
    return pl.BlockSpec(memory_space=pltpu.HBM)


def far(*values):
    return [pltpu.with_memory_space_constraint(value, pltpu.HBM) for value in values]


class Fetch:
    def __init__(self, sems, pairs):
        self.copies = [pltpu.make_async_copy(a, b, sems.at[i]) for i, (a, b) in enumerate(pairs)]
        for copy in self.copies:
            copy.start()

    def wait(self, *which):
        for i in which:
            self.copies[i].wait()


def carrying(kernel, n_in, n_out, n_carry):
    def wrapped(*refs):
        refs, sems = refs[:-1], refs[-1]
        ins, refs = refs[:n_in], refs[n_in:]
        sources, refs = refs[:n_carry], refs[n_carry:]
        outs, refs = refs[:n_out], refs[n_out:]
        targets, rest = refs[:n_carry], refs[n_carry:]
        fetch = Fetch(sems, tuple(zip(sources, targets)))
        kernel(*ins, *outs, *rest)
        fetch.wait(*range(n_carry))

    return wrapped


def carry_call(kernel, name, us, mib, operands, specs, outs, scratch, carry):
    n_carry = len(carry)
    return pl.pallas_call(
        carrying(kernel, len(operands), len(outs), n_carry),
        name=name,
        in_specs=list(specs) + [hspec()] * n_carry,
        out_specs=[vspec()] * (len(outs) + n_carry),
        out_shape=list(outs) + [VMEM(a.shape, a.dtype) for a in carry],
        scratch_shapes=list(scratch) + [pltpu.SemaphoreType.DMA((max(n_carry, 1),))],
        cost_estimate=took(us),
        compiler_params=params(mib),
    )(*operands, *far(*carry))


def fixed(shape):
    return pl.BlockSpec(shape, lambda *_: (0,) * len(shape))


def shape_of(shape, dtype):
    return jax.ShapeDtypeStruct(shape, dtype)


def params(mib):
    return pltpu.CompilerParams(vmem_limit_bytes=mib * MIB)


SCALE = 0.7


def took(us):
    return pl.CostEstimate(flops=int(us * SCALE * 1.15e9), bytes_accessed=0, transcendentals=0)


def windows(length):
    out, packed = [], 0
    for start in range(0, length, QB):
        low, high = max(0, start - MOST), min(length, start + QB + MOST)
        out.append((start, low, high, packed))
        packed += high - low
    return out, packed


def two_heads(pair):
    first = lax.broadcasted_iota(jnp.int32, pair.shape, 1) < HEAD_DIM
    zero = jnp.zeros((), pair.dtype)
    return jnp.concatenate([jnp.where(first, pair, zero), jnp.where(first, zero, pair)], axis=0)


def pick_heads(both):
    rows = both.shape[1] // 2
    return jnp.concatenate([both[:HEAD_DIM, :rows], both[HEAD_DIM:, rows:]], axis=0).T


def column_of(row):
    return jnp.broadcast_to(row, (8, row.shape[1])).T[:, :1]


def split_low(value):
    high = value.astype(BF16)
    return high, (value - high.astype(F32)).astype(BF16)


def normalise(value):
    middle = jnp.mean(value, axis=-1, keepdims=True)
    centered = value - middle
    spread = jnp.mean(centered * centered, axis=-1, keepdims=True)
    rstd = lax.rsqrt(spread + norm_epsilon)
    return centered * rstd, rstd


def vector(ref):
    return ref[...].astype(F32).reshape(1, ref.shape[0])


def softmax_down(own):
    top = jnp.max(own, axis=0, keepdims=True)
    weights = jnp.exp(own - top)
    total = jnp.sum(weights, axis=0, keepdims=True)
    return (weights * (1.0 / total)).astype(BF16)


def attend(length, qkv, bias, p_s, ctx_s):
    blocks, _ = windows(length)

    def lanes(part, h):
        return slice(part * D + h * PW, part * D + (h + 1) * PW)

    def score(h):
        q_all = qkv[:, lanes(0, h)] * jnp.asarray(HEAD_DIM**-0.5, BF16)
        k_all = qkv[:, lanes(1, h)]
        out = []
        for start, low, high, _ in blocks:
            out.append(nt(k_all[low:high], two_heads(q_all[start : start + QB])))
        return out, qkv[:, lanes(2, h)].T

    ahead = score(0)
    for h in range(PAIRS):
        scores, v_turned = ahead
        if h + 1 < PAIRS:
            ahead = score(h + 1)
        probs = []
        for own, (_, low, high, packed) in zip(scores, blocks):
            mask = bias[packed : packed + high - low, :]
            halves = [softmax_down(own[:, :QB] + mask), softmax_down(own[:, QB:] + mask)]
            probs.append(jnp.concatenate(halves, axis=1))
        for p, (_, low, high, packed) in zip(probs, blocks):
            p_s[h, packed : packed + high - low, :] = p
        outs = [nn(v_turned[:, low:high], p) for p, (_, low, high, _) in zip(probs, blocks)]
        ctx_s[:, lanes(0, h)] = jnp.concatenate([pick_heads(o.astype(BF16)) for o in outs], axis=0)


def forward_kernel(*refs):
    (hid_h, seg, wqkv_h, bq, bv, wout_h, bout, g1, b1, win_h, bin_, wdown_h, bdown, g2, b2) = refs[:15]
    outs, (unit_o, unitf_o, inv_o) = refs[15:25], refs[25:28]
    hid, wqkv, wout, win, wdown, bias_s, n1_s = refs[28:35]
    kept = refs[35:45]
    sems, osems = refs[45:47]
    qkv_s, p_s, ctx_s, nl_s, xh1_s, rs1_s, act_o, dg_o, xh2_o, rs2_o = kept
    rows = seg.shape[0]
    length = hid.shape[0] // rows
    blocks, _ = windows(length)
    toks = [slice(r * length, (r + 1) * length) for r in range(rows)]
    parts = [slice(part * D, (part + 1) * D) for part in range(3)]

    pairs = [(hid_h.at[toks[0]], hid.at[toks[0]])]
    pairs += [(wqkv_h.at[:, cols], wqkv.at[:, cols]) for cols in parts]
    first = Fetch(sems, pairs)
    later = []

    def fetch_rest():
        rest = [(wout_h, wout), (win_h, win), (wdown_h, wdown)]
        rest += [(hid_h.at[tok], hid.at[tok]) for tok in toks[1:]]
        for i, (source, target) in enumerate(rest):
            copy = pltpu.make_async_copy(source, target, sems.at[4 + i])
            copy.start()
            later.append(copy)

    def leaving(i, r):
        if i == 1:
            return pltpu.make_async_copy(p_s, outs[1].at[r], osems.at[r, 1])
        source = kept[i] if i in (0, 2) else kept[i].at[toks[r]]
        return pltpu.make_async_copy(source, outs[i].at[toks[r]], osems.at[r, i])

    seg_rows = [seg[r : r + 1, :].astype(F32) for r in range(rows)]

    def mask(r):
        seg_col = column_of(seg_rows[r])
        for start, low, high, packed in blocks:
            same = seg_col[low:high] == seg_rows[r][:, start : start + QB]
            bias_s[packed : packed + high - low, :] = jnp.where(same, 0.0, masked_score)

    def project(r):
        if r > 0:
            leaving(0, r - 1).wait()
            later[2 + r].wait()
        for part, cols in enumerate(parts):
            if r == 0:
                first.wait(*((0, 1) if part == 0 else (part + 1,)))
                if part == 0:
                    fetch_rest()
            value = nn(hid[toks[r], :], wqkv[:, cols])
            if part == 0:
                value = value + vector(bq)
            if part == 2:
                value = value + vector(bv)
            qkv_s[:, cols] = value.astype(BF16)
        leaving(0, r).start()

    def attention(r):
        if r > 0:
            leaving(1, r - 1).wait()
            leaving(2, r - 1).wait()
        attend(length, qkv_s, bias_s, p_s, ctx_s)
        leaving(1, r).start()
        leaving(2, r).start()

    def mix(r):
        if r == 0:
            later[0].wait()
        return nn(ctx_s[...], wout[...])

    def norm_one(r, attended):
        tok = toks[r]
        xhat, rstd = normalise(hid[tok, :].astype(F32) + (attended + vector(bout)))
        xh1_s[tok, :] = xhat.astype(BF16)
        rs1_s[tok, :] = jnp.broadcast_to(rstd, (length, rs1_s.shape[1]))
        n1 = xhat * vector(g1) + vector(b1)
        n1_s[tok, :] = n1
        nl_s[tok, :] = n1.astype(BF16)
        for i in (3, 4, 5):
            leaving(i, r).start()

    chunk = 768
    count = FF // chunk
    bias_in = vector(bin_)

    def rise(r, c):
        cols = slice(c * chunk, (c + 1) * chunk)
        return nn(nl_s[toks[r], :], win[:, cols]) + bias_in[:, cols]

    def bend(r, c, pre):
        cols = slice(c * chunk, (c + 1) * chunk)
        half = 0.5 + 0.5 * lax.erf(pre * 0.5**0.5)
        act_o[toks[r], cols] = (pre * half).astype(BF16)
        bell = jnp.exp(pre * pre * -0.5) * 0.3989422804014327
        dg_o[toks[r], cols] = (half + pre * bell).astype(BF16)

    def norm_two(r, fallen):
        tok = toks[r]
        xhat, rstd = normalise(n1_s[tok, :] + (fallen + vector(bdown)))
        xh2_o[tok, :] = xhat.astype(BF16)
        rs2_o[tok, :] = jnp.broadcast_to(rstd, (length, rs2_o.shape[1]))
        leaving(8, r).start()
        leaving(9, r).start()
        out = xhat * vector(g2) + vector(b2)
        index = lax.broadcasted_iota(jnp.int32, (SEG, length), 0).astype(F32)
        member = (index == seg_rows[r]).astype(F32)
        counts = jnp.sum(member, axis=1, keepdims=True)
        high, low = split_low(out)
        member = member.astype(BF16)
        pooled = (nn(member, high) + nn(member, low)) / counts
        inv = lax.rsqrt(jnp.mean(pooled * pooled, axis=-1, keepdims=True) + unit_epsilon)
        unit = pooled * inv
        unitf_o[r] = unit
        unit_o[r] = unit.astype(BF16)
        inv_o[r] = jnp.broadcast_to(inv / counts, inv_o.shape[1:])

    mixed = None
    for r in range(rows):
        mask(r)
        project(r)
        if r > 0:
            norm_one(r - 1, mixed)
        attention(r)
        mixed = mix(r)
    steps = [(r, c) for r in range(rows) for c in range(count)]
    later[1].wait()
    if rows > 1:
        ahead = rise(0, 0)
        norm_one(rows - 1, mixed)
    else:
        norm_one(0, mixed)
        ahead = rise(0, 0)
    fallen = None
    for i, (r, c) in enumerate(steps):
        pre = ahead
        if i + 1 < len(steps):
            ahead = rise(*steps[i + 1])
        bend(r, c, pre)
        if c == 1 and fallen is not None:
            norm_two(r - 1, fallen)
        if c == count - 1:
            if r == 0:
                later[2].wait()
            leaving(6, r).start()
            leaving(7, r).start()
            fallen = nn(act_o[toks[r], :], wdown[...])
    norm_two(rows - 1, fallen)
    for r in range(rows):
        for i in range(10):
            if r == rows - 1 or i > 2:
                leaving(i, r).wait()


def forward(hidden, seg, weights):
    rows, length, _ = hidden.shape
    tokens = rows * length
    _, packed = windows(length)
    packed_shape = (PAIRS, packed, 2 * QB)
    far_shapes = [((tokens, 3 * D), BF16), ((rows,) + packed_shape, BF16)]
    far_shapes += [((tokens, D), BF16)] * 3 + [((tokens, 128), F32)]
    after = [((tokens, FF), BF16)] * 2 + [((tokens, D), BF16), ((tokens, 128), F32)]
    far_shapes += after
    near_shapes = [((rows, SEG, D), BF16), ((rows, SEG, D), F32), ((rows, SEG, 128), F32)]
    kept = [VMEM((length, 3 * D), BF16), VMEM(packed_shape, BF16), VMEM((length, D), BF16)]
    kept += [VMEM((tokens, D), BF16), VMEM((tokens, D), BF16), VMEM((tokens, 128), F32)]
    kept += [VMEM(*a) for a in after]
    large = (0, 3, 7, 9)
    hbm = hspec()
    return pl.pallas_call(
        forward_kernel,
        name="forward",
        in_specs=[hbm, vspec()] + [hbm if i in large else vspec() for i in range(13)],
        out_specs=[hbm] * 10 + [vspec()] * 3,
        out_shape=[pltpu.HBM(*a) for a in far_shapes] + [VMEM(*a) for a in near_shapes],
        scratch_shapes=[VMEM((tokens, D), BF16)]
        + [VMEM(weights[i].shape, BF16) for i in large]
        + [VMEM((packed, QB), F32), VMEM((tokens, D), F32)]
        + kept
        + [pltpu.SemaphoreType.DMA((7 + rows,)), pltpu.SemaphoreType.DMA((rows, 10))],
        cost_estimate=took(33),
        compiler_params=params(58),
    )(*far(hidden.reshape(tokens, D), seg, *weights))


def loss_kernel(flips, idx, *refs):
    pieces, refs = refs[: len(flips)], refs[len(flips) :]
    targets, seg, g2, unitf, inv, xh2_h, rs2_h, loss_o, gb_o, vec_o = refs[:10]
    slope_s, rows_s, units, xh2, rs2, sems = refs[10:]
    fetch = Fetch(sems, ((xh2_h, xh2), (rs2_h, rs2)))
    twin, me = idx[0], idx[1]
    count = units.shape[0] // 2
    sentences = unitf.shape[0]
    for piece, own_flips in zip(pieces, flips):
        if own_flips is None:
            units[...] = piece[...]
            continue
        for i, (twin_flip, flip) in enumerate(own_flips):
            at = (twin ^ twin_flip) * count + (me ^ flip) * sentences
            at = pl.multiple_of(at, sentences)
            units[pl.ds(at, sentences), :] = piece[i * sentences : (i + 1) * sentences, :]
    rows, length = seg.shape
    step = min(count, 256)
    factor = cosine_scale / D
    positives = units.at[pl.ds(count, count)]
    own = pl.ds(pl.multiple_of(me * sentences, sentences), sentences)

    def one_block(i, carry):
        lanes = pl.ds(pl.multiple_of(i * step, step), step)
        sims = nt(positives[...], units[lanes, :]) * factor
        top = jnp.max(sims, axis=0, keepdims=True)
        weights = jnp.exp(sims - top)
        total = jnp.sum(weights, axis=0, keepdims=True)
        hit = lax.broadcasted_iota(jnp.int32, sims.shape, 0) == targets[:, lanes]
        picked = jnp.sum(jnp.where(hit, sims, 0.0), axis=0, keepdims=True)
        loss_o[:, lanes] = top + jnp.log(total) - picked
        slope = loss_scale * (weights * (1.0 / total) - hit.astype(F32))
        slope_s[:, lanes] = slope.astype(BF16)
        return carry

    if count == step:
        one_block(0, 0)
    else:
        lax.fori_loop(0, count // step, one_block, 0)

    @pl.when(twin == 0)
    def _():
        def part(i, carry):
            lanes = pl.ds(pl.multiple_of(i * step, step), step)
            rows_s[lanes, :] = tn(slope_s[:, lanes], positives[...])
            return carry

        lax.fori_loop(0, count // step, part, 0)
        rows_s[pl.ds(0, sentences), :] = rows_s[own, :]

    @pl.when(twin == 1)
    def _():
        rows_s[pl.ds(0, sentences), :] = nn(slope_s[own, :], units[pl.ds(0, count), :])

    fetch.wait(0, 1)
    gu = rows_s[pl.ds(0, sentences), :] * factor
    unit = unitf[...]
    gs = inv[:, :1] * (gu - unit * jnp.mean(gu * unit, axis=-1, keepdims=True))
    gy = gs * vector(g2)
    u = gy - jnp.mean(gy, axis=-1, keepdims=True)
    gain = jnp.zeros((1, D), F32)
    shift = jnp.zeros((1, D), F32)
    summed = jnp.zeros((1, D), F32)
    for r in range(rows):
        part = slice(r * SEG, (r + 1) * SEG)
        tok = slice(r * length, (r + 1) * length)
        seg_row = seg[r : r + 1, :]
        hits = lax.broadcasted_iota(jnp.int32, (SEG, length), 0) == seg_row
        member = hits.astype(F32).astype(BF16)
        counts = jnp.sum(hits.astype(F32), axis=1, keepdims=True)
        xhat_low = xh2[tok, :]
        gain += jnp.sum(nn(member, xhat_low) * gs[part], axis=0, keepdims=True)
        shift += jnp.sum(counts * gs[part], axis=0, keepdims=True)
        xhat = xhat_low.astype(F32)
        high, low = split_low(u[part])
        spread = tn(member, high) + tn(member, low)
        inner = jnp.mean(spread * xhat, axis=-1, keepdims=True)
        grad = rs2[tok, :1] * (spread - xhat * inner)
        grad_low = grad.astype(BF16)
        gb_o[tok, :] = grad_low
        summed += jnp.sum(grad_low.astype(F32), axis=0, keepdims=True)
    vec_o[...] = jnp.concatenate([summed, gain, shift, jnp.zeros((5, D), F32)], axis=0)


def loss_stage(idx, gathered, targets, unitf, inv, seg, g2, xh2, rs2):
    pieces, flips = gathered
    tokens = xh2.shape[0]
    count = targets.shape[1]
    return pl.pallas_call(
        functools.partial(loss_kernel, flips),
        name="loss",
        in_specs=[sspec()] + [vspec()] * (5 + len(pieces)) + [hspec()] * 2,
        out_specs=[vspec()] * 3,
        out_shape=[shape_of((1, count), F32), shape_of((tokens, D), BF16), shape_of((8, D), F32)],
        scratch_shapes=[
            VMEM((count, count), BF16),
            VMEM((count, D), F32),
            VMEM((2 * count, D), BF16),
            VMEM(xh2.shape, xh2.dtype),
            VMEM(rs2.shape, rs2.dtype),
            pltpu.SemaphoreType.DMA((2,)),
        ],
        cost_estimate=took(4),
        compiler_params=params(20 if count <= 256 else 44),
    )(idx, *pieces, *far(targets, seg, g2), unitf, inv, *far(xh2, rs2))


def pre_kernel(gb, wdown, dg, out):
    n = 768

    def product(j):
        return nt(gb[...], wdown[j * n : (j + 1) * n, :])

    ahead = product(0)
    for j in range(FF // n):
        value = ahead
        if j + 1 < FF // n:
            ahead = product(j + 1)
        part = slice(j * n, (j + 1) * n)
        out[:, part] = (value * dg[:, part].astype(F32)).astype(BF16)


def pre_stage(gb, wdown, dg, carry):
    outs = [VMEM(dg.shape, BF16)]
    return carry_call(
        pre_kernel, "grad_pre", 5.2, 24, (gb, wdown, dg), [vspec()] * 3, outs, [], carry
    )


def normed_kernel(gp, win, gb, xh1, rs1, g1, wout, ga_o, gc_o, vec_o):
    m = 512
    count = gp.shape[0] // m
    gain, shift, summed = [jnp.zeros((1, D), F32) for _ in range(3)]
    grads = [nt(gp[i * m : (i + 1) * m, :], win[...]) for i in range(count)]
    for i in range(count):
        rows = slice(i * m, (i + 1) * m)
        grad = grads[i] + gb[rows, :].astype(F32)
        xhat = xh1[rows, :].astype(F32)
        gain += jnp.sum(grad * xhat, axis=0, keepdims=True)
        shift += jnp.sum(grad, axis=0, keepdims=True)
        gy = grad * vector(g1)
        inner = jnp.mean(gy * xhat, axis=-1, keepdims=True)
        total = rs1[rows, :1] * (gy - jnp.mean(gy, axis=-1, keepdims=True) - xhat * inner)
        low = total.astype(BF16)
        ga_o[rows, :] = low
        summed += jnp.sum(low.astype(F32), axis=0, keepdims=True)
    for i in range(count):
        rows = slice(i * m, (i + 1) * m)
        gc_o[rows, :] = nt(ga_o[rows, :], wout[...]).astype(BF16)
    vec_o[...] = jnp.concatenate([summed, gain, shift, jnp.zeros((5, D), F32)], axis=0)


def normed_stage(gp, win, gb, xh1, rs1, g1, wout, carry):
    tokens = gp.shape[0]
    outs = [shape_of((tokens, D), BF16), shape_of((tokens, D), BF16), shape_of((8, D), F32)]
    operands = (gp, win, gb, xh1, rs1, *far(g1), wout)
    return carry_call(
        normed_kernel, "grad_normed", 9, 28, operands, [vspec()] * 7, outs, [], carry
    )


def attend_back_kernel(q_ref, k_ref, v_ref, g_ref, p_ref, out_ref):
    length = q_ref.shape[0]
    blocks, _ = windows(length)
    group = q_ref.shape[1] // PW
    scale = HEAD_DIM**-0.5
    loaded, grads = [], []
    for h in range(group):
        lanes = slice(h * PW, (h + 1) * PW)
        q2 = [two_heads(q_ref[b[0] : b[0] + QB, lanes]) for b in blocks]
        g2 = [two_heads(g_ref[b[0] : b[0] + QB, lanes]) for b in blocks]
        loaded.append((q2, g2, k_ref[:, lanes].T))
        v_all = v_ref[:, lanes]
        grads.append([nt(v_all[b[1] : b[2]], g) for b, g in zip(blocks, g2)])
    slopes = []
    for h in range(group):
        own = []
        for gp, (_, low, high, packed) in zip(grads[h], blocks):
            p = p_ref[h, packed : packed + high - low, :].astype(F32)
            weighted = p * gp
            inner = jnp.sum(weighted, axis=0, keepdims=True)
            own.append((weighted - p * inner).astype(BF16))
        slopes.append(own)

    def gather(parts):
        out = []
        for block in range(len(blocks)):
            total = None
            for part, (_, low, high, _) in zip(parts, blocks):
                base = block * QB - low
                if 0 <= base < high - low:
                    piece = part[base : base + QB]
                    total = piece if total is None else total + piece
            out.append(total)
        return jnp.concatenate(out, axis=0)

    for h in range(group):
        lanes = slice(h * PW, (h + 1) * PW)
        q2, g2, k_turned = loaded[h]
        dq = [nn(k_turned[:, b[1] : b[2]], s) for b, s in zip(blocks, slopes[h])]
        dv = [nn(p_ref[h, b[3] : b[3] + b[2] - b[1], :], g) for b, g in zip(blocks, g2)]
        dk = [nn(s, q) for s, q in zip(slopes[h], q2)]
        turned = [pick_heads((part * scale).astype(BF16)) for part in dq]
        out_ref[0, :, lanes] = jnp.concatenate(turned, axis=0)
        out_ref[1, :, lanes] = (gather(dk) * scale).astype(BF16)
        out_ref[2, :, lanes] = gather(dv).astype(BF16)


def attend_back(qkv, grad_context, probs, rows, length, first, pairs):
    _, packed = windows(length)
    group = 2
    steps = pairs // group
    base = first // group
    width = group * PW

    def block(part):
        return pl.BlockSpec((length, width), lambda r, h: (r, part * (D // width) + base + h))

    return pl.pallas_call(
        attend_back_kernel,
        name="attend_back",
        grid=(rows, steps),
        in_specs=[
            block(0),
            block(1),
            block(2),
            block(0),
            pl.BlockSpec((None, group, packed, 2 * QB), lambda r, h: (r, base + h, 0, 0)),
        ],
        out_specs=pl.BlockSpec((3, length, width), lambda r, h: (0, r, h)),
        out_shape=shape_of((3, rows * length, pairs * PW), BF16),
        cost_estimate=took(2.0 * pairs),
        compiler_params=params(20),
    )(*far(qkv, qkv, qkv), grad_context, *far(probs))


def hidden_kernel(da, db, wqkv, ga, out):
    m = 512
    for i in range(ga.shape[0] // m):
        rows = slice(i * m, (i + 1) * m)
        total = ga[rows, :].astype(F32)
        for part in range(3):
            both = jnp.concatenate([da[part, rows, :], db[part, rows, :]], axis=1)
            total = total + nt(both, wqkv[:, part * D : (part + 1) * D])
        out[rows, :] = total.astype(BF16)


def hidden_stage(da, db, wqkv, ga):
    return pl.pallas_call(
        hidden_kernel,
        name="hidden_grad",
        in_specs=[vspec()] * 4,
        out_specs=vspec(),
        out_shape=shape_of(ga.shape, BF16),
        cost_estimate=took(5.7),
        compiler_params=params(22),
    )(da, db, wqkv, ga)


def place_of(half, quarter, owner):
    c, y, z0, z1 = owner & 1, (owner >> 1) & 1, (owner >> 2) & 1, owner >> 3
    order = (quarter, y, z0, z1, c) if half == 0 else (y, z0, z1, quarter, c)
    out = 0
    for bit in order:
        out = 2 * out + bit
    return out


def lanes_of(width):
    most = 128 if width <= 256 else 256
    return [(low, min(most, width - low)) for low in range(0, width, most)]


def half_shapes(width):
    shapes = [shape_of((32, 48, width), BF16)]
    return shapes + [shape_of((32, 48, n), BF16) for _, n in lanes_of(width)]


def store_piece(first, keep, sends, quarter, owner, piece_a, piece_b):
    at_a, at_b = place_of(0, quarter, owner), place_of(1, quarter, owner)
    keep[jnp.where(first, at_a, at_b)] = jnp.where(first, piece_a, piece_b)
    other = jnp.where(first, piece_b, piece_a)
    at = jnp.where(first, at_b, at_a)
    for send, (low, n) in zip(sends, lanes_of(keep.shape[2])):
        send[at] = other[:, low : low + n]


def down_kernel(idx, act, gb, keep, *sends):
    first = idx[2] == 0
    n = 768

    def product(j):
        return tn(act[:, j * n : (j + 1) * n], gb[...])

    ahead = product(0)
    for j in range(FF // n):
        total = ahead.astype(BF16)
        if j + 1 < FF // n:
            ahead = product(j + 1)
        for local in range(4):
            for quarter in range(2):
                base = local * 192 + quarter * 48
                a, b = total[base : base + 48], total[base + 96 : base + 144]
                store_piece(first, keep, sends, quarter, 4 * j + local, a, b)


def down_stage(idx, act, gb):
    shapes = half_shapes(D)
    return pl.pallas_call(
        down_kernel,
        name="grad_w_down",
        in_specs=[sspec(), vspec(), vspec()],
        out_specs=[vspec()] * len(shapes),
        out_shape=shapes,
        cost_estimate=took(7.5),
        compiler_params=params(22),
    )(idx, act, gb)


def in_kernel(idx, n1, gp, vec_o, keep, *refs):
    sends, turned = refs[:-1], refs[-1]
    first = idx[2] == 0
    turned[...] = n1[...].T

    def products(quarter):
        out = []
        for half in range(2):
            j = 2 * half + quarter
            out.append(nn(turned[...], gp[:, j * D : (j + 1) * D]))
        return out

    ahead = products(0)
    for quarter in range(2):
        a, b = [part.astype(BF16) for part in ahead]
        if quarter == 0:
            ahead = products(1)
        for owner in range(16):
            rows = slice(owner * 48, (owner + 1) * 48)
            store_piece(first, keep, sends, quarter, owner, a[rows], b[rows])
    vec_o[...] = jnp.sum(gp[...].astype(F32), axis=0, keepdims=True)


def in_stage(idx, n1, gp):
    shapes = half_shapes(D)
    return pl.pallas_call(
        in_kernel,
        name="grad_w_in",
        in_specs=[sspec(), vspec(), vspec()],
        out_specs=[vspec()] * (1 + len(shapes)),
        out_shape=[shape_of((1, FF), F32)] + shapes,
        scratch_shapes=[VMEM((D, n1.shape[0]), BF16)],
        cost_estimate=took(7.4),
        compiler_params=params(24),
    )(idx, n1, gp)


WIDE, NARROW = 640, 256


def store_all(first, keep, send, whole, width):
    for quarter in range(2):
        a = whole[:, quarter * width : (quarter + 1) * width]
        b = whole[:, (2 + quarter) * width : (3 + quarter) * width]
        for owner in range(16):
            rows = slice(owner * 48, (owner + 1) * 48)
            store_piece(first, keep, send, quarter, owner, a[rows], b[rows])


def wide_kernel(idx, hid, da, ctx, ga, turned_o, keep, *refs):
    sends, whole = refs[:-1], refs[-1]
    n = da.shape[2]
    turned_o[...] = hid[...].T
    for part in range(3):
        whole[:, part * n : (part + 1) * n] = nn(turned_o[...], da[part]).astype(BF16)
    whole[:, 3 * n : 3 * n + D] = tn(ctx[...], ga[...]).astype(BF16)
    whole[:, 3 * n + D :] = jnp.zeros((D, 4 * WIDE - 3 * n - D), BF16)
    store_all(idx[2] == 0, keep, sends, whole, WIDE)


def wide_stage(idx, hid, da, ctx, ga):
    shapes = half_shapes(WIDE)
    return pl.pallas_call(
        wide_kernel,
        name="grad_w_wide",
        in_specs=[sspec()] + [vspec()] * 4,
        out_specs=[vspec()] * (1 + len(shapes)),
        out_shape=[shape_of((D, hid.shape[0]), BF16)] + shapes,
        scratch_shapes=[VMEM((D, 4 * WIDE), BF16)],
        cost_estimate=took(6),
        compiler_params=params(24),
    )(idx, hid, da, ctx, ga)


def narrow_kernel(idx, turned, da, db, vec1, vec2, bias, keep, *refs):
    send, (whole, sums_s) = refs[:-2], refs[-2:]
    n = db.shape[2]
    for part in range(3):
        whole[:, part * n : (part + 1) * n] = nn(turned[...], db[part]).astype(BF16)
    sums_s[...] = jnp.zeros_like(sums_s)
    sums_s[2:5, :] = vec1[0:3, :]
    sums_s[5:8, :] = vec2[0:3, :]
    for row, part in ((0, 0), (1, 2)):
        for base, grads in ((0, da), (D - n, db)):
            lanes = slice(base, base + grads.shape[2])
            total = jnp.sum(grads[part].astype(F32), axis=0, keepdims=True)
            sums_s[row : row + 1, lanes] = total
    small = sums_s[...].T
    groups = [bias[:, i * 384 : (i + 1) * 384] for i in range(FF // 384)]
    folded = jnp.concatenate(groups, axis=0)
    turned_bias = [folded[:, i * 48 : (i + 1) * 48].T for i in range(8)]
    lane = lax.broadcasted_iota(jnp.int32, (48, 128), 1)
    for owner in range(16):
        own = small[owner * 48 : (owner + 1) * 48]
        for k in range(4):
            column = turned_bias[4 * (owner % 2) + k][:, owner // 2 : owner // 2 + 1]
            own = jnp.where(lane == 8 + k, column, own)
        whole[owner * 48 : (owner + 1) * 48, 3 * n : 3 * n + 128] = own.astype(BF16)
    whole[:, 3 * n + 128 :] = jnp.zeros((D, 4 * NARROW - 3 * n - 128), BF16)
    store_all(idx[2] == 0, keep, send, whole, NARROW)


def narrow_stage(idx, turned, da, db, vec1, vec2, bias):
    return pl.pallas_call(
        narrow_kernel,
        name="grad_w_narrow",
        in_specs=[sspec()] + [vspec()] * 6,
        out_specs=[vspec()] * len(half_shapes(NARROW)),
        out_shape=half_shapes(NARROW),
        scratch_shapes=[VMEM((D, 4 * NARROW), BF16), VMEM((128, D), F32)],
        cost_estimate=took(2.4),
        compiler_params=params(22),
    )(idx, turned, da, db, vec1, vec2, bias)


def swap_dp(value, flip):
    devices = lax.axis_size("dp")
    return lax.ppermute(value, "dp", [(i, i ^ flip) for i in range(devices)])


def swap_twin(value):
    return lax.ppermute(value, "twin", [(0, 1), (1, 0)])


TWIN = 16
ROUTES = ((TWIN, 2, 4, 8, TWIN), (2, 4, 8, TWIN, TWIN))


def step_swap(value, step):
    pairs = [(i, i ^ ROUTES[i & 1][step]) for i in range(2 * TWIN)]
    return lax.ppermute(value, ("twin", "dp"), pairs)


def plus(*values):
    total = values[0].astype(F32)
    for value in values[1:]:
        total = total + value.astype(F32)
    return total.astype(BF16)


def call_small(kernel, name, idx, operands, outs):
    return pl.pallas_call(
        kernel,
        name=name,
        in_specs=[sspec()] + [vspec()] * len(operands),
        out_specs=[vspec()] * len(outs),
        out_shape=[shape_of(shape, dtype) for shape, dtype in outs],
        cost_estimate=took(2.4),
        compiler_params=params(12),
    )(idx, *operands)


def half_kernel(step, idx, keep, recv, keep_o, send_o):
    count = keep_o.shape[0]
    bit = idx[3 + step]
    mine = pl.ds(bit * count, count)
    other = pl.ds((1 - bit) * count, count)
    keep_o[...] = plus(keep[mine], recv[mine])
    send_o[...] = plus(keep[other], recv[other])


def half_step(idx, step, keep, recv):
    count, rows, width = keep.shape
    shape = (count // 2, rows, width)
    kernel = functools.partial(half_kernel, step)
    return call_small(kernel, "sum_" + str(step), idx, (keep, recv), [(shape, BF16)] * 2)


def core_kernel(idx, keep, *refs):
    recvs, (keep_o, send_o) = refs[:-2], refs[-2:]
    bit = idx[3]
    for recv, (low, n) in zip(recvs, lanes_of(keep.shape[3])):
        lanes = slice(low, low + n)
        keep_o[:, :, lanes] = plus(keep[bit, :, :, lanes], recv[bit])
        send_o[:, :, lanes] = plus(keep[1 - bit, :, :, lanes], recv[1 - bit])


def core_step(idx, keep, recvs):
    count, rows, width = keep.shape
    half = count // 2
    pieces = 4
    part = half // pieces

    def spec(n):
        return pl.BlockSpec((2, part, rows, n), lambda i: (0, i, 0, 0))

    return pl.pallas_call(
        core_kernel,
        name="sum_core",
        grid=(pieces,),
        in_specs=[sspec(), spec(width)] + [spec(n) for _, n in lanes_of(width)],
        out_specs=[pl.BlockSpec((part, rows, width), lambda i: (i, 0, 0))] * 2,
        out_shape=[shape_of((half, rows, width), BF16)] * 2,
        cost_estimate=took(1.7),
        compiler_params=params(10),
    )(
        idx,
        keep.reshape(2, half, rows, width),
        *[recv.reshape(2, half, rows, recv.shape[2]) for recv in recvs],
    )


def own_kernel(idx, keep, recv, out):
    out[...] = plus(keep[...], recv[...])


def turn_kernel(idx, own, other, keep_o, send_o):
    twin, core = idx[0], idx[2]
    keep_o[twin] = own[core]
    keep_o[1 - twin] = other[core]
    send_o[twin] = own[1 - core]
    send_o[1 - twin] = other[1 - core]


class Order:
    def __init__(self):
        self.last = None

    def after(self, value, *others):
        if self.last is None:
            return value
        return lax.optimization_barrier((value, self.last) + others)[0]

    def done(self, value):
        self.last = value
        return value


class Exchange:
    def __init__(self, order, idx, keep, sends):
        self.order, self.idx, self.step = order, idx, 0
        self.keep, self.recv = keep, [swap_dp(send, 1) for send in sends]

    def advance(self):
        idx, order = self.idx, self.order
        keep, recv = order.after(self.keep), self.recv
        if self.step == 0:
            keep, send = core_step(idx, keep, recv)
            recv = step_swap(send, 0)
        elif self.step < 4:
            keep, send = half_step(idx, self.step, keep, recv)
            recv = step_swap(send, self.step)
        elif self.step == 4:
            shape = keep.shape
            (keep,) = call_small(own_kernel, "sum_4", idx, (keep, recv), [(shape, BF16)])
            recv = step_swap(keep, 4)
        else:
            shape = keep.shape
            keep, send = call_small(turn_kernel, "turn", idx, (keep, recv), [(shape, BF16)] * 2)
            recv = swap_dp(send, 1)
        order.done(keep)
        self.keep, self.recv = keep, recv
        self.step += 1

    def result(self):
        return self.keep, self.recv


def gather_units(unit):
    flips = [(0, 0)]
    for flip in (8, 4):
        unit = jnp.concatenate([unit, swap_dp(unit, flip)], axis=0)
        flips = flips + [(t, f ^ flip) for t, f in flips]
    pairs = [(i, i ^ (TWIN + 2)) for i in range(2 * TWIN)]
    far = lax.ppermute(unit, ("twin", "dp"), pairs)
    unit = jnp.concatenate([unit, swap_dp(unit, 2), swap_twin(unit), far], axis=0)
    flips = [(t ^ a, f ^ b) for a, b in ((0, 0), (0, 2), (1, 0), (1, 2)) for t, f in flips]
    return (unit, swap_dp(unit, 1)), (flips, [(t, f ^ 1) for t, f in flips])


def four_quarters(idx, keep, recv):
    first = idx[2] == 0
    low = [jnp.where(first, keep[i], recv[i]) for i in range(2)]
    high = [jnp.where(first, recv[i], keep[i]) for i in range(2)]
    return low + high


def final_in_kernel(idx, keep, recv, out):
    for i, part in enumerate(four_quarters(idx, keep, recv)):
        out[:, i * D : (i + 1) * D] = part.astype(F32)


def final_down_kernel(idx, keep, recv, out):
    for i, part in enumerate(four_quarters(idx, keep, recv)):
        out[i * 48 : (i + 1) * 48, :] = part.astype(F32)


def final_last_kernel(idx, wide_k, wide_r, narrow_k, narrow_r, qkv_o, out_o, vec_o):
    wide = jnp.concatenate(four_quarters(idx, wide_k, wide_r), axis=1).astype(F32)
    narrow = jnp.concatenate(four_quarters(idx, narrow_k, narrow_r), axis=1).astype(F32)
    low, high = 2 * D // 3, D // 3
    for part in range(3):
        qkv_o[:, part * D : part * D + low] = wide[:, part * low : (part + 1) * low]
        qkv_o[:, part * D + low : (part + 1) * D] = narrow[:, part * high : (part + 1) * high]
    out_o[...] = wide[:, 3 * low : 3 * low + D]
    small = narrow[:, 3 * high : 3 * high + 128]
    vec_o[...] = jnp.concatenate([small, jnp.zeros((80, 128), F32)], axis=0).T[:16]


def finish(order, idx, kernel, name, chunks, outs):
    operands = [value for chunk in chunks for value in chunk.result()]
    operands[0] = order.after(operands[0])
    out = call_small(kernel, name, idx, operands, outs)
    order.done(out[0])
    return out


def add_low(*parts):
    return lax.optimization_barrier(plus(*parts))


def digits_of(devices):
    out, rest = [], devices // 2
    while rest > 1:
        size = 4 if rest % 4 == 0 else 2
        out.append(size)
        rest //= size
    return out


def pick(value, index, axis):
    return lax.dynamic_index_in_dim(value, index, axis, keepdims=False)


def scatter(grad):
    devices = lax.axis_size("dp")
    me = lax.axis_index("dp")
    value = grad.reshape(devices, grad.shape[0] // devices, grad.shape[1])
    unit = 1
    for size in [2] + digits_of(devices):
        mine = (me // unit) % size
        view = value.reshape((value.shape[0] // size, size) + value.shape[1:])
        parts = [pick(view, mine, 1)]
        for flip in range(1, size):
            parts.append(swap_dp(pick(view, mine ^ flip, 1), flip * unit))
        value = add_low(*parts)
        unit *= size
    value = value[0]
    return value.astype(F32) + swap_twin(value).astype(F32)


SEQUENCE = (
    "down", "pre", "d", "in", "normed", "i", "d", "attend_a", "wide", "i", "d", "attend_b", "w",
    "narrow", "d", "i", "n", "hidden", "w", "n", "d", "i", "w", "n", "d", "i", "w", "n", "i",
    "w", "n", "final_d", "final_i", "w", "n",
)


def body(
    hidden,
    segment_ids,
    targets,
    w_qkv,
    b_query,
    b_value,
    w_out,
    b_out,
    ln1_gain,
    ln1_bias,
    w_in,
    b_in,
    w_down,
    b_down,
    ln2_gain,
    ln2_bias,
):
    row_count, length, width = hidden.shape
    tokens = row_count * length
    devices = lax.axis_size("dp")
    everyone = lax.axis_size(("twin", "dp"))
    me = lax.axis_index("dp")
    twin = lax.axis_index("twin")
    core, y, z0, z1 = me & 1, (me >> 1) & 1, (me >> 2) & 1, me >> 3
    first = core == 0
    bits = [jnp.where(first, a, b) for a, b in ((twin, y), (y, z0), (z0, z1), (z1, twin))]
    idx = jnp.stack([twin, me, core] + bits).astype(jnp.int32)
    weights = (w_qkv, b_query, b_value, w_out, b_out, ln1_gain, ln1_bias)
    weights += (w_in, b_in, w_down, b_down, ln2_gain, ln2_bias)
    qkv, probs, ctx, n1, xh1, rs1, act, dg, xh2, rs2, unit, unitf, inv = forward(
        hidden, segment_ids, weights
    )
    sentences = row_count * SEG
    unit = unit.reshape(sentences, width)
    direct = devices == TWIN and sentences == 16
    if direct:
        gathered = gather_units(unit)
    else:
        gathered = ((lax.all_gather(unit, ("twin", "dp"), axis=0, tiled=True),), (None,))
    losses, gb, vec2 = loss_stage(
        idx,
        gathered,
        targets.reshape(1, -1),
        unitf.reshape(sentences, width),
        inv.reshape(sentences, 128),
        segment_ids,
        ln2_gain,
        xh2,
        rs2,
    )
    share = losses.shape[1] // everyone
    losses = lax.dynamic_slice_in_dim(
        losses[0], lax.axis_index(("twin", "dp")) * share, share, 0
    )
    flat = hidden.reshape(tokens, width)
    if direct:
        order = Order()
        chunks = {}

        def begin(name, keep, sends):
            order.done(keep)
            chunks[name] = Exchange(order, idx, keep, sends)

        for stage in SEQUENCE:
            if stage == "down":
                halves_d = down_stage(idx, act, order.after(gb))
                begin("d", halves_d[0], halves_d[1:])
            elif stage == "pre":
                near = (n1, xh1, rs1)
                gp, *near = pre_stage(order.after(gb), w_down, dg, near)
                order.done(gp)
            elif stage == "in":
                sums, *halves_in = in_stage(idx, near[0], order.after(gp))
                begin("i", halves_in[0], halves_in[1:])
            elif stage == "normed":
                ga, gc, vec1, *later = normed_stage(
                    order.after(gp), w_in, gb, near[1], near[2], ln1_gain, w_out, (flat, ctx)
                )
                order.done(ga)
            elif stage == "attend_a":
                da = order.done(attend_back(qkv, order.after(gc), probs, row_count, length, 0, 4))
            elif stage == "attend_b":
                db = order.done(attend_back(qkv, order.after(gc), probs, row_count, length, 4, 2))
            elif stage == "wide":
                turned, *halves_w = wide_stage(idx, later[0], order.after(da), later[1], ga)
                begin("w", halves_w[0], halves_w[1:])
            elif stage == "narrow":
                halves_n = narrow_stage(idx, turned, da, order.after(db), vec1, vec2, sums)
                begin("n", halves_n[0], halves_n[1:])
            elif stage == "hidden":
                hidden_grad = order.done(hidden_stage(da, order.after(db), w_qkv, ga))
            elif stage == "final_d":
                outs = [((192, D), F32)]
                (grad_w_down,) = finish(order, idx, final_down_kernel, stage, [chunks["d"]], outs)
            elif stage == "final_i":
                outs = [((48, FF), F32)]
                (grad_w_in,) = finish(order, idx, final_in_kernel, stage, [chunks["i"]], outs)
            else:
                chunks[stage].advance()
        wide, narrow = chunks["w"], chunks["n"]
        shapes = [((48, 3 * D), F32), ((48, D), F32), ((16, 128), F32)]
        grad_w_qkv, grad_w_out, vec = finish(
            order, idx, final_last_kernel, "final_last", [wide, narrow], shapes
        )
        vec = vec[:, :48]
        vecs = [vec[i] for i in range(8)]
        grad_b_in = vec[8:12].reshape(-1)
    else:
        gp, _ = pre_stage(gb, w_down, dg, (n1,))
        ga, gc, vec1, _ = normed_stage(gp, w_in, gb, xh1, rs1, ln1_gain, w_out, (ctx,))
        da = attend_back(qkv, gc, probs, row_count, length, 0, 4)
        db = attend_back(qkv, gc, probs, row_count, length, 4, 2)
        hidden_grad = hidden_stage(da, db, w_qkv, ga)
        dqkv = jnp.concatenate([da, db], axis=2)
        grad_w_down = scatter(tn(act, gb).astype(BF16))
        grad_w_in = scatter(tn(n1, gp).astype(BF16))
        wide = jnp.concatenate([dqkv[0], dqkv[1], dqkv[2]], axis=1)
        grad_w_qkv = scatter(tn(flat, wide).astype(BF16))
        grad_w_out = scatter(tn(ctx, ga).astype(BF16))
        sums = jnp.sum(dqkv, axis=1, dtype=F32)
        vec = jnp.concatenate([sums[0:1], sums[2:3], vec1[:3], vec2[:3]])
        vec = scatter(jnp.pad(vec, ((0, 120), (0, 0))).T.astype(BF16)).T
        vecs = [vec[i] for i in range(8)]
        bias = jnp.sum(gp, axis=0, dtype=F32)
        grad_b_in = scatter(jnp.broadcast_to(bias[:, None], (FF, 128)).astype(BF16))[:, 0]
    return (
        losses,
        hidden_grad.reshape(row_count, length, width),
        grad_w_qkv,
        vecs[0],
        vecs[1],
        grad_w_out,
        vecs[2],
        vecs[3],
        vecs[4],
        grad_w_in,
        grad_b_in,
        grad_w_down,
        vecs[5],
        vecs[6],
        vecs[7],
    )


def solution(mesh):
    whole = (P(),) * 14
    placed = (P(("twin", "dp"), None, None), P(("twin", "dp"), None)) + whole
    return jax.shard_map(
        body,
        mesh=mesh,
        in_specs=placed,
        out_specs=(
            P(("twin", "dp")),
            P(("twin", "dp"), None, None),
            P("dp", None),
            P("dp"),
            P("dp"),
            P("dp", None),
            P("dp"),
            P("dp"),
            P("dp"),
            P("dp", None),
            P("dp"),
            P("dp", None),
            P("dp"),
            P("dp"),
            P("dp"),
        ),
        check_vma=False,
    )
```

```python
import functools

import jax
import jax.numpy as jnp
from jax import lax
from jax.experimental import pallas as pl
from jax.experimental.pallas import tpu as pltpu
from jax.sharding import PartitionSpec as P

D = 768
HEADS = 12
HEAD_DIM = 64
FF = 3072
SEG = 8
QB = 128
MOST = 128
PAIRS = HEADS // 2
PW = 2 * HEAD_DIM

cosine_scale = 64.0
loss_scale = 32.0
norm_epsilon = 1e-12
unit_epsilon = 1e-06
masked_score = -1e30

F32 = jnp.float32
BF16 = jnp.bfloat16
VMEM = pltpu.VMEM
ANY = pl.ANY
MIB = 1 << 20


def nn(left, right):
    return lax.dot_general(left, right, (((1,), (0,)), ((), ())), preferred_element_type=F32)


def nt(left, right):
    return lax.dot_general(left, right, (((1,), (1,)), ((), ())), preferred_element_type=F32)


def tn(left, right):
    return lax.dot_general(left, right, (((0,), (0,)), ((), ())), preferred_element_type=F32)


def vspec():
    return pl.BlockSpec(memory_space=VMEM)


def sspec():
    return pl.BlockSpec(memory_space=pltpu.SMEM)


def hspec():
    return pl.BlockSpec(memory_space=pltpu.HBM)


def far(*values):
    return [pltpu.with_memory_space_constraint(value, pltpu.HBM) for value in values]


class Fetch:
    def __init__(self, sems, pairs):
        self.copies = [pltpu.make_async_copy(a, b, sems.at[i]) for i, (a, b) in enumerate(pairs)]
        for copy in self.copies:
            copy.start()

    def wait(self, *which):
        for i in which:
            self.copies[i].wait()


def carrying(kernel, n_in, n_out, n_carry):
    def wrapped(*refs):
        refs, sems = refs[:-1], refs[-1]
        ins, refs = refs[:n_in], refs[n_in:]
        sources, refs = refs[:n_carry], refs[n_carry:]
        outs, refs = refs[:n_out], refs[n_out:]
        targets, rest = refs[:n_carry], refs[n_carry:]
        fetch = Fetch(sems, tuple(zip(sources, targets)))
        kernel(*ins, *outs, *rest)
        fetch.wait(*range(n_carry))

    return wrapped


def carry_call(kernel, name, us, mib, operands, specs, outs, scratch, carry):
    n_carry = len(carry)
    return pl.pallas_call(
        carrying(kernel, len(operands), len(outs), n_carry),
        name=name,
        in_specs=list(specs) + [hspec()] * n_carry,
        out_specs=[vspec()] * (len(outs) + n_carry),
        out_shape=list(outs) + [VMEM(a.shape, a.dtype) for a in carry],
        scratch_shapes=list(scratch) + [pltpu.SemaphoreType.DMA((max(n_carry, 1),))],
        cost_estimate=took(us),
        compiler_params=params(mib),
    )(*operands, *far(*carry))


def fixed(shape):
    return pl.BlockSpec(shape, lambda *_: (0,) * len(shape))


def shape_of(shape, dtype):
    return jax.ShapeDtypeStruct(shape, dtype)


def params(mib):
    return pltpu.CompilerParams(vmem_limit_bytes=mib * MIB)


SCALE = 0.4


def took(us):
    return pl.CostEstimate(flops=int(us * SCALE * 1.15e9), bytes_accessed=0, transcendentals=0)


def windows(length):
    out, packed = [], 0
    for start in range(0, length, QB):
        low, high = max(0, start - MOST), min(length, start + QB + MOST)
        out.append((start, low, high, packed))
        packed += high - low
    return out, packed


def two_heads(pair):
    first = lax.broadcasted_iota(jnp.int32, pair.shape, 1) < HEAD_DIM
    zero = jnp.zeros((), pair.dtype)
    return jnp.concatenate([jnp.where(first, pair, zero), jnp.where(first, zero, pair)], axis=0)


def pick_heads(both):
    rows = both.shape[1] // 2
    return jnp.concatenate([both[:HEAD_DIM, :rows], both[HEAD_DIM:, rows:]], axis=0).T


def column_of(row):
    return jnp.broadcast_to(row, (8, row.shape[1])).T[:, :1]


def split_low(value):
    high = value.astype(BF16)
    return high, (value - high.astype(F32)).astype(BF16)


def normalise(value):
    middle = jnp.mean(value, axis=-1, keepdims=True)
    centered = value - middle
    spread = jnp.mean(centered * centered, axis=-1, keepdims=True)
    rstd = lax.rsqrt(spread + norm_epsilon)
    return centered * rstd, rstd


def vector(ref):
    return ref[...].astype(F32).reshape(1, ref.shape[0])


def softmax_down(own):
    top = jnp.max(own, axis=0, keepdims=True)
    weights = jnp.exp(own - top)
    total = jnp.sum(weights, axis=0, keepdims=True)
    return (weights * (1.0 / total)).astype(BF16)


def attend(length, qkv, bias, p_s, ctx_s):
    blocks, _ = windows(length)

    def lanes(part, h):
        return slice(part * D + h * PW, part * D + (h + 1) * PW)

    def score(h):
        q_all = qkv[:, lanes(0, h)] * jnp.asarray(HEAD_DIM**-0.5, BF16)
        k_all = qkv[:, lanes(1, h)]
        out = []
        for start, low, high, _ in blocks:
            out.append(nt(k_all[low:high], two_heads(q_all[start : start + QB])))
        return out, qkv[:, lanes(2, h)].T

    ahead = score(0)
    for h in range(PAIRS):
        scores, v_turned = ahead
        if h + 1 < PAIRS:
            ahead = score(h + 1)
        probs = []
        for own, (_, low, high, packed) in zip(scores, blocks):
            mask = bias[packed : packed + high - low, :]
            halves = [softmax_down(own[:, :QB] + mask), softmax_down(own[:, QB:] + mask)]
            probs.append(jnp.concatenate(halves, axis=1))
        for p, (_, low, high, packed) in zip(probs, blocks):
            p_s[h, packed : packed + high - low, :] = p
        outs = [nn(v_turned[:, low:high], p) for p, (_, low, high, _) in zip(probs, blocks)]
        ctx_s[:, lanes(0, h)] = jnp.concatenate([pick_heads(o.astype(BF16)) for o in outs], axis=0)


def forward_kernel(*refs):
    (hid_h, seg, wqkv_h, bq, bv, wout_h, bout, g1, b1, win_h, bin_, wdown_h, bdown, g2, b2) = refs[:15]
    outs, (unit_o, unitf_o, inv_o) = refs[15:25], refs[25:28]
    hid, wqkv, wout, win, wdown, bias_s, n1_s = refs[28:35]
    kept = refs[35:45]
    sems, osems = refs[45:47]
    qkv_s, p_s, ctx_s, nl_s, xh1_s, rs1_s, act_o, dg_o, xh2_o, rs2_o = kept
    rows = seg.shape[0]
    length = hid.shape[0] // rows
    blocks, _ = windows(length)
    toks = [slice(r * length, (r + 1) * length) for r in range(rows)]
    parts = [slice(part * D, (part + 1) * D) for part in range(3)]

    pairs = [(hid_h.at[toks[0]], hid.at[toks[0]])]
    pairs += [(wqkv_h.at[:, cols], wqkv.at[:, cols]) for cols in parts]
    first = Fetch(sems, pairs)
    later = []

    def fetch_rest():
        rest = [(wout_h, wout), (win_h, win), (wdown_h, wdown)]
        rest += [(hid_h.at[tok], hid.at[tok]) for tok in toks[1:]]
        for i, (source, target) in enumerate(rest):
            copy = pltpu.make_async_copy(source, target, sems.at[4 + i])
            copy.start()
            later.append(copy)

    def leaving(i, r):
        if i == 1:
            return pltpu.make_async_copy(p_s, outs[1].at[r], osems.at[r, 1])
        source = kept[i] if i in (0, 2) else kept[i].at[toks[r]]
        return pltpu.make_async_copy(source, outs[i].at[toks[r]], osems.at[r, i])

    seg_rows = [seg[r : r + 1, :].astype(F32) for r in range(rows)]

    def mask(r):
        seg_col = column_of(seg_rows[r])
        for start, low, high, packed in blocks:
            same = seg_col[low:high] == seg_rows[r][:, start : start + QB]
            bias_s[packed : packed + high - low, :] = jnp.where(same, 0.0, masked_score)

    def project(r):
        if r > 0:
            leaving(0, r - 1).wait()
            later[2 + r].wait()
        for part, cols in enumerate(parts):
            if r == 0:
                first.wait(*((0, 1) if part == 0 else (part + 1,)))
                if part == 0:
                    fetch_rest()
            value = nn(hid[toks[r], :], wqkv[:, cols])
            if part == 0:
                value = value + vector(bq)
            if part == 2:
                value = value + vector(bv)
            qkv_s[:, cols] = value.astype(BF16)
        leaving(0, r).start()

    def attention(r):
        if r > 0:
            leaving(1, r - 1).wait()
            leaving(2, r - 1).wait()
        attend(length, qkv_s, bias_s, p_s, ctx_s)
        leaving(1, r).start()
        leaving(2, r).start()

    def mix(r):
        if r == 0:
            later[0].wait()
        return nn(ctx_s[...], wout[...])

    def norm_one(r, attended):
        tok = toks[r]
        xhat, rstd = normalise(hid[tok, :].astype(F32) + (attended + vector(bout)))
        xh1_s[tok, :] = xhat.astype(BF16)
        rs1_s[tok, :] = jnp.broadcast_to(rstd, (length, rs1_s.shape[1]))
        n1 = xhat * vector(g1) + vector(b1)
        n1_s[tok, :] = n1
        nl_s[tok, :] = n1.astype(BF16)
        for i in (3, 4, 5):
            leaving(i, r).start()

    chunk = 768
    count = FF // chunk
    bias_in = vector(bin_)

    def rise(r, c):
        cols = slice(c * chunk, (c + 1) * chunk)
        return nn(nl_s[toks[r], :], win[:, cols]) + bias_in[:, cols]

    def bend(r, c, pre):
        cols = slice(c * chunk, (c + 1) * chunk)
        half = 0.5 + 0.5 * lax.erf(pre * 0.5**0.5)
        act_o[toks[r], cols] = (pre * half).astype(BF16)
        bell = jnp.exp(pre * pre * -0.5) * 0.3989422804014327
        dg_o[toks[r], cols] = (half + pre * bell).astype(BF16)

    def norm_two(r, fallen):
        tok = toks[r]
        xhat, rstd = normalise(n1_s[tok, :] + (fallen + vector(bdown)))
        xh2_o[tok, :] = xhat.astype(BF16)
        rs2_o[tok, :] = jnp.broadcast_to(rstd, (length, rs2_o.shape[1]))
        leaving(8, r).start()
        leaving(9, r).start()
        out = xhat * vector(g2) + vector(b2)
        index = lax.broadcasted_iota(jnp.int32, (SEG, length), 0).astype(F32)
        member = (index == seg_rows[r]).astype(F32)
        counts = jnp.sum(member, axis=1, keepdims=True)
        high, low = split_low(out)
        member = member.astype(BF16)
        pooled = (nn(member, high) + nn(member, low)) / counts
        inv = lax.rsqrt(jnp.mean(pooled * pooled, axis=-1, keepdims=True) + unit_epsilon)
        unit = pooled * inv
        unitf_o[r] = unit
        unit_o[r] = unit.astype(BF16)
        inv_o[r] = jnp.broadcast_to(inv / counts, inv_o.shape[1:])

    mixed = None
    for r in range(rows):
        mask(r)
        project(r)
        if r > 0:
            norm_one(r - 1, mixed)
        attention(r)
        mixed = mix(r)
    steps = [(r, c) for r in range(rows) for c in range(count)]
    later[1].wait()
    if rows > 1:
        ahead = rise(0, 0)
        norm_one(rows - 1, mixed)
    else:
        norm_one(0, mixed)
        ahead = rise(0, 0)
    fallen = None
    for i, (r, c) in enumerate(steps):
        pre = ahead
        if i + 1 < len(steps):
            ahead = rise(*steps[i + 1])
        bend(r, c, pre)
        if c == 1 and fallen is not None:
            norm_two(r - 1, fallen)
        if c == count - 1:
            if r == 0:
                later[2].wait()
            leaving(6, r).start()
            leaving(7, r).start()
            fallen = nn(act_o[toks[r], :], wdown[...])
    norm_two(rows - 1, fallen)
    for r in range(rows):
        for i in range(10):
            if r == rows - 1 or i > 2:
                leaving(i, r).wait()


def forward(hidden, seg, weights):
    rows, length, _ = hidden.shape
    tokens = rows * length
    _, packed = windows(length)
    packed_shape = (PAIRS, packed, 2 * QB)
    far_shapes = [((tokens, 3 * D), BF16), ((rows,) + packed_shape, BF16)]
    far_shapes += [((tokens, D), BF16)] * 3 + [((tokens, 128), F32)]
    after = [((tokens, FF), BF16)] * 2 + [((tokens, D), BF16), ((tokens, 128), F32)]
    far_shapes += after
    near_shapes = [((rows, SEG, D), BF16), ((rows, SEG, D), F32), ((rows, SEG, 128), F32)]
    kept = [VMEM((length, 3 * D), BF16), VMEM(packed_shape, BF16), VMEM((length, D), BF16)]
    kept += [VMEM((tokens, D), BF16), VMEM((tokens, D), BF16), VMEM((tokens, 128), F32)]
    kept += [VMEM(*a) for a in after]
    large = (0, 3, 7, 9)
    hbm = hspec()
    return pl.pallas_call(
        forward_kernel,
        name="forward",
        in_specs=[hbm, vspec()] + [hbm if i in large else vspec() for i in range(13)],
        out_specs=[hbm] * 10 + [vspec()] * 3,
        out_shape=[pltpu.HBM(*a) for a in far_shapes] + [VMEM(*a) for a in near_shapes],
        scratch_shapes=[VMEM((tokens, D), BF16)]
        + [VMEM(weights[i].shape, BF16) for i in large]
        + [VMEM((packed, QB), F32), VMEM((tokens, D), F32)]
        + kept
        + [pltpu.SemaphoreType.DMA((7 + rows,)), pltpu.SemaphoreType.DMA((rows, 10))],
        cost_estimate=took(33),
        compiler_params=params(58),
    )(*far(hidden.reshape(tokens, D), seg, *weights))


def loss_kernel(flips, idx, *refs):
    pieces, refs = refs[: len(flips)], refs[len(flips) :]
    targets, seg, g2, unitf, inv, xh2, rs2, loss_o, gb_o, vec_o, slope_s, rows_s, units = refs
    twin, me = idx[0], idx[1]
    count = units.shape[0] // 2
    sentences = unitf.shape[0]
    for piece, own_flips in zip(pieces, flips):
        if own_flips is None:
            units[...] = piece[...]
            continue
        for i, (twin_flip, flip) in enumerate(own_flips):
            at = (twin ^ twin_flip) * count + (me ^ flip) * sentences
            at = pl.multiple_of(at, sentences)
            units[pl.ds(at, sentences), :] = piece[i * sentences : (i + 1) * sentences, :]
    rows, length = seg.shape
    step = min(count, 256)
    factor = cosine_scale / D
    positives = units.at[pl.ds(count, count)]
    own = pl.ds(pl.multiple_of(me * sentences, sentences), sentences)

    def one_block(i, carry):
        lanes = pl.ds(pl.multiple_of(i * step, step), step)
        sims = nt(positives[...], units[lanes, :]) * factor
        top = jnp.max(sims, axis=0, keepdims=True)
        weights = jnp.exp(sims - top)
        total = jnp.sum(weights, axis=0, keepdims=True)
        hit = lax.broadcasted_iota(jnp.int32, sims.shape, 0) == targets[:, lanes]
        picked = jnp.sum(jnp.where(hit, sims, 0.0), axis=0, keepdims=True)
        loss_o[:, lanes] = top + jnp.log(total) - picked
        slope = loss_scale * (weights * (1.0 / total) - hit.astype(F32))
        slope_s[:, lanes] = slope.astype(BF16)
        return carry

    if count == step:
        one_block(0, 0)
    else:
        lax.fori_loop(0, count // step, one_block, 0)

    @pl.when(twin == 0)
    def _():
        def part(i, carry):
            lanes = pl.ds(pl.multiple_of(i * step, step), step)
            rows_s[lanes, :] = tn(slope_s[:, lanes], positives[...])
            return carry

        lax.fori_loop(0, count // step, part, 0)
        rows_s[pl.ds(0, sentences), :] = rows_s[own, :]

    @pl.when(twin == 1)
    def _():
        rows_s[pl.ds(0, sentences), :] = nn(slope_s[own, :], units[pl.ds(0, count), :])

    gu = rows_s[pl.ds(0, sentences), :] * factor
    unit = unitf[...]
    gs = inv[:, :1] * (gu - unit * jnp.mean(gu * unit, axis=-1, keepdims=True))
    gy = gs * vector(g2)
    u = gy - jnp.mean(gy, axis=-1, keepdims=True)
    gain = jnp.zeros((1, D), F32)
    shift = jnp.zeros((1, D), F32)
    summed = jnp.zeros((1, D), F32)
    for r in range(rows):
        part = slice(r * SEG, (r + 1) * SEG)
        tok = slice(r * length, (r + 1) * length)
        seg_row = seg[r : r + 1, :]
        hits = lax.broadcasted_iota(jnp.int32, (SEG, length), 0) == seg_row
        member = hits.astype(F32).astype(BF16)
        counts = jnp.sum(hits.astype(F32), axis=1, keepdims=True)
        xhat_low = xh2[tok, :]
        gain += jnp.sum(nn(member, xhat_low) * gs[part], axis=0, keepdims=True)
        shift += jnp.sum(counts * gs[part], axis=0, keepdims=True)
        xhat = xhat_low.astype(F32)
        high, low = split_low(u[part])
        spread = tn(member, high) + tn(member, low)
        inner = jnp.mean(spread * xhat, axis=-1, keepdims=True)
        grad = rs2[tok, :1] * (spread - xhat * inner)
        grad_low = grad.astype(BF16)
        gb_o[tok, :] = grad_low
        summed += jnp.sum(grad_low.astype(F32), axis=0, keepdims=True)
    vec_o[...] = jnp.concatenate([summed, gain, shift, jnp.zeros((5, D), F32)], axis=0)


def loss_stage(idx, gathered, targets, unitf, inv, seg, g2, xh2, rs2, carry):
    pieces, flips = gathered
    tokens = xh2.shape[0]
    count = targets.shape[1]
    return carry_call(
        functools.partial(loss_kernel, flips),
        "loss",
        4,
        20 if count <= 256 else 44,
        (idx, *pieces, *far(targets, seg, g2), unitf, inv, xh2, rs2),
        [sspec()] + [vspec()] * (7 + len(pieces)),
        [shape_of((1, count), F32), shape_of((tokens, D), BF16), shape_of((8, D), F32)],
        [VMEM((count, count), BF16), VMEM((count, D), F32), VMEM((2 * count, D), BF16)],
        carry,
    )


def pre_kernel(gb, wdown, dg, out):
    n = 768

    def product(j):
        return nt(gb[...], wdown[j * n : (j + 1) * n, :])

    ahead = product(0)
    for j in range(FF // n):
        value = ahead
        if j + 1 < FF // n:
            ahead = product(j + 1)
        part = slice(j * n, (j + 1) * n)
        out[:, part] = (value * dg[:, part].astype(F32)).astype(BF16)


def pre_stage(gb, wdown, dg, carry):
    outs = [VMEM(dg.shape, BF16)]
    return carry_call(
        pre_kernel, "grad_pre", 5.2, 24, (gb, wdown, dg), [vspec()] * 3, outs, [], carry
    )


def normed_kernel(gp, win, gb, xh1, rs1, g1, wout, ga_o, gc_o, vec_o):
    m = 512
    count = gp.shape[0] // m
    gain, shift, summed = [jnp.zeros((1, D), F32) for _ in range(3)]
    grads = [nt(gp[i * m : (i + 1) * m, :], win[...]) for i in range(count)]
    for i in range(count):
        rows = slice(i * m, (i + 1) * m)
        grad = grads[i] + gb[rows, :].astype(F32)
        xhat = xh1[rows, :].astype(F32)
        gain += jnp.sum(grad * xhat, axis=0, keepdims=True)
        shift += jnp.sum(grad, axis=0, keepdims=True)
        gy = grad * vector(g1)
        inner = jnp.mean(gy * xhat, axis=-1, keepdims=True)
        total = rs1[rows, :1] * (gy - jnp.mean(gy, axis=-1, keepdims=True) - xhat * inner)
        low = total.astype(BF16)
        ga_o[rows, :] = low
        summed += jnp.sum(low.astype(F32), axis=0, keepdims=True)
    for i in range(count):
        rows = slice(i * m, (i + 1) * m)
        gc_o[rows, :] = nt(ga_o[rows, :], wout[...]).astype(BF16)
    vec_o[...] = jnp.concatenate([summed, gain, shift, jnp.zeros((5, D), F32)], axis=0)


def normed_stage(gp, win, gb, xh1, rs1, g1, wout, carry):
    tokens = gp.shape[0]
    outs = [shape_of((tokens, D), BF16), shape_of((tokens, D), BF16), shape_of((8, D), F32)]
    operands = (gp, win, gb, xh1, rs1, *far(g1), wout)
    return carry_call(
        normed_kernel, "grad_normed", 9, 28, operands, [vspec()] * 7, outs, [], carry
    )


def attend_back_kernel(q_ref, k_ref, v_ref, g_ref, p_ref, out_ref):
    length = q_ref.shape[0]
    blocks, _ = windows(length)
    group = q_ref.shape[1] // PW
    scale = HEAD_DIM**-0.5
    loaded, grads = [], []
    for h in range(group):
        lanes = slice(h * PW, (h + 1) * PW)
        q2 = [two_heads(q_ref[b[0] : b[0] + QB, lanes]) for b in blocks]
        g2 = [two_heads(g_ref[b[0] : b[0] + QB, lanes]) for b in blocks]
        loaded.append((q2, g2, k_ref[:, lanes].T))
        v_all = v_ref[:, lanes]
        grads.append([nt(v_all[b[1] : b[2]], g) for b, g in zip(blocks, g2)])
    slopes = []
    for h in range(group):
        own = []
        for gp, (_, low, high, packed) in zip(grads[h], blocks):
            p = p_ref[h, packed : packed + high - low, :].astype(F32)
            weighted = p * gp
            inner = jnp.sum(weighted, axis=0, keepdims=True)
            own.append((weighted - p * inner).astype(BF16))
        slopes.append(own)

    def gather(parts):
        out = []
        for block in range(len(blocks)):
            total = None
            for part, (_, low, high, _) in zip(parts, blocks):
                base = block * QB - low
                if 0 <= base < high - low:
                    piece = part[base : base + QB]
                    total = piece if total is None else total + piece
            out.append(total)
        return jnp.concatenate(out, axis=0)

    for h in range(group):
        lanes = slice(h * PW, (h + 1) * PW)
        q2, g2, k_turned = loaded[h]
        dq = [nn(k_turned[:, b[1] : b[2]], s) for b, s in zip(blocks, slopes[h])]
        dv = [nn(p_ref[h, b[3] : b[3] + b[2] - b[1], :], g) for b, g in zip(blocks, g2)]
        dk = [nn(s, q) for s, q in zip(slopes[h], q2)]
        turned = [pick_heads((part * scale).astype(BF16)) for part in dq]
        out_ref[0, :, lanes] = jnp.concatenate(turned, axis=0)
        out_ref[1, :, lanes] = (gather(dk) * scale).astype(BF16)
        out_ref[2, :, lanes] = gather(dv).astype(BF16)


def attend_back(qkv, grad_context, probs, rows, length, first, pairs):
    _, packed = windows(length)
    group = 2
    steps = pairs // group
    base = first // group
    width = group * PW

    def block(part):
        return pl.BlockSpec((length, width), lambda r, h: (r, part * (D // width) + base + h))

    return pl.pallas_call(
        attend_back_kernel,
        name="attend_back",
        grid=(rows, steps),
        in_specs=[
            block(0),
            block(1),
            block(2),
            block(0),
            pl.BlockSpec((None, group, packed, 2 * QB), lambda r, h: (r, base + h, 0, 0)),
        ],
        out_specs=pl.BlockSpec((3, length, width), lambda r, h: (0, r, h)),
        out_shape=shape_of((3, rows * length, pairs * PW), BF16),
        cost_estimate=took(2.0 * pairs),
        compiler_params=params(20),
    )(*far(qkv, qkv, qkv), grad_context, *far(probs))


def hidden_kernel(da, db, wqkv, ga, out):
    m = 512
    for i in range(ga.shape[0] // m):
        rows = slice(i * m, (i + 1) * m)
        total = ga[rows, :].astype(F32)
        for part in range(3):
            both = jnp.concatenate([da[part, rows, :], db[part, rows, :]], axis=1)
            total = total + nt(both, wqkv[:, part * D : (part + 1) * D])
        out[rows, :] = total.astype(BF16)


def hidden_stage(da, db, wqkv, ga):
    return pl.pallas_call(
        hidden_kernel,
        name="hidden_grad",
        in_specs=[vspec()] * 4,
        out_specs=vspec(),
        out_shape=shape_of(ga.shape, BF16),
        cost_estimate=took(5.7),
        compiler_params=params(22),
    )(da, db, wqkv, ga)


def place_of(half, quarter, owner):
    c, y, z0, z1 = owner & 1, (owner >> 1) & 1, (owner >> 2) & 1, owner >> 3
    order = (quarter, y, z0, z1, c) if half == 0 else (y, z0, z1, quarter, c)
    out = 0
    for bit in order:
        out = 2 * out + bit
    return out


def lanes_of(width):
    most = 128 if width <= 256 else 256
    return [(low, min(most, width - low)) for low in range(0, width, most)]


def half_shapes(width):
    shapes = [shape_of((32, 48, width), BF16)]
    return shapes + [shape_of((32, 48, n), BF16) for _, n in lanes_of(width)]


def store_piece(first, keep, sends, quarter, owner, piece_a, piece_b):
    at_a, at_b = place_of(0, quarter, owner), place_of(1, quarter, owner)
    keep[jnp.where(first, at_a, at_b)] = jnp.where(first, piece_a, piece_b)
    other = jnp.where(first, piece_b, piece_a)
    at = jnp.where(first, at_b, at_a)
    for send, (low, n) in zip(sends, lanes_of(keep.shape[2])):
        send[at] = other[:, low : low + n]


def down_kernel(idx, act, gb, keep, *sends):
    first = idx[2] == 0
    n = 768

    def product(j):
        return tn(act[:, j * n : (j + 1) * n], gb[...])

    ahead = product(0)
    for j in range(FF // n):
        total = ahead.astype(BF16)
        if j + 1 < FF // n:
            ahead = product(j + 1)
        for local in range(4):
            for quarter in range(2):
                base = local * 192 + quarter * 48
                a, b = total[base : base + 48], total[base + 96 : base + 144]
                store_piece(first, keep, sends, quarter, 4 * j + local, a, b)


def down_stage(idx, act, gb):
    shapes = half_shapes(D)
    return pl.pallas_call(
        down_kernel,
        name="grad_w_down",
        in_specs=[sspec(), vspec(), vspec()],
        out_specs=[vspec()] * len(shapes),
        out_shape=shapes,
        cost_estimate=took(7.5),
        compiler_params=params(22),
    )(idx, act, gb)


def in_kernel(idx, n1, gp, vec_o, keep, *refs):
    sends, turned = refs[:-1], refs[-1]
    first = idx[2] == 0
    turned[...] = n1[...].T

    def products(quarter):
        out = []
        for half in range(2):
            j = 2 * half + quarter
            out.append(nn(turned[...], gp[:, j * D : (j + 1) * D]))
        return out

    ahead = products(0)
    for quarter in range(2):
        a, b = [part.astype(BF16) for part in ahead]
        if quarter == 0:
            ahead = products(1)
        for owner in range(16):
            rows = slice(owner * 48, (owner + 1) * 48)
            store_piece(first, keep, sends, quarter, owner, a[rows], b[rows])
    vec_o[...] = jnp.sum(gp[...].astype(F32), axis=0, keepdims=True)


def in_stage(idx, n1, gp):
    shapes = half_shapes(D)
    return pl.pallas_call(
        in_kernel,
        name="grad_w_in",
        in_specs=[sspec(), vspec(), vspec()],
        out_specs=[vspec()] * (1 + len(shapes)),
        out_shape=[shape_of((1, FF), F32)] + shapes,
        scratch_shapes=[VMEM((D, n1.shape[0]), BF16)],
        cost_estimate=took(7.4),
        compiler_params=params(24),
    )(idx, n1, gp)


WIDE, NARROW = 640, 256


def store_all(first, keep, send, whole, width):
    for quarter in range(2):
        a = whole[:, quarter * width : (quarter + 1) * width]
        b = whole[:, (2 + quarter) * width : (3 + quarter) * width]
        for owner in range(16):
            rows = slice(owner * 48, (owner + 1) * 48)
            store_piece(first, keep, send, quarter, owner, a[rows], b[rows])


def wide_kernel(idx, hid, da, ctx, ga, turned_o, keep, *refs):
    sends, whole = refs[:-1], refs[-1]
    n = da.shape[2]
    turned_o[...] = hid[...].T
    for part in range(3):
        whole[:, part * n : (part + 1) * n] = nn(turned_o[...], da[part]).astype(BF16)
    whole[:, 3 * n : 3 * n + D] = tn(ctx[...], ga[...]).astype(BF16)
    whole[:, 3 * n + D :] = jnp.zeros((D, 4 * WIDE - 3 * n - D), BF16)
    store_all(idx[2] == 0, keep, sends, whole, WIDE)


def wide_stage(idx, hid, da, ctx, ga):
    shapes = half_shapes(WIDE)
    return pl.pallas_call(
        wide_kernel,
        name="grad_w_wide",
        in_specs=[sspec()] + [vspec()] * 4,
        out_specs=[vspec()] * (1 + len(shapes)),
        out_shape=[shape_of((D, hid.shape[0]), BF16)] + shapes,
        scratch_shapes=[VMEM((D, 4 * WIDE), BF16)],
        cost_estimate=took(6),
        compiler_params=params(24),
    )(idx, hid, da, ctx, ga)


def narrow_kernel(idx, turned, da, db, vec1, vec2, bias, keep, *refs):
    send, (whole, sums_s) = refs[:-2], refs[-2:]
    n = db.shape[2]
    for part in range(3):
        whole[:, part * n : (part + 1) * n] = nn(turned[...], db[part]).astype(BF16)
    sums_s[...] = jnp.zeros_like(sums_s)
    sums_s[2:5, :] = vec1[0:3, :]
    sums_s[5:8, :] = vec2[0:3, :]
    for row, part in ((0, 0), (1, 2)):
        for base, grads in ((0, da), (D - n, db)):
            lanes = slice(base, base + grads.shape[2])
            total = jnp.sum(grads[part].astype(F32), axis=0, keepdims=True)
            sums_s[row : row + 1, lanes] = total
    small = sums_s[...].T
    groups = [bias[:, i * 384 : (i + 1) * 384] for i in range(FF // 384)]
    folded = jnp.concatenate(groups, axis=0)
    turned_bias = [folded[:, i * 48 : (i + 1) * 48].T for i in range(8)]
    lane = lax.broadcasted_iota(jnp.int32, (48, 128), 1)
    for owner in range(16):
        own = small[owner * 48 : (owner + 1) * 48]
        for k in range(4):
            column = turned_bias[4 * (owner % 2) + k][:, owner // 2 : owner // 2 + 1]
            own = jnp.where(lane == 8 + k, column, own)
        whole[owner * 48 : (owner + 1) * 48, 3 * n : 3 * n + 128] = own.astype(BF16)
    whole[:, 3 * n + 128 :] = jnp.zeros((D, 4 * NARROW - 3 * n - 128), BF16)
    store_all(idx[2] == 0, keep, send, whole, NARROW)


def narrow_stage(idx, turned, da, db, vec1, vec2, bias):
    return pl.pallas_call(
        narrow_kernel,
        name="grad_w_narrow",
        in_specs=[sspec()] + [vspec()] * 6,
        out_specs=[vspec()] * len(half_shapes(NARROW)),
        out_shape=half_shapes(NARROW),
        scratch_shapes=[VMEM((D, 4 * NARROW), BF16), VMEM((128, D), F32)],
        cost_estimate=took(2.4),
        compiler_params=params(22),
    )(idx, turned, da, db, vec1, vec2, bias)


def swap_dp(value, flip):
    devices = lax.axis_size("dp")
    return lax.ppermute(value, "dp", [(i, i ^ flip) for i in range(devices)])


def swap_twin(value):
    return lax.ppermute(value, "twin", [(0, 1), (1, 0)])


TWIN = 16
ROUTES = ((TWIN, 2, 4, 8, TWIN), (2, 4, 8, TWIN, TWIN))


def step_swap(value, step):
    pairs = [(i, i ^ ROUTES[i & 1][step]) for i in range(2 * TWIN)]
    return lax.ppermute(value, ("twin", "dp"), pairs)


def plus(*values):
    total = values[0].astype(F32)
    for value in values[1:]:
        total = total + value.astype(F32)
    return total.astype(BF16)


def call_small(kernel, name, idx, operands, outs):
    return pl.pallas_call(
        kernel,
        name=name,
        in_specs=[sspec()] + [vspec()] * len(operands),
        out_specs=[vspec()] * len(outs),
        out_shape=[shape_of(shape, dtype) for shape, dtype in outs],
        cost_estimate=took(2.4),
        compiler_params=params(12),
    )(idx, *operands)


def half_kernel(step, idx, keep, recv, keep_o, send_o):
    count = keep_o.shape[0]
    bit = idx[3 + step]
    mine = pl.ds(bit * count, count)
    other = pl.ds((1 - bit) * count, count)
    keep_o[...] = plus(keep[mine], recv[mine])
    send_o[...] = plus(keep[other], recv[other])


def half_step(idx, step, keep, recv):
    count, rows, width = keep.shape
    shape = (count // 2, rows, width)
    kernel = functools.partial(half_kernel, step)
    return call_small(kernel, "sum_" + str(step), idx, (keep, recv), [(shape, BF16)] * 2)


def core_kernel(idx, keep, *refs):
    recvs, (keep_o, send_o) = refs[:-2], refs[-2:]
    bit = idx[3]
    for recv, (low, n) in zip(recvs, lanes_of(keep.shape[3])):
        lanes = slice(low, low + n)
        keep_o[:, :, lanes] = plus(keep[bit, :, :, lanes], recv[bit])
        send_o[:, :, lanes] = plus(keep[1 - bit, :, :, lanes], recv[1 - bit])


def core_step(idx, keep, recvs):
    count, rows, width = keep.shape
    half = count // 2
    pieces = 4
    part = half // pieces

    def spec(n):
        return pl.BlockSpec((2, part, rows, n), lambda i: (0, i, 0, 0))

    return pl.pallas_call(
        core_kernel,
        name="sum_core",
        grid=(pieces,),
        in_specs=[sspec(), spec(width)] + [spec(n) for _, n in lanes_of(width)],
        out_specs=[pl.BlockSpec((part, rows, width), lambda i: (i, 0, 0))] * 2,
        out_shape=[shape_of((half, rows, width), BF16)] * 2,
        cost_estimate=took(1.7),
        compiler_params=params(10),
    )(
        idx,
        keep.reshape(2, half, rows, width),
        *[recv.reshape(2, half, rows, recv.shape[2]) for recv in recvs],
    )


def own_kernel(idx, keep, recv, out):
    out[...] = plus(keep[...], recv[...])


def turn_kernel(idx, own, other, keep_o, send_o):
    twin, core = idx[0], idx[2]
    keep_o[twin] = own[core]
    keep_o[1 - twin] = other[core]
    send_o[twin] = own[1 - core]
    send_o[1 - twin] = other[1 - core]


class Order:
    def __init__(self):
        self.last = None

    def after(self, value, *others):
        if self.last is None:
            return value
        return lax.optimization_barrier((value, self.last) + others)[0]

    def done(self, value):
        self.last = value
        return value


class Exchange:
    def __init__(self, order, idx, keep, sends):
        self.order, self.idx, self.step = order, idx, 0
        self.keep, self.recv = keep, [swap_dp(send, 1) for send in sends]

    def advance(self):
        idx, order = self.idx, self.order
        keep, recv = order.after(self.keep), self.recv
        if self.step == 0:
            keep, send = core_step(idx, keep, recv)
            recv = step_swap(send, 0)
        elif self.step < 4:
            keep, send = half_step(idx, self.step, keep, recv)
            recv = step_swap(send, self.step)
        elif self.step == 4:
            shape = keep.shape
            (keep,) = call_small(own_kernel, "sum_4", idx, (keep, recv), [(shape, BF16)])
            recv = step_swap(keep, 4)
        else:
            shape = keep.shape
            keep, send = call_small(turn_kernel, "turn", idx, (keep, recv), [(shape, BF16)] * 2)
            recv = swap_dp(send, 1)
        order.done(keep)
        self.keep, self.recv = keep, recv
        self.step += 1

    def result(self):
        return self.keep, self.recv


def bring_kernel(*refs):
    del refs


def bring(values):
    return carry_call(bring_kernel, "bring", 1.2, 4, (), [], [], [], values)


def gather_units(unit, wanted):
    flips = [(0, 0)]
    for flip in (8, 4):
        unit = jnp.concatenate([unit, swap_dp(unit, flip)], axis=0)
        flips = flips + [(t, f ^ flip) for t, f in flips]
    wanted = bring((lax.optimization_barrier((wanted[0], unit))[0],) + wanted[1:])
    pairs = [(i, i ^ (TWIN + 2)) for i in range(2 * TWIN)]
    corner = lax.ppermute(unit, ("twin", "dp"), pairs)
    unit = jnp.concatenate([unit, swap_dp(unit, 2), swap_twin(unit), corner], axis=0)
    flips = [(t ^ a, f ^ b) for a, b in ((0, 0), (0, 2), (1, 0), (1, 2)) for t, f in flips]
    return ((unit, swap_dp(unit, 1)), (flips, [(t, f ^ 1) for t, f in flips])), wanted


def four_quarters(idx, keep, recv):
    first = idx[2] == 0
    low = [jnp.where(first, keep[i], recv[i]) for i in range(2)]
    high = [jnp.where(first, recv[i], keep[i]) for i in range(2)]
    return low + high


def final_in_kernel(idx, keep, recv, out):
    for i, part in enumerate(four_quarters(idx, keep, recv)):
        out[:, i * D : (i + 1) * D] = part.astype(F32)


def final_down_kernel(idx, keep, recv, out):
    for i, part in enumerate(four_quarters(idx, keep, recv)):
        out[i * 48 : (i + 1) * 48, :] = part.astype(F32)


def final_last_kernel(idx, wide_k, wide_r, narrow_k, narrow_r, qkv_o, out_o, vec_o):
    wide = jnp.concatenate(four_quarters(idx, wide_k, wide_r), axis=1).astype(F32)
    narrow = jnp.concatenate(four_quarters(idx, narrow_k, narrow_r), axis=1).astype(F32)
    low, high = 2 * D // 3, D // 3
    for part in range(3):
        qkv_o[:, part * D : part * D + low] = wide[:, part * low : (part + 1) * low]
        qkv_o[:, part * D + low : (part + 1) * D] = narrow[:, part * high : (part + 1) * high]
    out_o[...] = wide[:, 3 * low : 3 * low + D]
    small = narrow[:, 3 * high : 3 * high + 128]
    vec_o[...] = jnp.concatenate([small, jnp.zeros((80, 128), F32)], axis=0).T[:16]


def finish(order, idx, kernel, name, chunks, outs):
    operands = [value for chunk in chunks for value in chunk.result()]
    operands[0] = order.after(operands[0])
    out = call_small(kernel, name, idx, operands, outs)
    order.done(out[0])
    return out


def add_low(*parts):
    return lax.optimization_barrier(plus(*parts))


def digits_of(devices):
    out, rest = [], devices // 2
    while rest > 1:
        size = 4 if rest % 4 == 0 else 2
        out.append(size)
        rest //= size
    return out


def pick(value, index, axis):
    return lax.dynamic_index_in_dim(value, index, axis, keepdims=False)


def scatter(grad):
    devices = lax.axis_size("dp")
    me = lax.axis_index("dp")
    value = grad.reshape(devices, grad.shape[0] // devices, grad.shape[1])
    unit = 1
    for size in [2] + digits_of(devices):
        mine = (me // unit) % size
        view = value.reshape((value.shape[0] // size, size) + value.shape[1:])
        parts = [pick(view, mine, 1)]
        for flip in range(1, size):
            parts.append(swap_dp(pick(view, mine ^ flip, 1), flip * unit))
        value = add_low(*parts)
        unit *= size
    value = value[0]
    return value.astype(F32) + swap_twin(value).astype(F32)


SEQUENCE = (
    "down", "pre", "d", "in", "normed", "i", "d", "attend_a", "d", "wide", "i", "attend_b", "w",
    "d", "narrow", "i", "hidden", "n", "d", "w", "i", "n", "d", "w", "i", "n", "final_d", "i",
    "w", "n", "final_i", "w", "n", "w", "n",
)


def body(
    hidden,
    segment_ids,
    targets,
    w_qkv,
    b_query,
    b_value,
    w_out,
    b_out,
    ln1_gain,
    ln1_bias,
    w_in,
    b_in,
    w_down,
    b_down,
    ln2_gain,
    ln2_bias,
):
    row_count, length, width = hidden.shape
    tokens = row_count * length
    devices = lax.axis_size("dp")
    everyone = lax.axis_size(("twin", "dp"))
    me = lax.axis_index("dp")
    twin = lax.axis_index("twin")
    core, y, z0, z1 = me & 1, (me >> 1) & 1, (me >> 2) & 1, me >> 3
    first = core == 0
    bits = [jnp.where(first, a, b) for a, b in ((twin, y), (y, z0), (z0, z1), (z1, twin))]
    idx = jnp.stack([twin, me, core] + bits).astype(jnp.int32)
    weights = (w_qkv, b_query, b_value, w_out, b_out, ln1_gain, ln1_bias)
    weights += (w_in, b_in, w_down, b_down, ln2_gain, ln2_bias)
    qkv, probs, ctx, n1, xh1, rs1, act, dg, xh2, rs2, unit, unitf, inv = forward(
        hidden, segment_ids, weights
    )
    sentences = row_count * SEG
    unit = unit.reshape(sentences, width)
    direct = devices == TWIN and sentences == 16
    if direct:
        gathered, (xh2, rs2) = gather_units(unit, (xh2, rs2))
    else:
        gathered = ((lax.all_gather(unit, ("twin", "dp"), axis=0, tiled=True),), (None,))
    losses, gb, vec2, act_near = loss_stage(
        idx,
        gathered,
        targets.reshape(1, -1),
        unitf.reshape(sentences, width),
        inv.reshape(sentences, 128),
        segment_ids,
        ln2_gain,
        xh2,
        rs2,
        (act,),
    )
    share = losses.shape[1] // everyone
    losses = lax.dynamic_slice_in_dim(
        losses[0], lax.axis_index(("twin", "dp")) * share, share, 0
    )
    flat = hidden.reshape(tokens, width)
    if direct:
        order = Order()
        chunks = {}

        def begin(name, keep, sends):
            order.done(keep)
            chunks[name] = Exchange(order, idx, keep, sends)

        for stage in SEQUENCE:
            if stage == "down":
                halves_d = down_stage(idx, act_near, order.after(gb))
                begin("d", halves_d[0], halves_d[1:])
            elif stage == "pre":
                near = (n1, xh1, rs1)
                gp, *near = pre_stage(order.after(gb), w_down, dg, near)
                order.done(gp)
            elif stage == "in":
                sums, *halves_in = in_stage(idx, near[0], order.after(gp))
                begin("i", halves_in[0], halves_in[1:])
            elif stage == "normed":
                ga, gc, vec1, *later = normed_stage(
                    order.after(gp), w_in, gb, near[1], near[2], ln1_gain, w_out, (flat, ctx)
                )
                order.done(ga)
            elif stage == "attend_a":
                da = order.done(attend_back(qkv, order.after(gc), probs, row_count, length, 0, 4))
            elif stage == "attend_b":
                db = order.done(attend_back(qkv, order.after(gc), probs, row_count, length, 4, 2))
            elif stage == "wide":
                turned, *halves_w = wide_stage(idx, later[0], order.after(da), later[1], ga)
                begin("w", halves_w[0], halves_w[1:])
            elif stage == "narrow":
                halves_n = narrow_stage(idx, turned, da, order.after(db), vec1, vec2, sums)
                begin("n", halves_n[0], halves_n[1:])
            elif stage == "hidden":
                hidden_grad = order.done(hidden_stage(da, order.after(db), w_qkv, ga))
            elif stage == "final_d":
                outs = [((192, D), F32)]
                (grad_w_down,) = finish(order, idx, final_down_kernel, stage, [chunks["d"]], outs)
            elif stage == "final_i":
                outs = [((48, FF), F32)]
                (grad_w_in,) = finish(order, idx, final_in_kernel, stage, [chunks["i"]], outs)
            else:
                chunks[stage].advance()
        wide, narrow = chunks["w"], chunks["n"]
        shapes = [((48, 3 * D), F32), ((48, D), F32), ((16, 128), F32)]
        grad_w_qkv, grad_w_out, vec = finish(
            order, idx, final_last_kernel, "final_last", [wide, narrow], shapes
        )
        vec = vec[:, :48]
        vecs = [vec[i] for i in range(8)]
        grad_b_in = vec[8:12].reshape(-1)
    else:
        gp, _ = pre_stage(gb, w_down, dg, (n1,))
        ga, gc, vec1, _ = normed_stage(gp, w_in, gb, xh1, rs1, ln1_gain, w_out, (ctx,))
        da = attend_back(qkv, gc, probs, row_count, length, 0, 4)
        db = attend_back(qkv, gc, probs, row_count, length, 4, 2)
        hidden_grad = hidden_stage(da, db, w_qkv, ga)
        dqkv = jnp.concatenate([da, db], axis=2)
        grad_w_down = scatter(tn(act, gb).astype(BF16))
        grad_w_in = scatter(tn(n1, gp).astype(BF16))
        wide = jnp.concatenate([dqkv[0], dqkv[1], dqkv[2]], axis=1)
        grad_w_qkv = scatter(tn(flat, wide).astype(BF16))
        grad_w_out = scatter(tn(ctx, ga).astype(BF16))
        sums = jnp.sum(dqkv, axis=1, dtype=F32)
        vec = jnp.concatenate([sums[0:1], sums[2:3], vec1[:3], vec2[:3]])
        vec = scatter(jnp.pad(vec, ((0, 120), (0, 0))).T.astype(BF16)).T
        vecs = [vec[i] for i in range(8)]
        bias = jnp.sum(gp, axis=0, dtype=F32)
        grad_b_in = scatter(jnp.broadcast_to(bias[:, None], (FF, 128)).astype(BF16))[:, 0]
    return (
        losses,
        hidden_grad.reshape(row_count, length, width),
        grad_w_qkv,
        vecs[0],
        vecs[1],
        grad_w_out,
        vecs[2],
        vecs[3],
        vecs[4],
        grad_w_in,
        grad_b_in,
        grad_w_down,
        vecs[5],
        vecs[6],
        vecs[7],
    )


def solution(mesh):
    whole = (P(),) * 14
    placed = (P(("twin", "dp"), None, None), P(("twin", "dp"), None)) + whole
    return jax.shard_map(
        body,
        mesh=mesh,
        in_specs=placed,
        out_specs=(
            P(("twin", "dp")),
            P(("twin", "dp"), None, None),
            P("dp", None),
            P("dp"),
            P("dp"),
            P("dp", None),
            P("dp"),
            P("dp"),
            P("dp"),
            P("dp", None),
            P("dp"),
            P("dp", None),
            P("dp"),
            P("dp"),
            P("dp"),
        ),
        check_vma=False,
    )
```

```python
import functools

import jax
import jax.numpy as jnp
from jax import lax
from jax.experimental import pallas as pl
from jax.experimental.pallas import tpu as pltpu
from jax.sharding import PartitionSpec as P

D = 768
HEADS = 12
HEAD_DIM = 64
FF = 3072
SEG = 8
QB = 128
MOST = 128
PAIRS = HEADS // 2
PW = 2 * HEAD_DIM

cosine_scale = 64.0
loss_scale = 32.0
norm_epsilon = 1e-12
unit_epsilon = 1e-06
masked_score = -1e30

F32 = jnp.float32
BF16 = jnp.bfloat16
VMEM = pltpu.VMEM
ANY = pl.ANY
MIB = 1 << 20


def nn(left, right):
    return lax.dot_general(left, right, (((1,), (0,)), ((), ())), preferred_element_type=F32)


def nt(left, right):
    return lax.dot_general(left, right, (((1,), (1,)), ((), ())), preferred_element_type=F32)


def tn(left, right):
    return lax.dot_general(left, right, (((0,), (0,)), ((), ())), preferred_element_type=F32)


def vspec():
    return pl.BlockSpec(memory_space=VMEM)


def sspec():
    return pl.BlockSpec(memory_space=pltpu.SMEM)


def hspec():
    return pl.BlockSpec(memory_space=pltpu.HBM)


def far(*values):
    return [pltpu.with_memory_space_constraint(value, pltpu.HBM) for value in values]


class Fetch:
    def __init__(self, sems, pairs):
        self.copies = [pltpu.make_async_copy(a, b, sems.at[i]) for i, (a, b) in enumerate(pairs)]
        for copy in self.copies:
            copy.start()

    def wait(self, *which):
        for i in which:
            self.copies[i].wait()


def carrying(kernel, n_in, n_out, n_carry):
    def wrapped(*refs):
        refs, sems = refs[:-1], refs[-1]
        ins, refs = refs[:n_in], refs[n_in:]
        sources, refs = refs[:n_carry], refs[n_carry:]
        outs, refs = refs[:n_out], refs[n_out:]
        targets, rest = refs[:n_carry], refs[n_carry:]
        fetch = Fetch(sems, tuple(zip(sources, targets)))
        kernel(*ins, *outs, *rest)
        fetch.wait(*range(n_carry))

    return wrapped


def carry_call(kernel, name, us, mib, operands, specs, outs, scratch, carry):
    n_carry = len(carry)
    return pl.pallas_call(
        carrying(kernel, len(operands), len(outs), n_carry),
        name=name,
        in_specs=list(specs) + [hspec()] * n_carry,
        out_specs=[vspec()] * (len(outs) + n_carry),
        out_shape=list(outs) + [VMEM(a.shape, a.dtype) for a in carry],
        scratch_shapes=list(scratch) + [pltpu.SemaphoreType.DMA((max(n_carry, 1),))],
        cost_estimate=took(us),
        compiler_params=params(mib),
    )(*operands, *far(*carry))


def fixed(shape):
    return pl.BlockSpec(shape, lambda *_: (0,) * len(shape))


def shape_of(shape, dtype):
    return jax.ShapeDtypeStruct(shape, dtype)


def params(mib):
    return pltpu.CompilerParams(vmem_limit_bytes=mib * MIB)


SCALE = 0.4


def took(us):
    return pl.CostEstimate(flops=int(us * SCALE * 1.15e9), bytes_accessed=0, transcendentals=0)


def windows(length):
    out, packed = [], 0
    for start in range(0, length, QB):
        low, high = max(0, start - MOST), min(length, start + QB + MOST)
        out.append((start, low, high, packed))
        packed += high - low
    return out, packed


def two_heads(pair):
    first = lax.broadcasted_iota(jnp.int32, pair.shape, 1) < HEAD_DIM
    zero = jnp.zeros((), pair.dtype)
    return jnp.concatenate([jnp.where(first, pair, zero), jnp.where(first, zero, pair)], axis=0)


def pick_heads(both):
    rows = both.shape[1] // 2
    return jnp.concatenate([both[:HEAD_DIM, :rows], both[HEAD_DIM:, rows:]], axis=0).T


def column_of(row):
    return jnp.broadcast_to(row, (8, row.shape[1])).T[:, :1]


def split_low(value):
    high = value.astype(BF16)
    return high, (value - high.astype(F32)).astype(BF16)


def normalise(value):
    middle = jnp.mean(value, axis=-1, keepdims=True)
    centered = value - middle
    spread = jnp.mean(centered * centered, axis=-1, keepdims=True)
    rstd = lax.rsqrt(spread + norm_epsilon)
    return centered * rstd, rstd


def vector(ref):
    return ref[...].astype(F32).reshape(1, ref.shape[0])


def softmax_down(own):
    top = jnp.max(own, axis=0, keepdims=True)
    weights = jnp.exp(own - top)
    total = jnp.sum(weights, axis=0, keepdims=True)
    return (weights * (1.0 / total)).astype(BF16)


def attend(length, qkv, bias, p_s, ctx_s):
    blocks, _ = windows(length)

    def lanes(part, h):
        return slice(part * D + h * PW, part * D + (h + 1) * PW)

    def score(h):
        q_all = qkv[:, lanes(0, h)] * jnp.asarray(HEAD_DIM**-0.5, BF16)
        k_all = qkv[:, lanes(1, h)]
        out = []
        for start, low, high, _ in blocks:
            out.append(nt(k_all[low:high], two_heads(q_all[start : start + QB])))
        return out, qkv[:, lanes(2, h)].T

    ahead = score(0)
    for h in range(PAIRS):
        scores, v_turned = ahead
        if h + 1 < PAIRS:
            ahead = score(h + 1)
        probs = []
        for own, (_, low, high, packed) in zip(scores, blocks):
            mask = bias[packed : packed + high - low, :]
            halves = [softmax_down(own[:, :QB] + mask), softmax_down(own[:, QB:] + mask)]
            probs.append(jnp.concatenate(halves, axis=1))
        for p, (_, low, high, packed) in zip(probs, blocks):
            p_s[h, packed : packed + high - low, :] = p
        outs = [nn(v_turned[:, low:high], p) for p, (_, low, high, _) in zip(probs, blocks)]
        ctx_s[:, lanes(0, h)] = jnp.concatenate([pick_heads(o.astype(BF16)) for o in outs], axis=0)


def forward_kernel(*refs):
    (hid_h, seg, wqkv_h, bq, bv, wout_h, bout, g1, b1, win_h, bin_, wdown_h, bdown, g2, b2) = refs[:15]
    outs, (unit_o, unitf_o, inv_o) = refs[15:25], refs[25:28]
    hid, wqkv, wout, win, wdown, bias_s, n1_s = refs[28:35]
    kept = refs[35:45]
    sems, osems = refs[45:47]
    qkv_s, p_s, ctx_s, nl_s, xh1_s, rs1_s, act_o, dg_o, xh2_o, rs2_o = kept
    rows = seg.shape[0]
    length = hid.shape[0] // rows
    blocks, _ = windows(length)
    toks = [slice(r * length, (r + 1) * length) for r in range(rows)]
    parts = [slice(part * D, (part + 1) * D) for part in range(3)]

    pairs = [(hid_h.at[toks[0]], hid.at[toks[0]])]
    pairs += [(wqkv_h.at[:, cols], wqkv.at[:, cols]) for cols in parts]
    first = Fetch(sems, pairs)
    later = []

    def fetch_rest():
        rest = [(wout_h, wout), (win_h, win), (wdown_h, wdown)]
        rest += [(hid_h.at[tok], hid.at[tok]) for tok in toks[1:]]
        for i, (source, target) in enumerate(rest):
            copy = pltpu.make_async_copy(source, target, sems.at[4 + i])
            copy.start()
            later.append(copy)

    def leaving(i, r):
        if i == 1:
            return pltpu.make_async_copy(p_s, outs[1].at[r], osems.at[r, 1])
        source = kept[i] if i in (0, 2) else kept[i].at[toks[r]]
        return pltpu.make_async_copy(source, outs[i].at[toks[r]], osems.at[r, i])

    seg_rows = [seg[r : r + 1, :].astype(F32) for r in range(rows)]

    def mask(r):
        seg_col = column_of(seg_rows[r])
        for start, low, high, packed in blocks:
            same = seg_col[low:high] == seg_rows[r][:, start : start + QB]
            bias_s[packed : packed + high - low, :] = jnp.where(same, 0.0, masked_score)

    def project(r):
        if r > 0:
            leaving(0, r - 1).wait()
            later[2 + r].wait()
        for part, cols in enumerate(parts):
            if r == 0:
                first.wait(*((0, 1) if part == 0 else (part + 1,)))
                if part == 0:
                    fetch_rest()
            value = nn(hid[toks[r], :], wqkv[:, cols])
            if part == 0:
                value = value + vector(bq)
            if part == 2:
                value = value + vector(bv)
            qkv_s[:, cols] = value.astype(BF16)
        leaving(0, r).start()

    def attention(r):
        if r > 0:
            leaving(1, r - 1).wait()
            leaving(2, r - 1).wait()
        attend(length, qkv_s, bias_s, p_s, ctx_s)
        leaving(1, r).start()
        leaving(2, r).start()

    def mix(r):
        if r == 0:
            later[0].wait()
        return nn(ctx_s[...], wout[...])

    def norm_one(r, attended):
        tok = toks[r]
        xhat, rstd = normalise(hid[tok, :].astype(F32) + (attended + vector(bout)))
        xh1_s[tok, :] = xhat.astype(BF16)
        rs1_s[tok, :] = jnp.broadcast_to(rstd, (length, rs1_s.shape[1]))
        n1 = xhat * vector(g1) + vector(b1)
        n1_s[tok, :] = n1
        nl_s[tok, :] = n1.astype(BF16)
        for i in (3, 4, 5):
            leaving(i, r).start()

    chunk = 768
    count = FF // chunk
    bias_in = vector(bin_)

    def rise(r, c):
        cols = slice(c * chunk, (c + 1) * chunk)
        return nn(nl_s[toks[r], :], win[:, cols]) + bias_in[:, cols]

    def bend(r, c, pre):
        cols = slice(c * chunk, (c + 1) * chunk)
        half = 0.5 + 0.5 * lax.erf(pre * 0.5**0.5)
        act_o[toks[r], cols] = (pre * half).astype(BF16)
        bell = jnp.exp(pre * pre * -0.5) * 0.3989422804014327
        dg_o[toks[r], cols] = (half + pre * bell).astype(BF16)

    def norm_two(r, fallen):
        tok = toks[r]
        xhat, rstd = normalise(n1_s[tok, :] + (fallen + vector(bdown)))
        xh2_o[tok, :] = xhat.astype(BF16)
        rs2_o[tok, :] = jnp.broadcast_to(rstd, (length, rs2_o.shape[1]))
        leaving(8, r).start()
        leaving(9, r).start()
        out = xhat * vector(g2) + vector(b2)
        index = lax.broadcasted_iota(jnp.int32, (SEG, length), 0).astype(F32)
        member = (index == seg_rows[r]).astype(F32)
        counts = jnp.sum(member, axis=1, keepdims=True)
        high, low = split_low(out)
        member = member.astype(BF16)
        pooled = (nn(member, high) + nn(member, low)) / counts
        inv = lax.rsqrt(jnp.mean(pooled * pooled, axis=-1, keepdims=True) + unit_epsilon)
        unit = pooled * inv
        unitf_o[r] = unit
        unit_o[r] = unit.astype(BF16)
        inv_o[r] = jnp.broadcast_to(inv / counts, inv_o.shape[1:])

    mixed = None
    for r in range(rows):
        mask(r)
        project(r)
        if r > 0:
            norm_one(r - 1, mixed)
        attention(r)
        mixed = mix(r)
    steps = [(r, c) for r in range(rows) for c in range(count)]
    later[1].wait()
    if rows > 1:
        ahead = rise(0, 0)
        norm_one(rows - 1, mixed)
    else:
        norm_one(0, mixed)
        ahead = rise(0, 0)
    fallen = None
    for i, (r, c) in enumerate(steps):
        pre = ahead
        if i + 1 < len(steps):
            ahead = rise(*steps[i + 1])
        bend(r, c, pre)
        if c == 1 and fallen is not None:
            norm_two(r - 1, fallen)
        if c == count - 1:
            if r == 0:
                later[2].wait()
            leaving(6, r).start()
            leaving(7, r).start()
            fallen = nn(act_o[toks[r], :], wdown[...])
    norm_two(rows - 1, fallen)
    for r in range(rows):
        for i in range(10):
            if r == rows - 1 or i > 2:
                leaving(i, r).wait()


def forward(hidden, seg, weights):
    rows, length, _ = hidden.shape
    tokens = rows * length
    _, packed = windows(length)
    packed_shape = (PAIRS, packed, 2 * QB)
    far_shapes = [((tokens, 3 * D), BF16), ((rows,) + packed_shape, BF16)]
    far_shapes += [((tokens, D), BF16)] * 3 + [((tokens, 128), F32)]
    after = [((tokens, FF), BF16)] * 2 + [((tokens, D), BF16), ((tokens, 128), F32)]
    far_shapes += after
    near_shapes = [((rows, SEG, D), BF16), ((rows, SEG, D), F32), ((rows, SEG, 128), F32)]
    kept = [VMEM((length, 3 * D), BF16), VMEM(packed_shape, BF16), VMEM((length, D), BF16)]
    kept += [VMEM((tokens, D), BF16), VMEM((tokens, D), BF16), VMEM((tokens, 128), F32)]
    kept += [VMEM(*a) for a in after]
    large = (0, 3, 7, 9)
    hbm = hspec()
    return pl.pallas_call(
        forward_kernel,
        name="forward",
        in_specs=[hbm, vspec()] + [hbm if i in large else vspec() for i in range(13)],
        out_specs=[hbm] * 10 + [vspec()] * 3,
        out_shape=[pltpu.HBM(*a) for a in far_shapes] + [VMEM(*a) for a in near_shapes],
        scratch_shapes=[VMEM((tokens, D), BF16)]
        + [VMEM(weights[i].shape, BF16) for i in large]
        + [VMEM((packed, QB), F32), VMEM((tokens, D), F32)]
        + kept
        + [pltpu.SemaphoreType.DMA((7 + rows,)), pltpu.SemaphoreType.DMA((rows, 10))],
        cost_estimate=took(33),
        compiler_params=params(58),
    )(*far(hidden.reshape(tokens, D), seg, *weights))


def loss_kernel(flips, idx, *refs):
    pieces, refs = refs[: len(flips)], refs[len(flips) :]
    targets, seg, g2, unitf, inv, xh2, rs2, loss_o, gb_o, vec_o, slope_s, rows_s, units = refs
    twin, me = idx[0], idx[1]
    count = units.shape[0] // 2
    sentences = unitf.shape[0]
    for piece, own_flips in zip(pieces, flips):
        if own_flips is None:
            units[...] = piece[...]
            continue
        for i, (twin_flip, flip) in enumerate(own_flips):
            at = (twin ^ twin_flip) * count + (me ^ flip) * sentences
            at = pl.multiple_of(at, sentences)
            units[pl.ds(at, sentences), :] = piece[i * sentences : (i + 1) * sentences, :]
    rows, length = seg.shape
    step = min(count, 256)
    factor = cosine_scale / D
    positives = units.at[pl.ds(count, count)]
    own = pl.ds(pl.multiple_of(me * sentences, sentences), sentences)

    def one_block(i, carry):
        lanes = pl.ds(pl.multiple_of(i * step, step), step)
        sims = nt(positives[...], units[lanes, :]) * factor
        top = jnp.max(sims, axis=0, keepdims=True)
        weights = jnp.exp(sims - top)
        total = jnp.sum(weights, axis=0, keepdims=True)
        hit = lax.broadcasted_iota(jnp.int32, sims.shape, 0) == targets[:, lanes]
        picked = jnp.sum(jnp.where(hit, sims, 0.0), axis=0, keepdims=True)
        loss_o[:, lanes] = top + jnp.log(total) - picked
        slope = loss_scale * (weights * (1.0 / total) - hit.astype(F32))
        slope_s[:, lanes] = slope.astype(BF16)
        return carry

    if count == step:
        one_block(0, 0)
    else:
        lax.fori_loop(0, count // step, one_block, 0)

    @pl.when(twin == 0)
    def _():
        def part(i, carry):
            lanes = pl.ds(pl.multiple_of(i * step, step), step)
            rows_s[lanes, :] = tn(slope_s[:, lanes], positives[...])
            return carry

        lax.fori_loop(0, count // step, part, 0)
        rows_s[pl.ds(0, sentences), :] = rows_s[own, :]

    @pl.when(twin == 1)
    def _():
        rows_s[pl.ds(0, sentences), :] = nn(slope_s[own, :], units[pl.ds(0, count), :])

    gu = rows_s[pl.ds(0, sentences), :] * factor
    unit = unitf[...]
    gs = inv[:, :1] * (gu - unit * jnp.mean(gu * unit, axis=-1, keepdims=True))
    gy = gs * vector(g2)
    u = gy - jnp.mean(gy, axis=-1, keepdims=True)
    gain = jnp.zeros((1, D), F32)
    shift = jnp.zeros((1, D), F32)
    summed = jnp.zeros((1, D), F32)
    for r in range(rows):
        part = slice(r * SEG, (r + 1) * SEG)
        tok = slice(r * length, (r + 1) * length)
        seg_row = seg[r : r + 1, :]
        hits = lax.broadcasted_iota(jnp.int32, (SEG, length), 0) == seg_row
        member = hits.astype(F32).astype(BF16)
        counts = jnp.sum(hits.astype(F32), axis=1, keepdims=True)
        xhat_low = xh2[tok, :]
        gain += jnp.sum(nn(member, xhat_low) * gs[part], axis=0, keepdims=True)
        shift += jnp.sum(counts * gs[part], axis=0, keepdims=True)
        xhat = xhat_low.astype(F32)
        high, low = split_low(u[part])
        spread = tn(member, high) + tn(member, low)
        inner = jnp.mean(spread * xhat, axis=-1, keepdims=True)
        grad = rs2[tok, :1] * (spread - xhat * inner)
        grad_low = grad.astype(BF16)
        gb_o[tok, :] = grad_low
        summed += jnp.sum(grad_low.astype(F32), axis=0, keepdims=True)
    vec_o[...] = jnp.concatenate([summed, gain, shift, jnp.zeros((5, D), F32)], axis=0)


def loss_stage(idx, gathered, targets, unitf, inv, seg, g2, xh2, rs2, carry):
    pieces, flips = gathered
    tokens = xh2.shape[0]
    count = targets.shape[1]
    return carry_call(
        functools.partial(loss_kernel, flips),
        "loss",
        4,
        20 if count <= 256 else 44,
        (idx, *pieces, *far(targets, seg, g2), unitf, inv, xh2, rs2),
        [sspec()] + [vspec()] * (7 + len(pieces)),
        [shape_of((1, count), F32), shape_of((tokens, D), BF16), shape_of((8, D), F32)],
        [VMEM((count, count), BF16), VMEM((count, D), F32), VMEM((2 * count, D), BF16)],
        carry,
    )


def pre_kernel(gb, wdown, dg, out):
    n = 768

    def product(j):
        return nt(gb[...], wdown[j * n : (j + 1) * n, :])

    ahead = product(0)
    for j in range(FF // n):
        value = ahead
        if j + 1 < FF // n:
            ahead = product(j + 1)
        part = slice(j * n, (j + 1) * n)
        out[:, part] = (value * dg[:, part].astype(F32)).astype(BF16)


def pre_stage(gb, wdown, dg, carry):
    outs = [VMEM(dg.shape, BF16)]
    return carry_call(
        pre_kernel, "grad_pre", 5.2, 24, (gb, wdown, dg), [vspec()] * 3, outs, [], carry
    )


def normed_kernel(gp, win, gb, xh1, rs1, g1, wout, ga_o, gc_o, vec_o):
    m = 512
    count = gp.shape[0] // m
    gain, shift, summed = [jnp.zeros((1, D), F32) for _ in range(3)]
    grads = [nt(gp[i * m : (i + 1) * m, :], win[...]) for i in range(count)]
    for i in range(count):
        rows = slice(i * m, (i + 1) * m)
        grad = grads[i] + gb[rows, :].astype(F32)
        xhat = xh1[rows, :].astype(F32)
        gain += jnp.sum(grad * xhat, axis=0, keepdims=True)
        shift += jnp.sum(grad, axis=0, keepdims=True)
        gy = grad * vector(g1)
        inner = jnp.mean(gy * xhat, axis=-1, keepdims=True)
        total = rs1[rows, :1] * (gy - jnp.mean(gy, axis=-1, keepdims=True) - xhat * inner)
        low = total.astype(BF16)
        ga_o[rows, :] = low
        summed += jnp.sum(low.astype(F32), axis=0, keepdims=True)
    for i in range(count):
        rows = slice(i * m, (i + 1) * m)
        gc_o[rows, :] = nt(ga_o[rows, :], wout[...]).astype(BF16)
    vec_o[...] = jnp.concatenate([summed, gain, shift, jnp.zeros((5, D), F32)], axis=0)


def normed_stage(gp, win, gb, xh1, rs1, g1, wout, carry):
    tokens = gp.shape[0]
    outs = [shape_of((tokens, D), BF16), shape_of((tokens, D), BF16), shape_of((8, D), F32)]
    operands = (gp, win, gb, xh1, rs1, *far(g1), wout)
    return carry_call(
        normed_kernel, "grad_normed", 9, 28, operands, [vspec()] * 7, outs, [], carry
    )


def attend_back_kernel(q_ref, k_ref, v_ref, g_ref, p_ref, out_ref):
    length = q_ref.shape[0]
    blocks, _ = windows(length)
    group = q_ref.shape[1] // PW
    scale = HEAD_DIM**-0.5
    loaded, grads = [], []
    for h in range(group):
        lanes = slice(h * PW, (h + 1) * PW)
        q2 = [two_heads(q_ref[b[0] : b[0] + QB, lanes]) for b in blocks]
        g2 = [two_heads(g_ref[b[0] : b[0] + QB, lanes]) for b in blocks]
        loaded.append((q2, g2, k_ref[:, lanes].T))
        v_all = v_ref[:, lanes]
        grads.append([nt(v_all[b[1] : b[2]], g) for b, g in zip(blocks, g2)])
    slopes = []
    for h in range(group):
        own = []
        for gp, (_, low, high, packed) in zip(grads[h], blocks):
            p = p_ref[h, packed : packed + high - low, :].astype(F32)
            weighted = p * gp
            inner = jnp.sum(weighted, axis=0, keepdims=True)
            own.append((weighted - p * inner).astype(BF16))
        slopes.append(own)

    def gather(parts):
        out = []
        for block in range(len(blocks)):
            total = None
            for part, (_, low, high, _) in zip(parts, blocks):
                base = block * QB - low
                if 0 <= base < high - low:
                    piece = part[base : base + QB]
                    total = piece if total is None else total + piece
            out.append(total)
        return jnp.concatenate(out, axis=0)

    for h in range(group):
        lanes = slice(h * PW, (h + 1) * PW)
        q2, g2, k_turned = loaded[h]
        dq = [nn(k_turned[:, b[1] : b[2]], s) for b, s in zip(blocks, slopes[h])]
        dv = [nn(p_ref[h, b[3] : b[3] + b[2] - b[1], :], g) for b, g in zip(blocks, g2)]
        dk = [nn(s, q) for s, q in zip(slopes[h], q2)]
        turned = [pick_heads((part * scale).astype(BF16)) for part in dq]
        out_ref[0, :, lanes] = jnp.concatenate(turned, axis=0)
        out_ref[1, :, lanes] = (gather(dk) * scale).astype(BF16)
        out_ref[2, :, lanes] = gather(dv).astype(BF16)


def attend_back(qkv, grad_context, probs, rows, length, first, pairs):
    _, packed = windows(length)
    group = 2
    steps = pairs // group
    base = first // group
    width = group * PW

    def block(part):
        return pl.BlockSpec((length, width), lambda r, h: (r, part * (D // width) + base + h))

    return pl.pallas_call(
        attend_back_kernel,
        name="attend_back",
        grid=(rows, steps),
        in_specs=[
            block(0),
            block(1),
            block(2),
            block(0),
            pl.BlockSpec((None, group, packed, 2 * QB), lambda r, h: (r, base + h, 0, 0)),
        ],
        out_specs=pl.BlockSpec((3, length, width), lambda r, h: (0, r, h)),
        out_shape=shape_of((3, rows * length, pairs * PW), BF16),
        cost_estimate=took(2.0 * pairs),
        compiler_params=params(20),
    )(*far(qkv, qkv, qkv), grad_context, *far(probs))


def hidden_kernel(da, db, wqkv, ga, out):
    m = 512
    for i in range(ga.shape[0] // m):
        rows = slice(i * m, (i + 1) * m)
        total = ga[rows, :].astype(F32)
        for part in range(3):
            both = jnp.concatenate([da[part, rows, :], db[part, rows, :]], axis=1)
            total = total + nt(both, wqkv[:, part * D : (part + 1) * D])
        out[rows, :] = total.astype(BF16)


def hidden_stage(da, db, wqkv, ga):
    return pl.pallas_call(
        hidden_kernel,
        name="hidden_grad",
        in_specs=[vspec()] * 4,
        out_specs=vspec(),
        out_shape=shape_of(ga.shape, BF16),
        cost_estimate=took(5.7),
        compiler_params=params(22),
    )(da, db, wqkv, ga)


def place_of(half, quarter, owner):
    c, y, z0, z1 = owner & 1, (owner >> 1) & 1, (owner >> 2) & 1, owner >> 3
    order = (quarter, y, z0, z1, c) if half == 0 else (y, z0, z1, quarter, c)
    out = 0
    for bit in order:
        out = 2 * out + bit
    return out


def lanes_of(width):
    most = 128 if width <= 256 else 256
    return [(low, min(most, width - low)) for low in range(0, width, most)]


def half_shapes(width):
    shapes = [shape_of((32, 48, width), BF16)]
    return shapes + [shape_of((32, 48, n), BF16) for _, n in lanes_of(width)]


def store_piece(first, keep, sends, quarter, owner, piece_a, piece_b):
    at_a, at_b = place_of(0, quarter, owner), place_of(1, quarter, owner)
    keep[jnp.where(first, at_a, at_b)] = jnp.where(first, piece_a, piece_b)
    other = jnp.where(first, piece_b, piece_a)
    at = jnp.where(first, at_b, at_a)
    for send, (low, n) in zip(sends, lanes_of(keep.shape[2])):
        send[at] = other[:, low : low + n]


def down_kernel(idx, act, gb, keep, *sends):
    first = idx[2] == 0
    n = 768

    def product(j):
        return tn(act[:, j * n : (j + 1) * n], gb[...])

    ahead = product(0)
    for j in range(FF // n):
        total = ahead.astype(BF16)
        if j + 1 < FF // n:
            ahead = product(j + 1)
        for local in range(4):
            for quarter in range(2):
                base = local * 192 + quarter * 48
                a, b = total[base : base + 48], total[base + 96 : base + 144]
                store_piece(first, keep, sends, quarter, 4 * j + local, a, b)


def down_stage(idx, act, gb):
    shapes = half_shapes(D)
    return pl.pallas_call(
        down_kernel,
        name="grad_w_down",
        in_specs=[sspec(), vspec(), vspec()],
        out_specs=[vspec()] * len(shapes),
        out_shape=shapes,
        cost_estimate=took(7.5),
        compiler_params=params(22),
    )(idx, act, gb)


def in_kernel(idx, n1, gp, vec_o, keep, *refs):
    sends, turned = refs[:-1], refs[-1]
    first = idx[2] == 0
    turned[...] = n1[...].T

    def products(quarter):
        out = []
        for half in range(2):
            j = 2 * half + quarter
            out.append(nn(turned[...], gp[:, j * D : (j + 1) * D]))
        return out

    ahead = products(0)
    for quarter in range(2):
        a, b = [part.astype(BF16) for part in ahead]
        if quarter == 0:
            ahead = products(1)
        for owner in range(16):
            rows = slice(owner * 48, (owner + 1) * 48)
            store_piece(first, keep, sends, quarter, owner, a[rows], b[rows])
    vec_o[...] = jnp.sum(gp[...].astype(F32), axis=0, keepdims=True)


def in_stage(idx, n1, gp):
    shapes = half_shapes(D)
    return pl.pallas_call(
        in_kernel,
        name="grad_w_in",
        in_specs=[sspec(), vspec(), vspec()],
        out_specs=[vspec()] * (1 + len(shapes)),
        out_shape=[shape_of((1, FF), F32)] + shapes,
        scratch_shapes=[VMEM((D, n1.shape[0]), BF16)],
        cost_estimate=took(7.4),
        compiler_params=params(24),
    )(idx, n1, gp)


WIDE, NARROW = 640, 256


def store_all(first, keep, send, whole, width):
    for quarter in range(2):
        a = whole[:, quarter * width : (quarter + 1) * width]
        b = whole[:, (2 + quarter) * width : (3 + quarter) * width]
        for owner in range(16):
            rows = slice(owner * 48, (owner + 1) * 48)
            store_piece(first, keep, send, quarter, owner, a[rows], b[rows])


def wide_kernel(idx, hid, da, ctx, ga, turned_o, keep, *refs):
    sends, whole = refs[:-1], refs[-1]
    n = da.shape[2]
    turned_o[...] = hid[...].T
    for part in range(3):
        whole[:, part * n : (part + 1) * n] = nn(turned_o[...], da[part]).astype(BF16)
    whole[:, 3 * n : 3 * n + D] = tn(ctx[...], ga[...]).astype(BF16)
    whole[:, 3 * n + D :] = jnp.zeros((D, 4 * WIDE - 3 * n - D), BF16)
    store_all(idx[2] == 0, keep, sends, whole, WIDE)


def wide_stage(idx, hid, da, ctx, ga):
    shapes = half_shapes(WIDE)
    return pl.pallas_call(
        wide_kernel,
        name="grad_w_wide",
        in_specs=[sspec()] + [vspec()] * 4,
        out_specs=[vspec()] * (1 + len(shapes)),
        out_shape=[shape_of((D, hid.shape[0]), BF16)] + shapes,
        scratch_shapes=[VMEM((D, 4 * WIDE), BF16)],
        cost_estimate=took(6),
        compiler_params=params(24),
    )(idx, hid, da, ctx, ga)


def narrow_kernel(idx, turned, da, db, vec1, vec2, bias, keep, *refs):
    send, (whole, sums_s) = refs[:-2], refs[-2:]
    n = db.shape[2]
    for part in range(3):
        whole[:, part * n : (part + 1) * n] = nn(turned[...], db[part]).astype(BF16)
    sums_s[...] = jnp.zeros_like(sums_s)
    sums_s[2:5, :] = vec1[0:3, :]
    sums_s[5:8, :] = vec2[0:3, :]
    for row, part in ((0, 0), (1, 2)):
        for base, grads in ((0, da), (D - n, db)):
            lanes = slice(base, base + grads.shape[2])
            total = jnp.sum(grads[part].astype(F32), axis=0, keepdims=True)
            sums_s[row : row + 1, lanes] = total
    small = sums_s[...].T
    groups = [bias[:, i * 384 : (i + 1) * 384] for i in range(FF // 384)]
    folded = jnp.concatenate(groups, axis=0)
    turned_bias = [folded[:, i * 48 : (i + 1) * 48].T for i in range(8)]
    lane = lax.broadcasted_iota(jnp.int32, (48, 128), 1)
    for owner in range(16):
        own = small[owner * 48 : (owner + 1) * 48]
        for k in range(4):
            column = turned_bias[4 * (owner % 2) + k][:, owner // 2 : owner // 2 + 1]
            own = jnp.where(lane == 8 + k, column, own)
        whole[owner * 48 : (owner + 1) * 48, 3 * n : 3 * n + 128] = own.astype(BF16)
    whole[:, 3 * n + 128 :] = jnp.zeros((D, 4 * NARROW - 3 * n - 128), BF16)
    store_all(idx[2] == 0, keep, send, whole, NARROW)


def narrow_stage(idx, turned, da, db, vec1, vec2, bias):
    return pl.pallas_call(
        narrow_kernel,
        name="grad_w_narrow",
        in_specs=[sspec()] + [vspec()] * 6,
        out_specs=[vspec()] * len(half_shapes(NARROW)),
        out_shape=half_shapes(NARROW),
        scratch_shapes=[VMEM((D, 4 * NARROW), BF16), VMEM((128, D), F32)],
        cost_estimate=took(2.4),
        compiler_params=params(22),
    )(idx, turned, da, db, vec1, vec2, bias)


def swap_dp(value, flip):
    devices = lax.axis_size("dp")
    return lax.ppermute(value, "dp", [(i, i ^ flip) for i in range(devices)])


def swap_twin(value):
    return lax.ppermute(value, "twin", [(0, 1), (1, 0)])


TWIN = 16
ROUTES = ((TWIN, 2, 4, 8, TWIN), (2, 4, 8, TWIN, TWIN))


def step_swap(value, step):
    pairs = [(i, i ^ ROUTES[i & 1][step]) for i in range(2 * TWIN)]
    return lax.ppermute(value, ("twin", "dp"), pairs)


def plus(*values):
    total = values[0].astype(F32)
    for value in values[1:]:
        total = total + value.astype(F32)
    return total.astype(BF16)


def call_small(kernel, name, idx, operands, outs):
    return pl.pallas_call(
        kernel,
        name=name,
        in_specs=[sspec()] + [vspec()] * len(operands),
        out_specs=[vspec()] * len(outs),
        out_shape=[shape_of(shape, dtype) for shape, dtype in outs],
        cost_estimate=took(2.4),
        compiler_params=params(12),
    )(idx, *operands)


def half_kernel(step, idx, keep, recv, keep_o, send_o):
    count = keep_o.shape[0]
    bit = idx[3 + step]
    mine = pl.ds(bit * count, count)
    other = pl.ds((1 - bit) * count, count)
    keep_o[...] = plus(keep[mine], recv[mine])
    send_o[...] = plus(keep[other], recv[other])


def half_step(idx, step, keep, recv):
    count, rows, width = keep.shape
    shape = (count // 2, rows, width)
    kernel = functools.partial(half_kernel, step)
    return call_small(kernel, "sum_" + str(step), idx, (keep, recv), [(shape, BF16)] * 2)


def core_kernel(idx, keep, *refs):
    recvs, (keep_o, send_o) = refs[:-2], refs[-2:]
    bit = idx[3]
    for recv, (low, n) in zip(recvs, lanes_of(keep.shape[3])):
        lanes = slice(low, low + n)
        keep_o[:, :, lanes] = plus(keep[bit, :, :, lanes], recv[bit])
        send_o[:, :, lanes] = plus(keep[1 - bit, :, :, lanes], recv[1 - bit])


def core_step(idx, keep, recvs):
    count, rows, width = keep.shape
    half = count // 2
    pieces = 4
    part = half // pieces

    def spec(n):
        return pl.BlockSpec((2, part, rows, n), lambda i: (0, i, 0, 0))

    return pl.pallas_call(
        core_kernel,
        name="sum_core",
        grid=(pieces,),
        in_specs=[sspec(), spec(width)] + [spec(n) for _, n in lanes_of(width)],
        out_specs=[pl.BlockSpec((part, rows, width), lambda i: (i, 0, 0))] * 2,
        out_shape=[shape_of((half, rows, width), BF16)] * 2,
        cost_estimate=took(1.7),
        compiler_params=params(10),
    )(
        idx,
        keep.reshape(2, half, rows, width),
        *[recv.reshape(2, half, rows, recv.shape[2]) for recv in recvs],
    )


def own_kernel(idx, keep, recv, out):
    out[...] = plus(keep[...], recv[...])


def turn_kernel(idx, own, other, keep_o, send_o):
    twin, core = idx[0], idx[2]
    keep_o[twin] = own[core]
    keep_o[1 - twin] = other[core]
    send_o[twin] = own[1 - core]
    send_o[1 - twin] = other[1 - core]


class Order:
    def __init__(self):
        self.last = None

    def after(self, value, *others):
        if self.last is None:
            return value
        return lax.optimization_barrier((value, self.last) + others)[0]

    def done(self, value):
        self.last = value
        return value


class Exchange:
    def __init__(self, order, idx, keep, sends):
        self.order, self.idx, self.step = order, idx, 0
        self.keep, self.recv = keep, [swap_dp(send, 1) for send in sends]

    def advance(self):
        idx, order = self.idx, self.order
        keep, recv = order.after(self.keep), self.recv
        if self.step == 0:
            keep, send = core_step(idx, keep, recv)
            recv = step_swap(send, 0)
        elif self.step < 4:
            keep, send = half_step(idx, self.step, keep, recv)
            recv = step_swap(send, self.step)
        elif self.step == 4:
            shape = keep.shape
            (keep,) = call_small(own_kernel, "sum_4", idx, (keep, recv), [(shape, BF16)])
            recv = step_swap(keep, 4)
        else:
            shape = keep.shape
            keep, send = call_small(turn_kernel, "turn", idx, (keep, recv), [(shape, BF16)] * 2)
            recv = swap_dp(send, 1)
        order.done(keep)
        self.keep, self.recv = keep, recv
        self.step += 1

    def result(self):
        return self.keep, self.recv


def bring_kernel(*refs):
    del refs


def bring(values):
    return carry_call(bring_kernel, "bring", 1.2, 4, (), [], [], [], values)


def gather_units(unit, wanted):
    flips = [(0, 0)]
    for flip in (8, 4):
        unit = jnp.concatenate([unit, swap_dp(unit, flip)], axis=0)
        flips = flips + [(t, f ^ flip) for t, f in flips]
    wanted = bring((lax.optimization_barrier((wanted[0], unit))[0],) + wanted[1:])
    pairs = [(i, i ^ (TWIN + 2)) for i in range(2 * TWIN)]
    corner = lax.ppermute(unit, ("twin", "dp"), pairs)
    unit = jnp.concatenate([unit, swap_dp(unit, 2), swap_twin(unit), corner], axis=0)
    flips = [(t ^ a, f ^ b) for a, b in ((0, 0), (0, 2), (1, 0), (1, 2)) for t, f in flips]
    return ((unit, swap_dp(unit, 1)), (flips, [(t, f ^ 1) for t, f in flips])), wanted


def four_quarters(idx, keep, recv):
    first = idx[2] == 0
    low = [jnp.where(first, keep[i], recv[i]) for i in range(2)]
    high = [jnp.where(first, recv[i], keep[i]) for i in range(2)]
    return low + high


def final_in_kernel(idx, keep, recv, out):
    for i, part in enumerate(four_quarters(idx, keep, recv)):
        out[:, i * D : (i + 1) * D] = part.astype(F32)


def final_down_kernel(idx, keep, recv, out):
    for i, part in enumerate(four_quarters(idx, keep, recv)):
        out[i * 48 : (i + 1) * 48, :] = part.astype(F32)


def final_last_kernel(idx, wide_k, wide_r, narrow_k, narrow_r, qkv_o, out_o, vec_o):
    wide = jnp.concatenate(four_quarters(idx, wide_k, wide_r), axis=1).astype(F32)
    narrow = jnp.concatenate(four_quarters(idx, narrow_k, narrow_r), axis=1).astype(F32)
    low, high = 2 * D // 3, D // 3
    for part in range(3):
        qkv_o[:, part * D : part * D + low] = wide[:, part * low : (part + 1) * low]
        qkv_o[:, part * D + low : (part + 1) * D] = narrow[:, part * high : (part + 1) * high]
    out_o[...] = wide[:, 3 * low : 3 * low + D]
    small = narrow[:, 3 * high : 3 * high + 128]
    vec_o[...] = jnp.concatenate([small, jnp.zeros((80, 128), F32)], axis=0).T[:16]


def finish(order, idx, kernel, name, chunks, outs):
    operands = [value for chunk in chunks for value in chunk.result()]
    operands[0] = order.after(operands[0])
    out = call_small(kernel, name, idx, operands, outs)
    order.done(out[0])
    return out


def add_low(*parts):
    return lax.optimization_barrier(plus(*parts))


def digits_of(devices):
    out, rest = [], devices // 2
    while rest > 1:
        size = 4 if rest % 4 == 0 else 2
        out.append(size)
        rest //= size
    return out


def pick(value, index, axis):
    return lax.dynamic_index_in_dim(value, index, axis, keepdims=False)


def scatter(grad):
    devices = lax.axis_size("dp")
    me = lax.axis_index("dp")
    value = grad.reshape(devices, grad.shape[0] // devices, grad.shape[1])
    unit = 1
    for size in [2] + digits_of(devices):
        mine = (me // unit) % size
        view = value.reshape((value.shape[0] // size, size) + value.shape[1:])
        parts = [pick(view, mine, 1)]
        for flip in range(1, size):
            parts.append(swap_dp(pick(view, mine ^ flip, 1), flip * unit))
        value = add_low(*parts)
        unit *= size
    value = value[0]
    return value.astype(F32) + swap_twin(value).astype(F32)


SEQUENCE = (
    "down", "pre", "d", "in", "normed", "i", "d", "attend_a", "attend_b", "d", "wide", "narrow",
    "i", "w", "d", "n", "hidden", "i", "d", "n", "w", "d", "i", "final_d", "n", "w", "i", "n",
    "w", "i", "final_i", "n", "w", "n", "w",
)


def body(
    hidden,
    segment_ids,
    targets,
    w_qkv,
    b_query,
    b_value,
    w_out,
    b_out,
    ln1_gain,
    ln1_bias,
    w_in,
    b_in,
    w_down,
    b_down,
    ln2_gain,
    ln2_bias,
):
    row_count, length, width = hidden.shape
    tokens = row_count * length
    devices = lax.axis_size("dp")
    everyone = lax.axis_size(("twin", "dp"))
    me = lax.axis_index("dp")
    twin = lax.axis_index("twin")
    core, y, z0, z1 = me & 1, (me >> 1) & 1, (me >> 2) & 1, me >> 3
    first = core == 0
    bits = [jnp.where(first, a, b) for a, b in ((twin, y), (y, z0), (z0, z1), (z1, twin))]
    idx = jnp.stack([twin, me, core] + bits).astype(jnp.int32)
    weights = (w_qkv, b_query, b_value, w_out, b_out, ln1_gain, ln1_bias)
    weights += (w_in, b_in, w_down, b_down, ln2_gain, ln2_bias)
    qkv, probs, ctx, n1, xh1, rs1, act, dg, xh2, rs2, unit, unitf, inv = forward(
        hidden, segment_ids, weights
    )
    sentences = row_count * SEG
    unit = unit.reshape(sentences, width)
    direct = devices == TWIN and sentences == 16
    if direct:
        gathered, (xh2, rs2) = gather_units(unit, (xh2, rs2))
    else:
        gathered = ((lax.all_gather(unit, ("twin", "dp"), axis=0, tiled=True),), (None,))
    losses, gb, vec2, act_near = loss_stage(
        idx,
        gathered,
        targets.reshape(1, -1),
        unitf.reshape(sentences, width),
        inv.reshape(sentences, 128),
        segment_ids,
        ln2_gain,
        xh2,
        rs2,
        (act,),
    )
    share = losses.shape[1] // everyone
    losses = lax.dynamic_slice_in_dim(
        losses[0], lax.axis_index(("twin", "dp")) * share, share, 0
    )
    flat = hidden.reshape(tokens, width)
    if direct:
        order = Order()
        chunks = {}

        def begin(name, keep, sends):
            order.done(keep)
            chunks[name] = Exchange(order, idx, keep, sends)

        for stage in SEQUENCE:
            if stage == "down":
                halves_d = down_stage(idx, act_near, order.after(gb))
                begin("d", halves_d[0], halves_d[1:])
            elif stage == "pre":
                near = (n1, xh1, rs1)
                gp, *near = pre_stage(order.after(gb), w_down, dg, near)
                order.done(gp)
            elif stage == "in":
                sums, *halves_in = in_stage(idx, near[0], order.after(gp))
                begin("i", halves_in[0], halves_in[1:])
            elif stage == "normed":
                ga, gc, vec1, *later = normed_stage(
                    order.after(gp), w_in, gb, near[1], near[2], ln1_gain, w_out, (flat, ctx)
                )
                order.done(ga)
            elif stage == "attend_a":
                da = order.done(attend_back(qkv, order.after(gc), probs, row_count, length, 0, 4))
            elif stage == "attend_b":
                db = order.done(attend_back(qkv, order.after(gc), probs, row_count, length, 4, 2))
            elif stage == "wide":
                turned, *halves_w = wide_stage(idx, later[0], order.after(da), later[1], ga)
                begin("w", halves_w[0], halves_w[1:])
            elif stage == "narrow":
                halves_n = narrow_stage(idx, turned, da, order.after(db), vec1, vec2, sums)
                begin("n", halves_n[0], halves_n[1:])
            elif stage == "hidden":
                hidden_grad = order.done(hidden_stage(da, order.after(db), w_qkv, ga))
            elif stage == "final_d":
                outs = [((192, D), F32)]
                (grad_w_down,) = finish(order, idx, final_down_kernel, stage, [chunks["d"]], outs)
            elif stage == "final_i":
                outs = [((48, FF), F32)]
                (grad_w_in,) = finish(order, idx, final_in_kernel, stage, [chunks["i"]], outs)
            else:
                chunks[stage].advance()
        wide, narrow = chunks["w"], chunks["n"]
        shapes = [((48, 3 * D), F32), ((48, D), F32), ((16, 128), F32)]
        grad_w_qkv, grad_w_out, vec = finish(
            order, idx, final_last_kernel, "final_last", [wide, narrow], shapes
        )
        vec = vec[:, :48]
        vecs = [vec[i] for i in range(8)]
        grad_b_in = vec[8:12].reshape(-1)
    else:
        gp, _ = pre_stage(gb, w_down, dg, (n1,))
        ga, gc, vec1, _ = normed_stage(gp, w_in, gb, xh1, rs1, ln1_gain, w_out, (ctx,))
        da = attend_back(qkv, gc, probs, row_count, length, 0, 4)
        db = attend_back(qkv, gc, probs, row_count, length, 4, 2)
        hidden_grad = hidden_stage(da, db, w_qkv, ga)
        dqkv = jnp.concatenate([da, db], axis=2)
        grad_w_down = scatter(tn(act, gb).astype(BF16))
        grad_w_in = scatter(tn(n1, gp).astype(BF16))
        wide = jnp.concatenate([dqkv[0], dqkv[1], dqkv[2]], axis=1)
        grad_w_qkv = scatter(tn(flat, wide).astype(BF16))
        grad_w_out = scatter(tn(ctx, ga).astype(BF16))
        sums = jnp.sum(dqkv, axis=1, dtype=F32)
        vec = jnp.concatenate([sums[0:1], sums[2:3], vec1[:3], vec2[:3]])
        vec = scatter(jnp.pad(vec, ((0, 120), (0, 0))).T.astype(BF16)).T
        vecs = [vec[i] for i in range(8)]
        bias = jnp.sum(gp, axis=0, dtype=F32)
        grad_b_in = scatter(jnp.broadcast_to(bias[:, None], (FF, 128)).astype(BF16))[:, 0]
    return (
        losses,
        hidden_grad.reshape(row_count, length, width),
        grad_w_qkv,
        vecs[0],
        vecs[1],
        grad_w_out,
        vecs[2],
        vecs[3],
        vecs[4],
        grad_w_in,
        grad_b_in,
        grad_w_down,
        vecs[5],
        vecs[6],
        vecs[7],
    )


def solution(mesh):
    whole = (P(),) * 14
    placed = (P(("twin", "dp"), None, None), P(("twin", "dp"), None)) + whole
    return jax.shard_map(
        body,
        mesh=mesh,
        in_specs=placed,
        out_specs=(
            P(("twin", "dp")),
            P(("twin", "dp"), None, None),
            P("dp", None),
            P("dp"),
            P("dp"),
            P("dp", None),
            P("dp"),
            P("dp"),
            P("dp"),
            P("dp", None),
            P("dp"),
            P("dp", None),
            P("dp"),
            P("dp"),
            P("dp"),
        ),
        check_vma=False,
    )
```

```python
import functools

import jax
import jax.numpy as jnp
from jax import lax
from jax.experimental import pallas as pl
from jax.experimental.pallas import tpu as pltpu
from jax.sharding import PartitionSpec as P

D = 768
HEADS = 12
HEAD_DIM = 64
FF = 3072
SEG = 8
QB = 128
MOST = 128
PAIRS = HEADS // 2
PW = 2 * HEAD_DIM

cosine_scale = 64.0
loss_scale = 32.0
norm_epsilon = 1e-12
unit_epsilon = 1e-06
masked_score = -1e30

F32 = jnp.float32
BF16 = jnp.bfloat16
VMEM = pltpu.VMEM
ANY = pl.ANY
MIB = 1 << 20


def nn(left, right):
    return lax.dot_general(left, right, (((1,), (0,)), ((), ())), preferred_element_type=F32)


def nt(left, right):
    return lax.dot_general(left, right, (((1,), (1,)), ((), ())), preferred_element_type=F32)


def tn(left, right):
    return lax.dot_general(left, right, (((0,), (0,)), ((), ())), preferred_element_type=F32)


def vspec():
    return pl.BlockSpec(memory_space=VMEM)


def sspec():
    return pl.BlockSpec(memory_space=pltpu.SMEM)


def hspec():
    return pl.BlockSpec(memory_space=pltpu.HBM)


def far(*values):
    return [pltpu.with_memory_space_constraint(value, pltpu.HBM) for value in values]


class Fetch:
    def __init__(self, sems, pairs):
        self.copies = [pltpu.make_async_copy(a, b, sems.at[i]) for i, (a, b) in enumerate(pairs)]
        for copy in self.copies:
            copy.start()

    def wait(self, *which):
        for i in which:
            self.copies[i].wait()


def carrying(kernel, n_in, n_out, n_carry):
    def wrapped(*refs):
        refs, sems = refs[:-1], refs[-1]
        ins, refs = refs[:n_in], refs[n_in:]
        sources, refs = refs[:n_carry], refs[n_carry:]
        outs, refs = refs[:n_out], refs[n_out:]
        targets, rest = refs[:n_carry], refs[n_carry:]
        fetch = Fetch(sems, tuple(zip(sources, targets)))
        kernel(*ins, *outs, *rest)
        fetch.wait(*range(n_carry))

    return wrapped


def carry_call(kernel, name, us, mib, operands, specs, outs, scratch, carry):
    n_carry = len(carry)
    return pl.pallas_call(
        carrying(kernel, len(operands), len(outs), n_carry),
        name=name,
        in_specs=list(specs) + [hspec()] * n_carry,
        out_specs=[vspec()] * (len(outs) + n_carry),
        out_shape=list(outs) + [VMEM(a.shape, a.dtype) for a in carry],
        scratch_shapes=list(scratch) + [pltpu.SemaphoreType.DMA((max(n_carry, 1),))],
        cost_estimate=took(us),
        compiler_params=params(mib),
    )(*operands, *far(*carry))


def fixed(shape):
    return pl.BlockSpec(shape, lambda *_: (0,) * len(shape))


def shape_of(shape, dtype):
    return jax.ShapeDtypeStruct(shape, dtype)


def params(mib):
    return pltpu.CompilerParams(vmem_limit_bytes=mib * MIB)


SCALE = 0.4


def took(us):
    return pl.CostEstimate(flops=int(us * SCALE * 1.15e9), bytes_accessed=0, transcendentals=0)


def windows(length):
    out, packed = [], 0
    for start in range(0, length, QB):
        low, high = max(0, start - MOST), min(length, start + QB + MOST)
        out.append((start, low, high, packed))
        packed += high - low
    return out, packed


def two_heads(pair):
    first = lax.broadcasted_iota(jnp.int32, pair.shape, 1) < HEAD_DIM
    zero = jnp.zeros((), pair.dtype)
    return jnp.concatenate([jnp.where(first, pair, zero), jnp.where(first, zero, pair)], axis=0)


def pick_heads(both):
    rows = both.shape[1] // 2
    return jnp.concatenate([both[:HEAD_DIM, :rows], both[HEAD_DIM:, rows:]], axis=0).T


def column_of(row):
    return jnp.broadcast_to(row, (8, row.shape[1])).T[:, :1]


def split_low(value):
    high = value.astype(BF16)
    return high, (value - high.astype(F32)).astype(BF16)


def normalise(value):
    middle = jnp.mean(value, axis=-1, keepdims=True)
    centered = value - middle
    spread = jnp.mean(centered * centered, axis=-1, keepdims=True)
    rstd = lax.rsqrt(spread + norm_epsilon)
    return centered * rstd, rstd


def vector(ref):
    return ref[...].astype(F32).reshape(1, ref.shape[0])


def softmax_down(own):
    top = jnp.max(own, axis=0, keepdims=True)
    weights = jnp.exp(own - top)
    total = jnp.sum(weights, axis=0, keepdims=True)
    return (weights * (1.0 / total)).astype(BF16)


def attend(length, qkv, bias, p_s, ctx_s):
    blocks, _ = windows(length)

    def lanes(part, h):
        return slice(part * D + h * PW, part * D + (h + 1) * PW)

    def score(h):
        q_all = qkv[:, lanes(0, h)] * jnp.asarray(HEAD_DIM**-0.5, BF16)
        k_all = qkv[:, lanes(1, h)]
        out = []
        for start, low, high, _ in blocks:
            out.append(nt(k_all[low:high], two_heads(q_all[start : start + QB])))
        return out, qkv[:, lanes(2, h)].T

    ahead = score(0)
    for h in range(PAIRS):
        scores, v_turned = ahead
        if h + 1 < PAIRS:
            ahead = score(h + 1)
        probs = []
        for own, (_, low, high, packed) in zip(scores, blocks):
            mask = bias[packed : packed + high - low, :]
            halves = [softmax_down(own[:, :QB] + mask), softmax_down(own[:, QB:] + mask)]
            probs.append(jnp.concatenate(halves, axis=1))
        for p, (_, low, high, packed) in zip(probs, blocks):
            p_s[h, packed : packed + high - low, :] = p
        outs = [nn(v_turned[:, low:high], p) for p, (_, low, high, _) in zip(probs, blocks)]
        ctx_s[:, lanes(0, h)] = jnp.concatenate([pick_heads(o.astype(BF16)) for o in outs], axis=0)


def forward_kernel(*refs):
    (hid_h, seg, wqkv_h, bq, bv, wout_h, bout, g1, b1, win_h, bin_, wdown_h, bdown, g2, b2) = refs[:15]
    outs, (unit_o, unitf_o, inv_o) = refs[15:25], refs[25:28]
    hid, wqkv, wout, win, wdown, bias_s, n1_s = refs[28:35]
    kept = refs[35:45]
    sems, osems = refs[45:47]
    qkv_s, p_s, ctx_s, nl_s, xh1_s, rs1_s, act_o, dg_o, xh2_o, rs2_o = kept
    rows = seg.shape[0]
    length = hid.shape[0] // rows
    blocks, _ = windows(length)
    toks = [slice(r * length, (r + 1) * length) for r in range(rows)]
    parts = [slice(part * D, (part + 1) * D) for part in range(3)]

    pairs = [(hid_h.at[toks[0]], hid.at[toks[0]])]
    pairs += [(wqkv_h.at[:, cols], wqkv.at[:, cols]) for cols in parts]
    first = Fetch(sems, pairs)
    later = []

    def fetch_rest():
        rest = [(wout_h, wout), (win_h, win), (wdown_h, wdown)]
        rest += [(hid_h.at[tok], hid.at[tok]) for tok in toks[1:]]
        for i, (source, target) in enumerate(rest):
            copy = pltpu.make_async_copy(source, target, sems.at[4 + i])
            copy.start()
            later.append(copy)

    def leaving(i, r):
        if i == 1:
            return pltpu.make_async_copy(p_s, outs[1].at[r], osems.at[r, 1])
        source = kept[i] if i in (0, 2) else kept[i].at[toks[r]]
        return pltpu.make_async_copy(source, outs[i].at[toks[r]], osems.at[r, i])

    seg_rows = [seg[r : r + 1, :].astype(F32) for r in range(rows)]

    def mask(r):
        seg_col = column_of(seg_rows[r])
        for start, low, high, packed in blocks:
            same = seg_col[low:high] == seg_rows[r][:, start : start + QB]
            bias_s[packed : packed + high - low, :] = jnp.where(same, 0.0, masked_score)

    def project(r):
        if r > 0:
            leaving(0, r - 1).wait()
            later[2 + r].wait()
        for part, cols in enumerate(parts):
            if r == 0:
                first.wait(*((0, 1) if part == 0 else (part + 1,)))
                if part == 0:
                    fetch_rest()
            value = nn(hid[toks[r], :], wqkv[:, cols])
            if part == 0:
                value = value + vector(bq)
            if part == 2:
                value = value + vector(bv)
            qkv_s[:, cols] = value.astype(BF16)
        leaving(0, r).start()

    def attention(r):
        if r > 0:
            leaving(1, r - 1).wait()
            leaving(2, r - 1).wait()
        attend(length, qkv_s, bias_s, p_s, ctx_s)
        leaving(1, r).start()
        leaving(2, r).start()

    def mix(r):
        if r == 0:
            later[0].wait()
        return nn(ctx_s[...], wout[...])

    def norm_one(r, attended):
        tok = toks[r]
        xhat, rstd = normalise(hid[tok, :].astype(F32) + (attended + vector(bout)))
        xh1_s[tok, :] = xhat.astype(BF16)
        rs1_s[tok, :] = jnp.broadcast_to(rstd, (length, rs1_s.shape[1]))
        n1 = xhat * vector(g1) + vector(b1)
        n1_s[tok, :] = n1
        nl_s[tok, :] = n1.astype(BF16)
        for i in (3, 4, 5):
            leaving(i, r).start()

    chunk = 768
    count = FF // chunk
    bias_in = vector(bin_)

    def rise(r, c):
        cols = slice(c * chunk, (c + 1) * chunk)
        return nn(nl_s[toks[r], :], win[:, cols]) + bias_in[:, cols]

    def bend(r, c, pre):
        cols = slice(c * chunk, (c + 1) * chunk)
        half = 0.5 + 0.5 * lax.erf(pre * 0.5**0.5)
        act_o[toks[r], cols] = (pre * half).astype(BF16)
        bell = jnp.exp(pre * pre * -0.5) * 0.3989422804014327
        dg_o[toks[r], cols] = (half + pre * bell).astype(BF16)

    def norm_two(r, fallen):
        tok = toks[r]
        xhat, rstd = normalise(n1_s[tok, :] + (fallen + vector(bdown)))
        xh2_o[tok, :] = xhat.astype(BF16)
        rs2_o[tok, :] = jnp.broadcast_to(rstd, (length, rs2_o.shape[1]))
        leaving(8, r).start()
        leaving(9, r).start()
        out = xhat * vector(g2) + vector(b2)
        index = lax.broadcasted_iota(jnp.int32, (SEG, length), 0).astype(F32)
        member = (index == seg_rows[r]).astype(F32)
        counts = jnp.sum(member, axis=1, keepdims=True)
        high, low = split_low(out)
        member = member.astype(BF16)
        pooled = (nn(member, high) + nn(member, low)) / counts
        inv = lax.rsqrt(jnp.mean(pooled * pooled, axis=-1, keepdims=True) + unit_epsilon)
        unit = pooled * inv
        unitf_o[r] = unit
        unit_o[r] = unit.astype(BF16)
        inv_o[r] = jnp.broadcast_to(inv / counts, inv_o.shape[1:])

    mixed = None
    for r in range(rows):
        mask(r)
        project(r)
        if r > 0:
            norm_one(r - 1, mixed)
        attention(r)
        mixed = mix(r)
    steps = [(r, c) for r in range(rows) for c in range(count)]
    later[1].wait()
    if rows > 1:
        ahead = rise(0, 0)
        norm_one(rows - 1, mixed)
    else:
        norm_one(0, mixed)
        ahead = rise(0, 0)
    fallen = None
    for i, (r, c) in enumerate(steps):
        pre = ahead
        if i + 1 < len(steps):
            ahead = rise(*steps[i + 1])
        bend(r, c, pre)
        if c == 1 and fallen is not None:
            norm_two(r - 1, fallen)
        if c == count - 1:
            if r == 0:
                later[2].wait()
            leaving(6, r).start()
            leaving(7, r).start()
            fallen = nn(act_o[toks[r], :], wdown[...])
    norm_two(rows - 1, fallen)
    for r in range(rows):
        for i in range(10):
            if r == rows - 1 or i > 2:
                leaving(i, r).wait()


def forward(hidden, seg, weights):
    rows, length, _ = hidden.shape
    tokens = rows * length
    _, packed = windows(length)
    packed_shape = (PAIRS, packed, 2 * QB)
    far_shapes = [((tokens, 3 * D), BF16), ((rows,) + packed_shape, BF16)]
    far_shapes += [((tokens, D), BF16)] * 3 + [((tokens, 128), F32)]
    after = [((tokens, FF), BF16)] * 2 + [((tokens, D), BF16), ((tokens, 128), F32)]
    far_shapes += after
    near_shapes = [((rows, SEG, D), BF16), ((rows, SEG, D), F32), ((rows, SEG, 128), F32)]
    kept = [VMEM((length, 3 * D), BF16), VMEM(packed_shape, BF16), VMEM((length, D), BF16)]
    kept += [VMEM((tokens, D), BF16), VMEM((tokens, D), BF16), VMEM((tokens, 128), F32)]
    kept += [VMEM(*a) for a in after]
    large = (0, 3, 7, 9)
    hbm = hspec()
    return pl.pallas_call(
        forward_kernel,
        name="forward",
        in_specs=[hbm, vspec()] + [hbm if i in large else vspec() for i in range(13)],
        out_specs=[hbm] * 10 + [vspec()] * 3,
        out_shape=[pltpu.HBM(*a) for a in far_shapes] + [VMEM(*a) for a in near_shapes],
        scratch_shapes=[VMEM((tokens, D), BF16)]
        + [VMEM(weights[i].shape, BF16) for i in large]
        + [VMEM((packed, QB), F32), VMEM((tokens, D), F32)]
        + kept
        + [pltpu.SemaphoreType.DMA((7 + rows,)), pltpu.SemaphoreType.DMA((rows, 10))],
        cost_estimate=took(33),
        compiler_params=params(58),
    )(*far(hidden.reshape(tokens, D), seg, *weights))


def loss_kernel(flips, idx, *refs):
    pieces, refs = refs[: len(flips)], refs[len(flips) :]
    targets, seg, g2, unitf, inv, xh2, rs2, loss_o, gb_o, vec_o, slope_s, rows_s, units = refs
    twin, me = idx[0], idx[1]
    count = units.shape[0] // 2
    sentences = unitf.shape[0]
    for piece, own_flips in zip(pieces, flips):
        if own_flips is None:
            units[...] = piece[...]
            continue
        for i, (twin_flip, flip) in enumerate(own_flips):
            at = (twin ^ twin_flip) * count + (me ^ flip) * sentences
            at = pl.multiple_of(at, sentences)
            units[pl.ds(at, sentences), :] = piece[i * sentences : (i + 1) * sentences, :]
    rows, length = seg.shape
    step = min(count, 256)
    factor = cosine_scale / D
    positives = units.at[pl.ds(count, count)]
    own = pl.ds(pl.multiple_of(me * sentences, sentences), sentences)

    def one_block(i, carry):
        lanes = pl.ds(pl.multiple_of(i * step, step), step)
        sims = nt(positives[...], units[lanes, :]) * factor
        top = jnp.max(sims, axis=0, keepdims=True)
        weights = jnp.exp(sims - top)
        total = jnp.sum(weights, axis=0, keepdims=True)
        hit = lax.broadcasted_iota(jnp.int32, sims.shape, 0) == targets[:, lanes]
        picked = jnp.sum(jnp.where(hit, sims, 0.0), axis=0, keepdims=True)
        loss_o[:, lanes] = top + jnp.log(total) - picked
        slope = loss_scale * (weights * (1.0 / total) - hit.astype(F32))
        slope_s[:, lanes] = slope.astype(BF16)
        return carry

    if count == step:
        one_block(0, 0)
    else:
        lax.fori_loop(0, count // step, one_block, 0)

    @pl.when(twin == 0)
    def _():
        def part(i, carry):
            lanes = pl.ds(pl.multiple_of(i * step, step), step)
            rows_s[lanes, :] = tn(slope_s[:, lanes], positives[...])
            return carry

        lax.fori_loop(0, count // step, part, 0)
        rows_s[pl.ds(0, sentences), :] = rows_s[own, :]

    @pl.when(twin == 1)
    def _():
        rows_s[pl.ds(0, sentences), :] = nn(slope_s[own, :], units[pl.ds(0, count), :])

    gu = rows_s[pl.ds(0, sentences), :] * factor
    unit = unitf[...]
    gs = inv[:, :1] * (gu - unit * jnp.mean(gu * unit, axis=-1, keepdims=True))
    gy = gs * vector(g2)
    u = gy - jnp.mean(gy, axis=-1, keepdims=True)
    gain = jnp.zeros((1, D), F32)
    shift = jnp.zeros((1, D), F32)
    summed = jnp.zeros((1, D), F32)
    for r in range(rows):
        part = slice(r * SEG, (r + 1) * SEG)
        tok = slice(r * length, (r + 1) * length)
        seg_row = seg[r : r + 1, :]
        hits = lax.broadcasted_iota(jnp.int32, (SEG, length), 0) == seg_row
        member = hits.astype(F32).astype(BF16)
        counts = jnp.sum(hits.astype(F32), axis=1, keepdims=True)
        xhat_low = xh2[tok, :]
        gain += jnp.sum(nn(member, xhat_low) * gs[part], axis=0, keepdims=True)
        shift += jnp.sum(counts * gs[part], axis=0, keepdims=True)
        xhat = xhat_low.astype(F32)
        high, low = split_low(u[part])
        spread = tn(member, high) + tn(member, low)
        inner = jnp.mean(spread * xhat, axis=-1, keepdims=True)
        grad = rs2[tok, :1] * (spread - xhat * inner)
        grad_low = grad.astype(BF16)
        gb_o[tok, :] = grad_low
        summed += jnp.sum(grad_low.astype(F32), axis=0, keepdims=True)
    vec_o[...] = jnp.concatenate([summed, gain, shift, jnp.zeros((5, D), F32)], axis=0)


def loss_stage(idx, gathered, targets, unitf, inv, seg, g2, xh2, rs2, carry):
    pieces, flips = gathered
    tokens = xh2.shape[0]
    count = targets.shape[1]
    return carry_call(
        functools.partial(loss_kernel, flips),
        "loss",
        4,
        20 if count <= 256 else 44,
        (idx, *pieces, *far(targets, seg, g2), unitf, inv, xh2, rs2),
        [sspec()] + [vspec()] * (7 + len(pieces)),
        [shape_of((1, count), F32), shape_of((tokens, D), BF16), shape_of((8, D), F32)],
        [VMEM((count, count), BF16), VMEM((count, D), F32), VMEM((2 * count, D), BF16)],
        carry,
    )


def pre_kernel(gb, wdown, dg, out):
    n = 768

    def product(j):
        return nt(gb[...], wdown[j * n : (j + 1) * n, :])

    ahead = product(0)
    for j in range(FF // n):
        value = ahead
        if j + 1 < FF // n:
            ahead = product(j + 1)
        part = slice(j * n, (j + 1) * n)
        out[:, part] = (value * dg[:, part].astype(F32)).astype(BF16)


def pre_stage(gb, wdown, dg, carry):
    outs = [VMEM(dg.shape, BF16)]
    return carry_call(
        pre_kernel, "grad_pre", 5.2, 24, (gb, wdown, dg), [vspec()] * 3, outs, [], carry
    )


def normed_kernel(gp, win, gb, xh1, rs1, g1, wout, ga_o, gc_o, vec_o):
    m = 512
    count = gp.shape[0] // m
    gain, shift, summed = [jnp.zeros((1, D), F32) for _ in range(3)]
    grads = [nt(gp[i * m : (i + 1) * m, :], win[...]) for i in range(count)]
    for i in range(count):
        rows = slice(i * m, (i + 1) * m)
        grad = grads[i] + gb[rows, :].astype(F32)
        xhat = xh1[rows, :].astype(F32)
        gain += jnp.sum(grad * xhat, axis=0, keepdims=True)
        shift += jnp.sum(grad, axis=0, keepdims=True)
        gy = grad * vector(g1)
        inner = jnp.mean(gy * xhat, axis=-1, keepdims=True)
        total = rs1[rows, :1] * (gy - jnp.mean(gy, axis=-1, keepdims=True) - xhat * inner)
        low = total.astype(BF16)
        ga_o[rows, :] = low
        summed += jnp.sum(low.astype(F32), axis=0, keepdims=True)
    for i in range(count):
        rows = slice(i * m, (i + 1) * m)
        gc_o[rows, :] = nt(ga_o[rows, :], wout[...]).astype(BF16)
    vec_o[...] = jnp.concatenate([summed, gain, shift, jnp.zeros((5, D), F32)], axis=0)


def normed_stage(gp, win, gb, xh1, rs1, g1, wout, carry):
    tokens = gp.shape[0]
    outs = [shape_of((tokens, D), BF16), shape_of((tokens, D), BF16), shape_of((8, D), F32)]
    operands = (gp, win, gb, xh1, rs1, *far(g1), wout)
    return carry_call(
        normed_kernel, "grad_normed", 9, 28, operands, [vspec()] * 7, outs, [], carry
    )


def attend_back_kernel(q_ref, k_ref, v_ref, g_ref, p_ref, out_ref):
    length = q_ref.shape[0]
    blocks, _ = windows(length)
    group = q_ref.shape[1] // PW
    scale = HEAD_DIM**-0.5
    loaded, grads = [], []
    for h in range(group):
        lanes = slice(h * PW, (h + 1) * PW)
        q2 = [two_heads(q_ref[b[0] : b[0] + QB, lanes]) for b in blocks]
        g2 = [two_heads(g_ref[b[0] : b[0] + QB, lanes]) for b in blocks]
        loaded.append((q2, g2, k_ref[:, lanes].T))
        v_all = v_ref[:, lanes]
        grads.append([nt(v_all[b[1] : b[2]], g) for b, g in zip(blocks, g2)])
    slopes = []
    for h in range(group):
        own = []
        for gp, (_, low, high, packed) in zip(grads[h], blocks):
            p = p_ref[h, packed : packed + high - low, :].astype(F32)
            weighted = p * gp
            inner = jnp.sum(weighted, axis=0, keepdims=True)
            own.append((weighted - p * inner).astype(BF16))
        slopes.append(own)

    def gather(parts):
        out = []
        for block in range(len(blocks)):
            total = None
            for part, (_, low, high, _) in zip(parts, blocks):
                base = block * QB - low
                if 0 <= base < high - low:
                    piece = part[base : base + QB]
                    total = piece if total is None else total + piece
            out.append(total)
        return jnp.concatenate(out, axis=0)

    for h in range(group):
        lanes = slice(h * PW, (h + 1) * PW)
        q2, g2, k_turned = loaded[h]
        dq = [nn(k_turned[:, b[1] : b[2]], s) for b, s in zip(blocks, slopes[h])]
        dv = [nn(p_ref[h, b[3] : b[3] + b[2] - b[1], :], g) for b, g in zip(blocks, g2)]
        dk = [nn(s, q) for s, q in zip(slopes[h], q2)]
        turned = [pick_heads((part * scale).astype(BF16)) for part in dq]
        out_ref[0, :, lanes] = jnp.concatenate(turned, axis=0)
        out_ref[1, :, lanes] = (gather(dk) * scale).astype(BF16)
        out_ref[2, :, lanes] = gather(dv).astype(BF16)


def attend_back(qkv, grad_context, probs, rows, length, first, pairs):
    _, packed = windows(length)
    group = 2
    steps = pairs // group
    base = first // group
    width = group * PW

    def block(part):
        return pl.BlockSpec((length, width), lambda r, h: (r, part * (D // width) + base + h))

    return pl.pallas_call(
        attend_back_kernel,
        name="attend_back",
        grid=(rows, steps),
        in_specs=[
            block(0),
            block(1),
            block(2),
            block(0),
            pl.BlockSpec((None, group, packed, 2 * QB), lambda r, h: (r, base + h, 0, 0)),
        ],
        out_specs=pl.BlockSpec((3, length, width), lambda r, h: (0, r, h)),
        out_shape=shape_of((3, rows * length, pairs * PW), BF16),
        cost_estimate=took(2.0 * pairs),
        compiler_params=params(20),
    )(*far(qkv, qkv, qkv), grad_context, *far(probs))


def hidden_kernel(da, db, wqkv, ga, out):
    m = 512
    for i in range(ga.shape[0] // m):
        rows = slice(i * m, (i + 1) * m)
        total = ga[rows, :].astype(F32)
        for part in range(3):
            both = jnp.concatenate([da[part, rows, :], db[part, rows, :]], axis=1)
            total = total + nt(both, wqkv[:, part * D : (part + 1) * D])
        out[rows, :] = total.astype(BF16)


def hidden_stage(da, db, wqkv, ga):
    return pl.pallas_call(
        hidden_kernel,
        name="hidden_grad",
        in_specs=[vspec()] * 4,
        out_specs=vspec(),
        out_shape=shape_of(ga.shape, BF16),
        cost_estimate=took(5.7),
        compiler_params=params(22),
    )(da, db, wqkv, ga)


def place_of(half, quarter, owner):
    c, y, z0, z1 = owner & 1, (owner >> 1) & 1, (owner >> 2) & 1, owner >> 3
    order = (quarter, y, z0, z1, c) if half == 0 else (y, z0, z1, quarter, c)
    out = 0
    for bit in order:
        out = 2 * out + bit
    return out


def lanes_of(width):
    most = 128 if width <= 256 else 256
    return [(low, min(most, width - low)) for low in range(0, width, most)]


def half_shapes(width):
    shapes = [shape_of((32, 48, width), BF16)]
    return shapes + [shape_of((32, 48, n), BF16) for _, n in lanes_of(width)]


def store_piece(first, keep, sends, quarter, owner, piece_a, piece_b):
    at_a, at_b = place_of(0, quarter, owner), place_of(1, quarter, owner)
    keep[jnp.where(first, at_a, at_b)] = jnp.where(first, piece_a, piece_b)
    other = jnp.where(first, piece_b, piece_a)
    at = jnp.where(first, at_b, at_a)
    for send, (low, n) in zip(sends, lanes_of(keep.shape[2])):
        send[at] = other[:, low : low + n]


def down_kernel(idx, act, gb, keep, *sends):
    first = idx[2] == 0
    n = 768

    def product(j):
        return tn(act[:, j * n : (j + 1) * n], gb[...])

    ahead = product(0)
    for j in range(FF // n):
        total = ahead.astype(BF16)
        if j + 1 < FF // n:
            ahead = product(j + 1)
        for local in range(4):
            for quarter in range(2):
                base = local * 192 + quarter * 48
                a, b = total[base : base + 48], total[base + 96 : base + 144]
                store_piece(first, keep, sends, quarter, 4 * j + local, a, b)


def down_stage(idx, act, gb):
    shapes = half_shapes(D)
    return pl.pallas_call(
        down_kernel,
        name="grad_w_down",
        in_specs=[sspec(), vspec(), vspec()],
        out_specs=[vspec()] * len(shapes),
        out_shape=shapes,
        cost_estimate=took(7.5),
        compiler_params=params(22),
    )(idx, act, gb)


def in_kernel(idx, n1, gp, vec_o, keep, *refs):
    sends, turned = refs[:-1], refs[-1]
    first = idx[2] == 0
    turned[...] = n1[...].T

    def products(quarter):
        out = []
        for half in range(2):
            j = 2 * half + quarter
            out.append(nn(turned[...], gp[:, j * D : (j + 1) * D]))
        return out

    ahead = products(0)
    for quarter in range(2):
        a, b = [part.astype(BF16) for part in ahead]
        if quarter == 0:
            ahead = products(1)
        for owner in range(16):
            rows = slice(owner * 48, (owner + 1) * 48)
            store_piece(first, keep, sends, quarter, owner, a[rows], b[rows])
    vec_o[...] = jnp.sum(gp[...].astype(F32), axis=0, keepdims=True)


def in_stage(idx, n1, gp):
    shapes = half_shapes(D)
    return pl.pallas_call(
        in_kernel,
        name="grad_w_in",
        in_specs=[sspec(), vspec(), vspec()],
        out_specs=[vspec()] * (1 + len(shapes)),
        out_shape=[shape_of((1, FF), F32)] + shapes,
        scratch_shapes=[VMEM((D, n1.shape[0]), BF16)],
        cost_estimate=took(7.4),
        compiler_params=params(24),
    )(idx, n1, gp)


WIDE, NARROW = 640, 256


def store_all(first, keep, send, whole, width):
    for quarter in range(2):
        a = whole[:, quarter * width : (quarter + 1) * width]
        b = whole[:, (2 + quarter) * width : (3 + quarter) * width]
        for owner in range(16):
            rows = slice(owner * 48, (owner + 1) * 48)
            store_piece(first, keep, send, quarter, owner, a[rows], b[rows])


def wide_kernel(idx, hid, da, ctx, ga, turned_o, keep, *refs):
    sends, whole = refs[:-1], refs[-1]
    n = da.shape[2]
    turned_o[...] = hid[...].T
    for part in range(3):
        whole[:, part * n : (part + 1) * n] = nn(turned_o[...], da[part]).astype(BF16)
    whole[:, 3 * n : 3 * n + D] = tn(ctx[...], ga[...]).astype(BF16)
    whole[:, 3 * n + D :] = jnp.zeros((D, 4 * WIDE - 3 * n - D), BF16)
    store_all(idx[2] == 0, keep, sends, whole, WIDE)


def wide_stage(idx, hid, da, ctx, ga):
    shapes = half_shapes(WIDE)
    return pl.pallas_call(
        wide_kernel,
        name="grad_w_wide",
        in_specs=[sspec()] + [vspec()] * 4,
        out_specs=[vspec()] * (1 + len(shapes)),
        out_shape=[shape_of((D, hid.shape[0]), BF16)] + shapes,
        scratch_shapes=[VMEM((D, 4 * WIDE), BF16)],
        cost_estimate=took(6),
        compiler_params=params(24),
    )(idx, hid, da, ctx, ga)


def narrow_kernel(idx, turned, da, db, vec1, vec2, bias, keep, *refs):
    send, (whole, sums_s) = refs[:-2], refs[-2:]
    n = db.shape[2]
    for part in range(3):
        whole[:, part * n : (part + 1) * n] = nn(turned[...], db[part]).astype(BF16)
    sums_s[...] = jnp.zeros_like(sums_s)
    sums_s[2:5, :] = vec1[0:3, :]
    sums_s[5:8, :] = vec2[0:3, :]
    for row, part in ((0, 0), (1, 2)):
        for base, grads in ((0, da), (D - n, db)):
            lanes = slice(base, base + grads.shape[2])
            total = jnp.sum(grads[part].astype(F32), axis=0, keepdims=True)
            sums_s[row : row + 1, lanes] = total
    small = sums_s[...].T
    groups = [bias[:, i * 384 : (i + 1) * 384] for i in range(FF // 384)]
    folded = jnp.concatenate(groups, axis=0)
    turned_bias = [folded[:, i * 48 : (i + 1) * 48].T for i in range(8)]
    lane = lax.broadcasted_iota(jnp.int32, (48, 128), 1)
    for owner in range(16):
        own = small[owner * 48 : (owner + 1) * 48]
        for k in range(4):
            column = turned_bias[4 * (owner % 2) + k][:, owner // 2 : owner // 2 + 1]
            own = jnp.where(lane == 8 + k, column, own)
        whole[owner * 48 : (owner + 1) * 48, 3 * n : 3 * n + 128] = own.astype(BF16)
    whole[:, 3 * n + 128 :] = jnp.zeros((D, 4 * NARROW - 3 * n - 128), BF16)
    store_all(idx[2] == 0, keep, send, whole, NARROW)


def narrow_stage(idx, turned, da, db, vec1, vec2, bias):
    return pl.pallas_call(
        narrow_kernel,
        name="grad_w_narrow",
        in_specs=[sspec()] + [vspec()] * 6,
        out_specs=[vspec()] * len(half_shapes(NARROW)),
        out_shape=half_shapes(NARROW),
        scratch_shapes=[VMEM((D, 4 * NARROW), BF16), VMEM((128, D), F32)],
        cost_estimate=took(2.4),
        compiler_params=params(22),
    )(idx, turned, da, db, vec1, vec2, bias)


def swap_dp(value, flip):
    devices = lax.axis_size("dp")
    return lax.ppermute(value, "dp", [(i, i ^ flip) for i in range(devices)])


def swap_twin(value):
    return lax.ppermute(value, "twin", [(0, 1), (1, 0)])


TWIN = 16
ROUTES = ((TWIN, 2, 4, 8, TWIN), (2, 4, 8, TWIN, TWIN))


def step_swap(value, step):
    pairs = [(i, i ^ ROUTES[i & 1][step]) for i in range(2 * TWIN)]
    return lax.ppermute(value, ("twin", "dp"), pairs)


def plus(*values):
    total = values[0].astype(F32)
    for value in values[1:]:
        total = total + value.astype(F32)
    return total.astype(BF16)


def call_small(kernel, name, idx, operands, outs):
    return pl.pallas_call(
        kernel,
        name=name,
        in_specs=[sspec()] + [vspec()] * len(operands),
        out_specs=[vspec()] * len(outs),
        out_shape=[shape_of(shape, dtype) for shape, dtype in outs],
        cost_estimate=took(2.4),
        compiler_params=params(12),
    )(idx, *operands)


def half_kernel(step, idx, keep, recv, keep_o, send_o):
    count = keep_o.shape[0]
    bit = idx[3 + step]
    mine = pl.ds(bit * count, count)
    other = pl.ds((1 - bit) * count, count)
    keep_o[...] = plus(keep[mine], recv[mine])
    send_o[...] = plus(keep[other], recv[other])


def half_step(idx, step, keep, recv):
    count, rows, width = keep.shape
    shape = (count // 2, rows, width)
    kernel = functools.partial(half_kernel, step)
    return call_small(kernel, "sum_" + str(step), idx, (keep, recv), [(shape, BF16)] * 2)


def core_kernel(idx, keep, *refs):
    recvs, (keep_o, send_o) = refs[:-2], refs[-2:]
    bit = idx[3]
    for recv, (low, n) in zip(recvs, lanes_of(keep.shape[3])):
        lanes = slice(low, low + n)
        keep_o[:, :, lanes] = plus(keep[bit, :, :, lanes], recv[bit])
        send_o[:, :, lanes] = plus(keep[1 - bit, :, :, lanes], recv[1 - bit])


def core_step(idx, keep, recvs):
    count, rows, width = keep.shape
    half = count // 2
    pieces = 4
    part = half // pieces

    def spec(n):
        return pl.BlockSpec((2, part, rows, n), lambda i: (0, i, 0, 0))

    return pl.pallas_call(
        core_kernel,
        name="sum_core",
        grid=(pieces,),
        in_specs=[sspec(), spec(width)] + [spec(n) for _, n in lanes_of(width)],
        out_specs=[pl.BlockSpec((part, rows, width), lambda i: (i, 0, 0))] * 2,
        out_shape=[shape_of((half, rows, width), BF16)] * 2,
        cost_estimate=took(1.7),
        compiler_params=params(10),
    )(
        idx,
        keep.reshape(2, half, rows, width),
        *[recv.reshape(2, half, rows, recv.shape[2]) for recv in recvs],
    )


def own_kernel(idx, keep, recv, out):
    out[...] = plus(keep[...], recv[...])


def turn_kernel(idx, own, other, keep_o, send_o):
    twin, core = idx[0], idx[2]
    keep_o[twin] = own[core]
    keep_o[1 - twin] = other[core]
    send_o[twin] = own[1 - core]
    send_o[1 - twin] = other[1 - core]


class Order:
    def __init__(self):
        self.last = None

    def after(self, value, *others):
        if self.last is None:
            return value
        return lax.optimization_barrier((value, self.last) + others)[0]

    def done(self, value):
        self.last = value
        return value


class Exchange:
    def __init__(self, order, idx, keep, sends):
        self.order, self.idx, self.step = order, idx, 0
        self.keep, self.recv = keep, [swap_dp(send, 1) for send in sends]

    def advance(self):
        idx, order = self.idx, self.order
        keep, recv = order.after(self.keep), self.recv
        if self.step == 0:
            keep, send = core_step(idx, keep, recv)
            recv = step_swap(send, 0)
        elif self.step < 4:
            keep, send = half_step(idx, self.step, keep, recv)
            recv = step_swap(send, self.step)
        elif self.step == 4:
            shape = keep.shape
            (keep,) = call_small(own_kernel, "sum_4", idx, (keep, recv), [(shape, BF16)])
            recv = step_swap(keep, 4)
        else:
            shape = keep.shape
            keep, send = call_small(turn_kernel, "turn", idx, (keep, recv), [(shape, BF16)] * 2)
            recv = swap_dp(send, 1)
        order.done(keep)
        self.keep, self.recv = keep, recv
        self.step += 1

    def result(self):
        return self.keep, self.recv


def bring_kernel(*refs):
    del refs


def bring(values):
    return carry_call(bring_kernel, "bring", 1.2, 4, (), [], [], [], values)


def gather_units(unit, wanted):
    flips = [(0, 0)]
    for flip in (8, 4):
        unit = jnp.concatenate([unit, swap_dp(unit, flip)], axis=0)
        flips = flips + [(t, f ^ flip) for t, f in flips]
    wanted = bring((lax.optimization_barrier((wanted[0], unit))[0],) + wanted[1:])
    pairs = [(i, i ^ (TWIN + 2)) for i in range(2 * TWIN)]
    corner = lax.ppermute(unit, ("twin", "dp"), pairs)
    unit = jnp.concatenate([unit, swap_dp(unit, 2), swap_twin(unit), corner], axis=0)
    flips = [(t ^ a, f ^ b) for a, b in ((0, 0), (0, 2), (1, 0), (1, 2)) for t, f in flips]
    return ((unit, swap_dp(unit, 1)), (flips, [(t, f ^ 1) for t, f in flips])), wanted


def four_quarters(idx, keep, recv):
    first = idx[2] == 0
    low = [jnp.where(first, keep[i], recv[i]) for i in range(2)]
    high = [jnp.where(first, recv[i], keep[i]) for i in range(2)]
    return low + high


def final_in_kernel(idx, keep, recv, out):
    for i, part in enumerate(four_quarters(idx, keep, recv)):
        out[:, i * D : (i + 1) * D] = part.astype(F32)


def final_down_kernel(idx, keep, recv, out):
    for i, part in enumerate(four_quarters(idx, keep, recv)):
        out[i * 48 : (i + 1) * 48, :] = part.astype(F32)


def final_last_kernel(idx, wide_k, wide_r, narrow_k, narrow_r, qkv_o, out_o, *vec_o):
    wide = jnp.concatenate(four_quarters(idx, wide_k, wide_r), axis=1).astype(F32)
    narrow = jnp.concatenate(four_quarters(idx, narrow_k, narrow_r), axis=1).astype(F32)
    low, high = 2 * D // 3, D // 3
    for part in range(3):
        qkv_o[:, part * D : part * D + low] = wide[:, part * low : (part + 1) * low]
        qkv_o[:, part * D + low : (part + 1) * D] = narrow[:, part * high : (part + 1) * high]
    out_o[...] = wide[:, 3 * low : 3 * low + D]
    small = narrow[:, 3 * high : 3 * high + 128]
    turned = jnp.concatenate([small, jnp.zeros((80, 128), F32)], axis=0).T
    for i in range(8):
        vec_o[i][...] = turned[i, :48]
    whole = jnp.concatenate([turned[8 + i : 9 + i, :48] for i in range(4)], axis=1)
    vec_o[8][...] = whole.reshape(192)


def finish(order, idx, kernel, name, chunks, outs):
    operands = [value for chunk in chunks for value in chunk.result()]
    operands[0] = order.after(operands[0])
    out = call_small(kernel, name, idx, operands, outs)
    order.done(out[0])
    return out


def add_low(*parts):
    return lax.optimization_barrier(plus(*parts))


def digits_of(devices):
    out, rest = [], devices // 2
    while rest > 1:
        size = 4 if rest % 4 == 0 else 2
        out.append(size)
        rest //= size
    return out


def pick(value, index, axis):
    return lax.dynamic_index_in_dim(value, index, axis, keepdims=False)


def scatter(grad):
    devices = lax.axis_size("dp")
    me = lax.axis_index("dp")
    value = grad.reshape(devices, grad.shape[0] // devices, grad.shape[1])
    unit = 1
    for size in [2] + digits_of(devices):
        mine = (me // unit) % size
        view = value.reshape((value.shape[0] // size, size) + value.shape[1:])
        parts = [pick(view, mine, 1)]
        for flip in range(1, size):
            parts.append(swap_dp(pick(view, mine ^ flip, 1), flip * unit))
        value = add_low(*parts)
        unit *= size
    value = value[0]
    return value.astype(F32) + swap_twin(value).astype(F32)


SEQUENCE = (
    "down", "pre", "d", "in", "normed", "d", "i", "attend_a", "d", "wide", "i", "attend_b", "w",
    "d", "narrow", "i", "n", "hidden", "d", "w", "i", "n", "d", "w", "i", "n", "final_d", "i",
    "w", "n", "final_i", "w", "n", "w", "n",
)


def body(
    hidden,
    segment_ids,
    targets,
    w_qkv,
    b_query,
    b_value,
    w_out,
    b_out,
    ln1_gain,
    ln1_bias,
    w_in,
    b_in,
    w_down,
    b_down,
    ln2_gain,
    ln2_bias,
):
    row_count, length, width = hidden.shape
    tokens = row_count * length
    devices = lax.axis_size("dp")
    everyone = lax.axis_size(("twin", "dp"))
    me = lax.axis_index("dp")
    twin = lax.axis_index("twin")
    core, y, z0, z1 = me & 1, (me >> 1) & 1, (me >> 2) & 1, me >> 3
    first = core == 0
    bits = [jnp.where(first, a, b) for a, b in ((twin, y), (y, z0), (z0, z1), (z1, twin))]
    idx = jnp.stack([twin, me, core] + bits).astype(jnp.int32)
    weights = (w_qkv, b_query, b_value, w_out, b_out, ln1_gain, ln1_bias)
    weights += (w_in, b_in, w_down, b_down, ln2_gain, ln2_bias)
    qkv, probs, ctx, n1, xh1, rs1, act, dg, xh2, rs2, unit, unitf, inv = forward(
        hidden, segment_ids, weights
    )
    sentences = row_count * SEG
    unit = unit.reshape(sentences, width)
    direct = devices == TWIN and sentences == 16
    if direct:
        gathered, (xh2, rs2) = gather_units(unit, (xh2, rs2))
    else:
        gathered = ((lax.all_gather(unit, ("twin", "dp"), axis=0, tiled=True),), (None,))
    losses, gb, vec2, act_near = loss_stage(
        idx,
        gathered,
        targets.reshape(1, -1),
        unitf.reshape(sentences, width),
        inv.reshape(sentences, 128),
        segment_ids,
        ln2_gain,
        xh2,
        rs2,
        (act,),
    )
    share = losses.shape[1] // everyone
    losses = lax.dynamic_slice_in_dim(
        losses[0], lax.axis_index(("twin", "dp")) * share, share, 0
    )
    flat = hidden.reshape(tokens, width)
    if direct:
        order = Order()
        chunks = {}

        def begin(name, keep, sends):
            order.done(keep)
            chunks[name] = Exchange(order, idx, keep, sends)

        for stage in SEQUENCE:
            if stage == "down":
                halves_d = down_stage(idx, act_near, order.after(gb))
                begin("d", halves_d[0], halves_d[1:])
            elif stage == "pre":
                near = (n1, xh1, rs1)
                gp, *near = pre_stage(order.after(gb), w_down, dg, near)
                order.done(gp)
            elif stage == "in":
                sums, *halves_in = in_stage(idx, near[0], order.after(gp))
                begin("i", halves_in[0], halves_in[1:])
            elif stage == "normed":
                ga, gc, vec1, *later = normed_stage(
                    order.after(gp), w_in, gb, near[1], near[2], ln1_gain, w_out, (flat, ctx)
                )
                order.done(ga)
            elif stage == "attend_a":
                da = order.done(attend_back(qkv, order.after(gc), probs, row_count, length, 0, 4))
            elif stage == "attend_b":
                db = order.done(attend_back(qkv, order.after(gc), probs, row_count, length, 4, 2))
            elif stage == "wide":
                turned, *halves_w = wide_stage(idx, later[0], order.after(da), later[1], ga)
                begin("w", halves_w[0], halves_w[1:])
            elif stage == "narrow":
                halves_n = narrow_stage(idx, turned, da, order.after(db), vec1, vec2, sums)
                begin("n", halves_n[0], halves_n[1:])
            elif stage == "hidden":
                hidden_grad = order.done(hidden_stage(da, order.after(db), w_qkv, ga))
            elif stage == "final_d":
                outs = [((192, D), F32)]
                (grad_w_down,) = finish(order, idx, final_down_kernel, stage, [chunks["d"]], outs)
            elif stage == "final_i":
                outs = [((48, FF), F32)]
                (grad_w_in,) = finish(order, idx, final_in_kernel, stage, [chunks["i"]], outs)
            else:
                chunks[stage].advance()
        wide, narrow = chunks["w"], chunks["n"]
        shapes = [((48, 3 * D), F32), ((48, D), F32)] + [((48,), F32)] * 8 + [((192,), F32)]
        grad_w_qkv, grad_w_out, *vecs, grad_b_in = finish(
            order, idx, final_last_kernel, "final_last", [wide, narrow], shapes
        )
    else:
        gp, _ = pre_stage(gb, w_down, dg, (n1,))
        ga, gc, vec1, _ = normed_stage(gp, w_in, gb, xh1, rs1, ln1_gain, w_out, (ctx,))
        da = attend_back(qkv, gc, probs, row_count, length, 0, 4)
        db = attend_back(qkv, gc, probs, row_count, length, 4, 2)
        hidden_grad = hidden_stage(da, db, w_qkv, ga)
        dqkv = jnp.concatenate([da, db], axis=2)
        grad_w_down = scatter(tn(act, gb).astype(BF16))
        grad_w_in = scatter(tn(n1, gp).astype(BF16))
        wide = jnp.concatenate([dqkv[0], dqkv[1], dqkv[2]], axis=1)
        grad_w_qkv = scatter(tn(flat, wide).astype(BF16))
        grad_w_out = scatter(tn(ctx, ga).astype(BF16))
        sums = jnp.sum(dqkv, axis=1, dtype=F32)
        vec = jnp.concatenate([sums[0:1], sums[2:3], vec1[:3], vec2[:3]])
        vec = scatter(jnp.pad(vec, ((0, 120), (0, 0))).T.astype(BF16)).T
        vecs = [vec[i] for i in range(8)]
        bias = jnp.sum(gp, axis=0, dtype=F32)
        grad_b_in = scatter(jnp.broadcast_to(bias[:, None], (FF, 128)).astype(BF16))[:, 0]
    return (
        losses,
        hidden_grad.reshape(row_count, length, width),
        grad_w_qkv,
        vecs[0],
        vecs[1],
        grad_w_out,
        vecs[2],
        vecs[3],
        vecs[4],
        grad_w_in,
        grad_b_in,
        grad_w_down,
        vecs[5],
        vecs[6],
        vecs[7],
    )


def solution(mesh):
    whole = (P(),) * 14
    placed = (P(("twin", "dp"), None, None), P(("twin", "dp"), None)) + whole
    return jax.shard_map(
        body,
        mesh=mesh,
        in_specs=placed,
        out_specs=(
            P(("twin", "dp")),
            P(("twin", "dp"), None, None),
            P("dp", None),
            P("dp"),
            P("dp"),
            P("dp", None),
            P("dp"),
            P("dp"),
            P("dp"),
            P("dp", None),
            P("dp"),
            P("dp", None),
            P("dp"),
            P("dp"),
            P("dp"),
        ),
        check_vma=False,
    )
```

```python
import functools

import jax
import jax.numpy as jnp
from jax import lax
from jax.experimental import pallas as pl
from jax.experimental.pallas import tpu as pltpu
from jax.sharding import PartitionSpec as P

D = 768
HEADS = 12
HEAD_DIM = 64
FF = 3072
SEG = 8
QB = 128
MOST = 128
PAIRS = HEADS // 2
PW = 2 * HEAD_DIM

cosine_scale = 64.0
loss_scale = 32.0
norm_epsilon = 1e-12
unit_epsilon = 1e-06
masked_score = -1e30

F32 = jnp.float32
BF16 = jnp.bfloat16
VMEM = pltpu.VMEM
ANY = pl.ANY
MIB = 1 << 20


def nn(left, right):
    return lax.dot_general(left, right, (((1,), (0,)), ((), ())), preferred_element_type=F32)


def nt(left, right):
    return lax.dot_general(left, right, (((1,), (1,)), ((), ())), preferred_element_type=F32)


def tn(left, right):
    return lax.dot_general(left, right, (((0,), (0,)), ((), ())), preferred_element_type=F32)


def vspec():
    return pl.BlockSpec(memory_space=VMEM)


def sspec():
    return pl.BlockSpec(memory_space=pltpu.SMEM)


def hspec():
    return pl.BlockSpec(memory_space=pltpu.HBM)


def far(*values):
    return [pltpu.with_memory_space_constraint(value, pltpu.HBM) for value in values]


class Fetch:
    def __init__(self, sems, pairs):
        self.copies = [pltpu.make_async_copy(a, b, sems.at[i]) for i, (a, b) in enumerate(pairs)]
        for copy in self.copies:
            copy.start()

    def wait(self, *which):
        for i in which:
            self.copies[i].wait()


def carrying(kernel, n_in, n_out, n_carry):
    def wrapped(*refs):
        refs, sems = refs[:-1], refs[-1]
        ins, refs = refs[:n_in], refs[n_in:]
        sources, refs = refs[:n_carry], refs[n_carry:]
        outs, refs = refs[:n_out], refs[n_out:]
        targets, rest = refs[:n_carry], refs[n_carry:]
        fetch = Fetch(sems, tuple(zip(sources, targets)))
        kernel(*ins, *outs, *rest)
        fetch.wait(*range(n_carry))

    return wrapped


def carry_call(kernel, name, us, mib, operands, specs, outs, scratch, carry):
    n_carry = len(carry)
    return pl.pallas_call(
        carrying(kernel, len(operands), len(outs), n_carry),
        name=name,
        in_specs=list(specs) + [hspec()] * n_carry,
        out_specs=[vspec()] * (len(outs) + n_carry),
        out_shape=list(outs) + [VMEM(a.shape, a.dtype) for a in carry],
        scratch_shapes=list(scratch) + [pltpu.SemaphoreType.DMA((max(n_carry, 1),))],
        cost_estimate=took(us),
        compiler_params=params(mib),
    )(*operands, *far(*carry))


def fixed(shape):
    return pl.BlockSpec(shape, lambda *_: (0,) * len(shape))


def shape_of(shape, dtype):
    return jax.ShapeDtypeStruct(shape, dtype)


def params(mib):
    return pltpu.CompilerParams(vmem_limit_bytes=mib * MIB)


SCALE = 0.4


def took(us):
    return pl.CostEstimate(flops=int(us * SCALE * 1.15e9), bytes_accessed=0, transcendentals=0)


def windows(length):
    out, packed = [], 0
    for start in range(0, length, QB):
        low, high = max(0, start - MOST), min(length, start + QB + MOST)
        out.append((start, low, high, packed))
        packed += high - low
    return out, packed


def two_heads(pair):
    first = lax.broadcasted_iota(jnp.int32, pair.shape, 1) < HEAD_DIM
    zero = jnp.zeros((), pair.dtype)
    return jnp.concatenate([jnp.where(first, pair, zero), jnp.where(first, zero, pair)], axis=0)


def pick_heads(both):
    rows = both.shape[1] // 2
    return jnp.concatenate([both[:HEAD_DIM, :rows], both[HEAD_DIM:, rows:]], axis=0).T


def column_of(row):
    return jnp.broadcast_to(row, (8, row.shape[1])).T[:, :1]


def split_low(value):
    high = value.astype(BF16)
    return high, (value - high.astype(F32)).astype(BF16)


def normalise(value):
    middle = jnp.mean(value, axis=-1, keepdims=True)
    centered = value - middle
    spread = jnp.mean(centered * centered, axis=-1, keepdims=True)
    rstd = lax.rsqrt(spread + norm_epsilon)
    return centered * rstd, rstd


def vector(ref):
    return ref[...].astype(F32).reshape(1, ref.shape[0])


def softmax_down(own):
    top = jnp.max(own, axis=0, keepdims=True)
    weights = jnp.exp(own - top)
    total = jnp.sum(weights, axis=0, keepdims=True)
    return (weights * (1.0 / total)).astype(BF16)


def attend(length, qkv, bias, p_s, ctx_s):
    blocks, _ = windows(length)

    def lanes(part, h):
        return slice(part * D + h * PW, part * D + (h + 1) * PW)

    def score(h):
        q_all = qkv[:, lanes(0, h)] * jnp.asarray(HEAD_DIM**-0.5, BF16)
        k_all = qkv[:, lanes(1, h)]
        out = []
        for start, low, high, _ in blocks:
            out.append(nt(k_all[low:high], two_heads(q_all[start : start + QB])))
        return out, qkv[:, lanes(2, h)].T

    ahead = score(0)
    for h in range(PAIRS):
        scores, v_turned = ahead
        if h + 1 < PAIRS:
            ahead = score(h + 1)
        probs = []
        for own, (_, low, high, packed) in zip(scores, blocks):
            mask = bias[packed : packed + high - low, :]
            halves = [softmax_down(own[:, :QB] + mask), softmax_down(own[:, QB:] + mask)]
            probs.append(jnp.concatenate(halves, axis=1))
        for p, (_, low, high, packed) in zip(probs, blocks):
            p_s[h, packed : packed + high - low, :] = p
        outs = [nn(v_turned[:, low:high], p) for p, (_, low, high, _) in zip(probs, blocks)]
        ctx_s[:, lanes(0, h)] = jnp.concatenate([pick_heads(o.astype(BF16)) for o in outs], axis=0)


def forward_kernel(*refs):
    (hid_h, seg, wqkv_h, bq, bv, wout_h, bout, g1, b1, win_h, bin_, wdown_h, bdown, g2, b2) = refs[:15]
    outs, (unit_o, unitf_o, inv_o) = refs[15:25], refs[25:28]
    hid, wqkv, wout, win, wdown, bias_s, n1_s = refs[28:35]
    kept = refs[35:45]
    sems, osems = refs[45:47]
    qkv_s, p_s, ctx_s, nl_s, xh1_s, rs1_s, act_o, dg_o, xh2_o, rs2_o = kept
    rows = seg.shape[0]
    length = hid.shape[0] // rows
    blocks, _ = windows(length)
    toks = [slice(r * length, (r + 1) * length) for r in range(rows)]
    parts = [slice(part * D, (part + 1) * D) for part in range(3)]

    pairs = [(hid_h.at[toks[0]], hid.at[toks[0]])]
    pairs += [(wqkv_h.at[:, cols], wqkv.at[:, cols]) for cols in parts]
    first = Fetch(sems, pairs)
    later = []

    def fetch_rest():
        rest = [(wout_h, wout), (win_h, win), (wdown_h, wdown)]
        rest += [(hid_h.at[tok], hid.at[tok]) for tok in toks[1:]]
        for i, (source, target) in enumerate(rest):
            copy = pltpu.make_async_copy(source, target, sems.at[4 + i])
            copy.start()
            later.append(copy)

    def leaving(i, r):
        if i == 1:
            return pltpu.make_async_copy(p_s, outs[1].at[r], osems.at[r, 1])
        source = kept[i] if i in (0, 2) else kept[i].at[toks[r]]
        return pltpu.make_async_copy(source, outs[i].at[toks[r]], osems.at[r, i])

    seg_rows = [seg[r : r + 1, :].astype(F32) for r in range(rows)]

    def mask(r):
        seg_col = column_of(seg_rows[r])
        for start, low, high, packed in blocks:
            same = seg_col[low:high] == seg_rows[r][:, start : start + QB]
            bias_s[packed : packed + high - low, :] = jnp.where(same, 0.0, masked_score)

    def project(r):
        if r > 0:
            leaving(0, r - 1).wait()
            later[2 + r].wait()
        for part, cols in enumerate(parts):
            if r == 0:
                first.wait(*((0, 1) if part == 0 else (part + 1,)))
                if part == 0:
                    fetch_rest()
            value = nn(hid[toks[r], :], wqkv[:, cols])
            if part == 0:
                value = value + vector(bq)
            if part == 2:
                value = value + vector(bv)
            qkv_s[:, cols] = value.astype(BF16)
        leaving(0, r).start()

    def attention(r):
        if r > 0:
            leaving(1, r - 1).wait()
            leaving(2, r - 1).wait()
        attend(length, qkv_s, bias_s, p_s, ctx_s)
        leaving(1, r).start()
        leaving(2, r).start()

    def mix(r):
        if r == 0:
            later[0].wait()
        return nn(ctx_s[...], wout[...])

    def norm_one(r, attended):
        tok = toks[r]
        xhat, rstd = normalise(hid[tok, :].astype(F32) + (attended + vector(bout)))
        xh1_s[tok, :] = xhat.astype(BF16)
        rs1_s[tok, :] = jnp.broadcast_to(rstd, (length, rs1_s.shape[1]))
        n1 = xhat * vector(g1) + vector(b1)
        n1_s[tok, :] = n1
        nl_s[tok, :] = n1.astype(BF16)
        for i in (3, 4, 5):
            leaving(i, r).start()

    chunk = 768
    count = FF // chunk
    bias_in = vector(bin_)

    def rise(r, c):
        cols = slice(c * chunk, (c + 1) * chunk)
        return nn(nl_s[toks[r], :], win[:, cols]) + bias_in[:, cols]

    def bend(r, c, pre):
        cols = slice(c * chunk, (c + 1) * chunk)
        half = 0.5 + 0.5 * lax.erf(pre * 0.5**0.5)
        act_o[toks[r], cols] = (pre * half).astype(BF16)
        bell = jnp.exp(pre * pre * -0.5) * 0.3989422804014327
        dg_o[toks[r], cols] = (half + pre * bell).astype(BF16)

    def norm_two(r, fallen):
        tok = toks[r]
        xhat, rstd = normalise(n1_s[tok, :] + (fallen + vector(bdown)))
        xh2_o[tok, :] = xhat.astype(BF16)
        rs2_o[tok, :] = jnp.broadcast_to(rstd, (length, rs2_o.shape[1]))
        leaving(8, r).start()
        leaving(9, r).start()
        out = xhat * vector(g2) + vector(b2)
        index = lax.broadcasted_iota(jnp.int32, (SEG, length), 0).astype(F32)
        member = (index == seg_rows[r]).astype(F32)
        counts = jnp.sum(member, axis=1, keepdims=True)
        high, low = split_low(out)
        member = member.astype(BF16)
        pooled = (nn(member, high) + nn(member, low)) / counts
        inv = lax.rsqrt(jnp.mean(pooled * pooled, axis=-1, keepdims=True) + unit_epsilon)
        unit = pooled * inv
        unitf_o[r] = unit
        unit_o[r] = unit.astype(BF16)
        inv_o[r] = jnp.broadcast_to(inv / counts, inv_o.shape[1:])

    mixed = None
    for r in range(rows):
        mask(r)
        project(r)
        if r > 0:
            norm_one(r - 1, mixed)
        attention(r)
        mixed = mix(r)
    steps = [(r, c) for r in range(rows) for c in range(count)]
    later[1].wait()
    if rows > 1:
        ahead = rise(0, 0)
        norm_one(rows - 1, mixed)
    else:
        norm_one(0, mixed)
        ahead = rise(0, 0)
    fallen = None
    for i, (r, c) in enumerate(steps):
        pre = ahead
        if i + 1 < len(steps):
            ahead = rise(*steps[i + 1])
        bend(r, c, pre)
        if c == 1 and fallen is not None:
            norm_two(r - 1, fallen)
        if c == count - 1:
            if r == 0:
                later[2].wait()
            leaving(6, r).start()
            leaving(7, r).start()
            fallen = nn(act_o[toks[r], :], wdown[...])
    norm_two(rows - 1, fallen)
    for r in range(rows):
        for i in range(10):
            if r == rows - 1 or i > 2:
                leaving(i, r).wait()


def forward(hidden, seg, weights):
    rows, length, _ = hidden.shape
    tokens = rows * length
    _, packed = windows(length)
    packed_shape = (PAIRS, packed, 2 * QB)
    far_shapes = [((tokens, 3 * D), BF16), ((rows,) + packed_shape, BF16)]
    far_shapes += [((tokens, D), BF16)] * 3 + [((tokens, 128), F32)]
    after = [((tokens, FF), BF16)] * 2 + [((tokens, D), BF16), ((tokens, 128), F32)]
    far_shapes += after
    near_shapes = [((rows, SEG, D), BF16), ((rows, SEG, D), F32), ((rows, SEG, 128), F32)]
    kept = [VMEM((length, 3 * D), BF16), VMEM(packed_shape, BF16), VMEM((length, D), BF16)]
    kept += [VMEM((tokens, D), BF16), VMEM((tokens, D), BF16), VMEM((tokens, 128), F32)]
    kept += [VMEM(*a) for a in after]
    large = (0, 3, 7, 9)
    hbm = hspec()
    return pl.pallas_call(
        forward_kernel,
        name="forward",
        in_specs=[hbm, vspec()] + [hbm if i in large else vspec() for i in range(13)],
        out_specs=[hbm] * 10 + [vspec()] * 3,
        out_shape=[pltpu.HBM(*a) for a in far_shapes] + [VMEM(*a) for a in near_shapes],
        scratch_shapes=[VMEM((tokens, D), BF16)]
        + [VMEM(weights[i].shape, BF16) for i in large]
        + [VMEM((packed, QB), F32), VMEM((tokens, D), F32)]
        + kept
        + [pltpu.SemaphoreType.DMA((7 + rows,)), pltpu.SemaphoreType.DMA((rows, 10))],
        cost_estimate=took(33),
        compiler_params=params(58),
    )(*far(hidden.reshape(tokens, D), seg, *weights))


def loss_kernel(flips, idx, *refs):
    pieces, refs = refs[: len(flips)], refs[len(flips) :]
    targets, seg, g2, unitf, inv, xh2, rs2, loss_o, gb_o, vec_o, slope_s, rows_s, units = refs
    twin, me = idx[0], idx[1]
    count = units.shape[0] // 2
    sentences = unitf.shape[0]
    for piece, own_flips in zip(pieces, flips):
        if own_flips is None:
            units[...] = piece[...]
            continue
        for i, (twin_flip, flip) in enumerate(own_flips):
            at = (twin ^ twin_flip) * count + (me ^ flip) * sentences
            at = pl.multiple_of(at, sentences)
            units[pl.ds(at, sentences), :] = piece[i * sentences : (i + 1) * sentences, :]
    rows, length = seg.shape
    step = min(count, 256)
    factor = cosine_scale / D
    positives = units.at[pl.ds(count, count)]
    own = pl.ds(pl.multiple_of(me * sentences, sentences), sentences)

    def one_block(i, carry):
        lanes = pl.ds(pl.multiple_of(i * step, step), step)
        sims = nt(positives[...], units[lanes, :]) * factor
        top = jnp.max(sims, axis=0, keepdims=True)
        weights = jnp.exp(sims - top)
        total = jnp.sum(weights, axis=0, keepdims=True)
        hit = lax.broadcasted_iota(jnp.int32, sims.shape, 0) == targets[:, lanes]
        picked = jnp.sum(jnp.where(hit, sims, 0.0), axis=0, keepdims=True)
        loss_o[:, lanes] = top + jnp.log(total) - picked
        slope = loss_scale * (weights * (1.0 / total) - hit.astype(F32))
        slope_s[:, lanes] = slope.astype(BF16)
        return carry

    if count == step:
        one_block(0, 0)
    else:
        lax.fori_loop(0, count // step, one_block, 0)

    @pl.when(twin == 0)
    def _():
        def part(i, carry):
            lanes = pl.ds(pl.multiple_of(i * step, step), step)
            rows_s[lanes, :] = tn(slope_s[:, lanes], positives[...])
            return carry

        lax.fori_loop(0, count // step, part, 0)
        rows_s[pl.ds(0, sentences), :] = rows_s[own, :]

    @pl.when(twin == 1)
    def _():
        rows_s[pl.ds(0, sentences), :] = nn(slope_s[own, :], units[pl.ds(0, count), :])

    gu = rows_s[pl.ds(0, sentences), :] * factor
    unit = unitf[...]
    gs = inv[:, :1] * (gu - unit * jnp.mean(gu * unit, axis=-1, keepdims=True))
    gy = gs * vector(g2)
    u = gy - jnp.mean(gy, axis=-1, keepdims=True)
    gain = jnp.zeros((1, D), F32)
    shift = jnp.zeros((1, D), F32)
    summed = jnp.zeros((1, D), F32)
    for r in range(rows):
        part = slice(r * SEG, (r + 1) * SEG)
        tok = slice(r * length, (r + 1) * length)
        seg_row = seg[r : r + 1, :]
        hits = lax.broadcasted_iota(jnp.int32, (SEG, length), 0) == seg_row
        member = hits.astype(F32).astype(BF16)
        counts = jnp.sum(hits.astype(F32), axis=1, keepdims=True)
        xhat_low = xh2[tok, :]
        gain += jnp.sum(nn(member, xhat_low) * gs[part], axis=0, keepdims=True)
        shift += jnp.sum(counts * gs[part], axis=0, keepdims=True)
        xhat = xhat_low.astype(F32)
        high, low = split_low(u[part])
        spread = tn(member, high) + tn(member, low)
        inner = jnp.mean(spread * xhat, axis=-1, keepdims=True)
        grad = rs2[tok, :1] * (spread - xhat * inner)
        grad_low = grad.astype(BF16)
        gb_o[tok, :] = grad_low
        summed += jnp.sum(grad_low.astype(F32), axis=0, keepdims=True)
    vec_o[...] = jnp.concatenate([summed, gain, shift, jnp.zeros((5, D), F32)], axis=0)


def loss_stage(idx, gathered, targets, unitf, inv, seg, g2, xh2, rs2, carry):
    pieces, flips = gathered
    tokens = xh2.shape[0]
    count = targets.shape[1]
    return carry_call(
        functools.partial(loss_kernel, flips),
        "loss",
        4,
        20 if count <= 256 else 44,
        (idx, *pieces, *far(targets, seg, g2), unitf, inv, xh2, rs2),
        [sspec()] + [vspec()] * (7 + len(pieces)),
        [shape_of((1, count), F32), shape_of((tokens, D), BF16), shape_of((8, D), F32)],
        [VMEM((count, count), BF16), VMEM((count, D), F32), VMEM((2 * count, D), BF16)],
        carry,
    )


def pre_kernel(gb, wdown, dg, out):
    n = 768

    def product(j):
        return nt(gb[...], wdown[j * n : (j + 1) * n, :])

    ahead = product(0)
    for j in range(FF // n):
        value = ahead
        if j + 1 < FF // n:
            ahead = product(j + 1)
        part = slice(j * n, (j + 1) * n)
        out[:, part] = (value * dg[:, part].astype(F32)).astype(BF16)


def pre_stage(gb, wdown, dg, carry):
    outs = [VMEM(dg.shape, BF16)]
    return carry_call(
        pre_kernel, "grad_pre", 5.2, 24, (gb, wdown, dg), [vspec()] * 3, outs, [], carry
    )


def normed_kernel(gp, win, gb, xh1, rs1, g1, wout, ga_o, gc_o, vec_o):
    m = 512
    count = gp.shape[0] // m
    gain, shift, summed = [jnp.zeros((1, D), F32) for _ in range(3)]
    grads = [nt(gp[i * m : (i + 1) * m, :], win[...]) for i in range(count)]
    for i in range(count):
        rows = slice(i * m, (i + 1) * m)
        grad = grads[i] + gb[rows, :].astype(F32)
        xhat = xh1[rows, :].astype(F32)
        gain += jnp.sum(grad * xhat, axis=0, keepdims=True)
        shift += jnp.sum(grad, axis=0, keepdims=True)
        gy = grad * vector(g1)
        inner = jnp.mean(gy * xhat, axis=-1, keepdims=True)
        total = rs1[rows, :1] * (gy - jnp.mean(gy, axis=-1, keepdims=True) - xhat * inner)
        low = total.astype(BF16)
        ga_o[rows, :] = low
        summed += jnp.sum(low.astype(F32), axis=0, keepdims=True)
    for i in range(count):
        rows = slice(i * m, (i + 1) * m)
        gc_o[rows, :] = nt(ga_o[rows, :], wout[...]).astype(BF16)
    vec_o[...] = jnp.concatenate([summed, gain, shift, jnp.zeros((5, D), F32)], axis=0)


def normed_stage(gp, win, gb, xh1, rs1, g1, wout, carry):
    tokens = gp.shape[0]
    outs = [shape_of((tokens, D), BF16), shape_of((tokens, D), BF16), shape_of((8, D), F32)]
    operands = (gp, win, gb, xh1, rs1, *far(g1), wout)
    return carry_call(
        normed_kernel, "grad_normed", 9, 28, operands, [vspec()] * 7, outs, [], carry
    )


def attend_back_kernel(q_ref, k_ref, v_ref, g_ref, p_ref, out_ref):
    length = q_ref.shape[0]
    blocks, _ = windows(length)
    group = q_ref.shape[1] // PW
    scale = HEAD_DIM**-0.5
    loaded, grads = [], []
    for h in range(group):
        lanes = slice(h * PW, (h + 1) * PW)
        q2 = [two_heads(q_ref[b[0] : b[0] + QB, lanes]) for b in blocks]
        g2 = [two_heads(g_ref[b[0] : b[0] + QB, lanes]) for b in blocks]
        loaded.append((q2, g2, k_ref[:, lanes].T))
        v_all = v_ref[:, lanes]
        grads.append([nt(v_all[b[1] : b[2]], g) for b, g in zip(blocks, g2)])
    slopes = []
    for h in range(group):
        own = []
        for gp, (_, low, high, packed) in zip(grads[h], blocks):
            p = p_ref[h, packed : packed + high - low, :].astype(F32)
            weighted = p * gp
            inner = jnp.sum(weighted, axis=0, keepdims=True)
            own.append((weighted - p * inner).astype(BF16))
        slopes.append(own)

    def gather(parts):
        out = []
        for block in range(len(blocks)):
            total = None
            for part, (_, low, high, _) in zip(parts, blocks):
                base = block * QB - low
                if 0 <= base < high - low:
                    piece = part[base : base + QB]
                    total = piece if total is None else total + piece
            out.append(total)
        return jnp.concatenate(out, axis=0)

    for h in range(group):
        lanes = slice(h * PW, (h + 1) * PW)
        q2, g2, k_turned = loaded[h]
        dq = [nn(k_turned[:, b[1] : b[2]], s) for b, s in zip(blocks, slopes[h])]
        dv = [nn(p_ref[h, b[3] : b[3] + b[2] - b[1], :], g) for b, g in zip(blocks, g2)]
        dk = [nn(s, q) for s, q in zip(slopes[h], q2)]
        turned = [pick_heads((part * scale).astype(BF16)) for part in dq]
        out_ref[0, :, lanes] = jnp.concatenate(turned, axis=0)
        out_ref[1, :, lanes] = (gather(dk) * scale).astype(BF16)
        out_ref[2, :, lanes] = gather(dv).astype(BF16)


def attend_back(qkv, grad_context, probs, rows, length, first, pairs):
    _, packed = windows(length)
    group = 2
    steps = pairs // group
    base = first // group
    width = group * PW

    def block(part):
        return pl.BlockSpec((length, width), lambda r, h: (r, part * (D // width) + base + h))

    return pl.pallas_call(
        attend_back_kernel,
        name="attend_back",
        grid=(rows, steps),
        in_specs=[
            block(0),
            block(1),
            block(2),
            block(0),
            pl.BlockSpec((None, group, packed, 2 * QB), lambda r, h: (r, base + h, 0, 0)),
        ],
        out_specs=pl.BlockSpec((3, length, width), lambda r, h: (0, r, h)),
        out_shape=shape_of((3, rows * length, pairs * PW), BF16),
        cost_estimate=took(2.0 * pairs),
        compiler_params=params(20),
    )(*far(qkv, qkv, qkv), grad_context, *far(probs))


def hidden_kernel(da, db, wqkv, ga, out):
    m = 512
    for i in range(ga.shape[0] // m):
        rows = slice(i * m, (i + 1) * m)
        total = ga[rows, :].astype(F32)
        for part in range(3):
            both = jnp.concatenate([da[part, rows, :], db[part, rows, :]], axis=1)
            total = total + nt(both, wqkv[:, part * D : (part + 1) * D])
        out[rows, :] = total.astype(BF16)


def hidden_stage(da, db, wqkv, ga):
    return pl.pallas_call(
        hidden_kernel,
        name="hidden_grad",
        in_specs=[vspec()] * 4,
        out_specs=vspec(),
        out_shape=shape_of(ga.shape, BF16),
        cost_estimate=took(5.7),
        compiler_params=params(22),
    )(da, db, wqkv, ga)


def place_of(half, quarter, owner):
    c, y, z0, z1 = owner & 1, (owner >> 1) & 1, (owner >> 2) & 1, owner >> 3
    order = (quarter, y, z0, z1, c) if half == 0 else (y, z0, z1, quarter, c)
    out = 0
    for bit in order:
        out = 2 * out + bit
    return out


def lanes_of(width):
    most = 128 if width <= 256 else 256
    return [(low, min(most, width - low)) for low in range(0, width, most)]


def half_shapes(width):
    shapes = [shape_of((32, 48, width), BF16)]
    return shapes + [shape_of((32, 48, n), BF16) for _, n in lanes_of(width)]


def store_piece(first, keep, sends, quarter, owner, piece_a, piece_b):
    at_a, at_b = place_of(0, quarter, owner), place_of(1, quarter, owner)
    keep[jnp.where(first, at_a, at_b)] = jnp.where(first, piece_a, piece_b)
    other = jnp.where(first, piece_b, piece_a)
    at = jnp.where(first, at_b, at_a)
    for send, (low, n) in zip(sends, lanes_of(keep.shape[2])):
        send[at] = other[:, low : low + n]


def down_kernel(idx, act, gb, keep, *sends):
    first = idx[2] == 0
    n = 768

    def product(j):
        return tn(act[:, j * n : (j + 1) * n], gb[...])

    ahead = product(0)
    for j in range(FF // n):
        total = ahead.astype(BF16)
        if j + 1 < FF // n:
            ahead = product(j + 1)
        for local in range(4):
            for quarter in range(2):
                base = local * 192 + quarter * 48
                a, b = total[base : base + 48], total[base + 96 : base + 144]
                store_piece(first, keep, sends, quarter, 4 * j + local, a, b)


def down_stage(idx, act, gb):
    shapes = half_shapes(D)
    return pl.pallas_call(
        down_kernel,
        name="grad_w_down",
        in_specs=[sspec(), vspec(), vspec()],
        out_specs=[vspec()] * len(shapes),
        out_shape=shapes,
        cost_estimate=took(7.5),
        compiler_params=params(22),
    )(idx, act, gb)


def in_kernel(idx, n1, gp, vec_o, keep, *refs):
    sends, turned = refs[:-1], refs[-1]
    first = idx[2] == 0
    turned[...] = n1[...].T

    def products(quarter):
        out = []
        for half in range(2):
            j = 2 * half + quarter
            out.append(nn(turned[...], gp[:, j * D : (j + 1) * D]))
        return out

    ahead = products(0)
    for quarter in range(2):
        a, b = [part.astype(BF16) for part in ahead]
        if quarter == 0:
            ahead = products(1)
        for owner in range(16):
            rows = slice(owner * 48, (owner + 1) * 48)
            store_piece(first, keep, sends, quarter, owner, a[rows], b[rows])
    vec_o[...] = jnp.sum(gp[...].astype(F32), axis=0, keepdims=True)


def in_stage(idx, n1, gp):
    shapes = half_shapes(D)
    return pl.pallas_call(
        in_kernel,
        name="grad_w_in",
        in_specs=[sspec(), vspec(), vspec()],
        out_specs=[vspec()] * (1 + len(shapes)),
        out_shape=[shape_of((1, FF), F32)] + shapes,
        scratch_shapes=[VMEM((D, n1.shape[0]), BF16)],
        cost_estimate=took(7.4),
        compiler_params=params(24),
    )(idx, n1, gp)


WIDE, NARROW = 640, 256


def store_all(first, keep, send, whole, width):
    for quarter in range(2):
        a = whole[:, quarter * width : (quarter + 1) * width]
        b = whole[:, (2 + quarter) * width : (3 + quarter) * width]
        for owner in range(16):
            rows = slice(owner * 48, (owner + 1) * 48)
            store_piece(first, keep, send, quarter, owner, a[rows], b[rows])


def wide_kernel(idx, hid, da, ctx, ga, turned_o, keep, *refs):
    sends, whole = refs[:-1], refs[-1]
    n = da.shape[2]
    turned_o[...] = hid[...].T
    for part in range(3):
        whole[:, part * n : (part + 1) * n] = nn(turned_o[...], da[part]).astype(BF16)
    whole[:, 3 * n : 3 * n + D] = tn(ctx[...], ga[...]).astype(BF16)
    whole[:, 3 * n + D :] = jnp.zeros((D, 4 * WIDE - 3 * n - D), BF16)
    store_all(idx[2] == 0, keep, sends, whole, WIDE)


def wide_stage(idx, hid, da, ctx, ga):
    shapes = half_shapes(WIDE)
    return pl.pallas_call(
        wide_kernel,
        name="grad_w_wide",
        in_specs=[sspec()] + [vspec()] * 4,
        out_specs=[vspec()] * (1 + len(shapes)),
        out_shape=[shape_of((D, hid.shape[0]), BF16)] + shapes,
        scratch_shapes=[VMEM((D, 4 * WIDE), BF16)],
        cost_estimate=took(6),
        compiler_params=params(24),
    )(idx, hid, da, ctx, ga)


def narrow_kernel(idx, turned, da, db, vec1, vec2, bias, keep, *refs):
    send, (whole, sums_s) = refs[:-2], refs[-2:]
    n = db.shape[2]
    for part in range(3):
        whole[:, part * n : (part + 1) * n] = nn(turned[...], db[part]).astype(BF16)
    sums_s[...] = jnp.zeros_like(sums_s)
    sums_s[2:5, :] = vec1[0:3, :]
    sums_s[5:8, :] = vec2[0:3, :]
    for row, part in ((0, 0), (1, 2)):
        for base, grads in ((0, da), (D - n, db)):
            lanes = slice(base, base + grads.shape[2])
            total = jnp.sum(grads[part].astype(F32), axis=0, keepdims=True)
            sums_s[row : row + 1, lanes] = total
    small = sums_s[...].T
    groups = [bias[:, i * 384 : (i + 1) * 384] for i in range(FF // 384)]
    folded = jnp.concatenate(groups, axis=0)
    turned_bias = [folded[:, i * 48 : (i + 1) * 48].T for i in range(8)]
    lane = lax.broadcasted_iota(jnp.int32, (48, 128), 1)
    for owner in range(16):
        own = small[owner * 48 : (owner + 1) * 48]
        for k in range(4):
            column = turned_bias[4 * (owner % 2) + k][:, owner // 2 : owner // 2 + 1]
            own = jnp.where(lane == 8 + k, column, own)
        whole[owner * 48 : (owner + 1) * 48, 3 * n : 3 * n + 128] = own.astype(BF16)
    whole[:, 3 * n + 128 :] = jnp.zeros((D, 4 * NARROW - 3 * n - 128), BF16)
    store_all(idx[2] == 0, keep, send, whole, NARROW)


def narrow_stage(idx, turned, da, db, vec1, vec2, bias):
    return pl.pallas_call(
        narrow_kernel,
        name="grad_w_narrow",
        in_specs=[sspec()] + [vspec()] * 6,
        out_specs=[vspec()] * len(half_shapes(NARROW)),
        out_shape=half_shapes(NARROW),
        scratch_shapes=[VMEM((D, 4 * NARROW), BF16), VMEM((128, D), F32)],
        cost_estimate=took(2.4),
        compiler_params=params(22),
    )(idx, turned, da, db, vec1, vec2, bias)


def swap_dp(value, flip):
    devices = lax.axis_size("dp")
    return lax.ppermute(value, "dp", [(i, i ^ flip) for i in range(devices)])


def swap_twin(value):
    return lax.ppermute(value, "twin", [(0, 1), (1, 0)])


TWIN = 16
ROUTES = ((TWIN, 2, 4, 8, TWIN), (2, 4, 8, TWIN, TWIN))


def step_swap(value, step):
    pairs = [(i, i ^ ROUTES[i & 1][step]) for i in range(2 * TWIN)]
    return lax.ppermute(value, ("twin", "dp"), pairs)


def plus(*values):
    total = values[0].astype(F32)
    for value in values[1:]:
        total = total + value.astype(F32)
    return total.astype(BF16)


def call_small(kernel, name, idx, operands, outs):
    return pl.pallas_call(
        kernel,
        name=name,
        in_specs=[sspec()] + [vspec()] * len(operands),
        out_specs=[vspec()] * len(outs),
        out_shape=[shape_of(shape, dtype) for shape, dtype in outs],
        cost_estimate=took(2.4),
        compiler_params=params(12),
    )(idx, *operands)


def half_kernel(step, idx, keep, recv, keep_o, send_o):
    count = keep_o.shape[0]
    bit = idx[3 + step]
    mine = pl.ds(bit * count, count)
    other = pl.ds((1 - bit) * count, count)
    keep_o[...] = plus(keep[mine], recv[mine])
    send_o[...] = plus(keep[other], recv[other])


def half_step(idx, step, keep, recv):
    count, rows, width = keep.shape
    shape = (count // 2, rows, width)
    kernel = functools.partial(half_kernel, step)
    return call_small(kernel, "sum_" + str(step), idx, (keep, recv), [(shape, BF16)] * 2)


def core_kernel(idx, keep, *refs):
    recvs, (keep_o, send_o) = refs[:-2], refs[-2:]
    bit = idx[3]
    for recv, (low, n) in zip(recvs, lanes_of(keep.shape[3])):
        lanes = slice(low, low + n)
        keep_o[:, :, lanes] = plus(keep[bit, :, :, lanes], recv[bit])
        send_o[:, :, lanes] = plus(keep[1 - bit, :, :, lanes], recv[1 - bit])


def core_step(idx, keep, recvs):
    count, rows, width = keep.shape
    half = count // 2
    pieces = 4
    part = half // pieces

    def spec(n):
        return pl.BlockSpec((2, part, rows, n), lambda i: (0, i, 0, 0))

    return pl.pallas_call(
        core_kernel,
        name="sum_core",
        grid=(pieces,),
        in_specs=[sspec(), spec(width)] + [spec(n) for _, n in lanes_of(width)],
        out_specs=[pl.BlockSpec((part, rows, width), lambda i: (i, 0, 0))] * 2,
        out_shape=[shape_of((half, rows, width), BF16)] * 2,
        cost_estimate=took(1.7),
        compiler_params=params(10),
    )(
        idx,
        keep.reshape(2, half, rows, width),
        *[recv.reshape(2, half, rows, recv.shape[2]) for recv in recvs],
    )


def own_kernel(idx, keep, recv, out):
    out[...] = plus(keep[...], recv[...])


def turn_kernel(idx, own, other, keep_o, send_o):
    twin, core = idx[0], idx[2]
    keep_o[twin] = own[core]
    keep_o[1 - twin] = other[core]
    send_o[twin] = own[1 - core]
    send_o[1 - twin] = other[1 - core]


class Order:
    def __init__(self):
        self.last = None

    def after(self, value, *others):
        if self.last is None:
            return value
        return lax.optimization_barrier((value, self.last) + others)[0]

    def done(self, value):
        self.last = value
        return value


class Exchange:
    def __init__(self, order, idx, keep, sends):
        self.order, self.idx, self.step = order, idx, 0
        self.keep, self.recv = keep, [swap_dp(send, 1) for send in sends]

    def advance(self):
        idx, order = self.idx, self.order
        keep, recv = order.after(self.keep), self.recv
        if self.step == 0:
            keep, send = core_step(idx, keep, recv)
            recv = step_swap(send, 0)
        elif self.step < 4:
            keep, send = half_step(idx, self.step, keep, recv)
            recv = step_swap(send, self.step)
        elif self.step == 4:
            shape = keep.shape
            (keep,) = call_small(own_kernel, "sum_4", idx, (keep, recv), [(shape, BF16)])
            recv = step_swap(keep, 4)
        else:
            shape = keep.shape
            keep, send = call_small(turn_kernel, "turn", idx, (keep, recv), [(shape, BF16)] * 2)
            recv = swap_dp(send, 1)
        order.done(keep)
        self.keep, self.recv = keep, recv
        self.step += 1

    def result(self):
        return self.keep, self.recv


def bring_kernel(*refs):
    del refs


def bring(values):
    return carry_call(bring_kernel, "bring", 1.2, 4, (), [], [], [], values)


def gather_units(unit, wanted):
    flips = [(0, 0)]
    for flip in (8, 4):
        unit = jnp.concatenate([unit, swap_dp(unit, flip)], axis=0)
        flips = flips + [(t, f ^ flip) for t, f in flips]
    wanted = bring((lax.optimization_barrier((wanted[0], unit))[0],) + wanted[1:])
    pairs = [(i, i ^ (TWIN + 2)) for i in range(2 * TWIN)]
    corner = lax.ppermute(unit, ("twin", "dp"), pairs)
    unit = jnp.concatenate([unit, swap_dp(unit, 2), swap_twin(unit), corner], axis=0)
    flips = [(t ^ a, f ^ b) for a, b in ((0, 0), (0, 2), (1, 0), (1, 2)) for t, f in flips]
    return ((unit, swap_dp(unit, 1)), (flips, [(t, f ^ 1) for t, f in flips])), wanted


def four_quarters(idx, keep, recv):
    first = idx[2] == 0
    low = [jnp.where(first, keep[i], recv[i]) for i in range(2)]
    high = [jnp.where(first, recv[i], keep[i]) for i in range(2)]
    return low + high


def final_in_kernel(idx, keep, recv, out):
    for i, part in enumerate(four_quarters(idx, keep, recv)):
        out[:, i * D : (i + 1) * D] = part.astype(F32)


def final_down_kernel(idx, keep, recv, out):
    for i, part in enumerate(four_quarters(idx, keep, recv)):
        out[i * 48 : (i + 1) * 48, :] = part.astype(F32)


def final_last_kernel(idx, wide_k, wide_r, narrow_k, narrow_r, qkv_o, out_o, *vec_o):
    wide = jnp.concatenate(four_quarters(idx, wide_k, wide_r), axis=1).astype(F32)
    narrow = jnp.concatenate(four_quarters(idx, narrow_k, narrow_r), axis=1).astype(F32)
    low, high = 2 * D // 3, D // 3
    for part in range(3):
        qkv_o[:, part * D : part * D + low] = wide[:, part * low : (part + 1) * low]
        qkv_o[:, part * D + low : (part + 1) * D] = narrow[:, part * high : (part + 1) * high]
    out_o[...] = wide[:, 3 * low : 3 * low + D]
    small = narrow[:, 3 * high : 3 * high + 128]
    turned = jnp.concatenate([small, jnp.zeros((80, 128), F32)], axis=0).T
    for i in range(8):
        vec_o[i][...] = turned[i, :48]
    whole = jnp.concatenate([turned[8 + i : 9 + i, :48] for i in range(4)], axis=1)
    vec_o[8][...] = whole.reshape(192)


def finish(order, idx, kernel, name, chunks, outs):
    operands = [value for chunk in chunks for value in chunk.result()]
    operands[0] = order.after(operands[0])
    out = call_small(kernel, name, idx, operands, outs)
    order.done(out[0])
    return out


def add_low(*parts):
    return lax.optimization_barrier(plus(*parts))


def digits_of(devices):
    out, rest = [], devices // 2
    while rest > 1:
        size = 4 if rest % 4 == 0 else 2
        out.append(size)
        rest //= size
    return out


def pick(value, index, axis):
    return lax.dynamic_index_in_dim(value, index, axis, keepdims=False)


def scatter(grad):
    devices = lax.axis_size("dp")
    me = lax.axis_index("dp")
    value = grad.reshape(devices, grad.shape[0] // devices, grad.shape[1])
    unit = 1
    for size in [2] + digits_of(devices):
        mine = (me // unit) % size
        view = value.reshape((value.shape[0] // size, size) + value.shape[1:])
        parts = [pick(view, mine, 1)]
        for flip in range(1, size):
            parts.append(swap_dp(pick(view, mine ^ flip, 1), flip * unit))
        value = add_low(*parts)
        unit *= size
    value = value[0]
    return value.astype(F32) + swap_twin(value).astype(F32)


SEQUENCE = (
    "down", "pre", "d", "in", "normed", "d", "i", "attend_a", "d", "wide", "i", "attend_b", "w",
    "d", "narrow", "i", "n", "hidden", "d", "w", "n", "i", "d", "w", "n", "i", "final_d", "w",
    "n", "i", "final_i", "w", "n", "w", "n",
)


def body(
    hidden,
    segment_ids,
    targets,
    w_qkv,
    b_query,
    b_value,
    w_out,
    b_out,
    ln1_gain,
    ln1_bias,
    w_in,
    b_in,
    w_down,
    b_down,
    ln2_gain,
    ln2_bias,
):
    row_count, length, width = hidden.shape
    tokens = row_count * length
    devices = lax.axis_size("dp")
    everyone = lax.axis_size(("twin", "dp"))
    me = lax.axis_index("dp")
    twin = lax.axis_index("twin")
    core, y, z0, z1 = me & 1, (me >> 1) & 1, (me >> 2) & 1, me >> 3
    first = core == 0
    bits = [jnp.where(first, a, b) for a, b in ((twin, y), (y, z0), (z0, z1), (z1, twin))]
    idx = jnp.stack([twin, me, core] + bits).astype(jnp.int32)
    weights = (w_qkv, b_query, b_value, w_out, b_out, ln1_gain, ln1_bias)
    weights += (w_in, b_in, w_down, b_down, ln2_gain, ln2_bias)
    qkv, probs, ctx, n1, xh1, rs1, act, dg, xh2, rs2, unit, unitf, inv = forward(
        hidden, segment_ids, weights
    )
    sentences = row_count * SEG
    unit = unit.reshape(sentences, width)
    direct = devices == TWIN and sentences == 16
    if direct:
        gathered, (xh2, rs2) = gather_units(unit, (xh2, rs2))
    else:
        gathered = ((lax.all_gather(unit, ("twin", "dp"), axis=0, tiled=True),), (None,))
    losses, gb, vec2, act_near = loss_stage(
        idx,
        gathered,
        targets.reshape(1, -1),
        unitf.reshape(sentences, width),
        inv.reshape(sentences, 128),
        segment_ids,
        ln2_gain,
        xh2,
        rs2,
        (act,),
    )
    share = losses.shape[1] // everyone
    losses = lax.dynamic_slice_in_dim(
        losses[0], lax.axis_index(("twin", "dp")) * share, share, 0
    )
    flat = hidden.reshape(tokens, width)
    if direct:
        order = Order()
        chunks = {}

        def begin(name, keep, sends):
            order.done(keep)
            chunks[name] = Exchange(order, idx, keep, sends)

        for stage in SEQUENCE:
            if stage == "down":
                halves_d = down_stage(idx, act_near, order.after(gb))
                begin("d", halves_d[0], halves_d[1:])
            elif stage == "pre":
                near = (n1, xh1, rs1)
                gp, *near = pre_stage(order.after(gb), w_down, dg, near)
                order.done(gp)
            elif stage == "in":
                sums, *halves_in = in_stage(idx, near[0], order.after(gp))
                begin("i", halves_in[0], halves_in[1:])
            elif stage == "normed":
                ga, gc, vec1, *later = normed_stage(
                    order.after(gp), w_in, gb, near[1], near[2], ln1_gain, w_out, (flat, ctx)
                )
                order.done(ga)
            elif stage == "attend_a":
                da = order.done(attend_back(qkv, order.after(gc), probs, row_count, length, 0, 4))
            elif stage == "attend_b":
                db = order.done(attend_back(qkv, order.after(gc), probs, row_count, length, 4, 2))
            elif stage == "wide":
                turned, *halves_w = wide_stage(idx, later[0], order.after(da), later[1], ga)
                begin("w", halves_w[0], halves_w[1:])
            elif stage == "narrow":
                halves_n = narrow_stage(idx, turned, da, order.after(db), vec1, vec2, sums)
                begin("n", halves_n[0], halves_n[1:])
            elif stage == "hidden":
                hidden_grad = order.done(hidden_stage(da, order.after(db), w_qkv, ga))
            elif stage == "final_d":
                outs = [((192, D), F32)]
                (grad_w_down,) = finish(order, idx, final_down_kernel, stage, [chunks["d"]], outs)
            elif stage == "final_i":
                outs = [((48, FF), F32)]
                (grad_w_in,) = finish(order, idx, final_in_kernel, stage, [chunks["i"]], outs)
            else:
                chunks[stage].advance()
        wide, narrow = chunks["w"], chunks["n"]
        shapes = [((48, 3 * D), F32), ((48, D), F32)] + [((48,), F32)] * 8 + [((192,), F32)]
        grad_w_qkv, grad_w_out, *vecs, grad_b_in = finish(
            order, idx, final_last_kernel, "final_last", [wide, narrow], shapes
        )
    else:
        gp, _ = pre_stage(gb, w_down, dg, (n1,))
        ga, gc, vec1, _ = normed_stage(gp, w_in, gb, xh1, rs1, ln1_gain, w_out, (ctx,))
        da = attend_back(qkv, gc, probs, row_count, length, 0, 4)
        db = attend_back(qkv, gc, probs, row_count, length, 4, 2)
        hidden_grad = hidden_stage(da, db, w_qkv, ga)
        dqkv = jnp.concatenate([da, db], axis=2)
        grad_w_down = scatter(tn(act, gb).astype(BF16))
        grad_w_in = scatter(tn(n1, gp).astype(BF16))
        wide = jnp.concatenate([dqkv[0], dqkv[1], dqkv[2]], axis=1)
        grad_w_qkv = scatter(tn(flat, wide).astype(BF16))
        grad_w_out = scatter(tn(ctx, ga).astype(BF16))
        sums = jnp.sum(dqkv, axis=1, dtype=F32)
        vec = jnp.concatenate([sums[0:1], sums[2:3], vec1[:3], vec2[:3]])
        vec = scatter(jnp.pad(vec, ((0, 120), (0, 0))).T.astype(BF16)).T
        vecs = [vec[i] for i in range(8)]
        bias = jnp.sum(gp, axis=0, dtype=F32)
        grad_b_in = scatter(jnp.broadcast_to(bias[:, None], (FF, 128)).astype(BF16))[:, 0]
    return (
        losses,
        hidden_grad.reshape(row_count, length, width),
        grad_w_qkv,
        vecs[0],
        vecs[1],
        grad_w_out,
        vecs[2],
        vecs[3],
        vecs[4],
        grad_w_in,
        grad_b_in,
        grad_w_down,
        vecs[5],
        vecs[6],
        vecs[7],
    )


def solution(mesh):
    whole = (P(),) * 14
    placed = (P(("twin", "dp"), None, None), P(("twin", "dp"), None)) + whole
    return jax.shard_map(
        body,
        mesh=mesh,
        in_specs=placed,
        out_specs=(
            P(("twin", "dp")),
            P(("twin", "dp"), None, None),
            P("dp", None),
            P("dp"),
            P("dp"),
            P("dp", None),
            P("dp"),
            P("dp"),
            P("dp"),
            P("dp", None),
            P("dp"),
            P("dp", None),
            P("dp"),
            P("dp"),
            P("dp"),
        ),
        check_vma=False,
    )
```
